256 devices in a mesh: span: 16 (over x, y), plane: 16 (over z, core).
Axes of the slice: x: 4, y: 4, z: 8, core: 2. Of those that a mesh axis runs over, the one named last changes fastest.
Arguments:
- state: float32 [512, 80, 640], P('span', 'plane'), may hold values from -8 to 8, as said below
- wall_tag: int32 [128], replicated, may hold values 0 or 1
Outputs:
- new_state: float32 [512, 80, 640], P('span', 'plane')
The draws below stay inside these ranges and needn't reach their ends.
Inputs may be any that keep to these rules, and one draw needn't show every extreme that they name: `state`: spectral coefficients of the conserved variable.
All inputs are finite; a program needn't handle non-finite values.
Results may differ from the reference program's by a relative error of at most 0.0001.
Values sent between devices are 32-bit elements; how exact they have to be, the bound alone decides.
No kernel may reach another device: no remote copies, remote signals or barrier semaphores. Data moves between devices by JAX's collectives and lax.ppermute only.
A program may use at most 64 MiB of HBM per device.

```python
import math
import jax
import jax.numpy as jnp
import numpy as np
from jax import lax

KMODES = 256
MODES = 512
PLANES = 768
GX = 128
ITERS = 3
ROWS = 80
COLS = 640


def draw_state(key, part):
    values = jnp.clip(jax.random.normal(key, (MODES, ROWS, COLS), jnp.float32), -4.0, 4.0)
    height = jnp.arange(ROWS, dtype=jnp.float32) / (ROWS - 1)
    profile = 0.6 * jnp.exp(height * math.log(3.0))
    return values * profile[None, :, None]


def set_ends(drawn, rng, smallest, largest):
    index_at = [jax.random.randint(jax.random.fold_in(rng, axis), (), 0, length) for axis, length in enumerate(drawn.shape)]
    longest = drawn.shape.index(max(drawn.shape))
    next_to = index_at[:longest] + [(index_at[longest] + 1) % drawn.shape[longest]] + index_at[longest + 1:]
    return drawn.at[tuple(index_at)].set(smallest).at[tuple(next_to)].set(largest)


def setup_inputs(seed: int = 0) -> dict:
    keys = jax.random.split(jax.random.key(seed), 3)
    return {
        "state": draw_state(jax.random.fold_in(keys[2], 71), 0),
        "wall_tag": set_ends((jax.random.randint(keys[1], (GX,), 0, 2) < 1).astype(jnp.int32), jax.random.fold_in(keys[1], 1), 0, 1),
    }


highest = lax.Precision.HIGHEST
step_size = 0.03
viscous = 0.05
span_stiff = 4.0

def gll_tables():
    abscissae = np.array([-1.0, -math.sqrt(3.0 / 7.0), 0.0, math.sqrt(3.0 / 7.0), 1.0])
    weights = np.array([0.1, 49.0 / 90.0, 32.0 / 45.0, 49.0 / 90.0, 0.1])
    squared = abscissae * abscissae
    legendre = (35.0 * squared * squared - 30.0 * squared + 3.0) / 8.0
    identity = np.eye(5)
    spacing = abscissae[:, None] - abscissae[None, :] + identity
    differ = np.where(identity > 0, 0.0, legendre[:, None] / legendre[None, :] / spacing)
    differ[0, 0] = -5.0
    differ[4, 4] = 5.0
    stiffness = differ.T @ (weights[:, None] * differ)
    return (jnp.asarray(differ, dtype=jnp.float32), jnp.asarray(weights, dtype=jnp.float32), jnp.asarray(stiffness, dtype=jnp.float32))

def inverse_basis(plane_ids, kmodes, planes):
    wavenumber = jnp.arange(kmodes, dtype=jnp.int32)
    phase_index = plane_ids[:, None] * wavenumber[None, :] % planes
    angles = phase_index.astype(jnp.float32) * (2.0 * math.pi / planes)
    basis = jnp.stack([jnp.cos(angles), jnp.sin(angles)], axis=2).reshape(plane_ids.shape[0], 2 * kmodes)
    return basis / math.sqrt(kmodes)

def forward_basis(kmodes, planes):
    wavenumber = jnp.arange(kmodes, dtype=jnp.int32)
    plane_ids = jnp.arange(planes, dtype=jnp.int32)
    phase_index = wavenumber[:, None] * plane_ids[None, :] % planes
    angles = phase_index.astype(jnp.float32) * (2.0 * math.pi / planes)
    factor = jnp.where(wavenumber == 0, 1.0, 2.0).astype(jnp.float32) * (math.sqrt(kmodes) / planes)
    basis = jnp.stack([jnp.cos(angles) * factor[:, None], jnp.sin(angles) * factor[:, None]], axis=1)
    return basis.reshape(2 * kmodes, planes)

def combine_spectra(inner_part, span_part, kmodes):
    shape = inner_part.shape
    inner_pair = inner_part.reshape((kmodes, 2) + shape[1:])
    span_pair = span_part.reshape((kmodes, 2) + shape[1:])
    ratio = (jnp.arange(kmodes, dtype=jnp.float32) / kmodes)[:, None, None]
    cos_part = inner_pair[:, 0] - ratio * span_pair[:, 1]
    sin_part = inner_pair[:, 1] + ratio * span_pair[:, 0]
    return jnp.stack([cos_part, sin_part], axis=1).reshape(shape)

def two_point(left_state, right_state):
    mean_part = (left_state * left_state + left_state * right_state + right_state * right_state) / 6.0
    speed = jnp.maximum(jnp.abs(left_state), jnp.abs(right_state))
    return mean_part - 0.5 * speed * (right_state - left_state)

def split_form(physical, below_row, above_row, differ):
    planes, row_count, col_count = physical.shape
    square = physical * physical
    slope_x = jnp.einsum('ai,prxi->prxa', differ, physical.reshape(planes, row_count, col_count // 5, 5), precision=highest).reshape(planes, row_count, col_count)
    square_x = jnp.einsum('ai,prxi->prxa', differ, square.reshape(planes, row_count, col_count // 5, 5), precision=highest).reshape(planes, row_count, col_count)
    slope_y = jnp.einsum('aj,pejc->peac', differ, physical.reshape(planes, row_count // 5, 5, col_count), precision=highest).reshape(planes, row_count, col_count)
    square_y = jnp.einsum('aj,pejc->peac', differ, square.reshape(planes, row_count // 5, 5, col_count), precision=highest).reshape(planes, row_count, col_count)
    volume = (square_x + physical * slope_x + square_y + physical * slope_y) / 3.0
    half_square = 0.5 * square
    col_node = (jnp.arange(col_count) % 5)[None, None, :]
    row_node = (jnp.arange(row_count) % 5)[:, None]
    left_side = jnp.roll(physical, 1, axis=2)
    right_side = jnp.roll(physical, -1, axis=2)
    surface_rhs = -volume
    surface_rhs = surface_rhs + jnp.where(col_node == 0, 10.0 * (two_point(left_side, physical) - half_square), 0.0)
    surface_rhs = surface_rhs - jnp.where(col_node == 4, 10.0 * (two_point(physical, right_side) - half_square), 0.0)
    surface_rhs = surface_rhs + jnp.where(row_node == 0, 10.0 * (two_point(below_row, physical) - half_square), 0.0)
    surface_rhs = surface_rhs - jnp.where(row_node == 4, 10.0 * (two_point(physical, above_row) - half_square), 0.0)
    return (surface_rhs, half_square)

def join_columns(values):
    mode_count, row_count, col_count = values.shape
    blocks = values.reshape(mode_count, row_count, col_count // 5, 5)
    pair_sum = blocks[..., 4] + jnp.roll(blocks[..., 0], -1, axis=2)
    blocks = jnp.concatenate([jnp.roll(pair_sum, 1, axis=2)[..., None], blocks[..., 1:4], pair_sum[..., None]], axis=3)
    return blocks.reshape(mode_count, row_count, col_count)

def join_rows(joined, below_row, above_row):
    row_node = (jnp.arange(joined.shape[1]) % 5)[:, None]
    return joined + jnp.where(row_node == 0, below_row, 0.0) + jnp.where(row_node == 4, above_row, 0.0)

def assemble_whole(values):
    joined = join_columns(values)
    zero_row = jnp.zeros_like(joined[:, :1])
    below_row = jnp.concatenate([zero_row, joined[:, :-1]], axis=1)
    above_row = jnp.concatenate([joined[:, 1:], zero_row], axis=1)
    return join_rows(joined, below_row, above_row)

def local_helmholtz(values, shift_coeff, row_weight, col_weight, stiffness):
    mode_count, row_count, col_count = values.shape
    stiff_x = jnp.einsum('ai,mrxi->mrxa', stiffness, values.reshape(mode_count, row_count, col_count // 5, 5), precision=highest).reshape(mode_count, row_count, col_count)
    stiff_y = jnp.einsum('aj,mejc->meac', stiffness, values.reshape(mode_count, row_count // 5, 5, col_count), precision=highest).reshape(mode_count, row_count, col_count)
    mass_diag = row_weight[:, None] * col_weight[None, :]
    return shift_coeff * mass_diag * values + viscous * (row_weight[:, None] * stiff_x + col_weight[None, :] * stiff_y)

def weighted_dot(first_vec, second_vec, inv_mult):
    return lax.optimization_barrier(jnp.sum(first_vec * second_vec * inv_mult, axis=(1, 2)))

def reference(state, wall_tag):
    differ, weights, stiffness = gll_tables()
    mode_count, row_count, col_count = state.shape
    inverse = inverse_basis(jnp.arange(PLANES, dtype=jnp.int32), KMODES, PLANES)
    physical = jnp.einsum('pm,mrc->prc', inverse, state, precision=highest)
    tag_cols = jnp.repeat(wall_tag, 5)[None, :]
    mirror = jnp.where(tag_cols == 1, -physical[:, 0, :], physical[:, 0, :])
    below_row = jnp.concatenate([mirror[:, None, :], physical[:, :-1]], axis=1)
    above_row = jnp.concatenate([physical[:, 1:], physical[:, -1:]], axis=1)
    surface_rhs, half_square = split_form(physical, below_row, above_row, differ)
    forward = forward_basis(KMODES, PLANES)
    inner_part = jnp.einsum('mp,prc->mrc', forward, surface_rhs, precision=highest)
    span_part = jnp.einsum('mp,prc->mrc', forward, half_square, precision=highest)
    tendency = combine_spectra(inner_part, span_part, KMODES)
    predicted = state + step_size * tendency
    wavenumber = (jnp.arange(mode_count, dtype=jnp.int32) // 2).astype(jnp.float32) / KMODES
    shift_coeff = (1.0 + span_stiff * wavenumber * wavenumber)[:, None, None]
    row_weight = jnp.tile(weights, row_count // 5)
    col_weight = jnp.tile(weights, col_count // 5)
    row_node = jnp.arange(row_count) % 5
    row_ids = jnp.arange(row_count)
    row_half = jnp.where(((row_node == 0) | (row_node == 4)) & (row_ids != 0) & (row_ids != row_count - 1), 0.5, 1.0)
    col_node = jnp.arange(col_count) % 5
    col_half = jnp.where((col_node == 0) | (col_node == 4), 0.5, 1.0)
    inv_mult = (row_half[:, None] * col_half[None, :]).astype(jnp.float32)
    load_vec = assemble_whole(row_weight[:, None] * col_weight[None, :] * predicted)
    solution = jnp.zeros_like(load_vec)
    residual = load_vec
    direction = load_vec
    norm_now = weighted_dot(residual, residual, inv_mult)
    for iteration in range(ITERS):
        applied = assemble_whole(local_helmholtz(direction, shift_coeff, row_weight, col_weight, stiffness))
        step_len = (norm_now / weighted_dot(direction, applied, inv_mult))[:, None, None]
        solution = solution + step_len * direction
        residual = residual - step_len * applied
        norm_next = weighted_dot(residual, residual, inv_mult)
        direction = residual + (norm_next / norm_now)[:, None, None] * direction
        norm_now = norm_next
    return solution
```

```python
import math

import jax
import jax.numpy as jnp
import numpy as np
from jax import lax
from jax.experimental import pallas as pl
from jax.experimental.pallas import tpu as pltpu
from jax.sharding import PartitionSpec as P

KMODES = 256
PLANES = 768
HALF = 384
ITERS = 3
GRID = 16
STEP_SIZE = 0.03
VISCOUS = 0.05
SPAN_STIFF = 4.0


def gll_tables():
    abscissae = np.array([-1.0, -math.sqrt(3.0 / 7.0), 0.0, math.sqrt(3.0 / 7.0), 1.0])
    weights = np.array([0.1, 49.0 / 90.0, 32.0 / 45.0, 49.0 / 90.0, 0.1])
    squared = abscissae * abscissae
    legendre = (35.0 * squared * squared - 30.0 * squared + 3.0) / 8.0
    identity = np.eye(5)
    spacing = abscissae[:, None] - abscissae[None, :] + identity
    differ = np.where(identity > 0, 0.0, legendre[:, None] / legendre[None, :] / spacing)
    differ[0, 0] = -5.0
    differ[4, 4] = 5.0
    stiffness = differ.T @ (weights[:, None] * differ)
    return differ, weights, stiffness


DIFFER, WEIGHTS, STIFFNESS = gll_tables()


def split_table(table):
    high = table.astype(np.float32).astype(jnp.bfloat16)
    low = (table - high.astype(np.float64)).astype(np.float32).astype(jnp.bfloat16)
    return jnp.asarray(high), jnp.asarray(low)


def transform_tables():
    plane = np.arange(HALF)
    inverse, forward = [], []
    for parity in range(2):
        k = 2 * np.arange(128) + parity
        angle = (k[:, None] * plane[None, :] % PLANES) * (2.0 * math.pi / PLANES)
        cosine, sine = np.cos(angle), np.sin(angle)
        inverse.append(np.concatenate([cosine, sine]) / math.sqrt(KMODES))
        scale = np.where(k == 0, 1.0, 2.0)[:, None] * math.sqrt(KMODES) / PLANES * STEP_SIZE
        ratio = (k / KMODES)[:, None]
        from_rhs = np.concatenate([cosine, sine]) * np.concatenate([scale, scale])
        from_flux = np.concatenate([-ratio * scale * sine, ratio * scale * cosine])
        forward.append(np.concatenate([from_rhs, from_flux], axis=1))
    return split_table(np.stack(inverse)), split_table(np.stack(forward))


def dot(left, right, contract):
    return lax.dot_general(
        left, right, (contract, ((), ())), preferred_element_type=jnp.float32
    )


def halves(value):
    high = value.astype(jnp.bfloat16)
    low = (value - high.astype(jnp.float32)).astype(jnp.bfloat16)
    return high, low


def thirds(value):
    high = value.astype(jnp.bfloat16)
    rest = value - high.astype(jnp.float32)
    middle = rest.astype(jnp.bfloat16)
    low = (rest - middle.astype(jnp.float32)).astype(jnp.bfloat16)
    return high, middle, low


def dot_split(left, right, contract):
    (left_high, left_low), (right_high, right_low) = left, right
    return (
        dot(left_high, right_low, contract)
        + dot(left_low, right_high, contract)
        + dot(left_high, right_high, contract)
    )


def column_order():
    column = lax.broadcasted_iota(jnp.int32, (640, 128), 0)
    element = lax.broadcasted_iota(jnp.int32, (640, 128), 1)
    tiles = [jnp.where(column == 5 * element + i, 1.0, 0.0).astype(jnp.bfloat16) for i in range(5)]
    return jnp.concatenate(tiles, axis=1)


def exchange_chunks(values):
    values = list(values)
    lane = lax.broadcasted_iota(jnp.int32, values[0].shape, 1)
    for bit in (1, 2, 4, 8):
        upper = (lane & (8 * bit)) != 0
        for a in range(16):
            if a & bit == 0:
                first, second = values[a], values[a | bit]
                values[a] = jnp.where(upper, pltpu.roll(second, 8 * bit, 1), first)
                values[a | bit] = jnp.where(upper, second, pltpu.roll(first, 128 - 8 * bit, 1))
    return values


def pack_kernel(state_ref, out_ref, chunk_ref):
    stacked = jnp.concatenate([state_ref[j] for j in range(5)], axis=0)
    order = column_order()
    contract = ((1,), (0,))
    high, middle, low = thirds(stacked)
    nodes = dot(low, order, contract) + dot(middle, order, contract) + dot(high, order, contract)
    for i in range(5):
        chunk_ref[160 * i : 160 * i + 160, :] = nodes[:, 128 * i : 128 * i + 128]
    chunk = [
        jnp.concatenate(
            [chunk_ref[pl.ds(160 * i + 32 * j + t, 8, stride=4), :] for t in range(4)], axis=0
        )
        for j in range(5)
        for i in range(5)
    ]
    lane = lax.broadcasted_iota(jnp.int32, (32, 128), 1) & 7
    for j in range(5):
        left = pltpu.roll(chunk[j * 5 + 4], 1, 1)
        right = pltpu.roll(chunk[j * 5], 127, 1)
        chunk.append(jnp.where(lane == 0, left, jnp.where(lane == 7, right, 0.0)))
    zero = jnp.zeros((32, 128), jnp.float32)
    chunk = chunk + [zero, zero]
    for half in range(2):
        block = exchange_chunks(chunk[16 * half : 16 * half + 16])
        for d in range(GRID):
            out_ref[d, :, 128 * half : 128 * half + 128] = block[d]


def turn_kernel(modal_ref, nodal_ref, low_ref, high_ref):
    for parity in range(2):
        rows = [
            modal_ref[s, 16 * parity + 8 * t : 16 * parity + 8 * t + 8, :]
            for t in range(2)
            for s in range(GRID)
        ]
        turned = jnp.concatenate(rows, axis=0).T
        nodal_ref[parity] = turned
        low_ref[parity] = turned[0:40]
        high_ref[parity] = turned[160:200]


def synthesize(nodal, high_ref, low_ref):
    part = [
        dot_split(
            halves(nodal[parity]), (high_ref[parity], low_ref[parity]), ((1,), (0,))
        )
        for parity in range(2)
    ]
    return part[0] + part[1], part[0] - part[1]


def two_point(left, right):
    mean = (left * left + left * right + right * right) * (1.0 / 6.0)
    speed = jnp.maximum(jnp.abs(left), jnp.abs(right))
    return mean - 0.5 * speed * (right - left)


def volume_kernel(nodal_ref, high_ref, low_ref, field_ref, rhs_ref, side_ref):
    nodal = [nodal_ref[0], nodal_ref[1]]
    pair = synthesize(nodal, high_ref, low_ref)
    for q in range(2):
        field_ref[:, HALF * q : HALF * q + HALF] = pair[q][0:200]
        side_ref[:, HALF * q : HALF * q + HALF] = pair[q][200:240]
    row = lax.broadcasted_iota(jnp.int32, (8, 128), 0)

    def column(block, carry):
        lanes = pl.ds(pl.multiple_of(block * 128, 128), 128)
        f = [field_ref[8 * n : 8 * n + 8, lanes] for n in range(25)]
        square = [v * v for v in f]
        for j in range(5):
            for i in range(5):
                n = j * 5 + i
                plain = None
                power = None
                for other in range(5):
                    terms = [(DIFFER[i][other], j * 5 + other), (DIFFER[j][other], other * 5 + i)]
                    for weight, m in terms:
                        if weight == 0.0:
                            continue
                        weight = float(weight) / -3.0
                        plain = weight * f[m] if plain is None else plain + weight * f[m]
                        power = weight * square[m] if power is None else power + weight * square[m]
                total = power + f[n] * plain
                own = (i == 4) + (j == 4) - (i == 0) - (j == 0)
                if own:
                    total = total + (5.0 * own) * square[n]
                if i == 0 or i == 4:
                    side = side_ref[8 * j : 8 * j + 8, lanes]
                    if i == 0:
                        left = jnp.where(row == 0, side, pltpu.roll(f[j * 5 + 4], 1, 0))
                        total = total + 10.0 * two_point(left, f[n])
                    else:
                        right = jnp.where(row == 7, side, pltpu.roll(f[j * 5], 7, 0))
                        total = total - 10.0 * two_point(f[n], right)
                rhs_ref[8 * n : 8 * n + 8, lanes] = total
        return carry

    lax.fori_loop(0, PLANES // 128, column, 0)


def forward_kernel(
    modal_ref, field_ref, rhs_ref, below_ref, above_ref, mirror_ref, edge_ref, inverse_high_ref,
    inverse_low_ref, forward_high_ref, forward_low_ref, out_ref, outer_ref,
):
    bottom = edge_ref[0] == 1
    top = edge_ref[1] == 1
    outer = [
        jnp.concatenate([below_ref[parity], above_ref[parity]], axis=0) for parity in range(2)
    ]
    pair = synthesize(outer, inverse_high_ref, inverse_low_ref)
    for q in range(2):
        outer_ref[:, HALF * q : HALF * q + HALF] = pair[q]
    mirror = jnp.concatenate([mirror_ref[...]] * 6, axis=1)
    bottom_rows, top_rows = [], []
    for i in range(5):
        inside = field_ref[8 * i : 8 * i + 8, :]
        below = jnp.where(bottom, mirror * inside, outer_ref[8 * i : 8 * i + 8, :])
        bottom_rows.append(
            rhs_ref[8 * i : 8 * i + 8, :] + 10.0 * two_point(below, inside)
        )
        n = 20 + i
        inside = field_ref[8 * n : 8 * n + 8, :]
        above = jnp.where(top, inside, outer_ref[40 + 8 * i : 48 + 8 * i, :])
        top_rows.append(rhs_ref[8 * n : 8 * n + 8, :] - 10.0 * two_point(inside, above))
    rhs = jnp.concatenate(bottom_rows + [rhs_ref[40:160, :]] + top_rows, axis=0)
    field = field_ref[...]
    flux = 0.5 * field * field
    for parity in range(2):
        if parity == 0:
            folded = [rhs[:, :HALF] + rhs[:, HALF:], flux[:, :HALF] + flux[:, HALF:]]
        else:
            folded = [rhs[:, :HALF] - rhs[:, HALF:], flux[:, :HALF] - flux[:, HALF:]]
        planar = jnp.concatenate(folded, axis=1)
        change = dot_split(
            (forward_high_ref[parity], forward_low_ref[parity]), halves(planar), ((1,), (1,))
        )
        for t in range(2):
            first = 16 * parity + 8 * t
            modal = jnp.concatenate(
                [modal_ref[s, first : first + 8, :] for s in range(GRID)], axis=0
            )
            rows = change[128 * t : 128 * t + 128]
            out_ref[pl.ds(4 * parity + 2 * t, 128, stride=8), :] = modal[:, :128] + rows[:, :128]
            out_ref[pl.ds(4 * parity + 2 * t + 1, 128, stride=8), 0:72] = (
                modal[:, 128:200] + rows[:, 128:200]
            )


def assemble(values):
    values = list(values)
    row = lax.broadcasted_iota(jnp.int32, (32, 128), 0) & 15
    for j in range(5):
        joint = values[j * 5 + 4] + pltpu.roll(values[j * 5], 127, 1)
        values[j * 5 + 4] = joint
        values[j * 5] = pltpu.roll(joint, 1, 1)
    for i in range(5):
        lower, upper = values[i], values[20 + i]
        values[i] = lower + jnp.where(row == 0, 0.0, pltpu.roll(upper, 1, 0))
        values[20 + i] = upper + jnp.where(row == 15, 0.0, pltpu.roll(lower, 31, 0))
    return values


def mode_sum(total):
    sums = [
        jnp.sum(total[16 * t : 16 * t + 16], axis=(0, 1), keepdims=True) for t in range(2)
    ]
    return jnp.concatenate([jnp.broadcast_to(s, (16, 128)) for s in sums], axis=0)


def weighted_square(values):
    row = lax.broadcasted_iota(jnp.int32, (32, 128), 0) & 15
    total = None
    for j in range(5):
        part = None
        for i in range(5):
            v = values[j * 5 + i]
            term = v * v if 0 < i < 4 else 0.5 * (v * v)
            part = term if part is None else part + term
        if j == 0:
            part = jnp.where(row == 0, part, 0.5 * part)
        elif j == 4:
            part = jnp.where(row == 15, part, 0.5 * part)
        total = part if total is None else total + part
    return mode_sum(total)


def solve_kernel(shift_ref, modal_ref, out_ref, residual_ref, direction_ref, applied_ref):
    shift = shift_ref[0, 0]
    predicted = []
    for half in range(2):
        block = [
            jnp.concatenate(
                [
                    modal_ref[pl.ds(64 * s + 2 * t + half, 16, stride=4), :] for t in range(2)
                ],
                axis=0,
            )
            for s in range(GRID)
        ]
        predicted += exchange_chunks(block)
    load = assemble(
        [float(WEIGHTS[n // 5] * WEIGHTS[n % 5]) * predicted[n] for n in range(25)]
    )
    for n in range(25):
        residual_ref[n] = load[n]
        direction_ref[n] = load[n]
    norm = weighted_square(load)
    for step in range(ITERS):
        direction = [direction_ref[n] for n in range(25)]
        total = None
        local = []
        for j in range(5):
            for i in range(5):
                n = j * 5 + i
                mass = float(WEIGHTS[j] * WEIGHTS[i])
                diagonal = VISCOUS * float(
                    WEIGHTS[j] * STIFFNESS[i][i] + WEIGHTS[i] * STIFFNESS[j][j]
                )
                value = (shift * mass + diagonal) * direction[n]
                for other in range(5):
                    if other != i:
                        weight = VISCOUS * float(WEIGHTS[j] * STIFFNESS[i][other])
                        value = value + weight * direction[j * 5 + other]
                    if other != j:
                        weight = VISCOUS * float(WEIGHTS[i] * STIFFNESS[j][other])
                        value = value + weight * direction[other * 5 + i]
                local.append(value)
                term = value * direction[n]
                total = term if total is None else total + term
        length = norm / mode_sum(total)
        if step < ITERS - 1:
            applied = assemble(local)
            residual = [residual_ref[n] - length * applied[n] for n in range(25)]
            fresh = weighted_square(residual)
            ratio = fresh / norm
            norm = fresh
        for n in range(25):
            gain = length * direction[n]
            applied_ref[n] = gain if step == 0 else applied_ref[n] + gain
            if step < ITERS - 1:
                residual_ref[n] = residual[n]
                direction_ref[n] = residual[n] + ratio * direction[n]
    for n in range(25):
        for t in range(2):
            out_ref[pl.ds(25 * t + n, 16, stride=56), :] = applied_ref[n, 16 * t : 16 * t + 16, :]


def unpack_kernel(modal_ref, out_ref, column_ref):
    order = column_order()
    rows = []
    for j in range(5):
        tiles = []
        for i in range(5):
            n = j * 5 + i
            tiles.append(
                jnp.concatenate(
                    [modal_ref[pl.ds(25 * t + n, 16, stride=56), :] for t in range(2)], axis=0
                )
            )
        rows.append(jnp.concatenate(tiles, axis=1))
    stacked = jnp.concatenate(rows, axis=0)
    contract = ((1,), (1,))
    high, middle, low = thirds(stacked)
    columns = dot(low, order, contract) + dot(middle, order, contract) + dot(high, order, contract)
    for i in range(5):
        for j in range(5):
            for t in range(2):
                first = 32 * j + 16 * t
                column_ref[pl.ds(160 * i + 32 * j + t, 16, stride=2), :] = columns[
                    first : first + 16, 128 * i : 128 * i + 128
                ]
    for j in range(5):
        for i in range(5):
            first = 160 * i + 32 * j
            out_ref[j, :, 128 * i : 128 * i + 128] = column_ref[first : first + 32, :]


def call(kernel, name, out_shapes, *args, smem=(), scratch=()):
    vmem = pl.BlockSpec(memory_space=pltpu.VMEM)
    scalar = pl.BlockSpec(memory_space=pltpu.SMEM)
    return pl.pallas_call(
        kernel,
        name=name,
        out_shape=[jax.ShapeDtypeStruct(s, jnp.float32) for s in out_shapes],
        in_specs=[scalar if n in smem else vmem for n in range(len(args))],
        out_specs=[vmem] * len(out_shapes),
        scratch_shapes=list(scratch),
        compiler_params=pltpu.CompilerParams(vmem_limit_bytes=48 * 1024 * 1024),
    )(*args)


def on_device(state, wall_tag):
    (inverse_high, inverse_low), (forward_high, forward_low) = transform_tables()
    span = lax.axis_index("span")
    plane = lax.axis_index("plane")
    last = lax.axis_size("plane") - 1
    wavenumber = (span * GRID + plane).astype(jnp.float32) / KMODES
    shift = (1.0 + SPAN_STIFF * wavenumber * wavenumber).reshape(1, 1)
    edge = jnp.stack([plane == 0, plane == last]).astype(jnp.int32)
    tags = lax.dynamic_slice_in_dim(wall_tag, span * 8, 8)
    mirror = jnp.broadcast_to(jnp.where(tags == 1, -1.0, 1.0).astype(jnp.float32)[:, None], (8, 128))

    (packed,) = call(
        pack_kernel, "pack", [(16, 32, 256)], jnp.transpose(state, (1, 0, 2)),
        scratch=[pltpu.VMEM((800, 128), jnp.float32)],
    )
    modal = lax.all_to_all(packed, "span", 0, 0, tiled=True)
    nodal, low, high = call(
        turn_kernel, "turn", [(2, 256, 256), (2, 40, 256), (2, 40, 256)], modal
    )
    below = lax.ppermute(high, "plane", [(p, (p + 1) % GRID) for p in range(GRID)])
    above = lax.ppermute(low, "plane", [(p, (p - 1) % GRID) for p in range(GRID)])
    field, rhs = call(
        volume_kernel, "volume", [(200, PLANES), (200, PLANES)], nodal, inverse_high, inverse_low,
        scratch=[pltpu.VMEM((40, PLANES), jnp.float32)],
    )
    (sent,) = call(
        forward_kernel, "forward", [(1024, 128)], modal, field, rhs, below, above, mirror, edge,
        inverse_high, inverse_low, forward_high, forward_low, smem=(6,),
        scratch=[pltpu.VMEM((80, PLANES), jnp.float32)],
    )
    predicted = lax.all_to_all(sent.reshape(256, 4, 128), ("span", "plane"), 0, 0, tiled=True)
    (solved,) = call(
        solve_kernel, "solve", [(896, 128)], shift, predicted.reshape(1024, 128), smem=(0,),
        scratch=[pltpu.VMEM((25, 32, 128), jnp.float32)] * 3,
    )
    returned = lax.all_to_all(solved.reshape(16, 56, 128), "plane", 0, 0, tiled=True)
    (columns,) = call(
        unpack_kernel, "unpack", [(5, 32, 640)], returned.reshape(896, 128),
        scratch=[pltpu.VMEM((800, 128), jnp.float32)],
    )
    return jnp.transpose(columns, (1, 0, 2))


def solution(mesh):
    in_specs = (P("span", "plane", None), P())
    out_specs = P("span", "plane", None)
    return jax.shard_map(
        on_device, mesh=mesh, in_specs=in_specs, out_specs=out_specs, check_vma=False
    )
```

```python
import math

import jax
import jax.numpy as jnp
import numpy as np
from jax import lax
from jax.experimental import pallas as pl
from jax.experimental.pallas import tpu as pltpu
from jax.sharding import PartitionSpec as P

KMODES = 256
PLANES = 768
HALF = 384
ITERS = 3
GRID = 16
STEP_SIZE = 0.03
VISCOUS = 0.05
SPAN_STIFF = 4.0


def gll_tables():
    abscissae = np.array([-1.0, -math.sqrt(3.0 / 7.0), 0.0, math.sqrt(3.0 / 7.0), 1.0])
    weights = np.array([0.1, 49.0 / 90.0, 32.0 / 45.0, 49.0 / 90.0, 0.1])
    squared = abscissae * abscissae
    legendre = (35.0 * squared * squared - 30.0 * squared + 3.0) / 8.0
    identity = np.eye(5)
    spacing = abscissae[:, None] - abscissae[None, :] + identity
    differ = np.where(identity > 0, 0.0, legendre[:, None] / legendre[None, :] / spacing)
    differ[0, 0] = -5.0
    differ[4, 4] = 5.0
    stiffness = differ.T @ (weights[:, None] * differ)
    return differ, weights, stiffness


DIFFER, WEIGHTS, STIFFNESS = gll_tables()


def split_table(table):
    high = table.astype(np.float32).astype(jnp.bfloat16)
    low = (table - high.astype(np.float64)).astype(np.float32).astype(jnp.bfloat16)
    return jnp.asarray(high), jnp.asarray(low)


def transform_tables():
    plane = np.arange(HALF)
    inverse, forward = [], []
    for parity in range(2):
        k = 2 * np.arange(128) + parity
        angle = (k[:, None] * plane[None, :] % PLANES) * (2.0 * math.pi / PLANES)
        cosine, sine = np.cos(angle), np.sin(angle)
        inverse.append(np.concatenate([cosine, sine]) / math.sqrt(KMODES))
        scale = np.where(k == 0, 1.0, 2.0)[:, None] * math.sqrt(KMODES) / PLANES * STEP_SIZE
        ratio = (k / KMODES)[:, None]
        from_rhs = np.concatenate([cosine, sine]) * np.concatenate([scale, scale])
        from_flux = np.concatenate([-ratio * scale * sine, ratio * scale * cosine])
        forward.append(np.concatenate([from_rhs, from_flux], axis=1))
    return split_table(np.stack(inverse)), split_table(np.stack(forward))


def dot(left, right, contract):
    return lax.dot_general(
        left, right, (contract, ((), ())), preferred_element_type=jnp.float32
    )


def halves(value):
    high = value.astype(jnp.bfloat16)
    low = (value - high.astype(jnp.float32)).astype(jnp.bfloat16)
    return high, low


def thirds(value):
    high = value.astype(jnp.bfloat16)
    rest = value - high.astype(jnp.float32)
    middle = rest.astype(jnp.bfloat16)
    low = (rest - middle.astype(jnp.float32)).astype(jnp.bfloat16)
    return high, middle, low


def dot_split(left, right, contract):
    (left_high, left_low), (right_high, right_low) = left, right
    return (
        dot(left_high, right_low, contract)
        + dot(left_low, right_high, contract)
        + dot(left_high, right_high, contract)
    )


def column_order():
    column = lax.broadcasted_iota(jnp.int32, (640, 128), 0)
    element = lax.broadcasted_iota(jnp.int32, (640, 128), 1)
    tiles = [jnp.where(column == 5 * element + i, 1.0, 0.0).astype(jnp.bfloat16) for i in range(5)]
    return jnp.concatenate(tiles, axis=1)


def exchange_chunks(values):
    values = list(values)
    lane = lax.broadcasted_iota(jnp.int32, values[0].shape, 1)
    for bit in (1, 2, 4, 8):
        upper = (lane & (8 * bit)) != 0
        for a in range(16):
            if a & bit == 0:
                first, second = values[a], values[a | bit]
                values[a] = jnp.where(upper, pltpu.roll(second, 8 * bit, 1), first)
                values[a | bit] = jnp.where(upper, second, pltpu.roll(first, 128 - 8 * bit, 1))
    return values


def pack_kernel(state_ref, out_ref, chunk_ref):
    stacked = jnp.concatenate([state_ref[j] for j in range(5)], axis=0)
    order = column_order()
    contract = ((1,), (0,))
    high, middle, low = thirds(stacked)
    nodes = dot(low, order, contract) + dot(middle, order, contract) + dot(high, order, contract)
    for i in range(5):
        chunk_ref[160 * i : 160 * i + 160, :] = nodes[:, 128 * i : 128 * i + 128]
    chunk = [
        jnp.concatenate(
            [chunk_ref[pl.ds(160 * i + 32 * j + t, 8, stride=4), :] for t in range(4)], axis=0
        )
        for j in range(5)
        for i in range(5)
    ]
    lane = lax.broadcasted_iota(jnp.int32, (32, 128), 1) & 7
    for j in range(5):
        left = pltpu.roll(chunk[j * 5 + 4], 1, 1)
        right = pltpu.roll(chunk[j * 5], 127, 1)
        chunk.append(jnp.where(lane == 0, left, jnp.where(lane == 7, right, 0.0)))
    zero = jnp.zeros((32, 128), jnp.float32)
    chunk = chunk + [zero, zero]
    for half in range(2):
        block = exchange_chunks(chunk[16 * half : 16 * half + 16])
        for d in range(GRID):
            out_ref[d, :, 128 * half : 128 * half + 128] = block[d]


def turn_kernel(modal_ref, nodal_ref, low_ref, high_ref):
    for parity in range(2):
        rows = [
            modal_ref[s, 16 * parity + 8 * t : 16 * parity + 8 * t + 8, :]
            for t in range(2)
            for s in range(GRID)
        ]
        turned = jnp.concatenate(rows, axis=0).T
        nodal_ref[parity] = turned
        low_ref[parity] = turned[0:40]
        high_ref[parity] = turned[160:200]


def synthesize(nodal, high_ref, low_ref):
    part = [
        dot_split(
            halves(nodal[parity]), (high_ref[parity], low_ref[parity]), ((1,), (0,))
        )
        for parity in range(2)
    ]
    return part[0] + part[1], part[0] - part[1]


def two_point(left, right):
    mean = (left * left + left * right + right * right) * (1.0 / 6.0)
    speed = jnp.maximum(jnp.abs(left), jnp.abs(right))
    return mean - 0.5 * speed * (right - left)


def volume_kernel(nodal_ref, high_ref, low_ref, field_ref, rhs_ref, side_ref):
    nodal = [nodal_ref[0], nodal_ref[1]]
    pair = synthesize(nodal, high_ref, low_ref)
    for q in range(2):
        field_ref[:, HALF * q : HALF * q + HALF] = pair[q][0:200]
        side_ref[:, HALF * q : HALF * q + HALF] = pair[q][200:240]
    row = lax.broadcasted_iota(jnp.int32, (8, 128), 0)

    def column(block, carry):
        lanes = pl.ds(pl.multiple_of(block * 128, 128), 128)
        f = [field_ref[8 * n : 8 * n + 8, lanes] for n in range(25)]
        square = [v * v for v in f]
        for j in range(5):
            for i in range(5):
                n = j * 5 + i
                plain = None
                power = None
                for other in range(5):
                    terms = [(DIFFER[i][other], j * 5 + other), (DIFFER[j][other], other * 5 + i)]
                    for weight, m in terms:
                        if weight == 0.0:
                            continue
                        weight = float(weight) / -3.0
                        plain = weight * f[m] if plain is None else plain + weight * f[m]
                        power = weight * square[m] if power is None else power + weight * square[m]
                total = power + f[n] * plain
                own = (i == 4) + (j == 4) - (i == 0) - (j == 0)
                if own:
                    total = total + (5.0 * own) * square[n]
                if i == 0 or i == 4:
                    side = side_ref[8 * j : 8 * j + 8, lanes]
                    if i == 0:
                        left = jnp.where(row == 0, side, pltpu.roll(f[j * 5 + 4], 1, 0))
                        total = total + 10.0 * two_point(left, f[n])
                    else:
                        right = jnp.where(row == 7, side, pltpu.roll(f[j * 5], 7, 0))
                        total = total - 10.0 * two_point(f[n], right)
                rhs_ref[8 * n : 8 * n + 8, lanes] = total
        return carry

    lax.fori_loop(0, PLANES // 128, column, 0)


def forward_kernel(
    modal_ref, field_ref, rhs_ref, below_ref, above_ref, mirror_ref, scalar_ref, inverse_high_ref,
    inverse_low_ref, forward_high_ref, forward_low_ref, out_ref, outer_ref,
):
    bottom = scalar_ref[0] == 1
    top = scalar_ref[1] == 1
    outer = [
        jnp.concatenate([below_ref[parity], above_ref[parity]], axis=0) for parity in range(2)
    ]
    pair = synthesize(outer, inverse_high_ref, inverse_low_ref)
    for q in range(2):
        outer_ref[:, HALF * q : HALF * q + HALF] = pair[q]
    mirror = jnp.concatenate([mirror_ref[...]] * 6, axis=1)
    bottom_rows, top_rows = [], []
    for i in range(5):
        inside = field_ref[8 * i : 8 * i + 8, :]
        below = jnp.where(bottom, mirror * inside, outer_ref[8 * i : 8 * i + 8, :])
        bottom_rows.append(
            rhs_ref[8 * i : 8 * i + 8, :] + 10.0 * two_point(below, inside)
        )
        n = 20 + i
        inside = field_ref[8 * n : 8 * n + 8, :]
        above = jnp.where(top, inside, outer_ref[40 + 8 * i : 48 + 8 * i, :])
        top_rows.append(rhs_ref[8 * n : 8 * n + 8, :] - 10.0 * two_point(inside, above))
    rhs = jnp.concatenate(bottom_rows + [rhs_ref[40:160, :]] + top_rows, axis=0)
    field = field_ref[...]
    flux = 0.5 * field * field
    for parity in range(2):
        if parity == 0:
            folded = [rhs[:, :HALF] + rhs[:, HALF:], flux[:, :HALF] + flux[:, HALF:]]
        else:
            folded = [rhs[:, :HALF] - rhs[:, HALF:], flux[:, :HALF] - flux[:, HALF:]]
        planar = jnp.concatenate(folded, axis=1)
        change = dot_split(
            (forward_high_ref[parity], forward_low_ref[parity]), halves(planar), ((1,), (1,))
        )
        for t in range(2):
            first = 16 * parity + 8 * t
            modal = jnp.concatenate(
                [modal_ref[s, first : first + 8, :] for s in range(GRID)], axis=0
            )
            rows = change[128 * t : 128 * t + 128]
            for s in range(GRID):
                part = slice(8 * s, 8 * s + 8)
                out_ref[s, first : first + 8, 0:128] = modal[part, :128] + rows[part, :128]
                out_ref[s, first : first + 8, 128:200] = modal[part, 128:200] + rows[part, 128:200]


def local_operator(values, shift):
    out = []
    for j in range(5):
        for i in range(5):
            n = j * 5 + i
            mass = float(WEIGHTS[j] * WEIGHTS[i])
            diagonal = VISCOUS * float(WEIGHTS[j] * STIFFNESS[i][i] + WEIGHTS[i] * STIFFNESS[j][j])
            value = (shift * mass + diagonal) * values[n]
            for other in range(5):
                if other != i:
                    weight = VISCOUS * float(WEIGHTS[j] * STIFFNESS[i][other])
                    value = value + weight * values[j * 5 + other]
                if other != j:
                    weight = VISCOUS * float(WEIGHTS[i] * STIFFNESS[j][other])
                    value = value + weight * values[other * 5 + i]
            out.append(value)
    return out


def store_joined(values, joined_ref, low_ref, high_ref):
    values = list(values)
    for j in range(5):
        joint = values[j * 5 + 4] + pltpu.roll(values[j * 5], 127, 1)
        values[j * 5 + 4] = joint
        values[j * 5] = pltpu.roll(joint, 1, 1)
    for n in range(25):
        joined_ref[n] = values[n]
    for i in range(5):
        low_ref[i] = values[i]
        high_ref[i] = values[20 + i]


def assembled(scalar_ref, joined_ref, below_ref, above_ref):
    values = [joined_ref[n] for n in range(25)]
    for i in range(5):
        values[i] = values[i] + jnp.where(scalar_ref[0] == 1, 0.0, below_ref[i])
        values[20 + i] = values[20 + i] + jnp.where(scalar_ref[1] == 1, 0.0, above_ref[i])
    return values


def mode_terms(scalar_ref):
    row = lax.broadcasted_iota(jnp.int32, (32, 128), 0)
    mode_pair = 16 * scalar_ref[2] + 2 * (row & 7) + (row >> 4)
    ratio = mode_pair.astype(jnp.float32) * (1.0 / KMODES)
    shift = 1.0 + SPAN_STIFF * ratio * ratio
    return shift, 0.2 * shift + 0.15


def inner(scalar_ref, left, right):
    total = None
    for j in range(5):
        part = None
        for i in range(5):
            term = left[j * 5 + i] * right[j * 5 + i]
            term = term if 0 < i < 4 else 0.5 * term
            part = term if part is None else part + term
        if j == 0:
            part = jnp.where(scalar_ref[0] == 1, 1.0, 0.5) * part
        elif j == 4:
            part = jnp.where(scalar_ref[1] == 1, 1.0, 0.5) * part
        total = part if total is None else total + part
    return total


def load_kernel(modal_ref, joined_ref, low_ref, high_ref):
    predicted = []
    for half in range(2):
        predicted += exchange_chunks(
            [modal_ref[s, :, 128 * half : 128 * half + 128] for s in range(GRID)]
        )
    weighted = [float(WEIGHTS[n // 5] * WEIGHTS[n % 5]) * predicted[n] for n in range(25)]
    store_joined(weighted, joined_ref, low_ref, high_ref)


def first_kernel(
    scalar_ref, joined_ref, below_ref, above_ref, vector_ref, next_ref, low_ref, high_ref
):
    shift, _ = mode_terms(scalar_ref)
    vector = assembled(scalar_ref, joined_ref, below_ref, above_ref)
    for n in range(25):
        vector_ref[n] = vector[n]
    store_joined(local_operator(vector, shift), next_ref, low_ref, high_ref)


def second_kernel(
    scalar_ref, joined_ref, below_ref, above_ref, before_ref, vector_ref, next_ref, low_ref,
    high_ref,
):
    shift, center = mode_terms(scalar_ref)
    applied = assembled(scalar_ref, joined_ref, below_ref, above_ref)
    vector = [applied[n] - center * before_ref[n] for n in range(25)]
    for n in range(25):
        vector_ref[n] = vector[n]
    store_joined(local_operator(vector, shift), next_ref, low_ref, high_ref)


def third_kernel(
    scalar_ref, joined_ref, below_ref, above_ref, first_ref, second_ref, vector_ref, sums_ref,
    turn_ref,
):
    shift, center = mode_terms(scalar_ref)
    applied = assembled(scalar_ref, joined_ref, below_ref, above_ref)
    first = [first_ref[n] for n in range(25)]
    second = [second_ref[n] for n in range(25)]
    third = [applied[n] - center * second[n] for n in range(25)]
    for n in range(25):
        vector_ref[n] = third[n]
    fourth = inner(scalar_ref, third, third)
    local = local_operator(third, shift)
    fifth = -center * fourth
    for n in range(25):
        fifth = fifth + local[n] * third[n]
    moments = [
        inner(scalar_ref, first, first),
        inner(scalar_ref, first, second),
        inner(scalar_ref, second, second),
        inner(scalar_ref, second, third),
        fourth,
        fifth,
    ]
    lane = lax.broadcasted_iota(jnp.int32, (32, 128), 1)
    packed = jnp.zeros((32, 128), jnp.float32)
    for n, moment in enumerate(moments):
        packed = jnp.where(lane == n, jnp.sum(moment, axis=1, keepdims=True), packed)
    turn_ref[...] = jnp.zeros((128, 128), jnp.float32)
    for t in range(4):
        turn_ref[pl.ds(t, 8, stride=4), :] = packed[8 * t : 8 * t + 8]
    turned = turn_ref[...].T[0:8]
    for p in range(GRID):
        sums_ref[p] = turned


def natural_kernel(vector_ref, out_ref, column_ref):
    order = column_order()
    stacked = jnp.concatenate(
        [
            jnp.concatenate([vector_ref[j * 5 + i] for i in range(5)], axis=1) for j in range(5)
        ],
        axis=0,
    )
    contract = ((1,), (1,))
    high, middle, low = thirds(stacked)
    columns = dot(low, order, contract) + dot(middle, order, contract) + dot(high, order, contract)
    for i in range(5):
        for j in range(5):
            for t in range(4):
                first = 32 * j + 8 * t
                column_ref[pl.ds(160 * i + 32 * j + t, 8, stride=4), :] = columns[
                    first : first + 8, 128 * i : 128 * i + 128
                ]
    for j in range(5):
        for i in range(5):
            first = 160 * i + 32 * j
            out_ref[j, :, 128 * i : 128 * i + 128] = column_ref[first : first + 32, :]


def combine_kernel(scalar_ref, sums_ref, first_ref, second_ref, third_ref, out_ref, turn_ref):
    total = sums_ref[0]
    for p in range(1, GRID):
        total = total + sums_ref[p]
    moment = [total[n : n + 1] for n in range(6)]
    lane = lax.broadcasted_iota(jnp.int32, (1, 128), 1)
    mode_pair = 16 * scalar_ref[2] + (lane >> 1)
    ratio = mode_pair.astype(jnp.float32) * (1.0 / KMODES)
    center = 0.2 * (1.0 + SPAN_STIFF * ratio * ratio) + 0.15

    def product(left, right):
        terms = None
        for a in range(len(left)):
            for b in range(len(right)):
                term = left[a] * right[b] * moment[a + b]
                terms = term if terms is None else terms + term
        return terms

    def operator(c):
        shifted = [center * v for v in c] + [0.0]
        return [shifted[0]] + [shifted[a + 1] + c[a] for a in range(len(c))]

    residual = [jnp.ones((1, 128), jnp.float32)]
    direction = residual
    result = [0.0, 0.0, 0.0]
    norm = moment[0]
    for step in range(ITERS):
        applied = operator(direction)
        length = norm / product(direction, applied)
        for a in range(len(direction)):
            result[a] = result[a] + length * direction[a]
        if step < ITERS - 1:
            padded = residual + [0.0]
            residual = [padded[a] - length * applied[a] for a in range(len(applied))]
            fresh = product(residual, residual)
            ratio = fresh / norm
            norm = fresh
            padded = direction + [0.0]
            direction = [residual[a] + ratio * padded[a] for a in range(len(residual))]
    turn_ref[...] = jnp.zeros((128, 128), jnp.float32)
    for a in range(3):
        turn_ref[a : a + 1, :] = result[a]
    turned = turn_ref[...].T[0:32]
    weight = [turned[:, a : a + 1] for a in range(3)]
    for j in range(5):
        out_ref[j] = (
            weight[0] * first_ref[j] + weight[1] * second_ref[j] + weight[2] * third_ref[j]
        )


def call(kernel, name, out_shapes, *args, smem=(), scratch=()):
    vmem = pl.BlockSpec(memory_space=pltpu.VMEM)
    scalar = pl.BlockSpec(memory_space=pltpu.SMEM)
    return pl.pallas_call(
        kernel,
        name=name,
        out_shape=[jax.ShapeDtypeStruct(s, jnp.float32) for s in out_shapes],
        in_specs=[scalar if n in smem else vmem for n in range(len(args))],
        out_specs=[vmem] * len(out_shapes),
        scratch_shapes=list(scratch),
        compiler_params=pltpu.CompilerParams(vmem_limit_bytes=48 * 1024 * 1024),
    )(*args)


def from_neighbours(low, high):
    below = lax.ppermute(high, "plane", [(p, (p + 1) % GRID) for p in range(GRID)])
    above = lax.ppermute(low, "plane", [(p, (p - 1) % GRID) for p in range(GRID)])
    return below, above


def on_device(state, wall_tag):
    (inverse_high, inverse_low), (forward_high, forward_low) = transform_tables()
    span = lax.axis_index("span")
    plane = lax.axis_index("plane")
    last = lax.axis_size("plane") - 1
    scalars = jnp.stack([(plane == 0).astype(jnp.int32), (plane == last).astype(jnp.int32), span])
    tags = lax.dynamic_slice_in_dim(wall_tag, span * 8, 8)
    mirror = jnp.broadcast_to(jnp.where(tags == 1, -1.0, 1.0).astype(jnp.float32)[:, None], (8, 128))

    (packed,) = call(
        pack_kernel, "pack", [(16, 32, 256)], jnp.transpose(state, (1, 0, 2)),
        scratch=[pltpu.VMEM((800, 128), jnp.float32)],
    )
    modal = lax.all_to_all(packed, "span", 0, 0, tiled=True)
    nodal, low, high = call(
        turn_kernel, "turn", [(2, 256, 256), (2, 40, 256), (2, 40, 256)], modal
    )
    below, above = from_neighbours(low, high)
    field, rhs = call(
        volume_kernel, "volume", [(200, PLANES), (200, PLANES)], nodal, inverse_high, inverse_low,
        scratch=[pltpu.VMEM((40, PLANES), jnp.float32)],
    )
    (sent,) = call(
        forward_kernel, "forward", [(16, 32, 256)], modal, field, rhs, below, above, mirror, scalars,
        inverse_high, inverse_low, forward_high, forward_low, smem=(6,),
        scratch=[pltpu.VMEM((80, PLANES), jnp.float32)],
    )
    predicted = lax.all_to_all(sent, "span", 0, 0, tiled=True)
    nodes, trace = (25, 32, 128), (5, 32, 128)
    joined, low, high = call(load_kernel, "load", [nodes, trace, trace], predicted)
    below, above = from_neighbours(low, high)
    first, joined, low, high = call(
        first_kernel, "first", [nodes, nodes, trace, trace], scalars, joined, below, above, smem=(0,)
    )
    below, above = from_neighbours(low, high)
    second, joined, low, high = call(
        second_kernel, "second", [nodes, nodes, trace, trace], scalars, joined, below, above, first,
        smem=(0,),
    )
    below, above = from_neighbours(low, high)
    third, sums = call(
        third_kernel, "third", [nodes, (16, 8, 128)], scalars, joined, below, above, first, second,
        smem=(0,), scratch=[pltpu.VMEM((128, 128), jnp.float32)],
    )
    sums = lax.all_to_all(sums, "plane", 0, 0, tiled=True)
    columns = [
        call(
            natural_kernel, "natural", [(5, 32, 640)], vector,
            scratch=[pltpu.VMEM((800, 128), jnp.float32)],
        )[0]
        for vector in (first, second, third)
    ]
    (columns,) = call(
        combine_kernel, "combine", [(5, 32, 640)], scalars, sums, *columns, smem=(0,),
        scratch=[pltpu.VMEM((128, 128), jnp.float32)],
    )
    return jnp.transpose(columns, (1, 0, 2))


def solution(mesh):
    in_specs = (P("span", "plane", None), P())
    out_specs = P("span", "plane", None)
    return jax.shard_map(
        on_device, mesh=mesh, in_specs=in_specs, out_specs=out_specs, check_vma=False
    )
```

```python
import math

import jax
import jax.numpy as jnp
import numpy as np
from jax import lax
from jax.experimental import pallas as pl
from jax.experimental.pallas import tpu as pltpu
from jax.sharding import PartitionSpec as P

KMODES = 256
PLANES = 768
HALF = 384
ITERS = 3
GRID = 16
STEP_SIZE = 0.03
VISCOUS = 0.05
SPAN_STIFF = 4.0


def gll_tables():
    abscissae = np.array([-1.0, -math.sqrt(3.0 / 7.0), 0.0, math.sqrt(3.0 / 7.0), 1.0])
    weights = np.array([0.1, 49.0 / 90.0, 32.0 / 45.0, 49.0 / 90.0, 0.1])
    squared = abscissae * abscissae
    legendre = (35.0 * squared * squared - 30.0 * squared + 3.0) / 8.0
    identity = np.eye(5)
    spacing = abscissae[:, None] - abscissae[None, :] + identity
    differ = np.where(identity > 0, 0.0, legendre[:, None] / legendre[None, :] / spacing)
    differ[0, 0] = -5.0
    differ[4, 4] = 5.0
    stiffness = differ.T @ (weights[:, None] * differ)
    return differ, weights, stiffness


DIFFER, WEIGHTS, STIFFNESS = gll_tables()


def split_table(table):
    high = table.astype(np.float32).astype(jnp.bfloat16)
    low = (table - high.astype(np.float64)).astype(np.float32).astype(jnp.bfloat16)
    return jnp.asarray(high), jnp.asarray(low)


def wave_table():
    plane = np.arange(HALF)
    waves = []
    for parity in range(2):
        k = 2 * np.arange(128) + parity
        angle = (k[:, None] * plane[None, :] % PLANES) * (2.0 * math.pi / PLANES)
        waves.append(np.concatenate([np.cos(angle), np.sin(angle)]))
    return split_table(np.stack(waves))


def dot(left, right, contract):
    return lax.dot_general(
        left, right, (contract, ((), ())), preferred_element_type=jnp.float32
    )


def halves(value):
    high = value.astype(jnp.bfloat16)
    low = (value - high.astype(jnp.float32)).astype(jnp.bfloat16)
    return high, low


def thirds(value):
    high = value.astype(jnp.bfloat16)
    rest = value - high.astype(jnp.float32)
    middle = rest.astype(jnp.bfloat16)
    low = (rest - middle.astype(jnp.float32)).astype(jnp.bfloat16)
    return high, middle, low


def dot_split(left, right, contract):
    (left_high, left_low), (right_high, right_low) = left, right
    return (
        dot(left_high, right_low, contract)
        + dot(left_low, right_high, contract)
        + dot(left_high, right_high, contract)
    )


def column_order():
    column = lax.broadcasted_iota(jnp.int32, (640, 128), 0)
    element = lax.broadcasted_iota(jnp.int32, (640, 128), 1)
    tiles = [jnp.where(column == 5 * element + i, 1.0, 0.0).astype(jnp.bfloat16) for i in range(5)]
    return jnp.concatenate(tiles, axis=1)


def exchange_chunks(values):
    values = list(values)
    lane = lax.broadcasted_iota(jnp.int32, values[0].shape, 1)
    for bit in (1, 2, 4, 8):
        upper = (lane & (8 * bit)) != 0
        for a in range(16):
            if a & bit == 0:
                first, second = values[a], values[a | bit]
                values[a] = jnp.where(upper, pltpu.roll(second, 8 * bit, 1), first)
                values[a | bit] = jnp.where(upper, second, pltpu.roll(first, 128 - 8 * bit, 1))
    return values


def pack_kernel(state_hbm, out_ref, chunk_ref, state_ref, order_ref, arrived):
    copy = pltpu.make_async_copy(state_hbm, state_ref, arrived)
    copy.start()
    order_ref[...] = column_order()
    copy.wait()
    stacked = jnp.concatenate([state_ref[j] for j in range(5)], axis=0)
    order = order_ref[...]
    contract = ((1,), (0,))
    high, middle, low = thirds(stacked)
    nodes = dot(low, order, contract) + dot(middle, order, contract) + dot(high, order, contract)
    for i in range(5):
        chunk_ref[160 * i : 160 * i + 160, :] = nodes[:, 128 * i : 128 * i + 128]
    chunk = [
        jnp.concatenate(
            [chunk_ref[pl.ds(160 * i + 32 * j + t, 8, stride=4), :] for t in range(4)], axis=0
        )
        for j in range(5)
        for i in range(5)
    ]
    lane = lax.broadcasted_iota(jnp.int32, (32, 128), 1) & 7
    for j in range(5):
        left = pltpu.roll(chunk[j * 5 + 4], 1, 1)
        right = pltpu.roll(chunk[j * 5], 127, 1)
        chunk.append(jnp.where(lane == 0, left, jnp.where(lane == 7, right, 0.0)))
    zero = jnp.zeros((32, 128), jnp.float32)
    chunk = chunk + [zero, zero]
    for half in range(2):
        block = exchange_chunks(chunk[16 * half : 16 * half + 16])
        for d in range(GRID):
            out_ref[d, :, 128 * half : 128 * half + 128] = block[d]


def turn_kernel(modal_ref, nodal_ref, low_ref, high_ref):
    for parity in range(2):
        rows = [
            modal_ref[s, 16 * parity + 8 * t : 16 * parity + 8 * t + 8, :]
            for t in range(2)
            for s in range(GRID)
        ]
        turned = jnp.concatenate(rows, axis=0).T
        nodal_ref[parity] = turned
        low_ref[parity] = turned[0:40]
        high_ref[parity] = turned[160:200]


def synthesize(nodal, high_ref, low_ref):
    part = [
        dot_split(
            halves(nodal[parity]), (high_ref[parity], low_ref[parity]), ((1,), (0,))
        )
        for parity in range(2)
    ]
    scale = 1.0 / math.sqrt(KMODES)
    return scale * (part[0] + part[1]), scale * (part[0] - part[1])


def two_point(left, right):
    mean = (left * left + left * right + right * right) * (1.0 / 6.0)
    speed = jnp.maximum(jnp.abs(left), jnp.abs(right))
    return mean - 0.5 * speed * (right - left)


def volume_kernel(
    nodal_ref, high_ref, low_ref, field_ref, rhs_ref, rhs_low_ref, rhs_high_ref, side_ref
):
    nodal = [nodal_ref[0], nodal_ref[1]]
    pair = synthesize(nodal, high_ref, low_ref)
    for q in range(2):
        field_ref[:, HALF * q : HALF * q + HALF] = pair[q][0:200]
        side_ref[:, HALF * q : HALF * q + HALF] = pair[q][200:240]
    row = lax.broadcasted_iota(jnp.int32, (8, 128), 0)

    def column(block, carry):
        lanes = pl.ds(pl.multiple_of(block * 128, 128), 128)
        f = [field_ref[8 * n : 8 * n + 8, lanes] for n in range(25)]
        square = [v * v for v in f]
        for j in range(5):
            for i in range(5):
                n = j * 5 + i
                plain = None
                power = None
                for other in range(5):
                    terms = [(DIFFER[i][other], j * 5 + other), (DIFFER[j][other], other * 5 + i)]
                    for weight, m in terms:
                        if weight == 0.0:
                            continue
                        weight = float(weight) / -3.0
                        plain = weight * f[m] if plain is None else plain + weight * f[m]
                        power = weight * square[m] if power is None else power + weight * square[m]
                total = power + f[n] * plain
                own = (i == 4) + (j == 4) - (i == 0) - (j == 0)
                if own:
                    total = total + (5.0 * own) * square[n]
                if i == 0 or i == 4:
                    side = side_ref[8 * j : 8 * j + 8, lanes]
                    if i == 0:
                        left = jnp.where(row == 0, side, pltpu.roll(f[j * 5 + 4], 1, 0))
                        total = total + 10.0 * two_point(left, f[n])
                    else:
                        right = jnp.where(row == 7, side, pltpu.roll(f[j * 5], 7, 0))
                        total = total - 10.0 * two_point(f[n], right)
                rhs_ref[8 * n : 8 * n + 8, lanes] = total
                if j == 0:
                    rhs_low_ref[8 * i : 8 * i + 8, lanes] = total
                elif j == 4:
                    rhs_high_ref[8 * i : 8 * i + 8, lanes] = total
        return carry

    lax.fori_loop(0, PLANES // 128, column, 0)


def project(planar, parity, high_ref, low_ref):
    folded = planar[:, :HALF] + planar[:, HALF:] if parity == 0 else planar[:, :HALF] - planar[:, HALF:]
    return dot_split((high_ref[parity], low_ref[parity]), halves(folded), ((1,), (1,)))


def tendency(parity, from_rhs, from_flux):
    k = 2 * lax.broadcasted_iota(jnp.int32, (128, 128), 0) + parity
    scale = jnp.where(k == 0, 1.0, 2.0) * (math.sqrt(KMODES) / PLANES * STEP_SIZE)
    ratio = k.astype(jnp.float32) * (1.0 / KMODES)
    return (
        scale * (from_rhs[0:128] - ratio * from_flux[128:256]),
        scale * (from_rhs[128:256] + ratio * from_flux[0:128]),
    )


def inside_kernel(modal_ref, field_ref, rhs_ref, high_ref, low_ref, out_ref):
    field = field_ref[...]
    flux = 0.5 * field * field
    rhs = rhs_ref[...]
    tail = jnp.zeros((56, PLANES), jnp.float32)
    flux = jnp.concatenate([flux, tail], axis=0)
    rhs = jnp.concatenate([rhs, tail], axis=0)
    for parity in range(2):
        from_rhs = project(rhs, parity, high_ref, low_ref)
        from_flux = project(flux, parity, high_ref, low_ref)
        for half in range(2):
            lanes = slice(128 * half, 128 * half + 128)
            change = tendency(parity, from_rhs[:, lanes], from_flux[:, lanes])
            for t in range(2):
                first = 16 * parity + 8 * t
                modal = jnp.concatenate(
                    [modal_ref[s, first : first + 8, lanes] for s in range(GRID)], axis=0
                )
                out_ref[parity, 128 * t : 128 * t + 128, lanes] = modal + change[t]


def facing_kernel(
    tag_ref, inside_ref, field_ref, below_ref, above_ref, rhs_below_ref, rhs_above_ref, high_ref,
    low_ref, out_ref, outer_ref,
):
    bottom, top = at_ends()
    span = lax.axis_index("span")
    row = lax.broadcasted_iota(jnp.int32, (8, 128), 0)
    mirror = jnp.ones((8, 128), jnp.float32)
    for e in range(8):
        mirror = jnp.where((row == e) & (tag_ref[8 * span + e] == 1), -1.0, mirror)
    outer = [
        jnp.concatenate([below_ref[parity], above_ref[parity]], axis=0) for parity in range(2)
    ]
    pair = synthesize(outer, high_ref, low_ref)
    for q in range(2):
        outer_ref[:, HALF * q : HALF * q + HALF] = pair[q]
    mirror = jnp.concatenate([mirror] * 6, axis=1)
    mirror = jnp.concatenate([mirror] * 5, axis=0)
    inside = field_ref[0:40, :]
    below = outer_ref[0:40, :]
    lift = 10.0 * two_point(jnp.where(bottom, mirror * inside, below), inside)
    rhs_lower = lift + jnp.where(bottom, 0.0, rhs_below_ref[...] - lift)
    flux_lower = jnp.where(bottom, 0.0, 0.5 * below * below)
    inside = field_ref[160:200, :]
    above = outer_ref[40:80, :]
    lift = 10.0 * two_point(inside, jnp.where(top, inside, above))
    rhs_upper = jnp.where(top, 0.0, rhs_above_ref[...] + lift) - lift
    flux_upper = jnp.where(top, 0.0, 0.5 * above * above)
    gap = jnp.zeros((48, PLANES), jnp.float32)
    planar = jnp.concatenate([rhs_lower, rhs_upper, gap, flux_lower, flux_upper, gap], axis=0)
    gap = jnp.zeros((48, 256), jnp.float32)
    keep_lower = jnp.where(bottom, 0.0, 1.0)
    keep_upper = jnp.where(top, 0.0, 1.0)
    lane = lax.broadcasted_iota(jnp.int32, (128, 128), 1)
    for parity in range(2):
        projected = project(planar, parity, high_ref, low_ref)
        change = tendency(parity, projected[:, 0:128], projected[:, 128:256])
        modal = jnp.concatenate(
            [keep_lower * below_ref[parity], keep_upper * above_ref[parity], gap], axis=0
        ).T
        for t in range(2):
            first = 16 * parity + 8 * t
            extra = change[t] + modal[128 * t : 128 * t + 128]
            lower = jnp.where(lane < 40, extra, 0.0)
            upper = pltpu.roll(jnp.where(lane < 40, 0.0, extra), 120, 1)
            for half, added in ((0, lower), (1, upper)):
                lanes = slice(128 * half, 128 * half + 128)
                total = inside_ref[parity, 128 * t : 128 * t + 128, lanes] + added
                for s in range(GRID):
                    out_ref[s, first : first + 8, lanes] = total[8 * s : 8 * s + 8]


def at_ends():
    plane = lax.axis_index("plane")
    return plane == 0, plane == GRID - 1


def local_operator(values, shift):
    out = []
    for j in range(5):
        for i in range(5):
            n = j * 5 + i
            mass = float(WEIGHTS[j] * WEIGHTS[i])
            diagonal = VISCOUS * float(WEIGHTS[j] * STIFFNESS[i][i] + WEIGHTS[i] * STIFFNESS[j][j])
            value = (shift * mass + diagonal) * values[n]
            for other in range(5):
                if other != i:
                    weight = VISCOUS * float(WEIGHTS[j] * STIFFNESS[i][other])
                    value = value + weight * values[j * 5 + other]
                if other != j:
                    weight = VISCOUS * float(WEIGHTS[i] * STIFFNESS[j][other])
                    value = value + weight * values[other * 5 + i]
            out.append(value)
    return out


def join_columns(values):
    values = list(values)
    for j in range(5):
        joint = values[j * 5 + 4] + pltpu.roll(values[j * 5], 127, 1)
        values[j * 5 + 4] = joint
        values[j * 5] = pltpu.roll(joint, 1, 1)
    return values


def store_joined(values, joined_ref, low_ref, high_ref):
    values = join_columns(values)
    for n in range(25):
        joined_ref[n] = values[n]
    for i in range(5):
        low_ref[i] = values[i]
        high_ref[i] = values[20 + i]


def assembled(joined_ref, below_ref, above_ref):
    values = [joined_ref[n] for n in range(25)]
    bottom, top = at_ends()
    for i in range(5):
        values[i] = values[i] + jnp.where(bottom, 0.0, below_ref[i])
        values[20 + i] = values[20 + i] + jnp.where(top, 0.0, above_ref[i])
    return values


def mode_terms():
    row = lax.broadcasted_iota(jnp.int32, (32, 128), 0)
    mode_pair = 16 * lax.axis_index("span") + 2 * (row & 7) + (row >> 4)
    ratio = mode_pair.astype(jnp.float32) * (1.0 / KMODES)
    shift = 1.0 + SPAN_STIFF * ratio * ratio
    return shift, 0.2 * shift + 0.15


def inner(left, right):
    bottom, top = at_ends()
    total = None
    for j in range(5):
        part = None
        for i in range(5):
            term = left[j * 5 + i] * right[j * 5 + i]
            term = term if 0 < i < 4 else 0.5 * term
            part = term if part is None else part + term
        if j == 0:
            part = jnp.where(bottom, 1.0, 0.5) * part
        elif j == 4:
            part = jnp.where(top, 1.0, 0.5) * part
        total = part if total is None else total + part
    return total


def first_kernel(modal_ref, vector_ref, next_ref, low_ref, high_ref):
    shift, _ = mode_terms()
    values = []
    for half in range(2):
        values += exchange_chunks(
            [modal_ref[s, :, 128 * half : 128 * half + 128] for s in range(GRID)]
        )
    values = [float(WEIGHTS[n // 5] * WEIGHTS[n % 5]) * values[n] for n in range(25)]
    vector = join_columns(values)
    for n in range(25):
        vector_ref[n] = vector[n]
    store_joined(local_operator(vector, shift), next_ref, low_ref, high_ref)


def second_kernel(
    joined_ref, below_ref, above_ref, before_ref, vector_ref, next_ref, low_ref,
    high_ref,
):
    shift, center = mode_terms()
    applied = assembled(joined_ref, below_ref, above_ref)
    vector = [applied[n] - center * before_ref[n] for n in range(25)]
    for n in range(25):
        vector_ref[n] = vector[n]
    store_joined(local_operator(vector, shift), next_ref, low_ref, high_ref)


def pack_moments(moments, first, packed):
    lane = lax.broadcasted_iota(jnp.int32, (32, 128), 1)
    for n, moment in enumerate(moments):
        packed = jnp.where(lane == first + n, jnp.sum(moment, axis=1, keepdims=True), packed)
    return packed


def early_kernel(first_ref, second_ref, packed_ref):
    first = [first_ref[n] for n in range(25)]
    second = [second_ref[n] for n in range(25)]
    moments = [
        inner(first, first),
        inner(first, second),
        inner(second, second),
    ]
    packed_ref[...] = pack_moments(moments, 0, jnp.zeros((32, 128), jnp.float32))


def third_kernel(
    joined_ref, below_ref, above_ref, second_ref, packed_ref, vector_ref, sums_ref,
    turn_ref,
):
    shift, center = mode_terms()
    applied = assembled(joined_ref, below_ref, above_ref)
    second = [second_ref[n] for n in range(25)]
    third = [applied[n] - center * second[n] for n in range(25)]
    for n in range(25):
        vector_ref[n] = third[n]
    fourth = inner(third, third)
    local = local_operator(third, shift)
    fifth = -center * fourth
    for n in range(25):
        fifth = fifth + local[n] * third[n]
    moments = [inner(second, third), fourth, fifth]
    packed = pack_moments(moments, 3, packed_ref[...])
    turn_ref[...] = jnp.zeros((128, 128), jnp.float32)
    for t in range(4):
        turn_ref[pl.ds(t, 8, stride=4), :] = packed[8 * t : 8 * t + 8]
    turned = turn_ref[...].T[0:8]
    for p in range(GRID):
        sums_ref[p] = turned


def natural_kernel(vector_ref, out_ref, column_ref):
    order = column_order()
    stacked = jnp.concatenate(
        [
            jnp.concatenate([vector_ref[j * 5 + i] for i in range(5)], axis=1) for j in range(5)
        ],
        axis=0,
    )
    contract = ((1,), (1,))
    high, middle, low = thirds(stacked)
    columns = dot(low, order, contract) + dot(middle, order, contract) + dot(high, order, contract)
    for i in range(5):
        for j in range(5):
            for t in range(4):
                first = 32 * j + 8 * t
                column_ref[pl.ds(160 * i + 32 * j + t, 8, stride=4), :] = columns[
                    first : first + 8, 128 * i : 128 * i + 128
                ]
    for j in range(5):
        for i in range(5):
            first = 160 * i + 32 * j
            out_ref[j, :, 128 * i : 128 * i + 128] = column_ref[first : first + 32, :]


def combine_kernel(sums_ref, first_ref, second_ref, third_ref, out_ref, turn_ref):
    total = sums_ref[0]
    for p in range(1, GRID):
        total = total + sums_ref[p]
    moment = [total[n : n + 1] for n in range(6)]
    lane = lax.broadcasted_iota(jnp.int32, (1, 128), 1)
    mode_pair = 16 * lax.axis_index("span") + (lane >> 1)
    ratio = mode_pair.astype(jnp.float32) * (1.0 / KMODES)
    center = 0.2 * (1.0 + SPAN_STIFF * ratio * ratio) + 0.15

    def product(left, right):
        terms = None
        for a in range(len(left)):
            for b in range(len(right)):
                term = left[a] * right[b] * moment[a + b]
                terms = term if terms is None else terms + term
        return terms

    def operator(c):
        shifted = [center * v for v in c] + [0.0]
        return [shifted[0]] + [shifted[a + 1] + c[a] for a in range(len(c))]

    residual = [jnp.ones((1, 128), jnp.float32)]
    direction = residual
    result = [0.0, 0.0, 0.0]
    norm = moment[0]
    for step in range(ITERS):
        applied = operator(direction)
        length = norm / product(direction, applied)
        for a in range(len(direction)):
            result[a] = result[a] + length * direction[a]
        if step < ITERS - 1:
            padded = residual + [0.0]
            residual = [padded[a] - length * applied[a] for a in range(len(applied))]
            fresh = product(residual, residual)
            ratio = fresh / norm
            norm = fresh
            padded = direction + [0.0]
            direction = [residual[a] + ratio * padded[a] for a in range(len(residual))]
    turn_ref[...] = jnp.zeros((128, 128), jnp.float32)
    for a in range(3):
        turn_ref[a : a + 1, :] = result[a]
    turned = turn_ref[...].T[0:32]
    weight = [turned[:, a : a + 1] for a in range(3)]
    for j in range(5):
        out_ref[j] = (
            weight[0] * first_ref[j] + weight[1] * second_ref[j] + weight[2] * third_ref[j]
        )


def call(kernel, name, out_shapes, *args, smem=(), anywhere=(), scratch=()):
    vmem = pl.BlockSpec(memory_space=pltpu.VMEM)
    spaces = {n: pl.BlockSpec(memory_space=pltpu.SMEM) for n in smem}
    spaces |= {n: pl.BlockSpec(memory_space=pltpu.HBM) for n in anywhere}
    return pl.pallas_call(
        kernel,
        name=name,
        out_shape=[jax.ShapeDtypeStruct(s, jnp.float32) for s in out_shapes],
        in_specs=[spaces.get(n, vmem) for n in range(len(args))],
        out_specs=[vmem] * len(out_shapes),
        scratch_shapes=list(scratch),
        compiler_params=pltpu.CompilerParams(vmem_limit_bytes=16 * 1024 * 1024),
    )(*args)


def from_neighbours(low, high):
    below = lax.ppermute(high, "plane", [(p, (p + 1) % GRID) for p in range(GRID)])
    above = lax.ppermute(low, "plane", [(p, (p - 1) % GRID) for p in range(GRID)])
    return below, above


def on_device(state, wall_tag):
    high_table, low_table = wave_table()
    (packed,) = call(
        pack_kernel, "pack", [(16, 32, 256)], jnp.transpose(state, (1, 0, 2)),
        anywhere=(0,),
        scratch=[
            pltpu.VMEM((800, 128), jnp.float32), pltpu.VMEM((5, 32, 640), jnp.float32),
            pltpu.VMEM((640, 640), jnp.bfloat16), pltpu.SemaphoreType.DMA(()),
        ],
    )
    modal = lax.all_to_all(packed, "span", 0, 0, tiled=True)
    nodal, low, high = call(
        turn_kernel, "turn", [(2, 256, 256), (2, 40, 256), (2, 40, 256)], modal
    )
    below, above = from_neighbours(low, high)
    rows = (40, PLANES)
    field, rhs, rhs_low, rhs_high = call(
        volume_kernel, "volume", [(200, PLANES), (200, PLANES), rows, rows], nodal, high_table,
        low_table, scratch=[pltpu.VMEM(rows, jnp.float32)],
    )
    rhs_below, rhs_above = from_neighbours(rhs_low, rhs_high)
    (inside,) = call(
        inside_kernel, "inside", [(2, 256, 256)], modal, field, rhs, high_table, low_table
    )
    (sent,) = call(
        facing_kernel, "facing", [(16, 32, 256)], wall_tag, inside, field, below, above, rhs_below,
        rhs_above, high_table, low_table, smem=(0,), scratch=[pltpu.VMEM((80, PLANES), jnp.float32)],
    )
    load = lax.all_to_all(sent, "span", 0, 0, tiled=True)
    nodes, trace = (25, 32, 128), (5, 32, 128)
    first, joined, low, high = call(first_kernel, "first", [nodes, nodes, trace, trace], load)
    below, above = from_neighbours(low, high)
    second, joined, low, high = call(
        second_kernel, "second", [nodes, nodes, trace, trace], joined, below, above, first
    )
    below, above = from_neighbours(low, high)
    (packed,) = call(early_kernel, "early", [(32, 128)], first, second)
    third, sums = call(
        third_kernel, "third", [nodes, (16, 8, 128)], joined, below, above, second, packed,
        scratch=[pltpu.VMEM((128, 128), jnp.float32)],
    )
    sums = lax.all_to_all(sums, "plane", 0, 0, tiled=True)
    columns = [
        call(
            natural_kernel, "natural", [(5, 32, 640)], vector,
            scratch=[pltpu.VMEM((800, 128), jnp.float32)],
        )[0]
        for vector in (first, second, third)
    ]
    (columns,) = call(
        combine_kernel, "combine", [(5, 32, 640)], sums, *columns,
        scratch=[pltpu.VMEM((128, 128), jnp.float32)],
    )
    return jnp.transpose(columns, (1, 0, 2))


def solution(mesh):
    in_specs = (P("span", "plane", None), P())
    out_specs = P("span", "plane", None)
    return jax.shard_map(
        on_device, mesh=mesh, in_specs=in_specs, out_specs=out_specs, check_vma=False
    )
```

```python
import math

import jax
import jax.numpy as jnp
import numpy as np
from jax import lax
from jax.experimental import pallas as pl
from jax.experimental.pallas import tpu as pltpu
from jax.sharding import PartitionSpec as P

KMODES = 256
PLANES = 768
HALF = 384
ITERS = 3
GRID = 16
STEP_SIZE = 0.03
VISCOUS = 0.05
SPAN_STIFF = 4.0


def gll_tables():
    abscissae = np.array([-1.0, -math.sqrt(3.0 / 7.0), 0.0, math.sqrt(3.0 / 7.0), 1.0])
    weights = np.array([0.1, 49.0 / 90.0, 32.0 / 45.0, 49.0 / 90.0, 0.1])
    squared = abscissae * abscissae
    legendre = (35.0 * squared * squared - 30.0 * squared + 3.0) / 8.0
    identity = np.eye(5)
    spacing = abscissae[:, None] - abscissae[None, :] + identity
    differ = np.where(identity > 0, 0.0, legendre[:, None] / legendre[None, :] / spacing)
    differ[0, 0] = -5.0
    differ[4, 4] = 5.0
    stiffness = differ.T @ (weights[:, None] * differ)
    return differ, weights, stiffness


DIFFER, WEIGHTS, STIFFNESS = gll_tables()


def split_table(table):
    high = table.astype(np.float32).astype(jnp.bfloat16)
    low = (table - high.astype(np.float64)).astype(np.float32).astype(jnp.bfloat16)
    return jnp.asarray(np.stack([high, low]))


def wave_table():
    plane = np.arange(HALF)
    waves = []
    for parity in range(2):
        k = 2 * np.arange(128) + parity
        angle = (k[:, None] * plane[None, :] % PLANES) * (2.0 * math.pi / PLANES)
        waves.append(np.concatenate([np.cos(angle), np.sin(angle)]))
    return split_table(np.stack(waves))


def dot(left, right, contract):
    return lax.dot_general(
        left, right, (contract, ((), ())), preferred_element_type=jnp.float32
    )


def halves(value):
    high = value.astype(jnp.bfloat16)
    low = (value - high.astype(jnp.float32)).astype(jnp.bfloat16)
    return high, low


def thirds(value):
    high = value.astype(jnp.bfloat16)
    rest = value - high.astype(jnp.float32)
    middle = rest.astype(jnp.bfloat16)
    low = (rest - middle.astype(jnp.float32)).astype(jnp.bfloat16)
    return high, middle, low


def dot_split(left, right, contract):
    (left_high, left_low), (right_high, right_low) = left, right
    return (
        dot(left_high, right_low, contract)
        + dot(left_low, right_high, contract)
        + dot(left_high, right_high, contract)
    )


def column_order():
    column = lax.broadcasted_iota(jnp.int32, (640, 128), 0)
    element = lax.broadcasted_iota(jnp.int32, (640, 128), 1)
    tiles = [jnp.where(column == 5 * element + i, 1.0, 0.0).astype(jnp.bfloat16) for i in range(5)]
    return jnp.concatenate(tiles, axis=1)


def exchange_chunks(values):
    values = list(values)
    lane = lax.broadcasted_iota(jnp.int32, values[0].shape, 1)
    for bit in (1, 2, 4, 8):
        upper = (lane & (8 * bit)) != 0
        for a in range(16):
            if a & bit == 0:
                first, second = values[a], values[a | bit]
                values[a] = jnp.where(upper, pltpu.roll(second, 8 * bit, 1), first)
                values[a | bit] = jnp.where(upper, second, pltpu.roll(first, 128 - 8 * bit, 1))
    return values


def pack_kernel(state_hbm, out_hbm, chunk_ref, state_ref, order_ref, packed_ref, arrived, sent):
    copy = pltpu.make_async_copy(state_hbm, state_ref, arrived)
    copy.start()
    order_ref[...] = column_order()
    copy.wait()
    stacked = jnp.concatenate([state_ref[j] for j in range(5)], axis=0)
    order = order_ref[...]
    contract = ((1,), (0,))
    high, low = halves(stacked)
    nodes = dot(low, order, contract) + dot(high, order, contract)
    for i in range(5):
        chunk_ref[160 * i : 160 * i + 160, :] = nodes[:, 128 * i : 128 * i + 128]
    chunk = [
        jnp.concatenate(
            [chunk_ref[pl.ds(160 * i + 32 * j + t, 8, stride=4), :] for t in range(4)], axis=0
        )
        for j in range(5)
        for i in range(5)
    ]
    lane = lax.broadcasted_iota(jnp.int32, (32, 128), 1) & 7
    for j in range(5):
        left = pltpu.roll(chunk[j * 5 + 4], 1, 1)
        right = pltpu.roll(chunk[j * 5], 127, 1)
        chunk.append(jnp.where(lane == 0, left, jnp.where(lane == 7, right, 0.0)))
    zero = jnp.zeros((32, 128), jnp.float32)
    chunk = chunk + [zero, zero]
    copies = []
    for half in range(2):
        block = exchange_chunks(chunk[16 * half : 16 * half + 16])
        for d in range(GRID):
            packed_ref[half, d] = block[d]
        lanes = pl.ds(128 * half, 128)
        copies.append(
            pltpu.make_async_copy(packed_ref.at[half], out_hbm.at[:, :, lanes], sent.at[half])
        )
        copies[half].start()
    for copy in copies:
        copy.wait()


def synthesize(nodal, table_ref):
    part = [
        dot_split(
            halves(nodal[parity]), (table_ref[0, parity], table_ref[1, parity]), ((1,), (0,))
        )
        for parity in range(2)
    ]
    scale = 1.0 / math.sqrt(KMODES)
    return scale * (part[0] + part[1]), scale * (part[0] - part[1])


def two_point(left, right):
    mean = (left * left + left * right + right * right) * (1.0 / 6.0)
    speed = jnp.maximum(jnp.abs(left), jnp.abs(right))
    return mean - 0.5 * speed * (right - left)


def volume_kernel(modal_ref, table_ref, field_ref, rhs_ref, low_ref, high_ref, side_ref):
    nodal = []
    for parity in range(2):
        rows = [
            modal_ref[s, 16 * parity + 8 * t : 16 * parity + 8 * t + 8, :]
            for t in range(2)
            for s in range(GRID)
        ]
        nodal.append(jnp.concatenate(rows, axis=0).T)
        lanes = slice(PLANES + 256 * parity, PLANES + 256 * parity + 256)
        low_ref[:, lanes] = nodal[parity][0:40]
        high_ref[:, lanes] = nodal[parity][160:200]
    pair = synthesize(nodal, table_ref)
    for q in range(2):
        field_ref[:, HALF * q : HALF * q + HALF] = pair[q][0:200]
        side_ref[:, HALF * q : HALF * q + HALF] = pair[q][200:240]
    row = lax.broadcasted_iota(jnp.int32, (8, 128), 0)

    def column(block, carry):
        lanes = pl.ds(pl.multiple_of(block * 128, 128), 128)
        f = [field_ref[8 * n : 8 * n + 8, lanes] for n in range(25)]
        square = [v * v for v in f]
        for j in range(5):
            for i in range(5):
                n = j * 5 + i
                plain = None
                power = None
                for other in range(5):
                    terms = [(DIFFER[i][other], j * 5 + other), (DIFFER[j][other], other * 5 + i)]
                    for weight, m in terms:
                        if weight == 0.0:
                            continue
                        weight = float(weight) / -3.0
                        plain = weight * f[m] if plain is None else plain + weight * f[m]
                        power = weight * square[m] if power is None else power + weight * square[m]
                total = power + f[n] * plain
                own = (i == 4) + (j == 4) - (i == 0) - (j == 0)
                if own:
                    total = total + (5.0 * own) * square[n]
                if i == 0 or i == 4:
                    side = side_ref[8 * j : 8 * j + 8, lanes]
                    if i == 0:
                        left = jnp.where(row == 0, side, pltpu.roll(f[j * 5 + 4], 1, 0))
                        total = total + 10.0 * two_point(left, f[n])
                    else:
                        right = jnp.where(row == 7, side, pltpu.roll(f[j * 5], 7, 0))
                        total = total - 10.0 * two_point(f[n], right)
                rhs_ref[8 * n : 8 * n + 8, lanes] = total
                if j == 0:
                    low_ref[8 * i : 8 * i + 8, lanes] = total
                elif j == 4:
                    high_ref[8 * i : 8 * i + 8, lanes] = total
        return carry

    lax.fori_loop(0, PLANES // 128, column, 0)


def project(planar, parity, table_ref):
    folded = planar[:, :HALF] + planar[:, HALF:] if parity == 0 else planar[:, :HALF] - planar[:, HALF:]
    return dot_split((table_ref[0, parity], table_ref[1, parity]), halves(folded), ((1,), (1,)))


def tendency(parity, from_rhs, from_flux):
    k = 2 * lax.broadcasted_iota(jnp.int32, (128, 128), 0) + parity
    scale = jnp.where(k == 0, 1.0, 2.0) * (math.sqrt(KMODES) / PLANES * STEP_SIZE)
    ratio = k.astype(jnp.float32) * (1.0 / KMODES)
    return (
        scale * (from_rhs[0:128] - ratio * from_flux[128:256]),
        scale * (from_rhs[128:256] + ratio * from_flux[0:128]),
    )


def inside_kernel(modal_ref, field_ref, rhs_ref, table_ref, out_ref):
    field = field_ref[...]
    flux = 0.5 * field * field
    rhs = rhs_ref[...]
    tail = jnp.zeros((56, PLANES), jnp.float32)
    flux = jnp.concatenate([flux, tail], axis=0)
    rhs = jnp.concatenate([rhs, tail], axis=0)
    for parity in range(2):
        from_rhs = project(rhs, parity, table_ref)
        from_flux = project(flux, parity, table_ref)
        for half in range(2):
            lanes = slice(128 * half, 128 * half + 128)
            change = tendency(parity, from_rhs[:, lanes], from_flux[:, lanes])
            for t in range(2):
                first = 16 * parity + 8 * t
                modal = jnp.concatenate(
                    [modal_ref[s, first : first + 8, lanes] for s in range(GRID)], axis=0
                )
                out_ref[parity, 128 * t : 128 * t + 128, lanes] = modal + change[t]


def facing_kernel(
    tag_ref, inside_ref, field_ref, below_ref, above_ref, table_ref, out_ref, outer_ref
):
    bottom, top = at_ends()
    span = lax.axis_index("span")
    row = lax.broadcasted_iota(jnp.int32, (8, 128), 0)
    mirror = jnp.ones((8, 128), jnp.float32)
    for e in range(8):
        mirror = jnp.where((row == e) & (tag_ref[8 * span + e] == 1), -1.0, mirror)
    below_modal, above_modal = [
        [ref[:, PLANES + 256 * parity : PLANES + 256 * parity + 256] for parity in range(2)]
        for ref in (below_ref, above_ref)
    ]
    outer = [
        jnp.concatenate([below_modal[parity], above_modal[parity]], axis=0) for parity in range(2)
    ]
    pair = synthesize(outer, table_ref)
    for q in range(2):
        outer_ref[:, HALF * q : HALF * q + HALF] = pair[q]
    mirror = jnp.concatenate([mirror] * 6, axis=1)
    mirror = jnp.concatenate([mirror] * 5, axis=0)
    inside = field_ref[0:40, :]
    below = outer_ref[0:40, :]
    lift = 10.0 * two_point(jnp.where(bottom, mirror * inside, below), inside)
    rhs_lower = lift + jnp.where(bottom, 0.0, below_ref[:, 0:PLANES] - lift)
    flux_lower = jnp.where(bottom, 0.0, 0.5 * below * below)
    inside = field_ref[160:200, :]
    above = outer_ref[40:80, :]
    lift = 10.0 * two_point(inside, jnp.where(top, inside, above))
    rhs_upper = jnp.where(top, 0.0, above_ref[:, 0:PLANES] + lift) - lift
    flux_upper = jnp.where(top, 0.0, 0.5 * above * above)
    gap = jnp.zeros((48, PLANES), jnp.float32)
    planar = jnp.concatenate([rhs_lower, rhs_upper, gap, flux_lower, flux_upper, gap], axis=0)
    gap = jnp.zeros((48, 256), jnp.float32)
    keep_lower = jnp.where(bottom, 0.0, 1.0)
    keep_upper = jnp.where(top, 0.0, 1.0)
    lane = lax.broadcasted_iota(jnp.int32, (128, 128), 1)
    for parity in range(2):
        projected = project(planar, parity, table_ref)
        change = tendency(parity, projected[:, 0:128], projected[:, 128:256])
        modal = jnp.concatenate(
            [keep_lower * below_modal[parity], keep_upper * above_modal[parity], gap], axis=0
        ).T
        for t in range(2):
            first = 16 * parity + 8 * t
            extra = change[t] + modal[128 * t : 128 * t + 128]
            lower = jnp.where(lane < 40, extra, 0.0)
            upper = pltpu.roll(jnp.where(lane < 40, 0.0, extra), 120, 1)
            for half, added in ((0, lower), (1, upper)):
                lanes = slice(128 * half, 128 * half + 128)
                total = inside_ref[parity, 128 * t : 128 * t + 128, lanes] + added
                for s in range(GRID):
                    out_ref[s, first : first + 8, lanes] = total[8 * s : 8 * s + 8]


def at_ends():
    plane = lax.axis_index("plane")
    return plane == 0, plane == GRID - 1


def local_operator(values, shift):
    out = []
    for j in range(5):
        for i in range(5):
            n = j * 5 + i
            mass = float(WEIGHTS[j] * WEIGHTS[i])
            diagonal = VISCOUS * float(WEIGHTS[j] * STIFFNESS[i][i] + WEIGHTS[i] * STIFFNESS[j][j])
            value = (shift * mass + diagonal) * values[n]
            for other in range(5):
                if other != i:
                    weight = VISCOUS * float(WEIGHTS[j] * STIFFNESS[i][other])
                    value = value + weight * values[j * 5 + other]
                if other != j:
                    weight = VISCOUS * float(WEIGHTS[i] * STIFFNESS[j][other])
                    value = value + weight * values[other * 5 + i]
            out.append(value)
    return out


def join_columns(values):
    values = list(values)
    for j in range(5):
        joint = values[j * 5 + 4] + pltpu.roll(values[j * 5], 127, 1)
        values[j * 5 + 4] = joint
        values[j * 5] = pltpu.roll(joint, 1, 1)
    return values


def store_joined(values, joined_ref, low_ref, high_ref):
    values = join_columns(values)
    for n in range(25):
        joined_ref[n] = values[n]
    for i in range(5):
        low_ref[i] = values[i]
        high_ref[i] = values[20 + i]


def assembled(joined_ref, below_ref, above_ref):
    values = [joined_ref[n] for n in range(25)]
    bottom, top = at_ends()
    for i in range(5):
        values[i] = values[i] + jnp.where(bottom, 0.0, below_ref[i])
        values[20 + i] = values[20 + i] + jnp.where(top, 0.0, above_ref[i])
    return values


def mode_terms():
    row = lax.broadcasted_iota(jnp.int32, (32, 128), 0)
    mode_pair = 16 * lax.axis_index("span") + 2 * (row & 7) + (row >> 4)
    ratio = mode_pair.astype(jnp.float32) * (1.0 / KMODES)
    shift = 1.0 + SPAN_STIFF * ratio * ratio
    return shift, 0.2 * shift + 0.15


def inner(left, right):
    bottom, top = at_ends()
    total = None
    for j in range(5):
        part = None
        for i in range(5):
            term = left[j * 5 + i] * right[j * 5 + i]
            term = term if 0 < i < 4 else 0.5 * term
            part = term if part is None else part + term
        if j == 0:
            part = jnp.where(bottom, 1.0, 0.5) * part
        elif j == 4:
            part = jnp.where(top, 1.0, 0.5) * part
        total = part if total is None else total + part
    return total


def first_kernel(modal_ref, vector_ref, next_ref, low_ref, high_ref):
    shift, _ = mode_terms()
    values = []
    for half in range(2):
        values += exchange_chunks(
            [modal_ref[s, :, 128 * half : 128 * half + 128] for s in range(GRID)]
        )
    values = [float(WEIGHTS[n // 5] * WEIGHTS[n % 5]) * values[n] for n in range(25)]
    vector = join_columns(values)
    for n in range(25):
        vector_ref[n] = vector[n]
    store_joined(local_operator(vector, shift), next_ref, low_ref, high_ref)


def second_kernel(
    joined_ref, below_ref, above_ref, before_ref, vector_ref, next_ref, low_ref,
    high_ref,
):
    shift, center = mode_terms()
    applied = assembled(joined_ref, below_ref, above_ref)
    vector = [applied[n] - center * before_ref[n] for n in range(25)]
    for n in range(25):
        vector_ref[n] = vector[n]
    store_joined(local_operator(vector, shift), next_ref, low_ref, high_ref)


def pack_moments(moments, first, packed):
    lane = lax.broadcasted_iota(jnp.int32, (32, 128), 1)
    for n, moment in enumerate(moments):
        packed = jnp.where(lane == first + n, jnp.sum(moment, axis=1, keepdims=True), packed)
    return packed


def early_kernel(first_ref, second_ref, packed_ref):
    first = [first_ref[n] for n in range(25)]
    second = [second_ref[n] for n in range(25)]
    moments = [
        inner(first, first),
        inner(first, second),
        inner(second, second),
    ]
    packed_ref[...] = pack_moments(moments, 0, jnp.zeros((32, 128), jnp.float32))


def third_kernel(
    joined_ref, below_ref, above_ref, second_ref, packed_ref, vector_ref, sums_ref,
    turn_ref,
):
    shift, center = mode_terms()
    applied = assembled(joined_ref, below_ref, above_ref)
    second = [second_ref[n] for n in range(25)]
    third = [applied[n] - center * second[n] for n in range(25)]
    for n in range(25):
        vector_ref[n] = third[n]
    fourth = inner(third, third)
    local = local_operator(third, shift)
    fifth = -center * fourth
    for n in range(25):
        fifth = fifth + local[n] * third[n]
    moments = [inner(second, third), fourth, fifth]
    packed = pack_moments(moments, 3, packed_ref[...])
    turn_ref[...] = jnp.zeros((128, 128), jnp.float32)
    for t in range(4):
        turn_ref[pl.ds(t, 8, stride=4), :] = packed[8 * t : 8 * t + 8]
    turned = turn_ref[...].T[0:8]
    for p in range(GRID):
        sums_ref[p] = turned


def natural_kernel(vector_ref, out_ref, column_ref):
    order = column_order()
    stacked = jnp.concatenate(
        [
            jnp.concatenate([vector_ref[j * 5 + i] for i in range(5)], axis=1) for j in range(5)
        ],
        axis=0,
    )
    contract = ((1,), (1,))
    high, middle, low = thirds(stacked)
    columns = dot(low, order, contract) + dot(middle, order, contract) + dot(high, order, contract)
    for i in range(5):
        for j in range(5):
            for t in range(4):
                first = 32 * j + 8 * t
                column_ref[pl.ds(160 * i + 32 * j + t, 8, stride=4), :] = columns[
                    first : first + 8, 128 * i : 128 * i + 128
                ]
    for j in range(5):
        for i in range(5):
            first = 160 * i + 32 * j
            out_ref[j, :, 128 * i : 128 * i + 128] = column_ref[first : first + 32, :]


def combine_kernel(sums_ref, first_ref, second_ref, third_ref, out_ref, turn_ref):
    total = sums_ref[0]
    for p in range(1, GRID):
        total = total + sums_ref[p]
    moment = [total[n : n + 1] for n in range(6)]
    lane = lax.broadcasted_iota(jnp.int32, (1, 128), 1)
    mode_pair = 16 * lax.axis_index("span") + (lane >> 1)
    ratio = mode_pair.astype(jnp.float32) * (1.0 / KMODES)
    center = 0.2 * (1.0 + SPAN_STIFF * ratio * ratio) + 0.15

    def product(left, right):
        terms = None
        for a in range(len(left)):
            for b in range(len(right)):
                term = left[a] * right[b] * moment[a + b]
                terms = term if terms is None else terms + term
        return terms

    def operator(c):
        shifted = [center * v for v in c] + [0.0]
        return [shifted[0]] + [shifted[a + 1] + c[a] for a in range(len(c))]

    residual = [jnp.ones((1, 128), jnp.float32)]
    direction = residual
    result = [0.0, 0.0, 0.0]
    norm = moment[0]
    for step in range(ITERS):
        applied = operator(direction)
        length = norm / product(direction, applied)
        for a in range(len(direction)):
            result[a] = result[a] + length * direction[a]
        if step < ITERS - 1:
            padded = residual + [0.0]
            residual = [padded[a] - length * applied[a] for a in range(len(applied))]
            fresh = product(residual, residual)
            ratio = fresh / norm
            norm = fresh
            padded = direction + [0.0]
            direction = [residual[a] + ratio * padded[a] for a in range(len(residual))]
    turn_ref[...] = jnp.zeros((128, 128), jnp.float32)
    for a in range(3):
        turn_ref[a : a + 1, :] = result[a]
    turned = turn_ref[...].T[0:32]
    weight = [turned[:, a : a + 1] for a in range(3)]
    for j in range(5):
        out_ref[j] = (
            weight[0] * first_ref[j] + weight[1] * second_ref[j] + weight[2] * third_ref[j]
        )


def call(kernel, name, out_shapes, *args, smem=(), anywhere=(), scratch=(), limit=16):
    vmem = pl.BlockSpec(memory_space=pltpu.VMEM)
    spaces = {n: pl.BlockSpec(memory_space=pltpu.SMEM) for n in smem}
    spaces |= {n: pl.BlockSpec(memory_space=pltpu.HBM) for n in anywhere}
    return pl.pallas_call(
        kernel,
        name=name,
        out_shape=[jax.ShapeDtypeStruct(s, jnp.float32) for s in out_shapes],
        in_specs=[spaces.get(n, vmem) for n in range(len(args))],
        out_specs=[pl.BlockSpec(memory_space=pltpu.HBM) if anywhere else vmem] * len(out_shapes),
        scratch_shapes=list(scratch),
        compiler_params=pltpu.CompilerParams(vmem_limit_bytes=limit * 1024 * 1024),
    )(*args)


def from_neighbours(low, high):
    below = lax.ppermute(high, "plane", [(p, (p + 1) % GRID) for p in range(GRID)])
    above = lax.ppermute(low, "plane", [(p, (p - 1) % GRID) for p in range(GRID)])
    return below, above


def on_device(state, wall_tag):
    table = wave_table()
    (packed,) = call(
        pack_kernel, "pack", [(16, 32, 256)], jnp.transpose(state, (1, 0, 2)),
        anywhere=(0,), limit=60,
        scratch=[
            pltpu.VMEM((800, 128), jnp.float32), pltpu.VMEM((5, 32, 640), jnp.float32),
            pltpu.VMEM((640, 640), jnp.bfloat16), pltpu.VMEM((2, 16, 32, 128), jnp.float32),
            pltpu.SemaphoreType.DMA(()), pltpu.SemaphoreType.DMA((2,)),
        ],
    )
    modal = lax.all_to_all(packed, "span", 0, 0, tiled=True)
    trace = (40, PLANES + 512)
    field, rhs, low, high = call(
        volume_kernel, "volume", [(200, PLANES), (200, PLANES), trace, trace], modal, table,
        scratch=[pltpu.VMEM((40, PLANES), jnp.float32)],
    )
    below, above = from_neighbours(low, high)
    (inside,) = call(inside_kernel, "inside", [(2, 256, 256)], modal, field, rhs, table)
    (sent,) = call(
        facing_kernel, "facing", [(16, 32, 256)], wall_tag, inside, field, below, above, table,
        smem=(0,), scratch=[pltpu.VMEM((80, PLANES), jnp.float32)],
    )
    load = lax.all_to_all(sent, "span", 0, 0, tiled=True)
    nodes, trace = (25, 32, 128), (5, 32, 128)
    first, joined, low, high = call(first_kernel, "first", [nodes, nodes, trace, trace], load)
    below, above = from_neighbours(low, high)
    second, joined, low, high = call(
        second_kernel, "second", [nodes, nodes, trace, trace], joined, below, above, first
    )
    below, above = from_neighbours(low, high)
    (packed,) = call(early_kernel, "early", [(32, 128)], first, second)
    third, sums = call(
        third_kernel, "third", [nodes, (16, 8, 128)], joined, below, above, second, packed,
        scratch=[pltpu.VMEM((128, 128), jnp.float32)],
    )
    sums = lax.all_to_all(sums, "plane", 0, 0, tiled=True)
    columns = [
        call(
            natural_kernel, "natural", [(5, 32, 640)], vector,
            scratch=[pltpu.VMEM((800, 128), jnp.float32)],
        )[0]
        for vector in (first, second, third)
    ]
    (columns,) = call(
        combine_kernel, "combine", [(5, 32, 640)], sums, *columns,
        scratch=[pltpu.VMEM((128, 128), jnp.float32)],
    )
    return jnp.transpose(columns, (1, 0, 2))


def solution(mesh):
    in_specs = (P("span", "plane", None), P())
    out_specs = P("span", "plane", None)
    return jax.shard_map(
        on_device, mesh=mesh, in_specs=in_specs, out_specs=out_specs, check_vma=False
    )
```

```python
import math

import jax
import jax.numpy as jnp
import numpy as np
from jax import lax
from jax.experimental import pallas as pl
from jax.experimental.pallas import tpu as pltpu
from jax.sharding import PartitionSpec as P

KMODES = 256
PLANES = 768
HALF = 384
ITERS = 3
GRID = 16
STEP_SIZE = 0.03
VISCOUS = 0.05
SPAN_STIFF = 4.0


def gll_tables():
    abscissae = np.array([-1.0, -math.sqrt(3.0 / 7.0), 0.0, math.sqrt(3.0 / 7.0), 1.0])
    weights = np.array([0.1, 49.0 / 90.0, 32.0 / 45.0, 49.0 / 90.0, 0.1])
    squared = abscissae * abscissae
    legendre = (35.0 * squared * squared - 30.0 * squared + 3.0) / 8.0
    identity = np.eye(5)
    spacing = abscissae[:, None] - abscissae[None, :] + identity
    differ = np.where(identity > 0, 0.0, legendre[:, None] / legendre[None, :] / spacing)
    differ[0, 0] = -5.0
    differ[4, 4] = 5.0
    stiffness = differ.T @ (weights[:, None] * differ)
    return differ, weights, stiffness


DIFFER, WEIGHTS, STIFFNESS = gll_tables()


def split_table(table):
    high = table.astype(np.float32).astype(jnp.bfloat16)
    low = (table - high.astype(np.float64)).astype(np.float32).astype(jnp.bfloat16)
    return jnp.asarray(np.stack([high, low]))


def wave_table():
    plane = np.arange(HALF)
    waves = []
    for parity in range(2):
        k = 2 * np.arange(128) + parity
        angle = (k[:, None] * plane[None, :] % PLANES) * (2.0 * math.pi / PLANES)
        waves.append(np.concatenate([np.cos(angle), np.sin(angle)]))
    return split_table(np.stack(waves))


def dot(left, right, contract):
    return lax.dot_general(
        left, right, (contract, ((), ())), preferred_element_type=jnp.float32
    )


def halves(value):
    high = value.astype(jnp.bfloat16)
    low = (value - high.astype(jnp.float32)).astype(jnp.bfloat16)
    return high, low


def thirds(value):
    high = value.astype(jnp.bfloat16)
    rest = value - high.astype(jnp.float32)
    middle = rest.astype(jnp.bfloat16)
    low = (rest - middle.astype(jnp.float32)).astype(jnp.bfloat16)
    return high, middle, low


def dot_split(left, right, contract):
    (left_high, left_low), (right_high, right_low) = left, right
    return (
        dot(left_high, right_low, contract)
        + dot(left_low, right_high, contract)
        + dot(left_high, right_high, contract)
    )


def column_order():
    column = lax.broadcasted_iota(jnp.int32, (640, 128), 0)
    element = lax.broadcasted_iota(jnp.int32, (640, 128), 1)
    tiles = [jnp.where(column == 5 * element + i, 1.0, 0.0).astype(jnp.bfloat16) for i in range(5)]
    return jnp.concatenate(tiles, axis=1)


def exchange_chunks(values):
    values = list(values)
    lane = lax.broadcasted_iota(jnp.int32, values[0].shape, 1)
    for bit in (1, 2, 4, 8):
        upper = (lane & (8 * bit)) != 0
        for a in range(16):
            if a & bit == 0:
                first, second = values[a], values[a | bit]
                values[a] = jnp.where(upper, pltpu.roll(second, 8 * bit, 1), first)
                values[a | bit] = jnp.where(upper, second, pltpu.roll(first, 128 - 8 * bit, 1))
    return values


def pack_kernel(state_hbm, out_ref, chunk_ref, state_ref, order_ref, arrived):
    copy = pltpu.make_async_copy(state_hbm, state_ref, arrived)
    copy.start()
    order_ref[...] = column_order()
    copy.wait()
    stacked = jnp.concatenate([state_ref[j] for j in range(5)], axis=0)
    order = order_ref[...]
    contract = ((1,), (0,))
    high, low = halves(stacked)
    nodes = dot(low, order, contract) + dot(high, order, contract)
    for i in range(5):
        chunk_ref[160 * i : 160 * i + 160, :] = nodes[:, 128 * i : 128 * i + 128]
    chunk = [
        jnp.concatenate(
            [chunk_ref[pl.ds(160 * i + 32 * j + t, 8, stride=4), :] for t in range(4)], axis=0
        )
        for j in range(5)
        for i in range(5)
    ]
    lane = lax.broadcasted_iota(jnp.int32, (32, 128), 1) & 7
    for j in range(5):
        left = pltpu.roll(chunk[j * 5 + 4], 1, 1)
        right = pltpu.roll(chunk[j * 5], 127, 1)
        chunk.append(jnp.where(lane == 0, left, jnp.where(lane == 7, right, 0.0)))
    zero = jnp.zeros((32, 128), jnp.float32)
    chunk = chunk + [zero, zero]
    for half in range(2):
        block = exchange_chunks(chunk[16 * half : 16 * half + 16])
        for d in range(GRID):
            out_ref[d, :, 128 * half : 128 * half + 128] = block[d]


def synthesize(nodal, table_ref):
    part = [
        dot_split(
            halves(nodal[parity]), (table_ref[0, parity], table_ref[1, parity]), ((1,), (0,))
        )
        for parity in range(2)
    ]
    scale = 1.0 / math.sqrt(KMODES)
    return scale * (part[0] + part[1]), scale * (part[0] - part[1])


def two_point(left, right):
    mean = (left * left + left * right + right * right) * (1.0 / 6.0)
    speed = jnp.maximum(jnp.abs(left), jnp.abs(right))
    return mean - 0.5 * speed * (right - left)


def volume_kernel(modal_ref, table_ref, field_ref, rhs_ref, cross_ref, chip_ref, side_ref):
    nodal = []
    for parity in range(2):
        rows = [
            modal_ref[s, 16 * parity + 8 * t : 16 * parity + 8 * t + 8, :]
            for t in range(2)
            for s in range(GRID)
        ]
        nodal.append(jnp.concatenate(rows, axis=0).T)
        lanes = slice(PLANES + 256 * parity, PLANES + 256 * parity + 256)
        cross_ref[:, lanes], chip_ref[:, lanes] = to_partners(
            nodal[parity][0:40], nodal[parity][160:200]
        )
    pair = synthesize(nodal, table_ref)
    for q in range(2):
        field_ref[:, HALF * q : HALF * q + HALF] = pair[q][0:200]
        side_ref[:, HALF * q : HALF * q + HALF] = pair[q][200:240]
    row = lax.broadcasted_iota(jnp.int32, (8, 128), 0)

    def column(block, carry):
        lanes = pl.ds(pl.multiple_of(block * 128, 128), 128)
        f = [field_ref[8 * n : 8 * n + 8, lanes] for n in range(25)]
        square = [v * v for v in f]
        low = []
        for j in range(5):
            for i in range(5):
                n = j * 5 + i
                plain = None
                power = None
                for other in range(5):
                    terms = [(DIFFER[i][other], j * 5 + other), (DIFFER[j][other], other * 5 + i)]
                    for weight, m in terms:
                        if weight == 0.0:
                            continue
                        weight = float(weight) / -3.0
                        plain = weight * f[m] if plain is None else plain + weight * f[m]
                        power = weight * square[m] if power is None else power + weight * square[m]
                total = power + f[n] * plain
                own = (i == 4) + (j == 4) - (i == 0) - (j == 0)
                if own:
                    total = total + (5.0 * own) * square[n]
                if i == 0 or i == 4:
                    side = side_ref[8 * j : 8 * j + 8, lanes]
                    if i == 0:
                        left = jnp.where(row == 0, side, pltpu.roll(f[j * 5 + 4], 1, 0))
                        total = total + 10.0 * two_point(left, f[n])
                    else:
                        right = jnp.where(row == 7, side, pltpu.roll(f[j * 5], 7, 0))
                        total = total - 10.0 * two_point(f[n], right)
                rhs_ref[8 * n : 8 * n + 8, lanes] = total
                if j == 0:
                    low.append(total)
                elif j == 4:
                    rows = slice(8 * i, 8 * i + 8)
                    cross_ref[rows, lanes], chip_ref[rows, lanes] = to_partners(low[i], total)
        return carry

    lax.fori_loop(0, PLANES // 128, column, 0)


def project(planar, parity, table_ref):
    folded = planar[:, :HALF] + planar[:, HALF:] if parity == 0 else planar[:, :HALF] - planar[:, HALF:]
    return dot_split((table_ref[0, parity], table_ref[1, parity]), halves(folded), ((1,), (1,)))


def tendency(parity, from_rhs, from_flux):
    k = 2 * lax.broadcasted_iota(jnp.int32, (128, 128), 0) + parity
    scale = jnp.where(k == 0, 1.0, 2.0) * (math.sqrt(KMODES) / PLANES * STEP_SIZE)
    ratio = k.astype(jnp.float32) * (1.0 / KMODES)
    return (
        scale * (from_rhs[0:128] - ratio * from_flux[128:256]),
        scale * (from_rhs[128:256] + ratio * from_flux[0:128]),
    )


def inside_kernel(modal_ref, field_ref, rhs_ref, table_ref, out_ref):
    field = field_ref[...]
    flux = 0.5 * field * field
    rhs = rhs_ref[...]
    tail = jnp.zeros((56, PLANES), jnp.float32)
    flux = jnp.concatenate([flux, tail], axis=0)
    rhs = jnp.concatenate([rhs, tail], axis=0)
    for parity in range(2):
        from_rhs = project(rhs, parity, table_ref)
        from_flux = project(flux, parity, table_ref)
        for half in range(2):
            lanes = slice(128 * half, 128 * half + 128)
            change = tendency(parity, from_rhs[:, lanes], from_flux[:, lanes])
            for t in range(2):
                first = 16 * parity + 8 * t
                modal = jnp.concatenate(
                    [modal_ref[s, first : first + 8, lanes] for s in range(GRID)], axis=0
                )
                out_ref[parity, 128 * t : 128 * t + 128, lanes] = modal + change[t]


def facing_kernel(
    tag_ref, inside_ref, field_ref, cross_ref, chip_ref, table_ref, out_ref, outer_ref
):
    bottom, top = at_ends()
    span = lax.axis_index("span")
    row = lax.broadcasted_iota(jnp.int32, (8, 128), 0)
    mirror = jnp.ones((8, 128), jnp.float32)
    for e in range(8):
        mirror = jnp.where((row == e) & (tag_ref[8 * span + e] == 1), -1.0, mirror)
    below_trace, above_trace = from_partners(cross_ref[...], chip_ref[...])
    below_modal, above_modal = [
        [trace[:, PLANES + 256 * parity : PLANES + 256 * parity + 256] for parity in range(2)]
        for trace in (below_trace, above_trace)
    ]
    outer = [
        jnp.concatenate([below_modal[parity], above_modal[parity]], axis=0) for parity in range(2)
    ]
    pair = synthesize(outer, table_ref)
    for q in range(2):
        outer_ref[:, HALF * q : HALF * q + HALF] = pair[q]
    mirror = jnp.concatenate([mirror] * 6, axis=1)
    mirror = jnp.concatenate([mirror] * 5, axis=0)
    inside = field_ref[0:40, :]
    below = outer_ref[0:40, :]
    lift = 10.0 * two_point(jnp.where(bottom, mirror * inside, below), inside)
    rhs_lower = lift + jnp.where(bottom, 0.0, below_trace[:, 0:PLANES] - lift)
    flux_lower = jnp.where(bottom, 0.0, 0.5 * below * below)
    inside = field_ref[160:200, :]
    above = outer_ref[40:80, :]
    lift = 10.0 * two_point(inside, jnp.where(top, inside, above))
    rhs_upper = jnp.where(top, 0.0, above_trace[:, 0:PLANES] + lift) - lift
    flux_upper = jnp.where(top, 0.0, 0.5 * above * above)
    gap = jnp.zeros((48, PLANES), jnp.float32)
    planar = jnp.concatenate([rhs_lower, rhs_upper, gap, flux_lower, flux_upper, gap], axis=0)
    gap = jnp.zeros((48, 256), jnp.float32)
    keep_lower = jnp.where(bottom, 0.0, 1.0)
    keep_upper = jnp.where(top, 0.0, 1.0)
    lane = lax.broadcasted_iota(jnp.int32, (128, 128), 1)
    for parity in range(2):
        projected = project(planar, parity, table_ref)
        change = tendency(parity, projected[:, 0:128], projected[:, 128:256])
        modal = jnp.concatenate(
            [keep_lower * below_modal[parity], keep_upper * above_modal[parity], gap], axis=0
        ).T
        for t in range(2):
            first = 16 * parity + 8 * t
            extra = change[t] + modal[128 * t : 128 * t + 128]
            lower = jnp.where(lane < 40, extra, 0.0)
            upper = pltpu.roll(jnp.where(lane < 40, 0.0, extra), 120, 1)
            for half, added in ((0, lower), (1, upper)):
                lanes = slice(128 * half, 128 * half + 128)
                total = inside_ref[parity, 128 * t : 128 * t + 128, lanes] + added
                for s in range(GRID):
                    out_ref[s, first : first + 8, lanes] = total[8 * s : 8 * s + 8]


def at_ends():
    plane = lax.axis_index("plane")
    return plane == 0, plane == GRID - 1


def to_partners(low, high):
    odd = lax.axis_index("plane") % 2 == 1
    return jnp.where(odd, high, low), jnp.where(odd, low, high)


def from_partners(cross, chip):
    odd = lax.axis_index("plane") % 2 == 1
    return jnp.where(odd, chip, cross), jnp.where(odd, cross, chip)


def local_operator(values, shift):
    out = []
    for j in range(5):
        for i in range(5):
            n = j * 5 + i
            mass = float(WEIGHTS[j] * WEIGHTS[i])
            diagonal = VISCOUS * float(WEIGHTS[j] * STIFFNESS[i][i] + WEIGHTS[i] * STIFFNESS[j][j])
            value = (shift * mass + diagonal) * values[n]
            for other in range(5):
                if other != i:
                    weight = VISCOUS * float(WEIGHTS[j] * STIFFNESS[i][other])
                    value = value + weight * values[j * 5 + other]
                if other != j:
                    weight = VISCOUS * float(WEIGHTS[i] * STIFFNESS[j][other])
                    value = value + weight * values[other * 5 + i]
            out.append(value)
    return out


def join_columns(values):
    values = list(values)
    for j in range(5):
        joint = values[j * 5 + 4] + pltpu.roll(values[j * 5], 127, 1)
        values[j * 5 + 4] = joint
        values[j * 5] = pltpu.roll(joint, 1, 1)
    return values


def store_joined(values, joined_ref, cross_ref, chip_ref):
    values = join_columns(values)
    for n in range(25):
        joined_ref[n] = values[n]
    for i in range(5):
        cross_ref[i], chip_ref[i] = to_partners(values[i], values[20 + i])


def assembled(joined_ref, cross_ref, chip_ref):
    values = [joined_ref[n] for n in range(25)]
    bottom, top = at_ends()
    for i in range(5):
        below, above = from_partners(cross_ref[i], chip_ref[i])
        values[i] = values[i] + jnp.where(bottom, 0.0, below)
        values[20 + i] = values[20 + i] + jnp.where(top, 0.0, above)
    return values


def mode_terms():
    row = lax.broadcasted_iota(jnp.int32, (32, 128), 0)
    mode_pair = 16 * lax.axis_index("span") + 2 * (row & 7) + (row >> 4)
    ratio = mode_pair.astype(jnp.float32) * (1.0 / KMODES)
    shift = 1.0 + SPAN_STIFF * ratio * ratio
    return shift, 0.2 * shift + 0.15


def inner(left, right):
    bottom, top = at_ends()
    total = None
    for j in range(5):
        part = None
        for i in range(5):
            term = left[j * 5 + i] * right[j * 5 + i]
            term = term if 0 < i < 4 else 0.5 * term
            part = term if part is None else part + term
        if j == 0:
            part = jnp.where(bottom, 1.0, 0.5) * part
        elif j == 4:
            part = jnp.where(top, 1.0, 0.5) * part
        total = part if total is None else total + part
    return total


def first_kernel(modal_ref, vector_ref, next_ref, cross_ref, chip_ref):
    shift, _ = mode_terms()
    values = []
    for half in range(2):
        values += exchange_chunks(
            [modal_ref[s, :, 128 * half : 128 * half + 128] for s in range(GRID)]
        )
    values = [float(WEIGHTS[n // 5] * WEIGHTS[n % 5]) * values[n] for n in range(25)]
    vector = join_columns(values)
    for n in range(25):
        vector_ref[n] = vector[n]
    store_joined(local_operator(vector, shift), next_ref, cross_ref, chip_ref)


def second_kernel(
    joined_ref, cross_in_ref, chip_in_ref, before_ref, vector_ref, next_ref, cross_ref, chip_ref
):
    shift, center = mode_terms()
    applied = assembled(joined_ref, cross_in_ref, chip_in_ref)
    vector = [applied[n] - center * before_ref[n] for n in range(25)]
    for n in range(25):
        vector_ref[n] = vector[n]
    store_joined(local_operator(vector, shift), next_ref, cross_ref, chip_ref)


def pack_moments(moments, first, packed):
    lane = lax.broadcasted_iota(jnp.int32, (32, 128), 1)
    for n, moment in enumerate(moments):
        packed = jnp.where(lane == first + n, jnp.sum(moment, axis=1, keepdims=True), packed)
    return packed


def early_kernel(first_ref, second_ref, packed_ref):
    first = [first_ref[n] for n in range(25)]
    second = [second_ref[n] for n in range(25)]
    moments = [
        inner(first, first),
        inner(first, second),
        inner(second, second),
    ]
    packed_ref[...] = pack_moments(moments, 0, jnp.zeros((32, 128), jnp.float32))


def third_kernel(
    joined_ref, cross_in_ref, chip_in_ref, second_ref, packed_ref, vector_ref, sums_ref,
    turn_ref,
):
    shift, center = mode_terms()
    applied = assembled(joined_ref, cross_in_ref, chip_in_ref)
    second = [second_ref[n] for n in range(25)]
    third = [applied[n] - center * second[n] for n in range(25)]
    for n in range(25):
        vector_ref[n] = third[n]
    fourth = inner(third, third)
    local = local_operator(third, shift)
    fifth = -center * fourth
    for n in range(25):
        fifth = fifth + local[n] * third[n]
    moments = [inner(second, third), fourth, fifth]
    packed = pack_moments(moments, 3, packed_ref[...])
    turn_ref[...] = jnp.zeros((128, 128), jnp.float32)
    for t in range(4):
        turn_ref[pl.ds(t, 8, stride=4), :] = packed[8 * t : 8 * t + 8]
    turned = turn_ref[...].T[0:8]
    for p in range(GRID):
        sums_ref[p] = turned


def natural_kernel(vector_ref, out_ref, column_ref):
    order = column_order()
    stacked = jnp.concatenate(
        [
            jnp.concatenate([vector_ref[j * 5 + i] for i in range(5)], axis=1) for j in range(5)
        ],
        axis=0,
    )
    contract = ((1,), (1,))
    high, middle, low = thirds(stacked)
    columns = dot(low, order, contract) + dot(middle, order, contract) + dot(high, order, contract)
    for i in range(5):
        for j in range(5):
            for t in range(4):
                first = 32 * j + 8 * t
                column_ref[pl.ds(160 * i + 32 * j + t, 8, stride=4), :] = columns[
                    first : first + 8, 128 * i : 128 * i + 128
                ]
    for j in range(5):
        for i in range(5):
            first = 160 * i + 32 * j
            out_ref[j, :, 128 * i : 128 * i + 128] = column_ref[first : first + 32, :]


def combine_kernel(sums_ref, first_ref, second_ref, third_ref, out_ref, turn_ref):
    total = sums_ref[0]
    for p in range(1, GRID):
        total = total + sums_ref[p]
    moment = [total[n : n + 1] for n in range(6)]
    lane = lax.broadcasted_iota(jnp.int32, (1, 128), 1)
    mode_pair = 16 * lax.axis_index("span") + (lane >> 1)
    ratio = mode_pair.astype(jnp.float32) * (1.0 / KMODES)
    center = 0.2 * (1.0 + SPAN_STIFF * ratio * ratio) + 0.15

    def product(left, right):
        terms = None
        for a in range(len(left)):
            for b in range(len(right)):
                term = left[a] * right[b] * moment[a + b]
                terms = term if terms is None else terms + term
        return terms

    def operator(c):
        shifted = [center * v for v in c] + [0.0]
        return [shifted[0]] + [shifted[a + 1] + c[a] for a in range(len(c))]

    residual = [jnp.ones((1, 128), jnp.float32)]
    direction = residual
    result = [0.0, 0.0, 0.0]
    norm = moment[0]
    for step in range(ITERS):
        applied = operator(direction)
        length = norm / product(direction, applied)
        for a in range(len(direction)):
            result[a] = result[a] + length * direction[a]
        if step < ITERS - 1:
            padded = residual + [0.0]
            residual = [padded[a] - length * applied[a] for a in range(len(applied))]
            fresh = product(residual, residual)
            ratio = fresh / norm
            norm = fresh
            padded = direction + [0.0]
            direction = [residual[a] + ratio * padded[a] for a in range(len(residual))]
    turn_ref[...] = jnp.zeros((128, 128), jnp.float32)
    for a in range(3):
        turn_ref[a : a + 1, :] = result[a]
    turned = turn_ref[...].T[0:32]
    weight = [turned[:, a : a + 1] for a in range(3)]
    for j in range(5):
        out_ref[j] = (
            weight[0] * first_ref[j] + weight[1] * second_ref[j] + weight[2] * third_ref[j]
        )


def call(kernel, name, out_shapes, *args, smem=(), anywhere=(), scratch=(), limit=16):
    vmem = pl.BlockSpec(memory_space=pltpu.VMEM)
    spaces = {n: pl.BlockSpec(memory_space=pltpu.SMEM) for n in smem}
    spaces |= {n: pl.BlockSpec(memory_space=pltpu.HBM) for n in anywhere}
    return pl.pallas_call(
        kernel,
        name=name,
        out_shape=[jax.ShapeDtypeStruct(s, jnp.float32) for s in out_shapes],
        in_specs=[spaces.get(n, vmem) for n in range(len(args))],
        out_specs=[vmem] * len(out_shapes),
        scratch_shapes=list(scratch),
        compiler_params=pltpu.CompilerParams(vmem_limit_bytes=limit * 1024 * 1024),
    )(*args)


def swap_traces(cross, chip):
    partner = [(p, (p + 1) % GRID if p % 2 else (p - 1) % GRID) for p in range(GRID)]
    cross = lax.ppermute(cross, "plane", partner)
    chip = lax.ppermute(chip, "plane", [(p, p ^ 1) for p in range(GRID)])
    return cross, chip


def on_device(state, wall_tag):
    table = wave_table()
    (packed,) = call(
        pack_kernel, "pack", [(16, 32, 256)],
        pltpu.with_memory_space_constraint(jnp.transpose(state, (1, 0, 2)), pltpu.HBM),
        anywhere=(0,),
        scratch=[
            pltpu.VMEM((800, 128), jnp.float32), pltpu.VMEM((5, 32, 640), jnp.float32),
            pltpu.VMEM((640, 640), jnp.bfloat16), pltpu.SemaphoreType.DMA(()),
        ],
    )
    modal = lax.all_to_all(packed, "span", 0, 0, tiled=True)
    trace = (40, PLANES + 512)
    field, rhs, cross, chip = call(
        volume_kernel, "volume", [(200, PLANES), (200, PLANES), trace, trace], modal, table,
        scratch=[pltpu.VMEM((40, PLANES), jnp.float32)],
    )
    cross, chip = swap_traces(cross, chip)
    (inside,) = call(inside_kernel, "inside", [(2, 256, 256)], modal, field, rhs, table)
    (sent,) = call(
        facing_kernel, "facing", [(16, 32, 256)], wall_tag, inside, field, cross, chip, table,
        smem=(0,), scratch=[pltpu.VMEM((80, PLANES), jnp.float32)],
    )
    load = lax.all_to_all(sent, "span", 0, 0, tiled=True)
    nodes, trace = (25, 32, 128), (5, 32, 128)
    first, joined, cross, chip = call(first_kernel, "first", [nodes, nodes, trace, trace], load)
    cross, chip = swap_traces(cross, chip)
    second, joined, cross, chip = call(
        second_kernel, "second", [nodes, nodes, trace, trace], joined, cross, chip, first
    )
    cross, chip = swap_traces(cross, chip)
    (packed,) = call(early_kernel, "early", [(32, 128)], first, second)
    third, sums = call(
        third_kernel, "third", [nodes, (16, 8, 128)], joined, cross, chip, second, packed,
        scratch=[pltpu.VMEM((128, 128), jnp.float32)],
    )
    sums = lax.all_to_all(sums, "plane", 0, 0, tiled=True)
    columns = [
        call(
            natural_kernel, "natural", [(5, 32, 640)], vector,
            scratch=[pltpu.VMEM((800, 128), jnp.float32)],
        )[0]
        for vector in (first, second, third)
    ]
    (columns,) = call(
        combine_kernel, "combine", [(5, 32, 640)], sums, *columns,
        scratch=[pltpu.VMEM((128, 128), jnp.float32)],
    )
    return jnp.transpose(columns, (1, 0, 2))


def solution(mesh):
    in_specs = (P("span", "plane", None), P())
    out_specs = P("span", "plane", None)
    return jax.shard_map(
        on_device, mesh=mesh, in_specs=in_specs, out_specs=out_specs, check_vma=False
    )
```

```python
import math

import jax
import jax.numpy as jnp
import numpy as np
from jax import lax
from jax.experimental import pallas as pl
from jax.experimental.pallas import tpu as pltpu
from jax.sharding import PartitionSpec as P


KMODES = 256
PLANES = 768
HALF = 384
ITERS = 3
GRID = 16
STEP_SIZE = 0.03
VISCOUS = 0.05
SPAN_STIFF = 4.0


def gll_tables():
    abscissae = np.array([-1.0, -math.sqrt(3.0 / 7.0), 0.0, math.sqrt(3.0 / 7.0), 1.0])
    weights = np.array([0.1, 49.0 / 90.0, 32.0 / 45.0, 49.0 / 90.0, 0.1])
    squared = abscissae * abscissae
    legendre = (35.0 * squared * squared - 30.0 * squared + 3.0) / 8.0
    identity = np.eye(5)
    spacing = abscissae[:, None] - abscissae[None, :] + identity
    differ = np.where(identity > 0, 0.0, legendre[:, None] / legendre[None, :] / spacing)
    differ[0, 0] = -5.0
    differ[4, 4] = 5.0
    stiffness = differ.T @ (weights[:, None] * differ)
    return differ, weights, stiffness


DIFFER, WEIGHTS, STIFFNESS = gll_tables()


def split_table(table):
    high = table.astype(np.float32).astype(jnp.bfloat16)
    low = (table - high.astype(np.float64)).astype(np.float32).astype(jnp.bfloat16)
    return jnp.asarray(np.stack([high, low]))


def wave_table():
    plane = np.arange(HALF)
    waves = []
    for parity in range(2):
        k = 2 * np.arange(128) + parity
        angle = (k[:, None] * plane[None, :] % PLANES) * (2.0 * math.pi / PLANES)
        waves.append(np.concatenate([np.cos(angle), np.sin(angle)]))
    return split_table(np.stack(waves))


def dot(left, right, contract):
    return lax.dot_general(
        left, right, (contract, ((), ())), preferred_element_type=jnp.float32
    )


def halves(value):
    high = value.astype(jnp.bfloat16)
    low = (value - high.astype(jnp.float32)).astype(jnp.bfloat16)
    return high, low


def dot_split(left, right, contract):
    (left_high, left_low), (right_high, right_low) = left, right
    return (
        dot(left_high, right_low, contract)
        + dot(left_low, right_high, contract)
        + dot(left_high, right_high, contract)
    )


def lanes_of(values, index):
    return jnp.take_along_axis(values, index, axis=1)


def split_columns(tiles):
    lane = lax.broadcasted_iota(jnp.int32, tiles[0].shape, 1)
    out = []
    for i in range(5):
        column = 5 * lane + i
        picked = lanes_of(tiles[0], column & 127)
        for t in range(1, 5):
            picked = jnp.where(column >= 128 * t, lanes_of(tiles[t], column & 127), picked)
        out.append(picked)
    return out


def merge_columns(tiles):
    lane = lax.broadcasted_iota(jnp.int32, tiles[0].shape, 1)
    out = []
    for t in range(5):
        column = lane + 128 * t
        element = (column * 13108) >> 16
        node = column - 5 * element
        picked = lanes_of(tiles[0], element)
        for i in range(1, 5):
            picked = jnp.where(node == i, lanes_of(tiles[i], element), picked)
        out.append(picked)
    return out


def exchange_chunks(values):
    values = list(values)
    lane = lax.broadcasted_iota(jnp.int32, values[0].shape, 1)
    for bit in (1, 2, 4, 8):
        upper = (lane & (8 * bit)) != 0
        other = lane ^ (8 * bit)
        for a in range(16):
            if a & bit == 0:
                first, second = values[a], values[a | bit]
                moved = jnp.where(upper, first, second)
                if bit == 8:
                    moved = pltpu.roll(moved, 64, 1)
                else:
                    moved = lanes_of(moved, other)
                values[a] = jnp.where(upper, moved, first)
                values[a | bit] = jnp.where(upper, second, moved)
    return values


def pack_kernel(state_hbm, out_ref, chunk_ref, state_ref, arrived):
    copies = [
        pltpu.make_async_copy(state_hbm.at[j], state_ref.at[j], arrived.at[j]) for j in range(5)
    ]
    for copy in copies:
        copy.start()
    for j in range(5):
        copies[j].wait()
        tiles = split_columns([state_ref[j, :, 128 * t : 128 * t + 128] for t in range(5)])
        for i in range(5):
            first = 32 * (5 * j + i)
            chunk_ref[first : first + 32, :] = tiles[i]
    chunk = [
        jnp.concatenate(
            [chunk_ref[pl.ds(32 * n + t, 8, stride=4), :] for t in range(4)], axis=0
        )
        for n in range(25)
    ]
    lane = lax.broadcasted_iota(jnp.int32, (32, 128), 1) & 7
    for j in range(5):
        left = pltpu.roll(chunk[j * 5 + 4], 1, 1)
        right = pltpu.roll(chunk[j * 5], 127, 1)
        chunk.append(jnp.where(lane == 0, left, jnp.where(lane == 7, right, 0.0)))
    zero = jnp.zeros((32, 128), jnp.float32)
    chunk = chunk + [zero, zero]
    for half in range(2):
        block = exchange_chunks(chunk[16 * half : 16 * half + 16])
        for d in range(GRID):
            out_ref[d, :, 128 * half : 128 * half + 128] = block[d]


def synthesize(nodal, table_ref):
    part = [
        dot_split(
            halves(nodal[parity]), (table_ref[0, parity], table_ref[1, parity]), ((1,), (0,))
        )
        for parity in range(2)
    ]
    scale = 1.0 / math.sqrt(KMODES)
    return scale * (part[0] + part[1]), scale * (part[0] - part[1])


def two_point(left, right):
    mean = (left * left + left * right + right * right) * (1.0 / 6.0)
    speed = jnp.maximum(jnp.abs(left), jnp.abs(right))
    return mean - 0.5 * speed * (right - left)


def turn_kernel(modal_ref, nodal_ref, cross_ref, chip_ref):
    for parity in range(2):
        rows = [
            modal_ref[s, 16 * parity + 8 * t : 16 * parity + 8 * t + 8, :]
            for t in range(2)
            for s in range(GRID)
        ]
        nodal = jnp.concatenate(rows, axis=0).T
        nodal_ref[parity] = nodal
        cross_ref[parity], chip_ref[parity] = to_partners(nodal[0:40], nodal[160:200])


def volume_kernel(nodal_ref, table_ref, field_ref, rhs_ref, cross_ref, chip_ref, side_ref):
    nodal = [nodal_ref[0], nodal_ref[1]]
    pair = synthesize(nodal, table_ref)
    for q in range(2):
        field_ref[:, HALF * q : HALF * q + HALF] = pair[q][0:200]
        side_ref[:, HALF * q : HALF * q + HALF] = pair[q][200:240]
    row = lax.broadcasted_iota(jnp.int32, (8, 128), 0)

    def column(block, carry):
        lanes = pl.ds(pl.multiple_of(block * 128, 128), 128)
        f = [field_ref[8 * n : 8 * n + 8, lanes] for n in range(25)]
        square = [v * v for v in f]
        low = []
        for j in range(5):
            for i in range(5):
                n = j * 5 + i
                plain = None
                power = None
                for other in range(5):
                    terms = [(DIFFER[i][other], j * 5 + other), (DIFFER[j][other], other * 5 + i)]
                    for weight, m in terms:
                        if weight == 0.0:
                            continue
                        weight = float(weight) / -3.0
                        plain = weight * f[m] if plain is None else plain + weight * f[m]
                        power = weight * square[m] if power is None else power + weight * square[m]
                total = power + f[n] * plain
                own = (i == 4) + (j == 4) - (i == 0) - (j == 0)
                if own:
                    total = total + (5.0 * own) * square[n]
                if i == 0 or i == 4:
                    side = side_ref[8 * j : 8 * j + 8, lanes]
                    if i == 0:
                        left = jnp.where(row == 0, side, pltpu.roll(f[j * 5 + 4], 1, 0))
                        total = total + 10.0 * two_point(left, f[n])
                    else:
                        right = jnp.where(row == 7, side, pltpu.roll(f[j * 5], 7, 0))
                        total = total - 10.0 * two_point(f[n], right)
                rhs_ref[8 * n : 8 * n + 8, lanes] = total
                if j == 0:
                    low.append(total)
                elif j == 4:
                    rows = slice(8 * i, 8 * i + 8)
                    cross_ref[rows, lanes], chip_ref[rows, lanes] = to_partners(low[i], total)
        return carry

    lax.fori_loop(0, PLANES // 128, column, 0)


def project(planar, parity, table_ref):
    folded = planar[:, :HALF] + planar[:, HALF:] if parity == 0 else planar[:, :HALF] - planar[:, HALF:]
    return dot_split((table_ref[0, parity], table_ref[1, parity]), halves(folded), ((1,), (1,)))


def tendency(parity, from_rhs, from_flux):
    k = 2 * lax.broadcasted_iota(jnp.int32, (128, 128), 0) + parity
    scale = jnp.where(k == 0, 1.0, 2.0) * (math.sqrt(KMODES) / PLANES * STEP_SIZE)
    ratio = k.astype(jnp.float32) * (1.0 / KMODES)
    return (
        scale * (from_rhs[0:128] - ratio * from_flux[128:256]),
        scale * (from_rhs[128:256] + ratio * from_flux[0:128]),
    )


def inside_kernel(modal_ref, field_ref, rhs_ref, table_ref, out_ref):
    field = field_ref[...]
    flux = 0.5 * field * field
    rhs = rhs_ref[...]
    tail = jnp.zeros((56, PLANES), jnp.float32)
    flux = jnp.concatenate([flux, tail], axis=0)
    rhs = jnp.concatenate([rhs, tail], axis=0)
    for parity in range(2):
        from_rhs = project(rhs, parity, table_ref)
        from_flux = project(flux, parity, table_ref)
        for half in range(2):
            lanes = slice(128 * half, 128 * half + 128)
            change = tendency(parity, from_rhs[:, lanes], from_flux[:, lanes])
            for t in range(2):
                first = 16 * parity + 8 * t
                modal = jnp.concatenate(
                    [modal_ref[s, first : first + 8, lanes] for s in range(GRID)], axis=0
                )
                out_ref[parity, 128 * t : 128 * t + 128, lanes] = modal + change[t]


def lift_kernel(
    tag_ref, field_ref, cross_ref, chip_ref, table_ref, lift_ref, flux_ref, modal_ref, outer_ref
):
    bottom, top = at_ends()
    span = lax.axis_index("span")
    row = lax.broadcasted_iota(jnp.int32, (8, 128), 0)
    mirror = jnp.ones((8, 128), jnp.float32)
    for e in range(8):
        mirror = jnp.where((row == e) & (tag_ref[8 * span + e] == 1), -1.0, mirror)
    keep_lower = jnp.where(bottom, 0.0, 1.0)
    keep_upper = jnp.where(top, 0.0, 1.0)
    gap = jnp.zeros((48, 256), jnp.float32)
    outer = []
    for parity in range(2):
        below, above = from_partners(cross_ref[parity], chip_ref[parity])
        outer.append(jnp.concatenate([below, above], axis=0))
        modal_ref[parity] = jnp.concatenate(
            [keep_lower * below, keep_upper * above, gap], axis=0
        ).T
    pair = synthesize(outer, table_ref)
    for q in range(2):
        outer_ref[:, HALF * q : HALF * q + HALF] = pair[q]
    mirror = jnp.concatenate([mirror] * 6, axis=1)
    mirror = jnp.concatenate([mirror] * 5, axis=0)
    inside = field_ref[0:40, :]
    below = outer_ref[0:40, :]
    lift_ref[0:40, :] = 10.0 * two_point(jnp.where(bottom, mirror * inside, below), inside)
    flux_ref[0:40, :] = keep_lower * (0.5 * below * below)
    inside = field_ref[160:200, :]
    above = outer_ref[40:80, :]
    lift_ref[40:80, :] = 10.0 * two_point(inside, jnp.where(top, inside, above))
    flux_ref[40:80, :] = keep_upper * (0.5 * above * above)


def facing_kernel(
    inside_ref, lift_ref, flux_ref, facing_ref, cross_ref, chip_ref, table_ref, out_ref
):
    bottom, top = at_ends()
    below, above = from_partners(cross_ref[...], chip_ref[...])
    lift = lift_ref[0:40, :]
    rhs_lower = lift + jnp.where(bottom, 0.0, below - lift)
    lift = lift_ref[40:80, :]
    rhs_upper = jnp.where(top, 0.0, above + lift) - lift
    gap = jnp.zeros((48, PLANES), jnp.float32)
    planar = jnp.concatenate([rhs_lower, rhs_upper, gap, flux_ref[...], gap], axis=0)
    lane = lax.broadcasted_iota(jnp.int32, (128, 128), 1)
    for parity in range(2):
        projected = project(planar, parity, table_ref)
        change = tendency(parity, projected[:, 0:128], projected[:, 128:256])
        for t in range(2):
            first = 16 * parity + 8 * t
            rows = slice(128 * t, 128 * t + 128)
            extra = change[t] + facing_ref[parity, rows, :]
            lower = jnp.where(lane < 40, extra, 0.0)
            upper = pltpu.roll(jnp.where(lane < 40, 0.0, extra), 120, 1)
            for half, added in ((0, lower), (1, upper)):
                lanes = slice(128 * half, 128 * half + 128)
                total = inside_ref[parity, rows, lanes] + added
                for s in range(GRID):
                    out_ref[s, first : first + 8, lanes] = total[8 * s : 8 * s + 8]


def at_ends():
    plane = lax.axis_index("plane")
    return plane == 0, plane == GRID - 1


def to_partners(low, high):
    odd = lax.axis_index("plane") % 2 == 1
    return jnp.where(odd, high, low), jnp.where(odd, low, high)


def from_partners(cross, chip):
    odd = lax.axis_index("plane") % 2 == 1
    return jnp.where(odd, chip, cross), jnp.where(odd, cross, chip)


def local_operator(values, shift):
    out = []
    for j in range(5):
        for i in range(5):
            n = j * 5 + i
            mass = float(WEIGHTS[j] * WEIGHTS[i])
            diagonal = VISCOUS * float(WEIGHTS[j] * STIFFNESS[i][i] + WEIGHTS[i] * STIFFNESS[j][j])
            value = (shift * mass + diagonal) * values[n]
            for other in range(5):
                if other != i:
                    weight = VISCOUS * float(WEIGHTS[j] * STIFFNESS[i][other])
                    value = value + weight * values[j * 5 + other]
                if other != j:
                    weight = VISCOUS * float(WEIGHTS[i] * STIFFNESS[j][other])
                    value = value + weight * values[other * 5 + i]
            out.append(value)
    return out


def join_columns(values):
    values = list(values)
    for j in range(5):
        joint = values[j * 5 + 4] + pltpu.roll(values[j * 5], 127, 1)
        values[j * 5 + 4] = joint
        values[j * 5] = pltpu.roll(joint, 1, 1)
    return values


def store_joined(values, joined_ref, cross_ref, chip_ref):
    values = join_columns(values)
    for n in range(25):
        joined_ref[n] = values[n]
    for i in range(5):
        cross_ref[i], chip_ref[i] = to_partners(values[i], values[20 + i])


def assembled(joined_ref, cross_ref, chip_ref):
    values = [joined_ref[n] for n in range(25)]
    bottom, top = at_ends()
    for i in range(5):
        below, above = from_partners(cross_ref[i], chip_ref[i])
        values[i] = values[i] + jnp.where(bottom, 0.0, below)
        values[20 + i] = values[20 + i] + jnp.where(top, 0.0, above)
    return values


def mode_terms():
    row = lax.broadcasted_iota(jnp.int32, (32, 128), 0)
    mode_pair = 16 * lax.axis_index("span") + 2 * (row & 7) + (row >> 4)
    ratio = mode_pair.astype(jnp.float32) * (1.0 / KMODES)
    shift = 1.0 + SPAN_STIFF * ratio * ratio
    return shift, 0.2 * shift + 0.15


def inner(left, right):
    bottom, top = at_ends()
    total = None
    for j in range(5):
        part = None
        for i in range(5):
            term = left[j * 5 + i] * right[j * 5 + i]
            term = term if 0 < i < 4 else 0.5 * term
            part = term if part is None else part + term
        if j == 0:
            part = jnp.where(bottom, 1.0, 0.5) * part
        elif j == 4:
            part = jnp.where(top, 1.0, 0.5) * part
        total = part if total is None else total + part
    return total


def first_kernel(modal_ref, vector_ref, next_ref, cross_ref, chip_ref):
    shift, _ = mode_terms()
    values = []
    for half in range(2):
        values += exchange_chunks(
            [modal_ref[s, :, 128 * half : 128 * half + 128] for s in range(GRID)]
        )
    values = [float(WEIGHTS[n // 5] * WEIGHTS[n % 5]) * values[n] for n in range(25)]
    vector = join_columns(values)
    for n in range(25):
        vector_ref[n] = vector[n]
    store_joined(local_operator(vector, shift), next_ref, cross_ref, chip_ref)


def second_kernel(
    joined_ref, cross_in_ref, chip_in_ref, before_ref, vector_ref, next_ref, cross_ref, chip_ref
):
    shift, center = mode_terms()
    applied = assembled(joined_ref, cross_in_ref, chip_in_ref)
    vector = [applied[n] - center * before_ref[n] for n in range(25)]
    for n in range(25):
        vector_ref[n] = vector[n]
    store_joined(local_operator(vector, shift), next_ref, cross_ref, chip_ref)


def pack_moments(moments, first, packed):
    lane = lax.broadcasted_iota(jnp.int32, (32, 128), 1)
    for n, moment in enumerate(moments):
        packed = jnp.where(lane == first + n, jnp.sum(moment, axis=1, keepdims=True), packed)
    return packed


def early_kernel(first_ref, second_ref, packed_ref):
    first = [first_ref[n] for n in range(25)]
    second = [second_ref[n] for n in range(25)]
    moments = [
        inner(first, first),
        inner(first, second),
        inner(second, second),
    ]
    packed_ref[...] = pack_moments(moments, 0, jnp.zeros((32, 128), jnp.float32))


def third_kernel(
    joined_ref, cross_in_ref, chip_in_ref, second_ref, packed_ref, vector_ref, sums_ref,
    turn_ref,
):
    shift, center = mode_terms()
    applied = assembled(joined_ref, cross_in_ref, chip_in_ref)
    second = [second_ref[n] for n in range(25)]
    third = [applied[n] - center * second[n] for n in range(25)]
    for n in range(25):
        vector_ref[n] = third[n]
    fourth = inner(third, third)
    local = local_operator(third, shift)
    fifth = -center * fourth
    for n in range(25):
        fifth = fifth + local[n] * third[n]
    moments = [inner(second, third), fourth, fifth]
    packed = pack_moments(moments, 3, packed_ref[...])
    for t in range(4):
        turn_ref[pl.ds(t, 8, stride=4), :] = packed[8 * t : 8 * t + 8]
    turned = turn_ref[...].T[0:8]
    for p in range(GRID):
        sums_ref[p, :, 0:32] = turned


def natural_kernel(vector_ref, out_ref, column_ref):
    for j in range(5):
        tiles = merge_columns([vector_ref[j * 5 + i] for i in range(5)])
        for i in range(5):
            first = 32 * (5 * j + i)
            for t in range(4):
                column_ref[pl.ds(first + t, 8, stride=4), :] = tiles[i][8 * t : 8 * t + 8]
            out_ref[j, :, 128 * i : 128 * i + 128] = column_ref[first : first + 32, :]


def combine_kernel(
    sums_ref, first_ref, second_ref, third_ref, out_hbm, turn_ref, result_ref, sent
):
    total = sums_ref[0]
    for p in range(1, GRID):
        total = total + sums_ref[p]
    moment = [total[n : n + 1] for n in range(6)]
    lane = lax.broadcasted_iota(jnp.int32, (1, 128), 1)
    mode_pair = 16 * lax.axis_index("span") + (lane >> 1)
    ratio = mode_pair.astype(jnp.float32) * (1.0 / KMODES)
    center = 0.2 * (1.0 + SPAN_STIFF * ratio * ratio) + 0.15

    def product(left, right):
        terms = None
        for a in range(len(left)):
            for b in range(len(right)):
                term = left[a] * right[b] * moment[a + b]
                terms = term if terms is None else terms + term
        return terms

    def operator(c):
        shifted = [center * v for v in c] + [0.0]
        return [shifted[0]] + [shifted[a + 1] + c[a] for a in range(len(c))]

    residual = [jnp.ones((1, 128), jnp.float32)]
    direction = residual
    result = [0.0, 0.0, 0.0]
    norm = moment[0]
    for step in range(ITERS):
        applied = operator(direction)
        length = norm / product(direction, applied)
        for a in range(len(direction)):
            result[a] = result[a] + length * direction[a]
        if step < ITERS - 1:
            padded = residual + [0.0]
            residual = [padded[a] - length * applied[a] for a in range(len(applied))]
            fresh = product(residual, residual)
            ratio = fresh / norm
            norm = fresh
            padded = direction + [0.0]
            direction = [residual[a] + ratio * padded[a] for a in range(len(residual))]
    turn_ref[...] = jnp.zeros((8, 128), jnp.float32)
    for a in range(3):
        turn_ref[a : a + 1, :] = result[a]
    turned = turn_ref[...].T[0:32]
    weight = [turned[:, a : a + 1] for a in range(3)]
    copies = []
    for j in range(5):
        result_ref[j] = (
            weight[0] * first_ref[j] + weight[1] * second_ref[j] + weight[2] * third_ref[j]
        )
        copies.append(pltpu.make_async_copy(result_ref.at[j], out_hbm.at[j], sent.at[j]))
        copies[j].start()
    for copy in copies:
        copy.wait()


def call(kernel, out_shapes, *args, smem=(), anywhere=(), scratch=(), out_space=pltpu.VMEM, covers=True):
    vmem = pl.BlockSpec(memory_space=pltpu.VMEM)
    spaces = {n: pl.BlockSpec(memory_space=pltpu.SMEM) for n in smem}
    spaces |= {n: pl.BlockSpec(memory_space=pltpu.HBM) for n in anywhere}
    return pl.pallas_call(
        kernel,
        out_shape=[jax.ShapeDtypeStruct(s, jnp.float32) for s in out_shapes],
        in_specs=[spaces.get(n, vmem) for n in range(len(args))],
        out_specs=[pl.BlockSpec(memory_space=out_space)] * len(out_shapes),
        scratch_shapes=list(scratch),
        cost_estimate=None if covers else pl.CostEstimate(flops=0, bytes_accessed=0, transcendentals=0),
        compiler_params=pltpu.CompilerParams(vmem_limit_bytes=16 * 1024 * 1024),
    )(*args)


def swap_traces(cross, chip):
    partner = [(p, (p + 1) % GRID if p % 2 else (p - 1) % GRID) for p in range(GRID)]
    cross = lax.ppermute(cross, "plane", partner)
    chip = lax.ppermute(chip, "plane", [(p, p ^ 1) for p in range(GRID)])
    return cross, chip


def on_device(state, wall_tag):
    table = wave_table()
    (packed,) = call(
        pack_kernel, [(16, 32, 256)],
        pltpu.with_memory_space_constraint(jnp.transpose(state, (1, 0, 2)), pltpu.HBM),
        anywhere=(0,),
        scratch=[
            pltpu.VMEM((800, 128), jnp.float32), pltpu.VMEM((5, 32, 640), jnp.float32),
            pltpu.SemaphoreType.DMA((5,)),
        ],
    )
    modal = lax.all_to_all(packed, "span", 0, 0, tiled=True)
    trace, rows = (2, 40, 256), (40, PLANES)
    nodal, cross, chip = call(turn_kernel, [(2, 256, 256), trace, trace], modal)
    modal_traces = swap_traces(cross, chip)
    field, rhs, cross, chip = call(
        volume_kernel, [(200, PLANES), (200, PLANES), rows, rows], nodal, table,
        scratch=[pltpu.VMEM(rows, jnp.float32)],
    )
    rhs_traces = swap_traces(cross, chip)
    (inside,) = call(inside_kernel, [(2, 256, 256)], modal, field, rhs, table, covers=False)
    lift, flux, facing = call(
        lift_kernel, [(80, PLANES), (80, PLANES), (2, 256, 128)], wall_tag, field,
        *modal_traces, table, smem=(0,), scratch=[pltpu.VMEM((80, PLANES), jnp.float32)],
        covers=False,
    )
    (sent,) = call(facing_kernel, [(16, 32, 256)], inside, lift, flux, facing, *rhs_traces, table)
    load = lax.all_to_all(sent, "span", 0, 0, tiled=True)
    nodes, trace = (25, 32, 128), (5, 32, 128)
    first, joined, cross, chip = call(first_kernel, [nodes, nodes, trace, trace], load)
    cross, chip = swap_traces(cross, chip)
    second, joined, cross, chip = call(
        second_kernel, [nodes, nodes, trace, trace], joined, cross, chip, first
    )
    cross, chip = swap_traces(cross, chip)
    (packed,) = call(early_kernel, [(32, 128)], first, second)
    third, sums = call(
        third_kernel, [nodes, (16, 8, 128)], joined, cross, chip, second, packed,
        scratch=[pltpu.VMEM((32, 128), jnp.float32)],
    )
    sums = lax.all_to_all(sums, "plane", 0, 0, tiled=True)
    columns = [
        call(
            natural_kernel, [(5, 32, 640)], vector,
            scratch=[pltpu.VMEM((800, 128), jnp.float32)],
        )[0]
        for vector in (first, second, third)
    ]
    (columns,) = call(
        combine_kernel, [(5, 32, 640)], sums, *columns, out_space=pltpu.HBM,
        scratch=[
            pltpu.VMEM((8, 128), jnp.float32), pltpu.VMEM((5, 32, 640), jnp.float32),
            pltpu.SemaphoreType.DMA((5,)),
        ],
    )
    return jnp.transpose(columns, (1, 0, 2))


def solution(mesh):
    return jax.shard_map(
        on_device,
        mesh=mesh,
        in_specs=(P("span", "plane", None), P()),
        out_specs=P("span", "plane", None),
        check_vma=False,
    )
```

```python
import math

import jax
import jax.numpy as jnp
import numpy as np
from jax import lax
from jax.experimental import pallas as pl
from jax.experimental.pallas import tpu as pltpu
from jax.sharding import PartitionSpec as P


KMODES = 256
PLANES = 768
HALF = 384
ITERS = 3
GRID = 16
STEP_SIZE = 0.03
VISCOUS = 0.05
SPAN_STIFF = 4.0


def gll_tables():
    abscissae = np.array([-1.0, -math.sqrt(3.0 / 7.0), 0.0, math.sqrt(3.0 / 7.0), 1.0])
    weights = np.array([0.1, 49.0 / 90.0, 32.0 / 45.0, 49.0 / 90.0, 0.1])
    squared = abscissae * abscissae
    legendre = (35.0 * squared * squared - 30.0 * squared + 3.0) / 8.0
    identity = np.eye(5)
    spacing = abscissae[:, None] - abscissae[None, :] + identity
    differ = np.where(identity > 0, 0.0, legendre[:, None] / legendre[None, :] / spacing)
    differ[0, 0] = -5.0
    differ[4, 4] = 5.0
    stiffness = differ.T @ (weights[:, None] * differ)
    return differ, weights, stiffness


DIFFER, WEIGHTS, STIFFNESS = gll_tables()


def split_table(table):
    high = table.astype(np.float32).astype(jnp.bfloat16)
    low = (table - high.astype(np.float64)).astype(np.float32).astype(jnp.bfloat16)
    return jnp.asarray(np.stack([high, low]))


def wave_table():
    plane = np.arange(HALF)
    waves = []
    for parity in range(2):
        k = 2 * np.arange(128) + parity
        angle = (k[:, None] * plane[None, :] % PLANES) * (2.0 * math.pi / PLANES)
        waves.append(np.concatenate([np.cos(angle), np.sin(angle)]))
    return split_table(np.stack(waves))


def dot(left, right, contract):
    return lax.dot_general(
        left, right, (contract, ((), ())), preferred_element_type=jnp.float32
    )


def halves(value):
    high = value.astype(jnp.bfloat16)
    low = (value - high.astype(jnp.float32)).astype(jnp.bfloat16)
    return high, low


def dot_split(left, right, contract):
    (left_high, left_low), (right_high, right_low) = left, right
    return (
        dot(left_high, right_low, contract)
        + dot(left_low, right_high, contract)
        + dot(left_high, right_high, contract)
    )


def lanes_of(values, index):
    return jnp.take_along_axis(values, index, axis=1)


def merge_columns(tiles):
    lane = lax.broadcasted_iota(jnp.int32, tiles[0].shape, 1)
    out = []
    for t in range(5):
        column = lane + 128 * t
        element = (column * 13108) >> 16
        node = column - 5 * element
        picked = lanes_of(tiles[0], element)
        for i in range(1, 5):
            picked = jnp.where(node == i, lanes_of(tiles[i], element), picked)
        out.append(picked)
    return out


def exchange_chunks(values):
    values = list(values)
    lane = lax.broadcasted_iota(jnp.int32, values[0].shape, 1)
    for bit in (1, 2, 4, 8):
        upper = (lane & (8 * bit)) != 0
        other = lane ^ (8 * bit)
        for a in range(16):
            if a & bit == 0:
                first, second = values[a], values[a | bit]
                moved = jnp.where(upper, first, second)
                if bit == 8:
                    moved = pltpu.roll(moved, 64, 1)
                else:
                    moved = lanes_of(moved, other)
                values[a] = jnp.where(upper, moved, first)
                values[a | bit] = jnp.where(upper, second, moved)
    return values


def column_order():
    column = lax.broadcasted_iota(jnp.int32, (640, 128), 0)
    element = lax.broadcasted_iota(jnp.int32, (640, 128), 1)
    tiles = [jnp.where(column == 5 * element + i, 1.0, 0.0).astype(jnp.bfloat16) for i in range(5)]
    return jnp.concatenate(tiles, axis=1)


def pack_rows(out_ref, d, whole, rest, count):
    out_ref[d, 0:32, :] = whole
    lane = lax.broadcasted_iota(jnp.int32, (8, 128), 1)
    free = 16 - count
    for g in range(3):
        tile = rest[8 * g : 8 * g + 8]
        if g * free < count:
            shift = 8 * (count - g * free)
            tile = jnp.where(lane < 8 * count, tile, pltpu.roll(rest[24:32], shift % 128, 1))
        out_ref[d, 32 + 8 * g : 40 + 8 * g, :] = tile


def unpack_last(tiles, count):
    lane = lax.broadcasted_iota(jnp.int32, (8, 128), 1)
    free = 16 - count
    last = pltpu.roll(tiles[0], 128 - 8 * count, 1)
    for g in range(1, 3):
        if g * free < count:
            shift = 8 * (count - g * free)
            last = jnp.where(lane < 8 * g * free, last, pltpu.roll(tiles[g], (128 - shift) % 128, 1))
    return last


def pack_kernel(state_hbm, out_ref, chunk_ref, state_ref, order_ref, arrived):
    copy = pltpu.make_async_copy(state_hbm, state_ref, arrived)
    copy.start()
    order_ref[...] = column_order()
    copy.wait()
    stacked = jnp.concatenate([state_ref[j] for j in range(5)], axis=0)
    order = order_ref[...]
    contract = ((1,), (0,))
    high, low = halves(stacked)
    nodes = dot(low, order, contract) + dot(high, order, contract)
    for i in range(5):
        chunk_ref[160 * i : 160 * i + 160, :] = nodes[:, 128 * i : 128 * i + 128]
    chunk = [
        jnp.concatenate(
            [chunk_ref[pl.ds(160 * i + 32 * j + t, 8, stride=4), :] for t in range(4)], axis=0
        )
        for j in range(5)
        for i in range(5)
    ]
    lane = lax.broadcasted_iota(jnp.int32, (32, 128), 1) & 7
    sides = [jnp.zeros((32, 128), jnp.float32), jnp.zeros((32, 128), jnp.float32)]
    for j in range(5):
        at = j & 3
        side = jnp.where(lane == at, pltpu.roll(chunk[j * 5 + 4], 1 + at, 1), sides[j // 4])
        sides[j // 4] = jnp.where(lane == 7 - at, pltpu.roll(chunk[j * 5], 127 - at, 1), side)
    chunk = chunk + sides
    whole = exchange_chunks(chunk[:16])
    rest = exchange_chunks(chunk[16:] + [jnp.zeros((32, 128), jnp.float32)] * 5)
    for d in range(GRID):
        pack_rows(out_ref, d, whole[d], rest[d], 11)


def turn(modal_ref, cross_ref, chip_ref):
    last = [
        unpack_last([modal_ref[s, 32 + 8 * g : 40 + 8 * g, :] for g in range(3)], 11)
        for s in range(GRID)
    ]
    nodal = []
    for parity in range(2):
        whole, rest = [], []
        for t in range(2):
            group = 2 * parity + t
            for s in range(GRID):
                whole.append(modal_ref[s, 8 * group : 8 * group + 8, :])
                rest.append(
                    last[s] if group == 3 else modal_ref[s, 32 + 8 * group : 40 + 8 * group, :]
                )
        turned = [jnp.concatenate(part, axis=0).T for part in (whole, rest)]
        nodal.append(jnp.concatenate([turned[0], turned[1][0:88]], axis=0))
        cross_ref[parity], chip_ref[parity] = to_partners(turned[0][0:40], turned[1][32:72])
    return nodal


def synthesize(nodal, table_ref):
    part = [
        dot_split(
            halves(nodal[parity]), (table_ref[0, parity], table_ref[1, parity]), ((1,), (0,))
        )
        for parity in range(2)
    ]
    scale = 1.0 / math.sqrt(KMODES)
    return scale * (part[0] + part[1]), scale * (part[0] - part[1])


def two_point(left, right):
    mean = (left * left + left * right + right * right) * (1.0 / 6.0)
    speed = jnp.maximum(jnp.abs(left), jnp.abs(right))
    return mean - 0.5 * speed * (right - left)


def volume_kernel(
    modal_ref, table_ref, field_ref, rhs_ref, modal_cross_ref, modal_chip_ref, cross_ref, chip_ref,
    side_ref,
):
    nodal = turn(modal_ref, modal_cross_ref, modal_chip_ref)
    pair = synthesize(nodal, table_ref)
    for q in range(2):
        field_ref[:, HALF * q : HALF * q + HALF] = pair[q][0:200]
        side_ref[:, HALF * q : HALF * q + HALF] = pair[q][200:216]
    row = lax.broadcasted_iota(jnp.int32, (8, 128), 0)

    def column(block, carry):
        lanes = pl.ds(pl.multiple_of(block * 128, 128), 128)
        f = [field_ref[8 * n : 8 * n + 8, lanes] for n in range(25)]
        square = [v * v for v in f]
        low = []
        for j in range(5):
            for i in range(5):
                n = j * 5 + i
                plain = None
                power = None
                for other in range(5):
                    terms = [(DIFFER[i][other], j * 5 + other), (DIFFER[j][other], other * 5 + i)]
                    for weight, m in terms:
                        if weight == 0.0:
                            continue
                        weight = float(weight) / -3.0
                        plain = weight * f[m] if plain is None else plain + weight * f[m]
                        power = weight * square[m] if power is None else power + weight * square[m]
                total = power + f[n] * plain
                own = (i == 4) + (j == 4) - (i == 0) - (j == 0)
                if own:
                    total = total + (5.0 * own) * square[n]
                if i == 0 or i == 4:
                    at = j & 3
                    side = side_ref[8 * (j // 4) : 8 * (j // 4) + 8, lanes]
                    if at:
                        side = pltpu.roll(side, 8 - at if i == 0 else at, 0)
                    if i == 0:
                        left = jnp.where(row == 0, side, pltpu.roll(f[j * 5 + 4], 1, 0))
                        total = total + 10.0 * two_point(left, f[n])
                    else:
                        right = jnp.where(row == 7, side, pltpu.roll(f[j * 5], 7, 0))
                        total = total - 10.0 * two_point(f[n], right)
                rhs_ref[8 * n : 8 * n + 8, lanes] = total
                if j == 0:
                    low.append(total)
                elif j == 4:
                    rows = slice(8 * i, 8 * i + 8)
                    cross_ref[rows, lanes], chip_ref[rows, lanes] = to_partners(low[i], total)
        return carry

    lax.fori_loop(0, PLANES // 128, column, 0)


def project(planar, parity, table_ref):
    folded = planar[:, :HALF] + planar[:, HALF:] if parity == 0 else planar[:, :HALF] - planar[:, HALF:]
    return dot_split((table_ref[0, parity], table_ref[1, parity]), halves(folded), ((1,), (1,)))


def tendency(parity, from_rhs, from_flux):
    k = 2 * lax.broadcasted_iota(jnp.int32, (128, 128), 0) + parity
    scale = jnp.where(k == 0, 1.0, 2.0) * (math.sqrt(KMODES) / PLANES * STEP_SIZE)
    ratio = k.astype(jnp.float32) * (1.0 / KMODES)
    return (
        scale * (from_rhs[0:128] - ratio * from_flux[128:256]),
        scale * (from_rhs[128:256] + ratio * from_flux[0:128]),
    )


def inside_kernel(modal_ref, field_ref, rhs_ref, table_ref, out_ref):
    last = [
        unpack_last([modal_ref[s, 32 + 8 * g : 40 + 8 * g, :] for g in range(3)], 11)
        for s in range(GRID)
    ]
    field = field_ref[...]
    flux = 0.5 * field * field
    rhs = rhs_ref[...]
    tail = jnp.zeros((56, PLANES), jnp.float32)
    flux = jnp.concatenate([flux, tail], axis=0)
    rhs = jnp.concatenate([rhs, tail], axis=0)
    for parity in range(2):
        from_rhs = project(rhs, parity, table_ref)
        from_flux = project(flux, parity, table_ref)
        for half in range(2):
            lanes = slice(128 * half, 128 * half + 128)
            change = tendency(parity, from_rhs[:, lanes], from_flux[:, lanes])
            for t in range(2):
                first = 16 * parity + 8 * t + 32 * half
                modal = jnp.concatenate(
                    last if first == 56 else [modal_ref[s, first : first + 8, :] for s in range(GRID)],
                    axis=0,
                )
                out_ref[parity, 128 * t : 128 * t + 128, lanes] = modal + change[t]


def lift_kernel(
    tag_ref, field_ref, cross_ref, chip_ref, table_ref, lift_ref, flux_ref, modal_ref, outer_ref
):
    bottom, top = at_ends()
    span = lax.axis_index("span")
    row = lax.broadcasted_iota(jnp.int32, (8, 128), 0)
    mirror = jnp.ones((8, 128), jnp.float32)
    for e in range(8):
        mirror = jnp.where((row == e) & (tag_ref[8 * span + e] == 1), -1.0, mirror)
    keep_lower = jnp.where(bottom, 0.0, 1.0)
    keep_upper = jnp.where(top, 0.0, 1.0)
    gap = jnp.zeros((48, 256), jnp.float32)
    outer = []
    for parity in range(2):
        below, above = from_partners(cross_ref[parity], chip_ref[parity])
        outer.append(jnp.concatenate([below, above], axis=0))
        modal_ref[parity] = jnp.concatenate(
            [keep_lower * below, keep_upper * above, gap], axis=0
        ).T
    pair = synthesize(outer, table_ref)
    for q in range(2):
        outer_ref[:, HALF * q : HALF * q + HALF] = pair[q]
    mirror = jnp.concatenate([mirror] * 6, axis=1)
    mirror = jnp.concatenate([mirror] * 5, axis=0)
    inside = field_ref[0:40, :]
    below = outer_ref[0:40, :]
    lift_ref[0:40, :] = 10.0 * two_point(jnp.where(bottom, mirror * inside, below), inside)
    flux_ref[0:40, :] = keep_lower * (0.5 * below * below)
    inside = field_ref[160:200, :]
    above = outer_ref[40:80, :]
    lift_ref[40:80, :] = 10.0 * two_point(inside, jnp.where(top, inside, above))
    flux_ref[40:80, :] = keep_upper * (0.5 * above * above)


def facing_kernel(
    inside_ref, lift_ref, flux_ref, facing_ref, cross_ref, chip_ref, table_ref, out_ref
):
    bottom, top = at_ends()
    below, above = from_partners(cross_ref[...], chip_ref[...])
    lift = lift_ref[0:40, :]
    rhs_lower = lift + jnp.where(bottom, 0.0, below - lift)
    lift = lift_ref[40:80, :]
    rhs_upper = jnp.where(top, 0.0, above + lift) - lift
    gap = jnp.zeros((48, PLANES), jnp.float32)
    planar = jnp.concatenate([rhs_lower, rhs_upper, gap, flux_ref[...], gap], axis=0)
    lane = lax.broadcasted_iota(jnp.int32, (128, 128), 1)
    whole, rest = [], []
    for parity in range(2):
        projected = project(planar, parity, table_ref)
        change = tendency(parity, projected[:, 0:128], projected[:, 128:256])
        for t in range(2):
            rows = slice(128 * t, 128 * t + 128)
            extra = change[t] + facing_ref[parity, rows, :]
            lower = jnp.where(lane < 40, extra, 0.0)
            upper = pltpu.roll(jnp.where(lane < 40, 0.0, extra), 120, 1)
            whole.append(inside_ref[parity, rows, 0:128] + lower)
            rest.append(inside_ref[parity, rows, 128:256] + upper)
    for s in range(GRID):
        part = slice(8 * s, 8 * s + 8)
        pack_rows(
            out_ref,
            s,
            jnp.concatenate([group[part] for group in whole], axis=0),
            jnp.concatenate([group[part] for group in rest], axis=0),
            9,
        )


def at_ends():
    plane = lax.axis_index("plane")
    return plane == 0, plane == GRID - 1


def to_partners(low, high):
    odd = lax.axis_index("plane") % 2 == 1
    return jnp.where(odd, high, low), jnp.where(odd, low, high)


def from_partners(cross, chip):
    odd = lax.axis_index("plane") % 2 == 1
    return jnp.where(odd, chip, cross), jnp.where(odd, cross, chip)


def local_operator(values, shift):
    out = []
    for j in range(5):
        for i in range(5):
            n = j * 5 + i
            mass = float(WEIGHTS[j] * WEIGHTS[i])
            diagonal = VISCOUS * float(WEIGHTS[j] * STIFFNESS[i][i] + WEIGHTS[i] * STIFFNESS[j][j])
            value = (shift * mass + diagonal) * values[n]
            for other in range(5):
                if other != i:
                    weight = VISCOUS * float(WEIGHTS[j] * STIFFNESS[i][other])
                    value = value + weight * values[j * 5 + other]
                if other != j:
                    weight = VISCOUS * float(WEIGHTS[i] * STIFFNESS[j][other])
                    value = value + weight * values[other * 5 + i]
            out.append(value)
    return out


def join_columns(values):
    values = list(values)
    for j in range(5):
        joint = values[j * 5 + 4] + pltpu.roll(values[j * 5], 127, 1)
        values[j * 5 + 4] = joint
        values[j * 5] = pltpu.roll(joint, 1, 1)
    return values


def store_joined(values, joined_ref, cross_ref, chip_ref):
    values = join_columns(values)
    for n in range(25):
        joined_ref[n] = values[n]
    for i in range(5):
        cross_ref[i], chip_ref[i] = to_partners(values[i], values[20 + i])


def assembled(joined_ref, cross_ref, chip_ref):
    values = [joined_ref[n] for n in range(25)]
    bottom, top = at_ends()
    for i in range(5):
        below, above = from_partners(cross_ref[i], chip_ref[i])
        values[i] = values[i] + jnp.where(bottom, 0.0, below)
        values[20 + i] = values[20 + i] + jnp.where(top, 0.0, above)
    return values


def mode_terms():
    row = lax.broadcasted_iota(jnp.int32, (32, 128), 0)
    mode_pair = 16 * lax.axis_index("span") + 2 * (row & 7) + (row >> 4)
    ratio = mode_pair.astype(jnp.float32) * (1.0 / KMODES)
    shift = 1.0 + SPAN_STIFF * ratio * ratio
    return shift, 0.2 * shift + 0.15


def inner(left, right):
    bottom, top = at_ends()
    total = None
    for j in range(5):
        part = None
        for i in range(5):
            term = left[j * 5 + i] * right[j * 5 + i]
            term = term if 0 < i < 4 else 0.5 * term
            part = term if part is None else part + term
        if j == 0:
            part = jnp.where(bottom, 1.0, 0.5) * part
        elif j == 4:
            part = jnp.where(top, 1.0, 0.5) * part
        total = part if total is None else total + part
    return total


def first_kernel(modal_ref, vector_ref, next_ref, cross_ref, chip_ref):
    shift, _ = mode_terms()
    values = exchange_chunks([modal_ref[s, 0:32, :] for s in range(GRID)])
    rest = []
    for s in range(GRID):
        tiles = [modal_ref[s, 32 + 8 * g : 40 + 8 * g, :] for g in range(3)]
        rest.append(jnp.concatenate(tiles + [unpack_last(tiles, 9)], axis=0))
    values += exchange_chunks(rest)
    values = [float(WEIGHTS[n // 5] * WEIGHTS[n % 5]) * values[n] for n in range(25)]
    vector = join_columns(values)
    for n in range(25):
        vector_ref[n] = vector[n]
    store_joined(local_operator(vector, shift), next_ref, cross_ref, chip_ref)


def second_kernel(
    joined_ref, cross_in_ref, chip_in_ref, before_ref, vector_ref, next_ref, cross_ref, chip_ref
):
    shift, center = mode_terms()
    applied = assembled(joined_ref, cross_in_ref, chip_in_ref)
    vector = [applied[n] - center * before_ref[n] for n in range(25)]
    for n in range(25):
        vector_ref[n] = vector[n]
    store_joined(local_operator(vector, shift), next_ref, cross_ref, chip_ref)


def pack_moments(moments, first, packed):
    lane = lax.broadcasted_iota(jnp.int32, (32, 128), 1)
    for n, moment in enumerate(moments):
        packed = jnp.where(lane == first + n, jnp.sum(moment, axis=1, keepdims=True), packed)
    return packed


def early_kernel(first_ref, second_ref, packed_ref):
    first = [first_ref[n] for n in range(25)]
    second = [second_ref[n] for n in range(25)]
    moments = [
        inner(first, first),
        inner(first, second),
        inner(second, second),
    ]
    packed_ref[...] = pack_moments(moments, 0, jnp.zeros((32, 128), jnp.float32))


def third_kernel(
    joined_ref, cross_in_ref, chip_in_ref, second_ref, packed_ref, vector_ref, sums_ref,
    turn_ref,
):
    shift, center = mode_terms()
    applied = assembled(joined_ref, cross_in_ref, chip_in_ref)
    second = [second_ref[n] for n in range(25)]
    third = [applied[n] - center * second[n] for n in range(25)]
    for n in range(25):
        vector_ref[n] = third[n]
    fourth = inner(third, third)
    local = local_operator(third, shift)
    fifth = -center * fourth
    for n in range(25):
        fifth = fifth + local[n] * third[n]
    moments = [inner(second, third), fourth, fifth]
    packed = pack_moments(moments, 3, packed_ref[...])
    for t in range(4):
        turn_ref[pl.ds(t, 8, stride=4), :] = packed[8 * t : 8 * t + 8]
    turned = turn_ref[...].T[0:8]
    for p in range(GRID):
        sums_ref[p, :, 0:32] = turned


def natural_kernel(vector_ref, out_ref, column_ref):
    for j in range(5):
        tiles = merge_columns([vector_ref[j * 5 + i] for i in range(5)])
        for i in range(5):
            first = 32 * (5 * j + i)
            for t in range(4):
                column_ref[pl.ds(first + t, 8, stride=4), :] = tiles[i][8 * t : 8 * t + 8]
            out_ref[j, :, 128 * i : 128 * i + 128] = column_ref[first : first + 32, :]


def combine_kernel(
    sums_ref, first_ref, second_ref, third_ref, out_hbm, turn_ref, result_ref, sent
):
    total = sums_ref[0]
    for p in range(1, GRID):
        total = total + sums_ref[p]
    moment = [total[n : n + 1] for n in range(6)]
    lane = lax.broadcasted_iota(jnp.int32, (1, 128), 1)
    mode_pair = 16 * lax.axis_index("span") + (lane >> 1)
    ratio = mode_pair.astype(jnp.float32) * (1.0 / KMODES)
    center = 0.2 * (1.0 + SPAN_STIFF * ratio * ratio) + 0.15

    def product(left, right):
        terms = None
        for a in range(len(left)):
            for b in range(len(right)):
                term = left[a] * right[b] * moment[a + b]
                terms = term if terms is None else terms + term
        return terms

    def operator(c):
        shifted = [center * v for v in c] + [0.0]
        return [shifted[0]] + [shifted[a + 1] + c[a] for a in range(len(c))]

    residual = [jnp.ones((1, 128), jnp.float32)]
    direction = residual
    result = [0.0, 0.0, 0.0]
    norm = moment[0]
    for step in range(ITERS):
        applied = operator(direction)
        length = norm / product(direction, applied)
        for a in range(len(direction)):
            result[a] = result[a] + length * direction[a]
        if step < ITERS - 1:
            padded = residual + [0.0]
            residual = [padded[a] - length * applied[a] for a in range(len(applied))]
            fresh = product(residual, residual)
            ratio = fresh / norm
            norm = fresh
            padded = direction + [0.0]
            direction = [residual[a] + ratio * padded[a] for a in range(len(residual))]
    turn_ref[...] = jnp.zeros((8, 128), jnp.float32)
    for a in range(3):
        turn_ref[a : a + 1, :] = result[a]
    turned = turn_ref[...].T[0:32]
    weight = [turned[:, a : a + 1] for a in range(3)]
    copies = []
    for j in range(5):
        result_ref[j] = (
            weight[0] * first_ref[j] + weight[1] * second_ref[j] + weight[2] * third_ref[j]
        )
        copies.append(pltpu.make_async_copy(result_ref.at[j], out_hbm.at[j], sent.at[j]))
        copies[j].start()
    for copy in copies:
        copy.wait()


def call(kernel, out_shapes, *args, smem=(), anywhere=(), scratch=(), out_space=pltpu.VMEM, covers=True):
    vmem = pl.BlockSpec(memory_space=pltpu.VMEM)
    spaces = {n: pl.BlockSpec(memory_space=pltpu.SMEM) for n in smem}
    spaces |= {n: pl.BlockSpec(memory_space=pltpu.HBM) for n in anywhere}
    return pl.pallas_call(
        kernel,
        out_shape=[jax.ShapeDtypeStruct(s, jnp.float32) for s in out_shapes],
        in_specs=[spaces.get(n, vmem) for n in range(len(args))],
        out_specs=[pl.BlockSpec(memory_space=out_space)] * len(out_shapes),
        scratch_shapes=list(scratch),
        cost_estimate=None if covers else pl.CostEstimate(flops=0, bytes_accessed=0, transcendentals=0),
        compiler_params=pltpu.CompilerParams(vmem_limit_bytes=16 * 1024 * 1024),
    )(*args)


def swap_traces(cross, chip):
    partner = [(p, (p + 1) % GRID if p % 2 else (p - 1) % GRID) for p in range(GRID)]
    cross = lax.ppermute(cross, "plane", partner)
    chip = lax.ppermute(chip, "plane", [(p, p ^ 1) for p in range(GRID)])
    return cross, chip


def on_device(state, wall_tag):
    table = wave_table()
    (packed,) = call(
        pack_kernel, [(16, 56, 128)],
        pltpu.with_memory_space_constraint(jnp.transpose(state, (1, 0, 2)), pltpu.HBM),
        anywhere=(0,),
        scratch=[
            pltpu.VMEM((800, 128), jnp.float32), pltpu.VMEM((5, 32, 640), jnp.float32),
            pltpu.VMEM((640, 640), jnp.bfloat16), pltpu.SemaphoreType.DMA(()),
        ],
    )
    modal = lax.all_to_all(packed, "span", 0, 0, tiled=True)
    trace, rows = (2, 40, 256), (40, PLANES)
    field, rhs, *modal_traces, cross, chip = call(
        volume_kernel, [(200, PLANES), (200, PLANES), trace, trace, rows, rows], modal,
        table, scratch=[pltpu.VMEM((16, PLANES), jnp.float32)],
    )
    modal_traces = swap_traces(*modal_traces)
    rhs_traces = swap_traces(cross, chip)
    (inside,) = call(inside_kernel, [(2, 256, 256)], modal, field, rhs, table, covers=False)
    lift, flux, facing = call(
        lift_kernel, [(80, PLANES), (80, PLANES), (2, 256, 128)], wall_tag, field,
        *modal_traces, table, smem=(0,), scratch=[pltpu.VMEM((80, PLANES), jnp.float32)],
        covers=False,
    )
    (sent,) = call(facing_kernel, [(16, 56, 128)], inside, lift, flux, facing, *rhs_traces, table)
    load = lax.all_to_all(sent, "span", 0, 0, tiled=True)
    nodes, trace = (25, 32, 128), (5, 32, 128)
    first, joined, cross, chip = call(first_kernel, [nodes, nodes, trace, trace], load)
    cross, chip = swap_traces(cross, chip)
    second, joined, cross, chip = call(
        second_kernel, [nodes, nodes, trace, trace], joined, cross, chip, first
    )
    cross, chip = swap_traces(cross, chip)
    (packed,) = call(early_kernel, [(32, 128)], first, second)
    third, sums = call(
        third_kernel, [nodes, (16, 8, 128)], joined, cross, chip, second, packed,
        scratch=[pltpu.VMEM((32, 128), jnp.float32)],
    )
    sums = lax.all_to_all(sums, "plane", 0, 0, tiled=True)
    columns = [
        call(
            natural_kernel, [(5, 32, 640)], vector,
            scratch=[pltpu.VMEM((800, 128), jnp.float32)],
        )[0]
        for vector in (first, second, third)
    ]
    (columns,) = call(
        combine_kernel, [(5, 32, 640)], sums, *columns, out_space=pltpu.HBM,
        scratch=[
            pltpu.VMEM((8, 128), jnp.float32), pltpu.VMEM((5, 32, 640), jnp.float32),
            pltpu.SemaphoreType.DMA((5,)),
        ],
    )
    return jnp.transpose(columns, (1, 0, 2))


def solution(mesh):
    return jax.shard_map(
        on_device,
        mesh=mesh,
        in_specs=(P("span", "plane", None), P()),
        out_specs=P("span", "plane", None),
        check_vma=False,
    )
```

```python
import math

import jax
import jax.numpy as jnp
import numpy as np
from jax import lax
from jax.experimental import pallas as pl
from jax.experimental.pallas import tpu as pltpu
from jax.sharding import PartitionSpec as P


KMODES = 256
PLANES = 768
HALF = 384
ITERS = 3
GRID = 16
STEP_SIZE = 0.03
VISCOUS = 0.05
SPAN_STIFF = 4.0


def gll_tables():
    abscissae = np.array([-1.0, -math.sqrt(3.0 / 7.0), 0.0, math.sqrt(3.0 / 7.0), 1.0])
    weights = np.array([0.1, 49.0 / 90.0, 32.0 / 45.0, 49.0 / 90.0, 0.1])
    squared = abscissae * abscissae
    legendre = (35.0 * squared * squared - 30.0 * squared + 3.0) / 8.0
    identity = np.eye(5)
    spacing = abscissae[:, None] - abscissae[None, :] + identity
    differ = np.where(identity > 0, 0.0, legendre[:, None] / legendre[None, :] / spacing)
    differ[0, 0] = -5.0
    differ[4, 4] = 5.0
    stiffness = differ.T @ (weights[:, None] * differ)
    return differ, weights, stiffness


DIFFER, WEIGHTS, STIFFNESS = gll_tables()


def split_table(table):
    high = table.astype(np.float32).astype(jnp.bfloat16)
    low = (table - high.astype(np.float64)).astype(np.float32).astype(jnp.bfloat16)
    return jnp.asarray(np.stack([high, low]))


def wave_table():
    plane = np.arange(HALF)
    waves = []
    for parity in range(2):
        k = 2 * np.arange(128) + parity
        angle = (k[:, None] * plane[None, :] % PLANES) * (2.0 * math.pi / PLANES)
        waves.append(np.concatenate([np.cos(angle), np.sin(angle)]))
    return split_table(np.stack(waves))


def dot(left, right, contract):
    return lax.dot_general(
        left, right, (contract, ((), ())), preferred_element_type=jnp.float32
    )


def halves(value):
    high = value.astype(jnp.bfloat16)
    low = (value - high.astype(jnp.float32)).astype(jnp.bfloat16)
    return high, low


def dot_split(left, right, contract):
    (left_high, left_low), (right_high, right_low) = left, right
    return (
        dot(left_high, right_low, contract)
        + dot(left_low, right_high, contract)
        + dot(left_high, right_high, contract)
    )


def lanes_of(values, index):
    return jnp.take_along_axis(values, index, axis=1)


def merge_columns(tiles):
    lane = lax.broadcasted_iota(jnp.int32, tiles[0].shape, 1)
    out = []
    for t in range(5):
        column = lane + 128 * t
        element = (column * 13108) >> 16
        node = column - 5 * element
        picked = lanes_of(tiles[0], element)
        for i in range(1, 5):
            picked = jnp.where(node == i, lanes_of(tiles[i], element), picked)
        out.append(picked)
    return out


def exchange_chunks(values):
    values = list(values)
    lane = lax.broadcasted_iota(jnp.int32, values[0].shape, 1)
    for bit in (1, 2, 4, 8):
        upper = (lane & (8 * bit)) != 0
        other = lane ^ (8 * bit)
        for a in range(16):
            if a & bit == 0:
                first, second = values[a], values[a | bit]
                moved = jnp.where(upper, first, second)
                if bit == 8:
                    moved = pltpu.roll(moved, 64, 1)
                else:
                    moved = lanes_of(moved, other)
                values[a] = jnp.where(upper, moved, first)
                values[a | bit] = jnp.where(upper, second, moved)
    return values


def column_order():
    column = lax.broadcasted_iota(jnp.int32, (640, 128), 0)
    element = lax.broadcasted_iota(jnp.int32, (640, 128), 1)
    tiles = [jnp.where(column == 5 * element + i, 1.0, 0.0).astype(jnp.bfloat16) for i in range(5)]
    return jnp.concatenate(tiles, axis=1)


def pack_rows(out_ref, d, whole, rest, count):
    out_ref[d, 0:32, :] = whole
    lane = lax.broadcasted_iota(jnp.int32, (8, 128), 1)
    free = 16 - count
    for g in range(3):
        tile = rest[8 * g : 8 * g + 8]
        if g * free < count:
            shift = 8 * (count - g * free)
            tile = jnp.where(lane < 8 * count, tile, pltpu.roll(rest[24:32], shift % 128, 1))
        out_ref[d, 32 + 8 * g : 40 + 8 * g, :] = tile


def unpack_last(tiles, count):
    lane = lax.broadcasted_iota(jnp.int32, (8, 128), 1)
    free = 16 - count
    last = pltpu.roll(tiles[0], 128 - 8 * count, 1)
    for g in range(1, 3):
        if g * free < count:
            shift = 8 * (count - g * free)
            last = jnp.where(lane < 8 * g * free, last, pltpu.roll(tiles[g], (128 - shift) % 128, 1))
    return last


def pack_kernel(state_hbm, out_ref, chunk_ref, state_ref, order_ref, arrived):
    copy = pltpu.make_async_copy(state_hbm, state_ref, arrived)
    copy.start()
    order_ref[...] = column_order()
    copy.wait()
    stacked = jnp.concatenate([state_ref[j] for j in range(5)], axis=0)
    order = order_ref[...]
    contract = ((1,), (0,))
    high, low = halves(stacked)
    nodes = dot(low, order, contract) + dot(high, order, contract)
    for i in range(5):
        chunk_ref[160 * i : 160 * i + 160, :] = nodes[:, 128 * i : 128 * i + 128]
    chunk = [
        jnp.concatenate(
            [chunk_ref[pl.ds(160 * i + 32 * j + t, 8, stride=4), :] for t in range(4)], axis=0
        )
        for j in range(5)
        for i in range(5)
    ]
    lane = lax.broadcasted_iota(jnp.int32, (32, 128), 1) & 7
    sides = [jnp.zeros((32, 128), jnp.float32), jnp.zeros((32, 128), jnp.float32)]
    for j in range(5):
        at = j & 3
        side = jnp.where(lane == at, pltpu.roll(chunk[j * 5 + 4], 1 + at, 1), sides[j // 4])
        sides[j // 4] = jnp.where(lane == 7 - at, pltpu.roll(chunk[j * 5], 127 - at, 1), side)
    chunk = chunk + sides
    whole = exchange_chunks(chunk[:16])
    rest = exchange_chunks(chunk[16:] + [jnp.zeros((32, 128), jnp.float32)] * 5)
    for d in range(GRID):
        pack_rows(out_ref, d, whole[d], rest[d], 11)


def turn(modal_ref, cross_ref, chip_ref):
    last = [
        unpack_last([modal_ref[s, 32 + 8 * g : 40 + 8 * g, :] for g in range(3)], 11)
        for s in range(GRID)
    ]
    nodal = []
    for parity in range(2):
        whole, rest = [], []
        for t in range(2):
            group = 2 * parity + t
            for s in range(GRID):
                whole.append(modal_ref[s, 8 * group : 8 * group + 8, :])
                rest.append(
                    last[s] if group == 3 else modal_ref[s, 32 + 8 * group : 40 + 8 * group, :]
                )
        turned = [jnp.concatenate(part, axis=0).T for part in (whole, rest)]
        nodal.append(jnp.concatenate([turned[0], turned[1][0:88]], axis=0))
        cross_ref[parity], chip_ref[parity] = to_partners(turned[0][0:40], turned[1][32:72])
    return nodal


def synthesize(nodal, table_ref):
    part = [
        dot_split(
            halves(nodal[parity]), (table_ref[0, parity], table_ref[1, parity]), ((1,), (0,))
        )
        for parity in range(2)
    ]
    scale = 1.0 / math.sqrt(KMODES)
    return scale * (part[0] + part[1]), scale * (part[0] - part[1])


def two_point(left, right):
    mean = (left * left + left * right + right * right) * (1.0 / 6.0)
    speed = jnp.maximum(jnp.abs(left), jnp.abs(right))
    return mean - 0.5 * speed * (right - left)


def volume_kernel(
    modal_ref, table_ref, field_ref, rhs_ref, modal_cross_ref, modal_chip_ref, cross_ref, chip_ref,
    side_ref,
):
    nodal = turn(modal_ref, modal_cross_ref, modal_chip_ref)
    pair = synthesize(nodal, table_ref)
    for q in range(2):
        field_ref[:, HALF * q : HALF * q + HALF] = pair[q][0:200]
        side_ref[:, HALF * q : HALF * q + HALF] = pair[q][200:216]
    row = lax.broadcasted_iota(jnp.int32, (8, 128), 0)

    def column(block, carry):
        lanes = pl.ds(pl.multiple_of(block * 128, 128), 128)
        f = [field_ref[8 * n : 8 * n + 8, lanes] for n in range(25)]
        square = [v * v for v in f]
        low = []
        for j in range(5):
            for i in range(5):
                n = j * 5 + i
                plain = None
                power = None
                for other in range(5):
                    terms = [(DIFFER[i][other], j * 5 + other), (DIFFER[j][other], other * 5 + i)]
                    for weight, m in terms:
                        if weight == 0.0:
                            continue
                        weight = float(weight) / -3.0
                        plain = weight * f[m] if plain is None else plain + weight * f[m]
                        power = weight * square[m] if power is None else power + weight * square[m]
                total = power + f[n] * plain
                own = (i == 4) + (j == 4) - (i == 0) - (j == 0)
                if own:
                    total = total + (5.0 * own) * square[n]
                if i == 0 or i == 4:
                    at = j & 3
                    side = side_ref[8 * (j // 4) : 8 * (j // 4) + 8, lanes]
                    if at:
                        side = pltpu.roll(side, 8 - at if i == 0 else at, 0)
                    if i == 0:
                        left = jnp.where(row == 0, side, pltpu.roll(f[j * 5 + 4], 1, 0))
                        total = total + 10.0 * two_point(left, f[n])
                    else:
                        right = jnp.where(row == 7, side, pltpu.roll(f[j * 5], 7, 0))
                        total = total - 10.0 * two_point(f[n], right)
                rhs_ref[8 * n : 8 * n + 8, lanes] = total
                if j == 0:
                    low.append(total)
                elif j == 4:
                    rows = slice(8 * i, 8 * i + 8)
                    cross_ref[rows, lanes], chip_ref[rows, lanes] = to_partners(low[i], total)
        return carry

    lax.fori_loop(0, PLANES // 128, column, 0)


def project(planar, parity, table_ref):
    folded = planar[:, :HALF] + planar[:, HALF:] if parity == 0 else planar[:, :HALF] - planar[:, HALF:]
    return dot_split((table_ref[0, parity], table_ref[1, parity]), halves(folded), ((1,), (1,)))


def tendency(parity, from_rhs, from_flux):
    k = 2 * lax.broadcasted_iota(jnp.int32, (128, 128), 0) + parity
    scale = jnp.where(k == 0, 1.0, 2.0) * (math.sqrt(KMODES) / PLANES * STEP_SIZE)
    ratio = k.astype(jnp.float32) * (1.0 / KMODES)
    return (
        scale * (from_rhs[0:128] - ratio * from_flux[128:256]),
        scale * (from_rhs[128:256] + ratio * from_flux[0:128]),
    )


def inside_kernel(modal_ref, field_ref, rhs_ref, table_ref, out_ref):
    last = [
        unpack_last([modal_ref[s, 32 + 8 * g : 40 + 8 * g, :] for g in range(3)], 11)
        for s in range(GRID)
    ]
    field = field_ref[...]
    flux = 0.5 * field * field
    rhs = rhs_ref[...]
    tail = jnp.zeros((56, PLANES), jnp.float32)
    flux = jnp.concatenate([flux, tail], axis=0)
    rhs = jnp.concatenate([rhs, tail], axis=0)
    for parity in range(2):
        from_rhs = project(rhs, parity, table_ref)
        from_flux = project(flux, parity, table_ref)
        for half in range(2):
            lanes = slice(128 * half, 128 * half + 128)
            change = tendency(parity, from_rhs[:, lanes], from_flux[:, lanes])
            for t in range(2):
                first = 16 * parity + 8 * t + 32 * half
                modal = jnp.concatenate(
                    last if first == 56 else [modal_ref[s, first : first + 8, :] for s in range(GRID)],
                    axis=0,
                )
                out_ref[parity, 128 * t : 128 * t + 128, lanes] = modal + change[t]


def lift_kernel(
    tag_ref, field_ref, cross_ref, chip_ref, table_ref, lift_ref, flux_ref, modal_ref, outer_ref
):
    bottom, top = at_ends()
    span = lax.axis_index("span")
    row = lax.broadcasted_iota(jnp.int32, (8, 128), 0)
    mirror = jnp.ones((8, 128), jnp.float32)
    for e in range(8):
        mirror = jnp.where((row == e) & (tag_ref[8 * span + e] == 1), -1.0, mirror)
    keep_lower = jnp.where(bottom, 0.0, 1.0)
    keep_upper = jnp.where(top, 0.0, 1.0)
    gap = jnp.zeros((48, 256), jnp.float32)
    outer = []
    for parity in range(2):
        below, above = from_partners(cross_ref[parity], chip_ref[parity])
        outer.append(jnp.concatenate([below, above], axis=0))
        modal_ref[parity] = jnp.concatenate(
            [keep_lower * below, keep_upper * above, gap], axis=0
        ).T
    pair = synthesize(outer, table_ref)
    for q in range(2):
        outer_ref[:, HALF * q : HALF * q + HALF] = pair[q]
    mirror = jnp.concatenate([mirror] * 6, axis=1)
    mirror = jnp.concatenate([mirror] * 5, axis=0)
    inside = field_ref[0:40, :]
    below = outer_ref[0:40, :]
    lift_ref[0:40, :] = 10.0 * two_point(jnp.where(bottom, mirror * inside, below), inside)
    flux_ref[0:40, :] = keep_lower * (0.5 * below * below)
    inside = field_ref[160:200, :]
    above = outer_ref[40:80, :]
    lift_ref[40:80, :] = 10.0 * two_point(inside, jnp.where(top, inside, above))
    flux_ref[40:80, :] = keep_upper * (0.5 * above * above)


def facing_kernel(
    inside_ref, lift_ref, flux_ref, facing_ref, cross_ref, chip_ref, table_ref, out_ref
):
    bottom, top = at_ends()
    below, above = from_partners(cross_ref[...], chip_ref[...])
    lift = lift_ref[0:40, :]
    rhs_lower = lift + jnp.where(bottom, 0.0, below - lift)
    lift = lift_ref[40:80, :]
    rhs_upper = jnp.where(top, 0.0, above + lift) - lift
    gap = jnp.zeros((48, PLANES), jnp.float32)
    planar = jnp.concatenate([rhs_lower, rhs_upper, gap, flux_ref[...], gap], axis=0)
    lane = lax.broadcasted_iota(jnp.int32, (128, 128), 1)
    whole, rest = [], []
    for parity in range(2):
        projected = project(planar, parity, table_ref)
        change = tendency(parity, projected[:, 0:128], projected[:, 128:256])
        for t in range(2):
            rows = slice(128 * t, 128 * t + 128)
            extra = change[t] + facing_ref[parity, rows, :]
            lower = jnp.where(lane < 40, extra, 0.0)
            upper = pltpu.roll(jnp.where(lane < 40, 0.0, extra), 120, 1)
            whole.append(inside_ref[parity, rows, 0:128] + lower)
            rest.append(inside_ref[parity, rows, 128:256] + upper)
    for s in range(GRID):
        part = slice(8 * s, 8 * s + 8)
        pack_rows(
            out_ref,
            s,
            jnp.concatenate([group[part] for group in whole], axis=0),
            jnp.concatenate([group[part] for group in rest], axis=0),
            9,
        )


def energy(values, shift):
    total = None
    for j in range(5):
        for i in range(5):
            n = j * 5 + i
            mass = float(WEIGHTS[j] * WEIGHTS[i])
            diagonal = VISCOUS * float(WEIGHTS[j] * STIFFNESS[i][i] + WEIGHTS[i] * STIFFNESS[j][j])
            value = (shift * mass + diagonal) * values[n]
            for other in range(i + 1, 5):
                weight = 2.0 * VISCOUS * float(WEIGHTS[j] * STIFFNESS[i][other])
                value = value + weight * values[j * 5 + other]
            for other in range(j + 1, 5):
                weight = 2.0 * VISCOUS * float(WEIGHTS[i] * STIFFNESS[j][other])
                value = value + weight * values[other * 5 + i]
            term = value * values[n]
            total = term if total is None else total + term
    return total


def at_ends():
    plane = lax.axis_index("plane")
    return plane == 0, plane == GRID - 1


def to_partners(low, high):
    odd = lax.axis_index("plane") % 2 == 1
    return jnp.where(odd, high, low), jnp.where(odd, low, high)


def from_partners(cross, chip):
    odd = lax.axis_index("plane") % 2 == 1
    return jnp.where(odd, chip, cross), jnp.where(odd, cross, chip)


def local_operator(values, shift):
    out = []
    for j in range(5):
        for i in range(5):
            n = j * 5 + i
            mass = float(WEIGHTS[j] * WEIGHTS[i])
            diagonal = VISCOUS * float(WEIGHTS[j] * STIFFNESS[i][i] + WEIGHTS[i] * STIFFNESS[j][j])
            value = (shift * mass + diagonal) * values[n]
            for other in range(5):
                if other != i:
                    weight = VISCOUS * float(WEIGHTS[j] * STIFFNESS[i][other])
                    value = value + weight * values[j * 5 + other]
                if other != j:
                    weight = VISCOUS * float(WEIGHTS[i] * STIFFNESS[j][other])
                    value = value + weight * values[other * 5 + i]
            out.append(value)
    return out


def join_columns(values):
    values = list(values)
    for j in range(5):
        joint = values[j * 5 + 4] + pltpu.roll(values[j * 5], 127, 1)
        values[j * 5 + 4] = joint
        values[j * 5] = pltpu.roll(joint, 1, 1)
    return values


def store_joined(values, joined_ref, cross_ref, chip_ref):
    values = join_columns(values)
    for n in range(25):
        joined_ref[n] = values[n]
    for i in range(4):
        cross_ref[i], chip_ref[i] = to_partners(values[i], values[20 + i])


def assembled(joined_ref, cross_ref, chip_ref):
    values = [joined_ref[n] for n in range(25)]
    bottom, top = at_ends()
    for i in range(4):
        below, above = from_partners(cross_ref[i], chip_ref[i])
        values[i] = values[i] + jnp.where(bottom, 0.0, below)
        values[20 + i] = values[20 + i] + jnp.where(top, 0.0, above)
    values[4] = pltpu.roll(values[0], 127, 1)
    values[24] = pltpu.roll(values[20], 127, 1)
    return values


def mode_terms():
    row = lax.broadcasted_iota(jnp.int32, (32, 128), 0)
    mode_pair = 16 * lax.axis_index("span") + 2 * (row & 7) + (row >> 4)
    ratio = mode_pair.astype(jnp.float32) * (1.0 / KMODES)
    shift = 1.0 + SPAN_STIFF * ratio * ratio
    return shift, 0.2 * shift + 0.15


def inner(left, right):
    bottom, top = at_ends()
    total = None
    for j in range(5):
        part = None
        for i in range(5):
            term = left[j * 5 + i] * right[j * 5 + i]
            term = term if 0 < i < 4 else 0.5 * term
            part = term if part is None else part + term
        if j == 0:
            part = jnp.where(bottom, 1.0, 0.5) * part
        elif j == 4:
            part = jnp.where(top, 1.0, 0.5) * part
        total = part if total is None else total + part
    return total


def first_kernel(modal_ref, vector_ref, next_ref, cross_ref, chip_ref):
    shift, _ = mode_terms()
    values = exchange_chunks([modal_ref[s, 0:32, :] for s in range(GRID)])
    rest = []
    for s in range(GRID):
        tiles = [modal_ref[s, 32 + 8 * g : 40 + 8 * g, :] for g in range(3)]
        rest.append(jnp.concatenate(tiles + [unpack_last(tiles, 9)], axis=0))
    values += exchange_chunks(rest)
    values = [float(WEIGHTS[n // 5] * WEIGHTS[n % 5]) * values[n] for n in range(25)]
    vector = join_columns(values)
    for n in range(25):
        vector_ref[n] = vector[n]
    store_joined(local_operator(vector, shift), next_ref, cross_ref, chip_ref)


def second_kernel(
    joined_ref, cross_in_ref, chip_in_ref, before_ref, vector_ref, next_ref, cross_ref, chip_ref
):
    shift, center = mode_terms()
    applied = assembled(joined_ref, cross_in_ref, chip_in_ref)
    vector = [applied[n] - center * before_ref[n] for n in range(25)]
    for n in range(25):
        vector_ref[n] = vector[n]
    store_joined(local_operator(vector, shift), next_ref, cross_ref, chip_ref)


def pack_moments(moments, first, packed):
    lane = lax.broadcasted_iota(jnp.int32, (32, 128), 1)
    for n, moment in enumerate(moments):
        packed = jnp.where(lane == first + n, jnp.sum(moment, axis=1, keepdims=True), packed)
    return packed


def early_kernel(first_ref, second_ref, joined_ref, packed_ref):
    _, center = mode_terms()
    first = [first_ref[n] for n in range(25)]
    second = [second_ref[n] for n in range(25)]
    square = inner(second, second)
    product = None
    for n in range(25):
        term = second[n] * joined_ref[n]
        term = term if 0 < n % 5 < 4 else 0.5 * term
        product = term if product is None else product + term
    moments = [inner(first, first), inner(first, second), square, product - center * square]
    packed_ref[...] = pack_moments(moments, 0, jnp.zeros((32, 128), jnp.float32))


def third_kernel(
    joined_ref, cross_in_ref, chip_in_ref, second_ref, packed_ref, vector_ref, sums_ref,
    turn_ref,
):
    shift, center = mode_terms()
    applied = assembled(joined_ref, cross_in_ref, chip_in_ref)
    second = [second_ref[n] for n in range(25)]
    third = [applied[n] - center * second[n] for n in range(25)]
    for n in range(25):
        vector_ref[n] = third[n]
    fourth = inner(third, third)
    moments = [fourth, energy(third, shift) - center * fourth]
    packed = pack_moments(moments, 4, packed_ref[...])
    for t in range(4):
        turn_ref[pl.ds(t, 8, stride=4), :] = packed[8 * t : 8 * t + 8]
    turned = turn_ref[...].T[0:8]
    for p in range(GRID):
        sums_ref[p, :, 0:32] = turned


def natural_kernel(vector_ref, out_ref, column_ref):
    for j in range(5):
        tiles = merge_columns([vector_ref[j * 5 + i] for i in range(5)])
        for i in range(5):
            first = 32 * (5 * j + i)
            for t in range(4):
                column_ref[pl.ds(first + t, 8, stride=4), :] = tiles[i][8 * t : 8 * t + 8]
            out_ref[j, :, 128 * i : 128 * i + 128] = column_ref[first : first + 32, :]


def tree(terms):
    while len(terms) > 1:
        terms = [sum(terms[n + 1 : n + 2], terms[n]) for n in range(0, len(terms), 2)]
    return terms[0]


def combine_kernel(
    sums_ref, first_ref, second_ref, third_ref, out_hbm, turn_ref, result_ref, sent
):
    total = tree([sums_ref[p] for p in range(GRID)])
    moment = [total[n : n + 1] for n in range(6)]
    lane = lax.broadcasted_iota(jnp.int32, (1, 128), 1)
    mode_pair = 16 * lax.axis_index("span") + (lane >> 1)
    ratio = mode_pair.astype(jnp.float32) * (1.0 / KMODES)
    center = 0.2 * (1.0 + SPAN_STIFF * ratio * ratio) + 0.15

    def product(left, right):
        return tree(
            [
                tree(
                    [
                        left[a] * right[power - a]
                        for a in range(len(left))
                        if 0 <= power - a < len(right)
                    ]
                )
                * moment[power]
                for power in range(len(left) + len(right) - 1)
            ]
        )

    def operator(c):
        shifted = [center * v for v in c] + [0.0]
        return [shifted[0]] + [shifted[a + 1] + c[a] for a in range(len(c))]

    residual = [jnp.ones((1, 128), jnp.float32)]
    direction = residual
    result = [0.0, 0.0, 0.0]
    norm = moment[0]
    for step in range(ITERS):
        applied = operator(direction)
        length = norm / product(direction, applied)
        for a in range(len(direction)):
            result[a] = result[a] + length * direction[a]
        if step < ITERS - 1:
            padded = residual + [0.0]
            residual = [padded[a] - length * applied[a] for a in range(len(applied))]
            fresh = product(residual, residual)
            ratio = fresh / norm
            norm = fresh
            padded = direction + [0.0]
            direction = [residual[a] + ratio * padded[a] for a in range(len(residual))]
    turn_ref[...] = jnp.zeros((8, 128), jnp.float32)
    for a in range(3):
        turn_ref[a : a + 1, :] = result[a]
    turned = turn_ref[...].T[0:32]
    weight = [turned[:, a : a + 1] for a in range(3)]
    copies = []
    for j in range(5):
        result_ref[j] = (
            weight[0] * first_ref[j] + weight[1] * second_ref[j] + weight[2] * third_ref[j]
        )
        copies.append(pltpu.make_async_copy(result_ref.at[j], out_hbm.at[j], sent.at[j]))
        copies[j].start()
    for copy in copies:
        copy.wait()


def call(kernel, out_shapes, *args, smem=(), anywhere=(), scratch=(), out_space=pltpu.VMEM, covers=True):
    vmem = pl.BlockSpec(memory_space=pltpu.VMEM)
    spaces = {n: pl.BlockSpec(memory_space=pltpu.SMEM) for n in smem}
    spaces |= {n: pl.BlockSpec(memory_space=pltpu.HBM) for n in anywhere}
    return pl.pallas_call(
        kernel,
        out_shape=[jax.ShapeDtypeStruct(s, jnp.float32) for s in out_shapes],
        in_specs=[spaces.get(n, vmem) for n in range(len(args))],
        out_specs=[pl.BlockSpec(memory_space=out_space)] * len(out_shapes),
        scratch_shapes=list(scratch),
        cost_estimate=None if covers else pl.CostEstimate(flops=0, bytes_accessed=0, transcendentals=0),
        compiler_params=pltpu.CompilerParams(vmem_limit_bytes=16 * 1024 * 1024),
    )(*args)


def swap_traces(cross, chip):
    partner = [(p, (p + 1) % GRID if p % 2 else (p - 1) % GRID) for p in range(GRID)]
    chip = lax.ppermute(chip, "plane", [(p, p ^ 1) for p in range(GRID)])
    cross = lax.ppermute(cross, "plane", partner)
    return cross, chip


def on_device(state, wall_tag):
    table = wave_table()
    (packed,) = call(
        pack_kernel, [(16, 56, 128)],
        pltpu.with_memory_space_constraint(jnp.transpose(state, (1, 0, 2)), pltpu.HBM),
        anywhere=(0,),
        scratch=[
            pltpu.VMEM((800, 128), jnp.float32), pltpu.VMEM((5, 32, 640), jnp.float32),
            pltpu.VMEM((640, 640), jnp.bfloat16), pltpu.SemaphoreType.DMA(()),
        ],
    )
    modal = lax.all_to_all(packed, "span", 0, 0, tiled=True)
    trace, rows = (2, 40, 256), (40, PLANES)
    field, rhs, *modal_traces, cross, chip = call(
        volume_kernel, [(200, PLANES), (200, PLANES), trace, trace, rows, rows], modal,
        table, scratch=[pltpu.VMEM((16, PLANES), jnp.float32)],
    )
    modal_traces = swap_traces(*modal_traces)
    rhs_traces = swap_traces(cross, chip)
    (inside,) = call(inside_kernel, [(2, 256, 256)], modal, field, rhs, table, covers=False)
    lift, flux, facing = call(
        lift_kernel, [(80, PLANES), (80, PLANES), (2, 256, 128)], wall_tag, field,
        *modal_traces, table, smem=(0,), scratch=[pltpu.VMEM((80, PLANES), jnp.float32)],
        covers=False,
    )
    (sent,) = call(facing_kernel, [(16, 56, 128)], inside, lift, flux, facing, *rhs_traces, table)
    load = lax.all_to_all(sent, "span", 0, 0, tiled=True)
    nodes, trace = (25, 32, 128), (4, 32, 128)
    first, joined, cross, chip = call(first_kernel, [nodes, nodes, trace, trace], load)
    cross, chip = swap_traces(cross, chip)
    second, joined, cross, chip = call(
        second_kernel, [nodes, nodes, trace, trace], joined, cross, chip, first
    )
    cross, chip = swap_traces(cross, chip)
    (packed,) = call(early_kernel, [(32, 128)], first, second, joined)
    third, sums = call(
        third_kernel, [nodes, (16, 8, 128)], joined, cross, chip, second, packed,
        scratch=[pltpu.VMEM((32, 128), jnp.float32)],
    )
    sums = lax.all_to_all(sums, "plane", 0, 0, tiled=True)
    columns = [
        call(
            natural_kernel, [(5, 32, 640)], vector,
            scratch=[pltpu.VMEM((800, 128), jnp.float32)],
        )[0]
        for vector in (first, second, third)
    ]
    (columns,) = call(
        combine_kernel, [(5, 32, 640)], sums, *columns, out_space=pltpu.HBM,
        scratch=[
            pltpu.VMEM((8, 128), jnp.float32), pltpu.VMEM((5, 32, 640), jnp.float32),
            pltpu.SemaphoreType.DMA((5,)),
        ],
    )
    return jnp.transpose(columns, (1, 0, 2))


def solution(mesh):
    return jax.shard_map(
        on_device,
        mesh=mesh,
        in_specs=(P("span", "plane", None), P()),
        out_specs=P("span", "plane", None),
        check_vma=False,
    )
```

```python
import math

import jax
import jax.numpy as jnp
import numpy as np
from jax import lax
from jax.experimental import pallas as pl
from jax.experimental.pallas import tpu as pltpu
from jax.sharding import PartitionSpec as P


KMODES = 256
PLANES = 768
HALF = 384
ITERS = 3
GRID = 16
STEP_SIZE = 0.03
VISCOUS = 0.05
SPAN_STIFF = 4.0


def gll_tables():
    abscissae = np.array([-1.0, -math.sqrt(3.0 / 7.0), 0.0, math.sqrt(3.0 / 7.0), 1.0])
    weights = np.array([0.1, 49.0 / 90.0, 32.0 / 45.0, 49.0 / 90.0, 0.1])
    squared = abscissae * abscissae
    legendre = (35.0 * squared * squared - 30.0 * squared + 3.0) / 8.0
    identity = np.eye(5)
    spacing = abscissae[:, None] - abscissae[None, :] + identity
    differ = np.where(identity > 0, 0.0, legendre[:, None] / legendre[None, :] / spacing)
    differ[0, 0] = -5.0
    differ[4, 4] = 5.0
    stiffness = differ.T @ (weights[:, None] * differ)
    return differ, weights, stiffness


DIFFER, WEIGHTS, STIFFNESS = gll_tables()


def split_table(table):
    high = table.astype(np.float32).astype(jnp.bfloat16)
    low = (table - high.astype(np.float64)).astype(np.float32).astype(jnp.bfloat16)
    return jnp.asarray(np.stack([high, low]))


def wave_table():
    plane = np.arange(HALF)
    waves = []
    for parity in range(2):
        k = 2 * np.arange(128) + parity
        angle = (k[:, None] * plane[None, :] % PLANES) * (2.0 * math.pi / PLANES)
        waves.append(np.concatenate([np.cos(angle), np.sin(angle)]))
    return split_table(np.stack(waves))


def dot(left, right, contract):
    return lax.dot_general(
        left, right, (contract, ((), ())), preferred_element_type=jnp.float32
    )


def halves(value):
    high = value.astype(jnp.bfloat16)
    low = (value - high.astype(jnp.float32)).astype(jnp.bfloat16)
    return high, low


def dot_split(left, right, contract):
    (left_high, left_low), (right_high, right_low) = left, right
    return (
        dot(left_high, right_low, contract)
        + dot(left_low, right_high, contract)
        + dot(left_high, right_high, contract)
    )


def lanes_of(values, index):
    return jnp.take_along_axis(values, index, axis=1)


def merge_columns(tiles):
    lane = lax.broadcasted_iota(jnp.int32, tiles[0].shape, 1)
    out = []
    for t in range(5):
        column = lane + 128 * t
        element = (column * 13108) >> 16
        node = column - 5 * element
        picked = lanes_of(tiles[0], element)
        for i in range(1, 5):
            picked = jnp.where(node == i, lanes_of(tiles[i], element), picked)
        out.append(picked)
    return out


def exchange_chunks(values):
    values = list(values)
    lane = lax.broadcasted_iota(jnp.int32, values[0].shape, 1)
    for bit in (1, 2, 4, 8):
        upper = (lane & (8 * bit)) != 0
        other = lane ^ (8 * bit)
        for a in range(16):
            if a & bit == 0:
                first, second = values[a], values[a | bit]
                moved = jnp.where(upper, first, second)
                if bit == 8:
                    moved = pltpu.roll(moved, 64, 1)
                else:
                    moved = lanes_of(moved, other)
                values[a] = jnp.where(upper, moved, first)
                values[a | bit] = jnp.where(upper, second, moved)
    return values


def column_order():
    column = lax.broadcasted_iota(jnp.int32, (640, 128), 0)
    element = lax.broadcasted_iota(jnp.int32, (640, 128), 1)
    tiles = [jnp.where(column == 5 * element + i, 1.0, 0.0).astype(jnp.bfloat16) for i in range(5)]
    return jnp.concatenate(tiles, axis=1)


def pack_rows(out_ref, d, whole, rest, count):
    out_ref[d, 0:32, :] = whole
    lane = lax.broadcasted_iota(jnp.int32, (8, 128), 1)
    free = 16 - count
    for g in range(3):
        tile = rest[8 * g : 8 * g + 8]
        if g * free < count:
            shift = 8 * (count - g * free)
            tile = jnp.where(lane < 8 * count, tile, pltpu.roll(rest[24:32], shift % 128, 1))
        out_ref[d, 32 + 8 * g : 40 + 8 * g, :] = tile


def unpack_last(tiles, count):
    lane = lax.broadcasted_iota(jnp.int32, (8, 128), 1)
    free = 16 - count
    last = pltpu.roll(tiles[0], 128 - 8 * count, 1)
    for g in range(1, 3):
        if g * free < count:
            shift = 8 * (count - g * free)
            last = jnp.where(lane < 8 * g * free, last, pltpu.roll(tiles[g], (128 - shift) % 128, 1))
    return last


def pack_kernel(state_hbm, out_ref, chunk_ref, state_ref, order_ref, arrived):
    copy = pltpu.make_async_copy(state_hbm, state_ref, arrived)
    copy.start()
    order_ref[...] = column_order()
    copy.wait()
    stacked = jnp.concatenate([state_ref[j] for j in range(5)], axis=0)
    order = order_ref[...]
    contract = ((1,), (0,))
    high, low = halves(stacked)
    nodes = dot(low, order, contract) + dot(high, order, contract)
    for i in range(5):
        chunk_ref[160 * i : 160 * i + 160, :] = nodes[:, 128 * i : 128 * i + 128]
    chunk = [
        jnp.concatenate(
            [chunk_ref[pl.ds(160 * i + 32 * j + t, 8, stride=4), :] for t in range(4)], axis=0
        )
        for j in range(5)
        for i in range(5)
    ]
    lane = lax.broadcasted_iota(jnp.int32, (32, 128), 1) & 7
    sides = [jnp.zeros((32, 128), jnp.float32), jnp.zeros((32, 128), jnp.float32)]
    for j in range(5):
        at = j & 3
        side = jnp.where(lane == at, pltpu.roll(chunk[j * 5 + 4], 1 + at, 1), sides[j // 4])
        sides[j // 4] = jnp.where(lane == 7 - at, pltpu.roll(chunk[j * 5], 127 - at, 1), side)
    chunk = chunk + sides
    whole = exchange_chunks(chunk[:16])
    rest = exchange_chunks(chunk[16:] + [jnp.zeros((32, 128), jnp.float32)] * 5)
    for d in range(GRID):
        pack_rows(out_ref, d, whole[d], rest[d], 11)


def turn(modal_ref, cross_ref, chip_ref):
    last = [
        unpack_last([modal_ref[s, 32 + 8 * g : 40 + 8 * g, :] for g in range(3)], 11)
        for s in range(GRID)
    ]
    nodal = []
    for parity in range(2):
        whole, rest = [], []
        for t in range(2):
            group = 2 * parity + t
            for s in range(GRID):
                whole.append(modal_ref[s, 8 * group : 8 * group + 8, :])
                rest.append(
                    last[s] if group == 3 else modal_ref[s, 32 + 8 * group : 40 + 8 * group, :]
                )
        turned = [jnp.concatenate(part, axis=0).T for part in (whole, rest)]
        nodal.append(jnp.concatenate([turned[0], turned[1][0:88]], axis=0))
        lanes = slice(PLANES + 256 * parity, PLANES + 256 * parity + 256)
        cross_ref[:, lanes], chip_ref[:, lanes] = to_partners(turned[0][0:40], turned[1][32:72])
    return nodal


def synthesize(nodal, table_ref):
    part = [
        dot_split(
            halves(nodal[parity]), (table_ref[0, parity], table_ref[1, parity]), ((1,), (0,))
        )
        for parity in range(2)
    ]
    scale = 1.0 / math.sqrt(KMODES)
    return scale * (part[0] + part[1]), scale * (part[0] - part[1])


def two_point(left, right):
    mean = (left * left + left * right + right * right) * (1.0 / 6.0)
    speed = jnp.maximum(jnp.abs(left), jnp.abs(right))
    return mean - 0.5 * speed * (right - left)


def volume_kernel(modal_ref, table_ref, field_ref, rhs_ref, cross_ref, chip_ref, side_ref):
    nodal = turn(modal_ref, cross_ref, chip_ref)
    pair = synthesize(nodal, table_ref)
    for q in range(2):
        field_ref[:, HALF * q : HALF * q + HALF] = pair[q][0:200]
        side_ref[:, HALF * q : HALF * q + HALF] = pair[q][200:216]
    row = lax.broadcasted_iota(jnp.int32, (8, 128), 0)

    def column(block, carry):
        lanes = pl.ds(pl.multiple_of(block * 128, 128), 128)
        f = [field_ref[8 * n : 8 * n + 8, lanes] for n in range(25)]
        square = [v * v for v in f]
        low = []
        for j in range(5):
            for i in range(5):
                n = j * 5 + i
                plain = None
                power = None
                for other in range(5):
                    terms = [(DIFFER[i][other], j * 5 + other), (DIFFER[j][other], other * 5 + i)]
                    for weight, m in terms:
                        if weight == 0.0:
                            continue
                        weight = float(weight) / -3.0
                        plain = weight * f[m] if plain is None else plain + weight * f[m]
                        power = weight * square[m] if power is None else power + weight * square[m]
                total = power + f[n] * plain
                own = (i == 4) + (j == 4) - (i == 0) - (j == 0)
                if own:
                    total = total + (5.0 * own) * square[n]
                if i == 0 or i == 4:
                    at = j & 3
                    side = side_ref[8 * (j // 4) : 8 * (j // 4) + 8, lanes]
                    if at:
                        side = pltpu.roll(side, 8 - at if i == 0 else at, 0)
                    if i == 0:
                        left = jnp.where(row == 0, side, pltpu.roll(f[j * 5 + 4], 1, 0))
                        total = total + 10.0 * two_point(left, f[n])
                    else:
                        right = jnp.where(row == 7, side, pltpu.roll(f[j * 5], 7, 0))
                        total = total - 10.0 * two_point(f[n], right)
                rhs_ref[8 * n : 8 * n + 8, lanes] = total
                if j == 0:
                    low.append(total)
                elif j == 4:
                    rows = slice(8 * i, 8 * i + 8)
                    cross_ref[rows, lanes], chip_ref[rows, lanes] = to_partners(low[i], total)
        return carry

    lax.fori_loop(0, PLANES // 128, column, 0)


def project(planar, parity, table_ref):
    folded = planar[:, :HALF] + planar[:, HALF:] if parity == 0 else planar[:, :HALF] - planar[:, HALF:]
    return dot_split((table_ref[0, parity], table_ref[1, parity]), halves(folded), ((1,), (1,)))


def tendency(parity, from_rhs, from_flux):
    k = 2 * lax.broadcasted_iota(jnp.int32, (128, 128), 0) + parity
    scale = jnp.where(k == 0, 1.0, 2.0) * (math.sqrt(KMODES) / PLANES * STEP_SIZE)
    ratio = k.astype(jnp.float32) * (1.0 / KMODES)
    return (
        scale * (from_rhs[0:128] - ratio * from_flux[128:256]),
        scale * (from_rhs[128:256] + ratio * from_flux[0:128]),
    )


def inside_kernel(modal_ref, field_ref, rhs_ref, table_ref, out_ref):
    last = [
        unpack_last([modal_ref[s, 32 + 8 * g : 40 + 8 * g, :] for g in range(3)], 11)
        for s in range(GRID)
    ]
    field = field_ref[...]
    flux = 0.5 * field * field
    rhs = rhs_ref[...]
    tail = jnp.zeros((56, PLANES), jnp.float32)
    flux = jnp.concatenate([flux, tail], axis=0)
    rhs = jnp.concatenate([rhs, tail], axis=0)
    for parity in range(2):
        from_rhs = project(rhs, parity, table_ref)
        from_flux = project(flux, parity, table_ref)
        for half in range(2):
            lanes = slice(128 * half, 128 * half + 128)
            change = tendency(parity, from_rhs[:, lanes], from_flux[:, lanes])
            for t in range(2):
                first = 16 * parity + 8 * t + 32 * half
                modal = jnp.concatenate(
                    last if first == 56 else [modal_ref[s, first : first + 8, :] for s in range(GRID)],
                    axis=0,
                )
                out_ref[parity, 128 * t : 128 * t + 128, lanes] = modal + change[t]


def lift_faces(
    tag_ref, field_ref, below_trace, above_trace, table_ref, lift_ref, flux_ref, modal_ref, outer_ref
):
    bottom, top = at_ends()
    span = lax.axis_index("span")
    row = lax.broadcasted_iota(jnp.int32, (8, 128), 0)
    mirror = jnp.ones((8, 128), jnp.float32)
    for e in range(8):
        mirror = jnp.where((row == e) & (tag_ref[8 * span + e] == 1), -1.0, mirror)
    keep_lower = jnp.where(bottom, 0.0, 1.0)
    keep_upper = jnp.where(top, 0.0, 1.0)
    gap = jnp.zeros((48, 256), jnp.float32)
    outer = []
    for parity in range(2):
        lanes = slice(PLANES + 256 * parity, PLANES + 256 * parity + 256)
        below, above = below_trace[:, lanes], above_trace[:, lanes]
        outer.append(jnp.concatenate([below, above], axis=0))
        modal_ref[parity] = jnp.concatenate(
            [keep_lower * below, keep_upper * above, gap], axis=0
        ).T
    pair = synthesize(outer, table_ref)
    for q in range(2):
        outer_ref[:, HALF * q : HALF * q + HALF] = pair[q]
    mirror = jnp.concatenate([mirror] * 6, axis=1)
    mirror = jnp.concatenate([mirror] * 5, axis=0)
    inside = field_ref[0:40, :]
    below = outer_ref[0:40, :]
    lift_ref[0:40, :] = 10.0 * two_point(jnp.where(bottom, mirror * inside, below), inside)
    flux_ref[0:40, :] = keep_lower * (0.5 * below * below)
    inside = field_ref[160:200, :]
    above = outer_ref[40:80, :]
    lift_ref[40:80, :] = 10.0 * two_point(inside, jnp.where(top, inside, above))
    flux_ref[40:80, :] = keep_upper * (0.5 * above * above)


def facing_kernel(
    tag_ref, inside_ref, field_ref, cross_ref, chip_ref, table_ref, out_ref, lift_ref, flux_ref,
    facing_ref, outer_ref,
):
    bottom, top = at_ends()
    below, above = from_partners(cross_ref[...], chip_ref[...])
    lift_faces(
        tag_ref, field_ref, below, above, table_ref, lift_ref, flux_ref, facing_ref, outer_ref
    )
    below, above = below[:, 0:PLANES], above[:, 0:PLANES]
    lift = lift_ref[0:40, :]
    rhs_lower = lift + jnp.where(bottom, 0.0, below - lift)
    lift = lift_ref[40:80, :]
    rhs_upper = jnp.where(top, 0.0, above + lift) - lift
    gap = jnp.zeros((48, PLANES), jnp.float32)
    planar = jnp.concatenate([rhs_lower, rhs_upper, gap, flux_ref[...], gap], axis=0)
    lane = lax.broadcasted_iota(jnp.int32, (128, 128), 1)
    whole, rest = [], []
    for parity in range(2):
        projected = project(planar, parity, table_ref)
        change = tendency(parity, projected[:, 0:128], projected[:, 128:256])
        for t in range(2):
            rows = slice(128 * t, 128 * t + 128)
            extra = change[t] + facing_ref[parity, rows, :]
            lower = jnp.where(lane < 40, extra, 0.0)
            upper = pltpu.roll(jnp.where(lane < 40, 0.0, extra), 120, 1)
            whole.append(inside_ref[parity, rows, 0:128] + lower)
            rest.append(inside_ref[parity, rows, 128:256] + upper)
    for s in range(GRID):
        part = slice(8 * s, 8 * s + 8)
        pack_rows(
            out_ref,
            s,
            jnp.concatenate([group[part] for group in whole], axis=0),
            jnp.concatenate([group[part] for group in rest], axis=0),
            9,
        )


def energy(values, shift):
    total = None
    for j in range(5):
        for i in range(5):
            n = j * 5 + i
            mass = float(WEIGHTS[j] * WEIGHTS[i])
            diagonal = VISCOUS * float(WEIGHTS[j] * STIFFNESS[i][i] + WEIGHTS[i] * STIFFNESS[j][j])
            value = (shift * mass + diagonal) * values[n]
            for other in range(i + 1, 5):
                weight = 2.0 * VISCOUS * float(WEIGHTS[j] * STIFFNESS[i][other])
                value = value + weight * values[j * 5 + other]
            for other in range(j + 1, 5):
                weight = 2.0 * VISCOUS * float(WEIGHTS[i] * STIFFNESS[j][other])
                value = value + weight * values[other * 5 + i]
            term = value * values[n]
            total = term if total is None else total + term
    return total


def at_ends():
    plane = lax.axis_index("plane")
    return plane == 0, plane == GRID - 1


def to_partners(low, high):
    odd = lax.axis_index("plane") % 2 == 1
    return jnp.where(odd, high, low), jnp.where(odd, low, high)


def from_partners(cross, chip):
    odd = lax.axis_index("plane") % 2 == 1
    return jnp.where(odd, chip, cross), jnp.where(odd, cross, chip)


def local_operator(values, shift):
    out = []
    for j in range(5):
        for i in range(5):
            n = j * 5 + i
            mass = float(WEIGHTS[j] * WEIGHTS[i])
            diagonal = VISCOUS * float(WEIGHTS[j] * STIFFNESS[i][i] + WEIGHTS[i] * STIFFNESS[j][j])
            value = (shift * mass + diagonal) * values[n]
            for other in range(5):
                if other != i:
                    weight = VISCOUS * float(WEIGHTS[j] * STIFFNESS[i][other])
                    value = value + weight * values[j * 5 + other]
                if other != j:
                    weight = VISCOUS * float(WEIGHTS[i] * STIFFNESS[j][other])
                    value = value + weight * values[other * 5 + i]
            out.append(value)
    return out


def join_columns(values):
    values = list(values)
    for j in range(5):
        joint = values[j * 5 + 4] + pltpu.roll(values[j * 5], 127, 1)
        values[j * 5 + 4] = joint
        values[j * 5] = pltpu.roll(joint, 1, 1)
    return values


def store_joined(values, joined_ref, cross_ref, chip_ref):
    values = join_columns(values)
    for n in range(25):
        joined_ref[n] = values[n]
    for i in range(4):
        cross_ref[i], chip_ref[i] = to_partners(values[i], values[20 + i])


def assembled(joined_ref, cross_ref, chip_ref):
    values = [joined_ref[n] for n in range(25)]
    bottom, top = at_ends()
    for i in range(4):
        below, above = from_partners(cross_ref[i], chip_ref[i])
        values[i] = values[i] + jnp.where(bottom, 0.0, below)
        values[20 + i] = values[20 + i] + jnp.where(top, 0.0, above)
    values[4] = pltpu.roll(values[0], 127, 1)
    values[24] = pltpu.roll(values[20], 127, 1)
    return values


def mode_terms():
    row = lax.broadcasted_iota(jnp.int32, (32, 128), 0)
    mode_pair = 16 * lax.axis_index("span") + 2 * (row & 7) + (row >> 4)
    ratio = mode_pair.astype(jnp.float32) * (1.0 / KMODES)
    shift = 1.0 + SPAN_STIFF * ratio * ratio
    return shift, 0.2 * shift + 0.15


def inner(left, right):
    bottom, top = at_ends()
    total = None
    for j in range(5):
        part = None
        for i in range(5):
            term = left[j * 5 + i] * right[j * 5 + i]
            term = term if 0 < i < 4 else 0.5 * term
            part = term if part is None else part + term
        if j == 0:
            part = jnp.where(bottom, 1.0, 0.5) * part
        elif j == 4:
            part = jnp.where(top, 1.0, 0.5) * part
        total = part if total is None else total + part
    return total


def first_kernel(modal_ref, vector_ref, next_ref, cross_ref, chip_ref):
    shift, _ = mode_terms()
    values = exchange_chunks([modal_ref[s, 0:32, :] for s in range(GRID)])
    rest = []
    for s in range(GRID):
        tiles = [modal_ref[s, 32 + 8 * g : 40 + 8 * g, :] for g in range(3)]
        rest.append(jnp.concatenate(tiles + [unpack_last(tiles, 9)], axis=0))
    values += exchange_chunks(rest)
    values = [float(WEIGHTS[n // 5] * WEIGHTS[n % 5]) * values[n] for n in range(25)]
    vector = join_columns(values)
    for n in range(25):
        vector_ref[n] = vector[n]
    store_joined(local_operator(vector, shift), next_ref, cross_ref, chip_ref)


def second_kernel(
    joined_ref, cross_in_ref, chip_in_ref, before_ref, vector_ref, next_ref, cross_ref, chip_ref
):
    shift, center = mode_terms()
    applied = assembled(joined_ref, cross_in_ref, chip_in_ref)
    vector = [applied[n] - center * before_ref[n] for n in range(25)]
    for n in range(25):
        vector_ref[n] = vector[n]
    store_joined(local_operator(vector, shift), next_ref, cross_ref, chip_ref)


def mode_sums(moment, turn_ref):
    for t in range(4):
        turn_ref[pl.ds(t, 8, stride=4), :] = moment[8 * t : 8 * t + 8]
    return jnp.sum(turn_ref[...].T, axis=0, keepdims=True)


def early_kernel(first_ref, second_ref, joined_ref, packed_ref, turn_ref):
    _, center = mode_terms()
    first = [first_ref[n] for n in range(25)]
    second = [second_ref[n] for n in range(25)]
    square = inner(second, second)
    product = None
    for n in range(25):
        term = second[n] * joined_ref[n]
        term = term if 0 < n % 5 < 4 else 0.5 * term
        product = term if product is None else product + term
    moments = [inner(first, first), inner(first, second), square, product - center * square]
    packed_ref[...] = jnp.zeros((8, 128), jnp.float32)
    for n, moment in enumerate(moments):
        packed_ref[n : n + 1, 0:32] = mode_sums(moment, turn_ref.at[n])


def third_kernel(
    joined_ref, cross_in_ref, chip_in_ref, second_ref, packed_ref, vector_ref, sums_ref,
    turn_ref,
):
    shift, center = mode_terms()
    applied = assembled(joined_ref, cross_in_ref, chip_in_ref)
    second = [second_ref[n] for n in range(25)]
    third = [applied[n] - center * second[n] for n in range(25)]
    for n in range(25):
        vector_ref[n] = third[n]
    fourth = inner(third, third)
    moments = [fourth, energy(third, shift) - center * fourth]
    sums_ref[0] = packed_ref[...]
    for n, moment in enumerate(moments):
        sums_ref[0, 4 + n : 5 + n, 0:32] = mode_sums(moment, turn_ref.at[n])
    sums = sums_ref[0]
    for p in range(1, GRID):
        sums_ref[p] = sums


def natural_kernel(vector_ref, out_ref, column_ref):
    for j in range(5):
        tiles = merge_columns([vector_ref[j * 5 + i] for i in range(5)])
        for i in range(5):
            first = 32 * (5 * j + i)
            for t in range(4):
                column_ref[pl.ds(first + t, 8, stride=4), :] = tiles[i][8 * t : 8 * t + 8]
            out_ref[j, :, 128 * i : 128 * i + 128] = column_ref[first : first + 32, :]


def tree(terms):
    while len(terms) > 1:
        terms = [sum(terms[n + 1 : n + 2], terms[n]) for n in range(0, len(terms), 2)]
    return terms[0]


def combine_kernel(
    sums_ref, first_ref, second_ref, third_ref, out_hbm, turn_ref, result_ref, sent
):
    total = tree([sums_ref[p] for p in range(GRID)])
    moment = [total[n : n + 1] for n in range(6)]
    lane = lax.broadcasted_iota(jnp.int32, (1, 128), 1)
    mode_pair = 16 * lax.axis_index("span") + (lane >> 1)
    ratio = mode_pair.astype(jnp.float32) * (1.0 / KMODES)
    center = 0.2 * (1.0 + SPAN_STIFF * ratio * ratio) + 0.15

    def product(left, right):
        return tree(
            [
                tree(
                    [
                        left[a] * right[power - a]
                        for a in range(len(left))
                        if 0 <= power - a < len(right)
                    ]
                )
                * moment[power]
                for power in range(len(left) + len(right) - 1)
            ]
        )

    def operator(c):
        shifted = [center * v for v in c] + [0.0]
        return [shifted[0]] + [shifted[a + 1] + c[a] for a in range(len(c))]

    residual = [jnp.ones((1, 128), jnp.float32)]
    direction = residual
    result = [0.0, 0.0, 0.0]
    norm = moment[0]
    for step in range(ITERS):
        applied = operator(direction)
        length = norm / product(direction, applied)
        for a in range(len(direction)):
            result[a] = result[a] + length * direction[a]
        if step < ITERS - 1:
            padded = residual + [0.0]
            residual = [padded[a] - length * applied[a] for a in range(len(applied))]
            fresh = product(residual, residual)
            ratio = fresh / norm
            norm = fresh
            padded = direction + [0.0]
            direction = [residual[a] + ratio * padded[a] for a in range(len(residual))]
    turn_ref[...] = jnp.zeros((8, 128), jnp.float32)
    for a in range(3):
        turn_ref[a : a + 1, :] = result[a]
    turned = turn_ref[...].T[0:32]
    weight = [turned[:, a : a + 1] for a in range(3)]
    copies = []
    for j in range(5):
        result_ref[j] = (
            weight[0] * first_ref[j] + weight[1] * second_ref[j] + weight[2] * third_ref[j]
        )
        copies.append(pltpu.make_async_copy(result_ref.at[j], out_hbm.at[j], sent.at[j]))
        copies[j].start()
    for copy in copies:
        copy.wait()


def call(kernel, out_shapes, *args, smem=(), anywhere=(), scratch=(), out_space=pltpu.VMEM):
    vmem = pl.BlockSpec(memory_space=pltpu.VMEM)
    spaces = {n: pl.BlockSpec(memory_space=pltpu.SMEM) for n in smem}
    spaces |= {n: pl.BlockSpec(memory_space=pltpu.HBM) for n in anywhere}
    return pl.pallas_call(
        kernel,
        out_shape=[jax.ShapeDtypeStruct(s, jnp.float32) for s in out_shapes],
        in_specs=[spaces.get(n, vmem) for n in range(len(args))],
        out_specs=[pl.BlockSpec(memory_space=out_space)] * len(out_shapes),
        scratch_shapes=list(scratch),
        compiler_params=pltpu.CompilerParams(vmem_limit_bytes=16 * 1024 * 1024),
    )(*args)


def swap_traces(cross, chip):
    partner = [(p, (p + 1) % GRID if p % 2 else (p - 1) % GRID) for p in range(GRID)]
    chip = lax.ppermute(chip, "plane", [(p, p ^ 1) for p in range(GRID)])
    cross = lax.ppermute(cross, "plane", partner)
    return cross, chip


def on_device(state, wall_tag):
    table = wave_table()
    (packed,) = call(
        pack_kernel, [(16, 56, 128)],
        pltpu.with_memory_space_constraint(jnp.transpose(state, (1, 0, 2)), pltpu.HBM),
        anywhere=(0,),
        scratch=[
            pltpu.VMEM((800, 128), jnp.float32), pltpu.VMEM((5, 32, 640), jnp.float32),
            pltpu.VMEM((640, 640), jnp.bfloat16), pltpu.SemaphoreType.DMA(()),
        ],
    )
    modal = lax.all_to_all(packed, "span", 0, 0, tiled=True)
    trace = (40, PLANES + 512)
    field, rhs, cross, chip = call(
        volume_kernel, [(200, PLANES), (200, PLANES), trace, trace], modal, table,
        scratch=[pltpu.VMEM((16, PLANES), jnp.float32)],
    )
    cross, chip = swap_traces(cross, chip)
    (inside,) = call(inside_kernel, [(2, 256, 256)], modal, field, rhs, table)
    (sent,) = call(
        facing_kernel, [(16, 56, 128)], wall_tag, inside, field, cross, chip, table,
        smem=(0,),
        scratch=[
            pltpu.VMEM((80, PLANES), jnp.float32), pltpu.VMEM((80, PLANES), jnp.float32),
            pltpu.VMEM((2, 256, 128), jnp.float32), pltpu.VMEM((80, PLANES), jnp.float32),
        ],
    )
    load = lax.all_to_all(sent, "span", 0, 0, tiled=True)
    nodes, trace = (25, 32, 128), (4, 32, 128)
    first, joined, cross, chip = call(first_kernel, [nodes, nodes, trace, trace], load)
    cross, chip = swap_traces(cross, chip)
    second, joined, cross, chip = call(
        second_kernel, [nodes, nodes, trace, trace], joined, cross, chip, first
    )
    cross, chip = swap_traces(cross, chip)
    (packed,) = call(
        early_kernel, [(8, 128)], first, second, joined,
        scratch=[pltpu.VMEM((4, 32, 128), jnp.float32)],
    )
    third, sums = call(
        third_kernel, [nodes, (16, 8, 128)], joined, cross, chip, second, packed,
        scratch=[pltpu.VMEM((2, 32, 128), jnp.float32)],
    )
    sums = lax.all_to_all(sums, "plane", 0, 0, tiled=True)
    columns = [
        call(
            natural_kernel, [(5, 32, 640)], vector,
            scratch=[pltpu.VMEM((800, 128), jnp.float32)],
        )[0]
        for vector in (first, second, third)
    ]
    (columns,) = call(
        combine_kernel, [(5, 32, 640)], sums, *columns, out_space=pltpu.HBM,
        scratch=[
            pltpu.VMEM((8, 128), jnp.float32), pltpu.VMEM((5, 32, 640), jnp.float32),
            pltpu.SemaphoreType.DMA((5,)),
        ],
    )
    return jnp.transpose(columns, (1, 0, 2))


def solution(mesh):
    return jax.shard_map(
        on_device,
        mesh=mesh,
        in_specs=(P("span", "plane", None), P()),
        out_specs=P("span", "plane", None),
        check_vma=False,
    )
```

```python
import math

import jax
import jax.numpy as jnp
import numpy as np
from jax import lax
from jax.experimental import pallas as pl
from jax.experimental.pallas import tpu as pltpu
from jax.sharding import PartitionSpec as P


KMODES = 256
PLANES = 768
HALF = 384
ITERS = 3
GRID = 16
STEP_SIZE = 0.03
VISCOUS = 0.05
SPAN_STIFF = 4.0


def gll_tables():
    abscissae = np.array([-1.0, -math.sqrt(3.0 / 7.0), 0.0, math.sqrt(3.0 / 7.0), 1.0])
    weights = np.array([0.1, 49.0 / 90.0, 32.0 / 45.0, 49.0 / 90.0, 0.1])
    squared = abscissae * abscissae
    legendre = (35.0 * squared * squared - 30.0 * squared + 3.0) / 8.0
    identity = np.eye(5)
    spacing = abscissae[:, None] - abscissae[None, :] + identity
    differ = np.where(identity > 0, 0.0, legendre[:, None] / legendre[None, :] / spacing)
    differ[0, 0] = -5.0
    differ[4, 4] = 5.0
    stiffness = differ.T @ (weights[:, None] * differ)
    return differ, weights, stiffness


DIFFER, WEIGHTS, STIFFNESS = gll_tables()


def split_table(table):
    high = table.astype(np.float32).astype(jnp.bfloat16)
    low = (table - high.astype(np.float64)).astype(np.float32).astype(jnp.bfloat16)
    return jnp.asarray(np.stack([high, low]))


def wave_table():
    plane = np.arange(HALF)
    waves = []
    for parity in range(2):
        k = 2 * np.arange(128) + parity
        angle = (k[:, None] * plane[None, :] % PLANES) * (2.0 * math.pi / PLANES)
        waves.append(np.concatenate([np.cos(angle), np.sin(angle)]))
    return split_table(np.stack(waves))


def dot(left, right, contract):
    return lax.dot_general(
        left, right, (contract, ((), ())), preferred_element_type=jnp.float32
    )


def halves(value):
    high = value.astype(jnp.bfloat16)
    low = (value - high.astype(jnp.float32)).astype(jnp.bfloat16)
    return high, low


def dot_split(left, right, contract):
    (left_high, left_low), (right_high, right_low) = left, right
    return (
        dot(left_high, right_low, contract)
        + dot(left_low, right_high, contract)
        + dot(left_high, right_high, contract)
    )


def lanes_of(values, index):
    return jnp.take_along_axis(values, index, axis=1)


def merge_columns(tiles):
    lane = lax.broadcasted_iota(jnp.int32, tiles[0].shape, 1)
    out = []
    for t in range(5):
        column = lane + 128 * t
        element = (column * 13108) >> 16
        node = column - 5 * element
        picked = lanes_of(tiles[0], element)
        for i in range(1, 5):
            picked = jnp.where(node == i, lanes_of(tiles[i], element), picked)
        out.append(picked)
    return out


def exchange_chunks(values):
    values = list(values)
    lane = lax.broadcasted_iota(jnp.int32, values[0].shape, 1)
    for bit in (1, 2, 4, 8):
        upper = (lane & (8 * bit)) != 0
        other = lane ^ (8 * bit)
        for a in range(16):
            if a & bit == 0:
                first, second = values[a], values[a | bit]
                moved = jnp.where(upper, first, second)
                if bit == 8:
                    moved = pltpu.roll(moved, 64, 1)
                else:
                    moved = lanes_of(moved, other)
                values[a] = jnp.where(upper, moved, first)
                values[a | bit] = jnp.where(upper, second, moved)
    return values


def column_order():
    column = lax.broadcasted_iota(jnp.int32, (640, 128), 0)
    element = lax.broadcasted_iota(jnp.int32, (640, 128), 1)
    tiles = [jnp.where(column == 5 * element + i, 1.0, 0.0).astype(jnp.bfloat16) for i in range(5)]
    return jnp.concatenate(tiles, axis=1)


def pack_rows(out_ref, d, whole, rest, count):
    out_ref[d, 0:32, :] = whole
    lane = lax.broadcasted_iota(jnp.int32, (8, 128), 1)
    free = 16 - count
    for g in range(3):
        tile = rest[8 * g : 8 * g + 8]
        if g * free < count:
            shift = 8 * (count - g * free)
            tile = jnp.where(lane < 8 * count, tile, pltpu.roll(rest[24:32], shift % 128, 1))
        out_ref[d, 32 + 8 * g : 40 + 8 * g, :] = tile


def unpack_last(tiles, count):
    lane = lax.broadcasted_iota(jnp.int32, (8, 128), 1)
    free = 16 - count
    last = pltpu.roll(tiles[0], 128 - 8 * count, 1)
    for g in range(1, 3):
        if g * free < count:
            shift = 8 * (count - g * free)
            last = jnp.where(lane < 8 * g * free, last, pltpu.roll(tiles[g], (128 - shift) % 128, 1))
    return last


def pack_kernel(state_hbm, out_ref, chunk_ref, state_ref, order_ref, arrived):
    copy = pltpu.make_async_copy(state_hbm, state_ref, arrived)
    copy.start()
    order_ref[...] = column_order()
    copy.wait()
    stacked = jnp.concatenate([state_ref[j] for j in range(5)], axis=0)
    order = order_ref[...]
    contract = ((1,), (0,))
    high, low = halves(stacked)
    nodes = dot(low, order, contract) + dot(high, order, contract)
    for i in range(5):
        chunk_ref[160 * i : 160 * i + 160, :] = nodes[:, 128 * i : 128 * i + 128]
    chunk = [
        jnp.concatenate(
            [chunk_ref[pl.ds(160 * i + 32 * j + t, 8, stride=4), :] for t in range(4)], axis=0
        )
        for j in range(5)
        for i in range(5)
    ]
    lane = lax.broadcasted_iota(jnp.int32, (32, 128), 1) & 7
    sides = [jnp.zeros((32, 128), jnp.float32), jnp.zeros((32, 128), jnp.float32)]
    for j in range(5):
        at = j & 3
        side = jnp.where(lane == at, pltpu.roll(chunk[j * 5 + 4], 1 + at, 1), sides[j // 4])
        sides[j // 4] = jnp.where(lane == 7 - at, pltpu.roll(chunk[j * 5], 127 - at, 1), side)
    chunk = chunk + sides
    whole = exchange_chunks(chunk[:16])
    rest = exchange_chunks(chunk[16:] + [jnp.zeros((32, 128), jnp.float32)] * 5)
    for d in range(GRID):
        pack_rows(out_ref, d, whole[d], rest[d], 11)


def turn(modal_ref, cross_ref, chip_ref):
    last = [
        unpack_last([modal_ref[s, 32 + 8 * g : 40 + 8 * g, :] for g in range(3)], 11)
        for s in range(GRID)
    ]
    nodal = []
    for parity in range(2):
        whole, rest = [], []
        for t in range(2):
            group = 2 * parity + t
            for s in range(GRID):
                whole.append(modal_ref[s, 8 * group : 8 * group + 8, :])
                rest.append(
                    last[s] if group == 3 else modal_ref[s, 32 + 8 * group : 40 + 8 * group, :]
                )
        turned = [jnp.concatenate(part, axis=0).T for part in (whole, rest)]
        nodal.append(jnp.concatenate([turned[0], turned[1][0:88]], axis=0))
        cross_ref[parity], chip_ref[parity] = to_partners(turned[0][0:40], turned[1][32:72])
    return nodal


def synthesize(nodal, table_ref):
    part = [
        dot_split(
            halves(nodal[parity]), (table_ref[0, parity], table_ref[1, parity]), ((1,), (0,))
        )
        for parity in range(2)
    ]
    scale = 1.0 / math.sqrt(KMODES)
    return scale * (part[0] + part[1]), scale * (part[0] - part[1])


def two_point(left, right):
    mean = (left * left + left * right + right * right) * (1.0 / 6.0)
    speed = jnp.maximum(jnp.abs(left), jnp.abs(right))
    return mean - 0.5 * speed * (right - left)


def row_rhs(field_ref, side_ref, lanes, rows):
    row = lax.broadcasted_iota(jnp.int32, (8, 128), 0)
    f = [field_ref[8 * n : 8 * n + 8, lanes] for n in range(25)]
    square = [v * v for v in f]
    out = {}
    for j in rows:
        for i in range(5):
            n = j * 5 + i
            plain = None
            power = None
            for other in range(5):
                terms = [(DIFFER[i][other], j * 5 + other), (DIFFER[j][other], other * 5 + i)]
                for weight, m in terms:
                    if weight == 0.0:
                        continue
                    weight = float(weight) / -3.0
                    plain = weight * f[m] if plain is None else plain + weight * f[m]
                    power = weight * square[m] if power is None else power + weight * square[m]
            total = power + f[n] * plain
            own = (i == 4) + (j == 4) - (i == 0) - (j == 0)
            if own:
                total = total + (5.0 * own) * square[n]
            if i == 0 or i == 4:
                at = j & 3
                side = side_ref[8 * (j // 4) : 8 * (j // 4) + 8, lanes]
                if at:
                    side = pltpu.roll(side, 8 - at if i == 0 else at, 0)
                if i == 0:
                    left = jnp.where(row == 0, side, pltpu.roll(f[j * 5 + 4], 1, 0))
                    total = total + 10.0 * two_point(left, f[n])
                else:
                    right = jnp.where(row == 7, side, pltpu.roll(f[j * 5], 7, 0))
                    total = total - 10.0 * two_point(f[n], right)
            out[n] = total
    return out


def each_lane_block(body):
    def step(block, carry):
        body(pl.ds(pl.multiple_of(block * 128, 128), 128))
        return carry

    lax.fori_loop(0, PLANES // 128, step, 0)


def volume_kernel(
    modal_ref, table_ref, field_ref, side_ref, edge_ref, modal_cross_ref, modal_chip_ref, cross_ref,
    chip_ref,
):
    nodal = turn(modal_ref, modal_cross_ref, modal_chip_ref)
    pair = synthesize(nodal, table_ref)
    for q in range(2):
        field_ref[:, HALF * q : HALF * q + HALF] = pair[q][0:200]
        side_ref[:, HALF * q : HALF * q + HALF] = pair[q][200:216]

    def body(lanes):
        total = row_rhs(field_ref, side_ref, lanes, (0, 4))
        for i in range(5):
            rows = slice(8 * i, 8 * i + 8)
            edge_ref[rows, lanes] = total[i]
            edge_ref[40 + 8 * i : 48 + 8 * i, lanes] = total[20 + i]
            cross_ref[rows, lanes], chip_ref[rows, lanes] = to_partners(total[i], total[20 + i])

    each_lane_block(body)


def project(planar, parity, table_ref):
    folded = planar[:, :HALF] + planar[:, HALF:] if parity == 0 else planar[:, :HALF] - planar[:, HALF:]
    return dot_split((table_ref[0, parity], table_ref[1, parity]), halves(folded), ((1,), (1,)))


def tendency(parity, from_rhs, from_flux):
    k = 2 * lax.broadcasted_iota(jnp.int32, (128, 128), 0) + parity
    scale = jnp.where(k == 0, 1.0, 2.0) * (math.sqrt(KMODES) / PLANES * STEP_SIZE)
    ratio = k.astype(jnp.float32) * (1.0 / KMODES)
    return (
        scale * (from_rhs[0:128] - ratio * from_flux[128:256]),
        scale * (from_rhs[128:256] + ratio * from_flux[0:128]),
    )


def inside_kernel(modal_ref, field_ref, side_ref, edge_ref, table_ref, out_ref, rhs_ref):
    last = [
        unpack_last([modal_ref[s, 32 + 8 * g : 40 + 8 * g, :] for g in range(3)], 11)
        for s in range(GRID)
    ]

    def body(lanes):
        total = row_rhs(field_ref, side_ref, lanes, (1, 2, 3))
        for n in range(5, 20):
            rhs_ref[8 * n - 40 : 8 * n - 32, lanes] = total[n]

    each_lane_block(body)
    field = field_ref[...]
    flux = 0.5 * field * field
    rhs = jnp.concatenate([edge_ref[0:40, :], rhs_ref[...], edge_ref[40:80, :]], axis=0)
    tail = jnp.zeros((56, PLANES), jnp.float32)
    flux = jnp.concatenate([flux, tail], axis=0)
    rhs = jnp.concatenate([rhs, tail], axis=0)
    for parity in range(2):
        from_rhs = project(rhs, parity, table_ref)
        from_flux = project(flux, parity, table_ref)
        for half in range(2):
            lanes = slice(128 * half, 128 * half + 128)
            change = tendency(parity, from_rhs[:, lanes], from_flux[:, lanes])
            for t in range(2):
                first = 16 * parity + 8 * t + 32 * half
                modal = jnp.concatenate(
                    last if first == 56 else [modal_ref[s, first : first + 8, :] for s in range(GRID)],
                    axis=0,
                )
                out_ref[parity, 128 * t : 128 * t + 128, lanes] = modal + change[t]


def lift_kernel(
    tag_ref, field_ref, cross_ref, chip_ref, table_ref, lift_ref, flux_ref, modal_ref, outer_ref
):
    bottom, top = at_ends()
    span = lax.axis_index("span")
    row = lax.broadcasted_iota(jnp.int32, (8, 128), 0)
    mirror = jnp.ones((8, 128), jnp.float32)
    for e in range(8):
        mirror = jnp.where((row == e) & (tag_ref[8 * span + e] == 1), -1.0, mirror)
    keep_lower = jnp.where(bottom, 0.0, 1.0)
    keep_upper = jnp.where(top, 0.0, 1.0)
    gap = jnp.zeros((48, 256), jnp.float32)
    outer = []
    for parity in range(2):
        below, above = from_partners(cross_ref[parity], chip_ref[parity])
        outer.append(jnp.concatenate([below, above], axis=0))
        modal_ref[parity] = jnp.concatenate(
            [keep_lower * below, keep_upper * above, gap], axis=0
        ).T
    pair = synthesize(outer, table_ref)
    for q in range(2):
        outer_ref[:, HALF * q : HALF * q + HALF] = pair[q]
    mirror = jnp.concatenate([mirror] * 6, axis=1)
    mirror = jnp.concatenate([mirror] * 5, axis=0)
    inside = field_ref[0:40, :]
    below = outer_ref[0:40, :]
    lift_ref[0:40, :] = 10.0 * two_point(jnp.where(bottom, mirror * inside, below), inside)
    flux_ref[0:40, :] = keep_lower * (0.5 * below * below)
    inside = field_ref[160:200, :]
    above = outer_ref[40:80, :]
    lift_ref[40:80, :] = 10.0 * two_point(inside, jnp.where(top, inside, above))
    flux_ref[40:80, :] = keep_upper * (0.5 * above * above)


def facing_kernel(
    inside_ref, lift_ref, flux_ref, facing_ref, cross_ref, chip_ref, table_ref, out_ref
):
    bottom, top = at_ends()
    below, above = from_partners(cross_ref[...], chip_ref[...])
    lift = lift_ref[0:40, :]
    rhs_lower = lift + jnp.where(bottom, 0.0, below - lift)
    lift = lift_ref[40:80, :]
    rhs_upper = jnp.where(top, 0.0, above + lift) - lift
    gap = jnp.zeros((48, PLANES), jnp.float32)
    planar = jnp.concatenate([rhs_lower, rhs_upper, gap, flux_ref[...], gap], axis=0)
    lane = lax.broadcasted_iota(jnp.int32, (128, 128), 1)
    whole, rest = [], []
    for parity in range(2):
        projected = project(planar, parity, table_ref)
        change = tendency(parity, projected[:, 0:128], projected[:, 128:256])
        for t in range(2):
            rows = slice(128 * t, 128 * t + 128)
            extra = change[t] + facing_ref[parity, rows, :]
            lower = jnp.where(lane < 40, extra, 0.0)
            upper = pltpu.roll(jnp.where(lane < 40, 0.0, extra), 120, 1)
            whole.append(inside_ref[parity, rows, 0:128] + lower)
            rest.append(inside_ref[parity, rows, 128:256] + upper)
    for s in range(GRID):
        part = slice(8 * s, 8 * s + 8)
        pack_rows(
            out_ref,
            s,
            jnp.concatenate([group[part] for group in whole], axis=0),
            jnp.concatenate([group[part] for group in rest], axis=0),
            9,
        )


def energy(values, shift):
    total = None
    for j in range(5):
        for i in range(5):
            n = j * 5 + i
            mass = float(WEIGHTS[j] * WEIGHTS[i])
            diagonal = VISCOUS * float(WEIGHTS[j] * STIFFNESS[i][i] + WEIGHTS[i] * STIFFNESS[j][j])
            value = (shift * mass + diagonal) * values[n]
            for other in range(i + 1, 5):
                weight = 2.0 * VISCOUS * float(WEIGHTS[j] * STIFFNESS[i][other])
                value = value + weight * values[j * 5 + other]
            for other in range(j + 1, 5):
                weight = 2.0 * VISCOUS * float(WEIGHTS[i] * STIFFNESS[j][other])
                value = value + weight * values[other * 5 + i]
            term = value * values[n]
            total = term if total is None else total + term
    return total


def at_ends():
    plane = lax.axis_index("plane")
    return plane == 0, plane == GRID - 1


def to_partners(low, high):
    odd = lax.axis_index("plane") % 2 == 1
    return jnp.where(odd, high, low), jnp.where(odd, low, high)


def from_partners(cross, chip):
    odd = lax.axis_index("plane") % 2 == 1
    return jnp.where(odd, chip, cross), jnp.where(odd, cross, chip)


def local_operator(values, shift):
    out = []
    for j in range(5):
        for i in range(5):
            n = j * 5 + i
            mass = float(WEIGHTS[j] * WEIGHTS[i])
            diagonal = VISCOUS * float(WEIGHTS[j] * STIFFNESS[i][i] + WEIGHTS[i] * STIFFNESS[j][j])
            value = (shift * mass + diagonal) * values[n]
            for other in range(5):
                if other != i:
                    weight = VISCOUS * float(WEIGHTS[j] * STIFFNESS[i][other])
                    value = value + weight * values[j * 5 + other]
                if other != j:
                    weight = VISCOUS * float(WEIGHTS[i] * STIFFNESS[j][other])
                    value = value + weight * values[other * 5 + i]
            out.append(value)
    return out


def join_columns(values):
    values = list(values)
    for j in range(5):
        joint = values[j * 5 + 4] + pltpu.roll(values[j * 5], 127, 1)
        values[j * 5 + 4] = joint
        values[j * 5] = pltpu.roll(joint, 1, 1)
    return values


def store_joined(values, joined_ref, cross_ref, chip_ref):
    values = join_columns(values)
    for n in range(25):
        joined_ref[n] = values[n]
    for i in range(4):
        cross_ref[i], chip_ref[i] = to_partners(values[i], values[20 + i])


def assembled(joined_ref, cross_ref, chip_ref):
    values = [joined_ref[n] for n in range(25)]
    bottom, top = at_ends()
    for i in range(4):
        below, above = from_partners(cross_ref[i], chip_ref[i])
        values[i] = values[i] + jnp.where(bottom, 0.0, below)
        values[20 + i] = values[20 + i] + jnp.where(top, 0.0, above)
    values[4] = pltpu.roll(values[0], 127, 1)
    values[24] = pltpu.roll(values[20], 127, 1)
    return values


def mode_terms():
    row = lax.broadcasted_iota(jnp.int32, (32, 128), 0)
    mode_pair = 16 * lax.axis_index("span") + 2 * (row & 7) + (row >> 4)
    ratio = mode_pair.astype(jnp.float32) * (1.0 / KMODES)
    shift = 1.0 + SPAN_STIFF * ratio * ratio
    return shift, 0.2 * shift + 0.15


def inner(left, right):
    bottom, top = at_ends()
    total = None
    for j in range(5):
        part = None
        for i in range(5):
            term = left[j * 5 + i] * right[j * 5 + i]
            term = term if 0 < i < 4 else 0.5 * term
            part = term if part is None else part + term
        if j == 0:
            part = jnp.where(bottom, 1.0, 0.5) * part
        elif j == 4:
            part = jnp.where(top, 1.0, 0.5) * part
        total = part if total is None else total + part
    return total


def first_kernel(modal_ref, vector_ref, next_ref, cross_ref, chip_ref):
    shift, _ = mode_terms()
    values = exchange_chunks([modal_ref[s, 0:32, :] for s in range(GRID)])
    rest = []
    for s in range(GRID):
        tiles = [modal_ref[s, 32 + 8 * g : 40 + 8 * g, :] for g in range(3)]
        rest.append(jnp.concatenate(tiles + [unpack_last(tiles, 9)], axis=0))
    values += exchange_chunks(rest)
    values = [float(WEIGHTS[n // 5] * WEIGHTS[n % 5]) * values[n] for n in range(25)]
    vector = join_columns(values)
    for n in range(25):
        vector_ref[n] = vector[n]
    store_joined(local_operator(vector, shift), next_ref, cross_ref, chip_ref)


def second_kernel(
    joined_ref, cross_in_ref, chip_in_ref, before_ref, vector_ref, next_ref, cross_ref, chip_ref
):
    shift, center = mode_terms()
    applied = assembled(joined_ref, cross_in_ref, chip_in_ref)
    vector = [applied[n] - center * before_ref[n] for n in range(25)]
    for n in range(25):
        vector_ref[n] = vector[n]
    store_joined(local_operator(vector, shift), next_ref, cross_ref, chip_ref)


def mode_sums(moment, turn_ref):
    for t in range(4):
        turn_ref[pl.ds(t, 8, stride=4), :] = moment[8 * t : 8 * t + 8]
    return jnp.sum(turn_ref[...].T, axis=0, keepdims=True)


def early_kernel(first_ref, second_ref, joined_ref, packed_ref, turn_ref):
    _, center = mode_terms()
    first = [first_ref[n] for n in range(25)]
    second = [second_ref[n] for n in range(25)]
    square = inner(second, second)
    product = None
    for n in range(25):
        term = second[n] * joined_ref[n]
        term = term if 0 < n % 5 < 4 else 0.5 * term
        product = term if product is None else product + term
    moments = [inner(first, first), inner(first, second), square, product - center * square]
    packed_ref[...] = jnp.zeros((8, 128), jnp.float32)
    for n, moment in enumerate(moments):
        packed_ref[n : n + 1, 0:32] = mode_sums(moment, turn_ref.at[n])


def third_kernel(
    joined_ref, cross_in_ref, chip_in_ref, second_ref, packed_ref, vector_ref, sums_ref,
    turn_ref,
):
    shift, center = mode_terms()
    applied = assembled(joined_ref, cross_in_ref, chip_in_ref)
    second = [second_ref[n] for n in range(25)]
    third = [applied[n] - center * second[n] for n in range(25)]
    for n in range(25):
        vector_ref[n] = third[n]
    fourth = inner(third, third)
    moments = [fourth, energy(third, shift) - center * fourth]
    sums_ref[0] = packed_ref[...]
    for n, moment in enumerate(moments):
        sums_ref[0, 4 + n : 5 + n, 0:32] = mode_sums(moment, turn_ref.at[n])
    sums = sums_ref[0]
    for p in range(1, GRID):
        sums_ref[p] = sums


def natural_kernel(vector_ref, out_ref, column_ref):
    for j in range(5):
        tiles = merge_columns([vector_ref[j * 5 + i] for i in range(5)])
        for i in range(5):
            first = 32 * (5 * j + i)
            for t in range(4):
                column_ref[pl.ds(first + t, 8, stride=4), :] = tiles[i][8 * t : 8 * t + 8]
            out_ref[j, :, 128 * i : 128 * i + 128] = column_ref[first : first + 32, :]


def tree(terms):
    while len(terms) > 1:
        terms = [sum(terms[n + 1 : n + 2], terms[n]) for n in range(0, len(terms), 2)]
    return terms[0]


def combine_kernel(
    sums_ref, first_ref, second_ref, third_ref, out_hbm, turn_ref, result_ref, sent
):
    total = tree([sums_ref[p] for p in range(GRID)])
    moment = [total[n : n + 1] for n in range(6)]
    lane = lax.broadcasted_iota(jnp.int32, (1, 128), 1)
    mode_pair = 16 * lax.axis_index("span") + (lane >> 1)
    ratio = mode_pair.astype(jnp.float32) * (1.0 / KMODES)
    center = 0.2 * (1.0 + SPAN_STIFF * ratio * ratio) + 0.15

    def product(left, right):
        return tree(
            [
                tree(
                    [
                        left[a] * right[power - a]
                        for a in range(len(left))
                        if 0 <= power - a < len(right)
                    ]
                )
                * moment[power]
                for power in range(len(left) + len(right) - 1)
            ]
        )

    def operator(c):
        shifted = [center * v for v in c] + [0.0]
        return [shifted[0]] + [shifted[a + 1] + c[a] for a in range(len(c))]

    residual = [jnp.ones((1, 128), jnp.float32)]
    direction = residual
    result = [0.0, 0.0, 0.0]
    norm = moment[0]
    for step in range(ITERS):
        applied = operator(direction)
        length = norm / product(direction, applied)
        for a in range(len(direction)):
            result[a] = result[a] + length * direction[a]
        if step < ITERS - 1:
            padded = residual + [0.0]
            residual = [padded[a] - length * applied[a] for a in range(len(applied))]
            fresh = product(residual, residual)
            ratio = fresh / norm
            norm = fresh
            padded = direction + [0.0]
            direction = [residual[a] + ratio * padded[a] for a in range(len(residual))]
    turn_ref[...] = jnp.zeros((8, 128), jnp.float32)
    for a in range(3):
        turn_ref[a : a + 1, :] = result[a]
    turned = turn_ref[...].T[0:32]
    weight = [turned[:, a : a + 1] for a in range(3)]
    copies = []
    for j in range(5):
        result_ref[j] = (
            weight[0] * first_ref[j] + weight[1] * second_ref[j] + weight[2] * third_ref[j]
        )
        copies.append(pltpu.make_async_copy(result_ref.at[j], out_hbm.at[j], sent.at[j]))
        copies[j].start()
    for copy in copies:
        copy.wait()


def call(kernel, out_shapes, *args, smem=(), anywhere=(), scratch=(), out_space=pltpu.VMEM, covers=True):
    vmem = pl.BlockSpec(memory_space=pltpu.VMEM)
    spaces = {n: pl.BlockSpec(memory_space=pltpu.SMEM) for n in smem}
    spaces |= {n: pl.BlockSpec(memory_space=pltpu.HBM) for n in anywhere}
    return pl.pallas_call(
        kernel,
        out_shape=[jax.ShapeDtypeStruct(s, jnp.float32) for s in out_shapes],
        in_specs=[spaces.get(n, vmem) for n in range(len(args))],
        out_specs=[pl.BlockSpec(memory_space=out_space)] * len(out_shapes),
        scratch_shapes=list(scratch),
        cost_estimate=None if covers else pl.CostEstimate(flops=0, bytes_accessed=0, transcendentals=0),
        compiler_params=pltpu.CompilerParams(vmem_limit_bytes=16 * 1024 * 1024),
    )(*args)


def swap_traces(cross, chip):
    partner = [(p, (p + 1) % GRID if p % 2 else (p - 1) % GRID) for p in range(GRID)]
    chip = lax.ppermute(chip, "plane", [(p, p ^ 1) for p in range(GRID)])
    cross = lax.ppermute(cross, "plane", partner)
    return cross, chip


def on_device(state, wall_tag):
    table = wave_table()
    (packed,) = call(
        pack_kernel, [(16, 56, 128)],
        pltpu.with_memory_space_constraint(jnp.transpose(state, (1, 0, 2)), pltpu.HBM),
        anywhere=(0,),
        scratch=[
            pltpu.VMEM((800, 128), jnp.float32), pltpu.VMEM((5, 32, 640), jnp.float32),
            pltpu.VMEM((640, 640), jnp.bfloat16), pltpu.SemaphoreType.DMA(()),
        ],
    )
    modal = lax.all_to_all(packed, "span", 0, 0, tiled=True)
    trace, rows = (2, 40, 256), (40, PLANES)
    field, side, edge, *modal_traces, cross, chip = call(
        volume_kernel,
        [(200, PLANES), (16, PLANES), (80, PLANES), trace, trace, rows, rows], modal, table,
    )
    modal_traces = swap_traces(*modal_traces)
    rhs_traces = swap_traces(cross, chip)
    (inside,) = call(
        inside_kernel, [(2, 256, 256)], modal, field, side, edge, table, covers=False,
        scratch=[pltpu.VMEM((120, PLANES), jnp.float32)],
    )
    lift, flux, facing = call(
        lift_kernel, [(80, PLANES), (80, PLANES), (2, 256, 128)], wall_tag, field,
        *modal_traces, table, smem=(0,), scratch=[pltpu.VMEM((80, PLANES), jnp.float32)],
        covers=False,
    )
    (sent,) = call(facing_kernel, [(16, 56, 128)], inside, lift, flux, facing, *rhs_traces, table)
    load = lax.all_to_all(sent, "span", 0, 0, tiled=True)
    nodes, trace = (25, 32, 128), (4, 32, 128)
    first, joined, cross, chip = call(first_kernel, [nodes, nodes, trace, trace], load)
    cross, chip = swap_traces(cross, chip)
    second, joined, cross, chip = call(
        second_kernel, [nodes, nodes, trace, trace], joined, cross, chip, first
    )
    cross, chip = swap_traces(cross, chip)
    (packed,) = call(
        early_kernel, [(8, 128)], first, second, joined,
        scratch=[pltpu.VMEM((4, 32, 128), jnp.float32)],
    )
    third, sums = call(
        third_kernel, [nodes, (16, 8, 128)], joined, cross, chip, second, packed,
        scratch=[pltpu.VMEM((2, 32, 128), jnp.float32)],
    )
    sums = lax.all_to_all(sums, "plane", 0, 0, tiled=True)
    columns = [
        call(
            natural_kernel, [(5, 32, 640)], vector,
            scratch=[pltpu.VMEM((800, 128), jnp.float32)],
        )[0]
        for vector in (first, second, third)
    ]
    (columns,) = call(
        combine_kernel, [(5, 32, 640)], sums, *columns, out_space=pltpu.HBM,
        scratch=[
            pltpu.VMEM((8, 128), jnp.float32), pltpu.VMEM((5, 32, 640), jnp.float32),
            pltpu.SemaphoreType.DMA((5,)),
        ],
    )
    return jnp.transpose(columns, (1, 0, 2))


def solution(mesh):
    return jax.shard_map(
        on_device,
        mesh=mesh,
        in_specs=(P("span", "plane", None), P()),
        out_specs=P("span", "plane", None),
        check_vma=False,
    )
```

```python
import math

import jax
import jax.numpy as jnp
import numpy as np
from jax import lax
from jax.experimental import pallas as pl
from jax.experimental.pallas import tpu as pltpu
from jax.sharding import PartitionSpec as P


KMODES = 256
PLANES = 768
HALF = 384
ITERS = 3
GRID = 16
STEP_SIZE = 0.03
VISCOUS = 0.05
SPAN_STIFF = 4.0


def gll_tables():
    abscissae = np.array([-1.0, -math.sqrt(3.0 / 7.0), 0.0, math.sqrt(3.0 / 7.0), 1.0])
    weights = np.array([0.1, 49.0 / 90.0, 32.0 / 45.0, 49.0 / 90.0, 0.1])
    squared = abscissae * abscissae
    legendre = (35.0 * squared * squared - 30.0 * squared + 3.0) / 8.0
    identity = np.eye(5)
    spacing = abscissae[:, None] - abscissae[None, :] + identity
    differ = np.where(identity > 0, 0.0, legendre[:, None] / legendre[None, :] / spacing)
    differ[0, 0] = -5.0
    differ[4, 4] = 5.0
    stiffness = differ.T @ (weights[:, None] * differ)
    return differ, weights, stiffness


DIFFER, WEIGHTS, STIFFNESS = gll_tables()


def split_table(table):
    high = table.astype(np.float32).astype(jnp.bfloat16)
    low = (table - high.astype(np.float64)).astype(np.float32).astype(jnp.bfloat16)
    return jnp.asarray(np.stack([high, low]))


def wave_table():
    plane = np.arange(HALF)
    waves = []
    for parity in range(2):
        k = 2 * np.arange(128) + parity
        angle = (k[:, None] * plane[None, :] % PLANES) * (2.0 * math.pi / PLANES)
        waves.append(np.concatenate([np.cos(angle), np.sin(angle)]))
    return split_table(np.stack(waves))


def dot(left, right, contract):
    return lax.dot_general(
        left, right, (contract, ((), ())), preferred_element_type=jnp.float32
    )


def halves(value):
    high = value.astype(jnp.bfloat16)
    low = (value - high.astype(jnp.float32)).astype(jnp.bfloat16)
    return high, low


def dot_split(left, right, contract):
    (left_high, left_low), (right_high, right_low) = left, right
    return (
        dot(left_high, right_low, contract)
        + dot(left_low, right_high, contract)
        + dot(left_high, right_high, contract)
    )


def lanes_of(values, index):
    return jnp.take_along_axis(values, index, axis=1)


def merge_columns(tiles):
    lane = lax.broadcasted_iota(jnp.int32, tiles[0].shape, 1)
    out = []
    for t in range(5):
        column = lane + 128 * t
        element = (column * 13108) >> 16
        node = column - 5 * element
        picked = lanes_of(tiles[0], element)
        for i in range(1, 5):
            picked = jnp.where(node == i, lanes_of(tiles[i], element), picked)
        out.append(picked)
    return out


def exchange_chunks(values):
    values = list(values)
    lane = lax.broadcasted_iota(jnp.int32, values[0].shape, 1)
    for bit in (1, 2, 4, 8):
        upper = (lane & (8 * bit)) != 0
        other = lane ^ (8 * bit)
        for a in range(16):
            if a & bit == 0:
                first, second = values[a], values[a | bit]
                moved = jnp.where(upper, first, second)
                if bit == 8:
                    moved = pltpu.roll(moved, 64, 1)
                else:
                    moved = lanes_of(moved, other)
                values[a] = jnp.where(upper, moved, first)
                values[a | bit] = jnp.where(upper, second, moved)
    return values


def column_order():
    column = lax.broadcasted_iota(jnp.int32, (640, 128), 0)
    element = lax.broadcasted_iota(jnp.int32, (640, 128), 1)
    tiles = [jnp.where(column == 5 * element + i, 1.0, 0.0).astype(jnp.bfloat16) for i in range(5)]
    return jnp.concatenate(tiles, axis=1)


def pack_rows(out_ref, d, whole, rest, count):
    out_ref[d, 0:32, :] = whole
    lane = lax.broadcasted_iota(jnp.int32, (8, 128), 1)
    free = 16 - count
    for g in range(3):
        tile = rest[8 * g : 8 * g + 8]
        if g * free < count:
            shift = 8 * (count - g * free)
            tile = jnp.where(lane < 8 * count, tile, pltpu.roll(rest[24:32], shift % 128, 1))
        out_ref[d, 32 + 8 * g : 40 + 8 * g, :] = tile


def unpack_last(tiles, count):
    lane = lax.broadcasted_iota(jnp.int32, (8, 128), 1)
    free = 16 - count
    last = pltpu.roll(tiles[0], 128 - 8 * count, 1)
    for g in range(1, 3):
        if g * free < count:
            shift = 8 * (count - g * free)
            last = jnp.where(lane < 8 * g * free, last, pltpu.roll(tiles[g], (128 - shift) % 128, 1))
    return last


def pack_kernel(state_hbm, out_ref, chunk_ref, state_ref, order_ref, arrived):
    copy = pltpu.make_async_copy(state_hbm, state_ref, arrived)
    copy.start()
    order_ref[...] = column_order()
    copy.wait()
    stacked = jnp.concatenate([state_ref[j] for j in range(5)], axis=0)
    order = order_ref[...]
    contract = ((1,), (0,))
    high, low = halves(stacked)
    nodes = dot(low, order, contract) + dot(high, order, contract)
    for i in range(5):
        chunk_ref[160 * i : 160 * i + 160, :] = nodes[:, 128 * i : 128 * i + 128]
    chunk = [
        jnp.concatenate(
            [chunk_ref[pl.ds(160 * i + 32 * j + t, 8, stride=4), :] for t in range(4)], axis=0
        )
        for j in range(5)
        for i in range(5)
    ]
    lane = lax.broadcasted_iota(jnp.int32, (32, 128), 1) & 7
    sides = [jnp.zeros((32, 128), jnp.float32), jnp.zeros((32, 128), jnp.float32)]
    for j in range(5):
        at = j & 3
        side = jnp.where(lane == at, pltpu.roll(chunk[j * 5 + 4], 1 + at, 1), sides[j // 4])
        sides[j // 4] = jnp.where(lane == 7 - at, pltpu.roll(chunk[j * 5], 127 - at, 1), side)
    chunk = chunk + sides
    whole = exchange_chunks(chunk[:16])
    rest = exchange_chunks(chunk[16:] + [jnp.zeros((32, 128), jnp.float32)] * 5)
    for d in range(GRID):
        pack_rows(out_ref, d, whole[d], rest[d], 11)


def turn(modal_ref, cross_ref, chip_ref):
    last = [
        unpack_last([modal_ref[s, 32 + 8 * g : 40 + 8 * g, :] for g in range(3)], 11)
        for s in range(GRID)
    ]
    nodal = []
    for parity in range(2):
        whole, rest = [], []
        for t in range(2):
            group = 2 * parity + t
            for s in range(GRID):
                whole.append(modal_ref[s, 8 * group : 8 * group + 8, :])
                rest.append(
                    last[s] if group == 3 else modal_ref[s, 32 + 8 * group : 40 + 8 * group, :]
                )
        turned = [jnp.concatenate(part, axis=0).T for part in (whole, rest)]
        nodal.append(jnp.concatenate([turned[0], turned[1][0:88]], axis=0))
        cross_ref[parity], chip_ref[parity] = to_partners(turned[0][0:40], turned[1][32:72])
    return nodal


def synthesize(nodal, table_ref):
    part = [
        dot_split(
            halves(nodal[parity]), (table_ref[0, parity], table_ref[1, parity]), ((1,), (0,))
        )
        for parity in range(2)
    ]
    scale = 1.0 / math.sqrt(KMODES)
    return scale * (part[0] + part[1]), scale * (part[0] - part[1])


def two_point(left, right):
    mean = (left * left + left * right + right * right) * (1.0 / 6.0)
    speed = jnp.maximum(jnp.abs(left), jnp.abs(right))
    return mean - 0.5 * speed * (right - left)


def row_rhs(field_ref, side_ref, lanes, rows):
    row = lax.broadcasted_iota(jnp.int32, (8, 128), 0)
    f = [field_ref[8 * n : 8 * n + 8, lanes] for n in range(25)]
    square = [v * v for v in f]
    out = {}
    for j in rows:
        for i in range(5):
            n = j * 5 + i
            plain = None
            power = None
            for other in range(5):
                terms = [(DIFFER[i][other], j * 5 + other), (DIFFER[j][other], other * 5 + i)]
                for weight, m in terms:
                    if weight == 0.0:
                        continue
                    weight = float(weight) / -3.0
                    plain = weight * f[m] if plain is None else plain + weight * f[m]
                    power = weight * square[m] if power is None else power + weight * square[m]
            total = power + f[n] * plain
            own = (i == 4) + (j == 4) - (i == 0) - (j == 0)
            if own:
                total = total + (5.0 * own) * square[n]
            if i == 0 or i == 4:
                at = j & 3
                side = side_ref[8 * (j // 4) : 8 * (j // 4) + 8, lanes]
                if at:
                    side = pltpu.roll(side, 8 - at if i == 0 else at, 0)
                if i == 0:
                    left = jnp.where(row == 0, side, pltpu.roll(f[j * 5 + 4], 1, 0))
                    total = total + 10.0 * two_point(left, f[n])
                else:
                    right = jnp.where(row == 7, side, pltpu.roll(f[j * 5], 7, 0))
                    total = total - 10.0 * two_point(f[n], right)
            out[n] = total
    return out


def each_lane_block(body):
    def step(block, carry):
        body(pl.ds(pl.multiple_of(block * 128, 128), 128))
        return carry

    lax.fori_loop(0, PLANES // 128, step, 0)


def volume_kernel(
    modal_ref, table_ref, field_ref, side_ref, edge_ref, modal_cross_ref, modal_chip_ref, cross_ref,
    chip_ref,
):
    nodal = turn(modal_ref, modal_cross_ref, modal_chip_ref)
    pair = synthesize(nodal, table_ref)
    for q in range(2):
        field_ref[:, HALF * q : HALF * q + HALF] = pair[q][0:200]
        side_ref[:, HALF * q : HALF * q + HALF] = pair[q][200:216]

    def body(lanes):
        total = row_rhs(field_ref, side_ref, lanes, (0, 4))
        for i in range(5):
            rows = slice(8 * i, 8 * i + 8)
            edge_ref[rows, lanes] = total[i]
            edge_ref[40 + 8 * i : 48 + 8 * i, lanes] = total[20 + i]
            cross_ref[rows, lanes], chip_ref[rows, lanes] = to_partners(total[i], total[20 + i])

    each_lane_block(body)


def project(planar, parity, table_ref):
    folded = planar[:, :HALF] + planar[:, HALF:] if parity == 0 else planar[:, :HALF] - planar[:, HALF:]
    return dot_split((table_ref[0, parity], table_ref[1, parity]), halves(folded), ((1,), (1,)))


def tendency(parity, from_rhs, from_flux):
    k = 2 * lax.broadcasted_iota(jnp.int32, (128, 128), 0) + parity
    scale = jnp.where(k == 0, 1.0, 2.0) * (math.sqrt(KMODES) / PLANES * STEP_SIZE)
    ratio = k.astype(jnp.float32) * (1.0 / KMODES)
    return (
        scale * (from_rhs[0:128] - ratio * from_flux[128:256]),
        scale * (from_rhs[128:256] + ratio * from_flux[0:128]),
    )


def inside_kernel(modal_ref, field_ref, side_ref, edge_ref, table_ref, out_ref, rhs_ref):
    last = [
        unpack_last([modal_ref[s, 32 + 8 * g : 40 + 8 * g, :] for g in range(3)], 11)
        for s in range(GRID)
    ]

    def body(lanes):
        total = row_rhs(field_ref, side_ref, lanes, (1, 2, 3))
        for n in range(5, 20):
            rhs_ref[8 * n - 40 : 8 * n - 32, lanes] = total[n]

    each_lane_block(body)
    field = field_ref[...]
    flux = 0.5 * field * field
    rhs = jnp.concatenate([edge_ref[0:40, :], rhs_ref[...], edge_ref[40:80, :]], axis=0)
    tail = jnp.zeros((56, PLANES), jnp.float32)
    flux = jnp.concatenate([flux, tail], axis=0)
    rhs = jnp.concatenate([rhs, tail], axis=0)
    for parity in range(2):
        from_rhs = project(rhs, parity, table_ref)
        from_flux = project(flux, parity, table_ref)
        for half in range(2):
            lanes = slice(128 * half, 128 * half + 128)
            change = tendency(parity, from_rhs[:, lanes], from_flux[:, lanes])
            for t in range(2):
                first = 16 * parity + 8 * t + 32 * half
                modal = jnp.concatenate(
                    last if first == 56 else [modal_ref[s, first : first + 8, :] for s in range(GRID)],
                    axis=0,
                )
                out_ref[parity, 128 * t : 128 * t + 128, lanes] = modal + change[t]


def lift_kernel(
    tag_ref, field_ref, cross_ref, chip_ref, table_ref, lift_ref, flux_ref, modal_ref, outer_ref
):
    bottom, top = at_ends()
    span = lax.axis_index("span")
    row = lax.broadcasted_iota(jnp.int32, (8, 128), 0)
    mirror = jnp.ones((8, 128), jnp.float32)
    for e in range(8):
        mirror = jnp.where((row == e) & (tag_ref[8 * span + e] == 1), -1.0, mirror)
    keep_lower = jnp.where(bottom, 0.0, 1.0)
    keep_upper = jnp.where(top, 0.0, 1.0)
    gap = jnp.zeros((48, 256), jnp.float32)
    outer = []
    for parity in range(2):
        below, above = from_partners(cross_ref[parity], chip_ref[parity])
        outer.append(jnp.concatenate([below, above], axis=0))
        modal_ref[parity] = jnp.concatenate(
            [keep_lower * below, keep_upper * above, gap], axis=0
        ).T
    pair = synthesize(outer, table_ref)
    for q in range(2):
        outer_ref[:, HALF * q : HALF * q + HALF] = pair[q]
    mirror = jnp.concatenate([mirror] * 6, axis=1)
    mirror = jnp.concatenate([mirror] * 5, axis=0)
    inside = field_ref[0:40, :]
    below = outer_ref[0:40, :]
    lift_ref[0:40, :] = 10.0 * two_point(jnp.where(bottom, mirror * inside, below), inside)
    flux_ref[0:40, :] = keep_lower * (0.5 * below * below)
    inside = field_ref[160:200, :]
    above = outer_ref[40:80, :]
    lift_ref[40:80, :] = 10.0 * two_point(inside, jnp.where(top, inside, above))
    flux_ref[40:80, :] = keep_upper * (0.5 * above * above)


def facing_kernel(
    inside_ref, lift_ref, flux_ref, facing_ref, cross_ref, chip_ref, table_ref, out_ref
):
    bottom, top = at_ends()
    below, above = from_partners(cross_ref[...], chip_ref[...])
    lift = lift_ref[0:40, :]
    rhs_lower = lift + jnp.where(bottom, 0.0, below - lift)
    lift = lift_ref[40:80, :]
    rhs_upper = jnp.where(top, 0.0, above + lift) - lift
    gap = jnp.zeros((48, PLANES), jnp.float32)
    planar = jnp.concatenate([rhs_lower, rhs_upper, gap, flux_ref[...], gap], axis=0)
    lane = lax.broadcasted_iota(jnp.int32, (128, 128), 1)
    whole, rest = [], []
    for parity in range(2):
        projected = project(planar, parity, table_ref)
        change = tendency(parity, projected[:, 0:128], projected[:, 128:256])
        for t in range(2):
            rows = slice(128 * t, 128 * t + 128)
            extra = change[t] + facing_ref[parity, rows, :]
            lower = jnp.where(lane < 40, extra, 0.0)
            upper = pltpu.roll(jnp.where(lane < 40, 0.0, extra), 120, 1)
            whole.append(inside_ref[parity, rows, 0:128] + lower)
            rest.append(inside_ref[parity, rows, 128:256] + upper)
    for s in range(GRID):
        part = slice(8 * s, 8 * s + 8)
        pack_rows(
            out_ref,
            s,
            jnp.concatenate([group[part] for group in whole], axis=0),
            jnp.concatenate([group[part] for group in rest], axis=0),
            9,
        )


def energy(values, shift):
    total = None
    for j in range(5):
        for i in range(5):
            n = j * 5 + i
            mass = float(WEIGHTS[j] * WEIGHTS[i])
            diagonal = VISCOUS * float(WEIGHTS[j] * STIFFNESS[i][i] + WEIGHTS[i] * STIFFNESS[j][j])
            value = (shift * mass + diagonal) * values[n]
            for other in range(i + 1, 5):
                weight = 2.0 * VISCOUS * float(WEIGHTS[j] * STIFFNESS[i][other])
                value = value + weight * values[j * 5 + other]
            for other in range(j + 1, 5):
                weight = 2.0 * VISCOUS * float(WEIGHTS[i] * STIFFNESS[j][other])
                value = value + weight * values[other * 5 + i]
            term = value * values[n]
            total = term if total is None else total + term
    return total


def at_ends():
    plane = lax.axis_index("plane")
    return plane == 0, plane == GRID - 1


def to_partners(low, high):
    odd = lax.axis_index("plane") % 2 == 1
    return jnp.where(odd, high, low), jnp.where(odd, low, high)


def from_partners(cross, chip):
    odd = lax.axis_index("plane") % 2 == 1
    return jnp.where(odd, chip, cross), jnp.where(odd, cross, chip)


def local_operator(values, shift):
    out = []
    for j in range(5):
        for i in range(5):
            n = j * 5 + i
            mass = float(WEIGHTS[j] * WEIGHTS[i])
            diagonal = VISCOUS * float(WEIGHTS[j] * STIFFNESS[i][i] + WEIGHTS[i] * STIFFNESS[j][j])
            value = (shift * mass + diagonal) * values[n]
            for other in range(5):
                if other != i:
                    weight = VISCOUS * float(WEIGHTS[j] * STIFFNESS[i][other])
                    value = value + weight * values[j * 5 + other]
                if other != j:
                    weight = VISCOUS * float(WEIGHTS[i] * STIFFNESS[j][other])
                    value = value + weight * values[other * 5 + i]
            out.append(value)
    return out


def join_columns(values):
    values = list(values)
    for j in range(5):
        joint = values[j * 5 + 4] + pltpu.roll(values[j * 5], 127, 1)
        values[j * 5 + 4] = joint
        values[j * 5] = pltpu.roll(joint, 1, 1)
    return values


def store_joined(values, joined_ref, cross_ref, chip_ref):
    values = join_columns(values)
    for n in range(25):
        joined_ref[n] = values[n]
    for i in range(4):
        cross_ref[i], chip_ref[i] = to_partners(values[i], values[20 + i])


def assembled(joined_ref, cross_ref, chip_ref):
    values = [joined_ref[n] for n in range(25)]
    bottom, top = at_ends()
    for i in range(4):
        below, above = from_partners(cross_ref[i], chip_ref[i])
        values[i] = values[i] + jnp.where(bottom, 0.0, below)
        values[20 + i] = values[20 + i] + jnp.where(top, 0.0, above)
    values[4] = pltpu.roll(values[0], 127, 1)
    values[24] = pltpu.roll(values[20], 127, 1)
    return values


def mode_terms():
    row = lax.broadcasted_iota(jnp.int32, (32, 128), 0)
    mode_pair = 16 * lax.axis_index("span") + 2 * (row & 7) + (row >> 4)
    ratio = mode_pair.astype(jnp.float32) * (1.0 / KMODES)
    shift = 1.0 + SPAN_STIFF * ratio * ratio
    return shift, 0.2 * shift + 0.15


def inner(left, right):
    bottom, top = at_ends()
    total = None
    for j in range(5):
        part = None
        for i in range(5):
            term = left[j * 5 + i] * right[j * 5 + i]
            term = term if 0 < i < 4 else 0.5 * term
            part = term if part is None else part + term
        if j == 0:
            part = jnp.where(bottom, 1.0, 0.5) * part
        elif j == 4:
            part = jnp.where(top, 1.0, 0.5) * part
        total = part if total is None else total + part
    return total


def first_kernel(modal_ref, vector_ref, next_ref, cross_ref, chip_ref):
    shift, _ = mode_terms()
    values = exchange_chunks([modal_ref[s, 0:32, :] for s in range(GRID)])
    rest = []
    for s in range(GRID):
        tiles = [modal_ref[s, 32 + 8 * g : 40 + 8 * g, :] for g in range(3)]
        rest.append(jnp.concatenate(tiles + [unpack_last(tiles, 9)], axis=0))
    values += exchange_chunks(rest)
    values = [float(WEIGHTS[n // 5] * WEIGHTS[n % 5]) * values[n] for n in range(25)]
    vector = join_columns(values)
    for n in range(25):
        vector_ref[n] = vector[n]
    store_joined(local_operator(vector, shift), next_ref, cross_ref, chip_ref)


def second_kernel(
    joined_ref, cross_in_ref, chip_in_ref, before_ref, vector_ref, next_ref, cross_ref, chip_ref
):
    shift, center = mode_terms()
    applied = assembled(joined_ref, cross_in_ref, chip_in_ref)
    vector = [applied[n] - center * before_ref[n] for n in range(25)]
    for n in range(25):
        vector_ref[n] = vector[n]
    store_joined(local_operator(vector, shift), next_ref, cross_ref, chip_ref)


def mode_sums(moment, turn_ref):
    for t in range(4):
        turn_ref[pl.ds(t, 8, stride=4), :] = moment[8 * t : 8 * t + 8]
    return jnp.sum(turn_ref[...].T, axis=0, keepdims=True)


def early_kernel(first_ref, second_ref, joined_ref, packed_ref, turn_ref):
    _, center = mode_terms()
    first = [first_ref[n] for n in range(25)]
    second = [second_ref[n] for n in range(25)]
    square = inner(second, second)
    product = None
    for n in range(25):
        term = second[n] * joined_ref[n]
        term = term if 0 < n % 5 < 4 else 0.5 * term
        product = term if product is None else product + term
    moments = [inner(first, first), inner(first, second), square, product - center * square]
    packed_ref[...] = jnp.zeros((8, 128), jnp.float32)
    for n, moment in enumerate(moments):
        packed_ref[n : n + 1, 0:32] = mode_sums(moment, turn_ref.at[n])


def store_natural(tiles, out_ref, row, column_ref):
    columns = merge_columns(tiles)
    for i in range(5):
        first = 32 * (5 * row + i)
        for t in range(4):
            column_ref[pl.ds(first + t, 8, stride=4), :] = columns[i][8 * t : 8 * t + 8]
        out_ref[row, :, 128 * i : 128 * i + 128] = column_ref[first : first + 32, :]


def natural_kernel(vector_ref, out_ref, column_ref):
    for j in range(5):
        store_natural([vector_ref[j * 5 + i] for i in range(5)], out_ref, j, column_ref)


def inner_kernel(joined_ref, second_ref, out_ref, column_ref):
    _, center = mode_terms()
    for j in range(1, 4):
        tiles = [
            joined_ref[n] - center * second_ref[n] for n in range(5 * j, 5 * j + 5)
        ]
        store_natural(tiles, out_ref, j - 1, column_ref)


def third_kernel(
    joined_ref, cross_in_ref, chip_in_ref, second_ref, packed_ref, edge_ref, sums_ref, turn_ref,
    column_ref,
):
    shift, center = mode_terms()
    applied = assembled(joined_ref, cross_in_ref, chip_in_ref)
    second = [second_ref[n] for n in range(25)]
    third = [applied[n] - center * second[n] for n in range(25)]
    for row in range(2):
        store_natural(third[20 * row : 20 * row + 5], edge_ref, row, column_ref)
    fourth = inner(third, third)
    moments = [fourth, energy(third, shift) - center * fourth]
    sums_ref[0] = packed_ref[...]
    for n, moment in enumerate(moments):
        sums_ref[0, 4 + n : 5 + n, 0:32] = mode_sums(moment, turn_ref.at[n])
    sums = sums_ref[0]
    for p in range(1, GRID):
        sums_ref[p] = sums


def tree(terms):
    while len(terms) > 1:
        terms = [sum(terms[n + 1 : n + 2], terms[n]) for n in range(0, len(terms), 2)]
    return terms[0]


def combine_kernel(
    sums_ref, first_ref, second_ref, inner_ref, edge_ref, out_hbm, turn_ref, result_ref, sent
):
    total = tree([sums_ref[p] for p in range(GRID)])
    moment = [total[n : n + 1] for n in range(6)]
    lane = lax.broadcasted_iota(jnp.int32, (1, 128), 1)
    mode_pair = 16 * lax.axis_index("span") + (lane >> 1)
    ratio = mode_pair.astype(jnp.float32) * (1.0 / KMODES)
    center = 0.2 * (1.0 + SPAN_STIFF * ratio * ratio) + 0.15

    def product(left, right):
        return tree(
            [
                tree(
                    [
                        left[a] * right[power - a]
                        for a in range(len(left))
                        if 0 <= power - a < len(right)
                    ]
                )
                * moment[power]
                for power in range(len(left) + len(right) - 1)
            ]
        )

    def operator(c):
        shifted = [center * v for v in c] + [0.0]
        return [shifted[0]] + [shifted[a + 1] + c[a] for a in range(len(c))]

    residual = [jnp.ones((1, 128), jnp.float32)]
    direction = residual
    result = [0.0, 0.0, 0.0]
    norm = moment[0]
    for step in range(ITERS):
        applied = operator(direction)
        length = norm / product(direction, applied)
        for a in range(len(direction)):
            result[a] = result[a] + length * direction[a]
        if step < ITERS - 1:
            padded = residual + [0.0]
            residual = [padded[a] - length * applied[a] for a in range(len(applied))]
            fresh = product(residual, residual)
            ratio = fresh / norm
            norm = fresh
            padded = direction + [0.0]
            direction = [residual[a] + ratio * padded[a] for a in range(len(residual))]
    turn_ref[...] = jnp.zeros((8, 128), jnp.float32)
    for a in range(3):
        turn_ref[a : a + 1, :] = result[a]
    turned = turn_ref[...].T[0:32]
    weight = [turned[:, a : a + 1] for a in range(3)]
    copies = []
    for j in range(5):
        third = inner_ref[j - 1] if 0 < j < 4 else edge_ref[j // 4]
        result_ref[j] = weight[0] * first_ref[j] + weight[1] * second_ref[j] + weight[2] * third
        copies.append(pltpu.make_async_copy(result_ref.at[j], out_hbm.at[j], sent.at[j]))
        copies[j].start()
    for copy in copies:
        copy.wait()


def call(kernel, out_shapes, *args, smem=(), anywhere=(), scratch=(), out_space=pltpu.VMEM, covers=True):
    vmem = pl.BlockSpec(memory_space=pltpu.VMEM)
    spaces = {n: pl.BlockSpec(memory_space=pltpu.SMEM) for n in smem}
    spaces |= {n: pl.BlockSpec(memory_space=pltpu.HBM) for n in anywhere}
    return pl.pallas_call(
        kernel,
        out_shape=[jax.ShapeDtypeStruct(s, jnp.float32) for s in out_shapes],
        in_specs=[spaces.get(n, vmem) for n in range(len(args))],
        out_specs=[pl.BlockSpec(memory_space=out_space)] * len(out_shapes),
        scratch_shapes=list(scratch),
        cost_estimate=None if covers else pl.CostEstimate(flops=0, bytes_accessed=0, transcendentals=0),
        compiler_params=pltpu.CompilerParams(vmem_limit_bytes=16 * 1024 * 1024),
    )(*args)


def swap_traces(cross, chip):
    partner = [(p, (p + 1) % GRID if p % 2 else (p - 1) % GRID) for p in range(GRID)]
    chip = lax.ppermute(chip, "plane", [(p, p ^ 1) for p in range(GRID)])
    cross = lax.ppermute(cross, "plane", partner)
    return cross, chip


def on_device(state, wall_tag):
    table = wave_table()
    (packed,) = call(
        pack_kernel, [(16, 56, 128)],
        pltpu.with_memory_space_constraint(jnp.transpose(state, (1, 0, 2)), pltpu.HBM),
        anywhere=(0,),
        scratch=[
            pltpu.VMEM((800, 128), jnp.float32), pltpu.VMEM((5, 32, 640), jnp.float32),
            pltpu.VMEM((640, 640), jnp.bfloat16), pltpu.SemaphoreType.DMA(()),
        ],
    )
    modal = lax.all_to_all(packed, "span", 0, 0, tiled=True)
    trace, rows = (2, 40, 256), (40, PLANES)
    field, side, edge, *modal_traces, cross, chip = call(
        volume_kernel,
        [(200, PLANES), (16, PLANES), (80, PLANES), trace, trace, rows, rows], modal, table,
    )
    modal_traces = swap_traces(*modal_traces)
    rhs_traces = swap_traces(cross, chip)
    (inside,) = call(
        inside_kernel, [(2, 256, 256)], modal, field, side, edge, table, covers=False,
        scratch=[pltpu.VMEM((120, PLANES), jnp.float32)],
    )
    lift, flux, facing = call(
        lift_kernel, [(80, PLANES), (80, PLANES), (2, 256, 128)], wall_tag, field,
        *modal_traces, table, smem=(0,), scratch=[pltpu.VMEM((80, PLANES), jnp.float32)],
        covers=False,
    )
    (sent,) = call(facing_kernel, [(16, 56, 128)], inside, lift, flux, facing, *rhs_traces, table)
    load = lax.all_to_all(sent, "span", 0, 0, tiled=True)
    nodes, trace = (25, 32, 128), (4, 32, 128)
    first, joined, cross, chip = call(first_kernel, [nodes, nodes, trace, trace], load)
    cross, chip = swap_traces(cross, chip)
    second, joined, cross, chip = call(
        second_kernel, [nodes, nodes, trace, trace], joined, cross, chip, first
    )
    cross, chip = swap_traces(cross, chip)
    (packed,) = call(
        early_kernel, [(8, 128)], first, second, joined,
        scratch=[pltpu.VMEM((4, 32, 128), jnp.float32)],
    )
    natural = [
        call(
            natural_kernel, [(5, 32, 640)], vector,
            scratch=[pltpu.VMEM((800, 128), jnp.float32)],
        )[0]
        for vector in (first, second)
    ]
    (inside,) = call(
        inner_kernel, [(3, 32, 640)], joined, second,
        scratch=[pltpu.VMEM((480, 128), jnp.float32)],
    )
    edges, sums = call(
        third_kernel, [(2, 32, 640), (16, 8, 128)], joined, cross, chip, second, packed,
        scratch=[pltpu.VMEM((2, 32, 128), jnp.float32), pltpu.VMEM((320, 128), jnp.float32)],
    )
    sums = lax.all_to_all(sums, "plane", 0, 0, tiled=True)
    (columns,) = call(
        combine_kernel, [(5, 32, 640)], sums, *natural, inside, edges,
        out_space=pltpu.HBM,
        scratch=[
            pltpu.VMEM((8, 128), jnp.float32), pltpu.VMEM((5, 32, 640), jnp.float32),
            pltpu.SemaphoreType.DMA((5,)),
        ],
    )
    return jnp.transpose(columns, (1, 0, 2))


def solution(mesh):
    return jax.shard_map(
        on_device,
        mesh=mesh,
        in_specs=(P("span", "plane", None), P()),
        out_specs=P("span", "plane", None),
        check_vma=False,
    )
```

```python
import math

import jax
import jax.numpy as jnp
import numpy as np
from jax import lax
from jax.experimental import pallas as pl
from jax.experimental.pallas import tpu as pltpu
from jax.sharding import PartitionSpec as P


KMODES = 256
PLANES = 768
HALF = 384
ITERS = 3
GRID = 16
STEP_SIZE = 0.03
VISCOUS = 0.05
SPAN_STIFF = 4.0


def gll_tables():
    abscissae = np.array([-1.0, -math.sqrt(3.0 / 7.0), 0.0, math.sqrt(3.0 / 7.0), 1.0])
    weights = np.array([0.1, 49.0 / 90.0, 32.0 / 45.0, 49.0 / 90.0, 0.1])
    squared = abscissae * abscissae
    legendre = (35.0 * squared * squared - 30.0 * squared + 3.0) / 8.0
    identity = np.eye(5)
    spacing = abscissae[:, None] - abscissae[None, :] + identity
    differ = np.where(identity > 0, 0.0, legendre[:, None] / legendre[None, :] / spacing)
    differ[0, 0] = -5.0
    differ[4, 4] = 5.0
    stiffness = differ.T @ (weights[:, None] * differ)
    return differ, weights, stiffness


DIFFER, WEIGHTS, STIFFNESS = gll_tables()


def split_table(table):
    high = table.astype(np.float32).astype(jnp.bfloat16)
    low = (table - high.astype(np.float64)).astype(np.float32).astype(jnp.bfloat16)
    return jnp.asarray(np.stack([high, low]))


def wave_table():
    plane = np.arange(HALF)
    waves = []
    for parity in range(2):
        k = 2 * np.arange(128) + parity
        angle = (k[:, None] * plane[None, :] % PLANES) * (2.0 * math.pi / PLANES)
        waves.append(np.concatenate([np.cos(angle), np.sin(angle)]))
    return split_table(np.stack(waves))


def dot(left, right, contract):
    return lax.dot_general(
        left, right, (contract, ((), ())), preferred_element_type=jnp.float32
    )


def halves(value):
    high = value.astype(jnp.bfloat16)
    low = (value - high.astype(jnp.float32)).astype(jnp.bfloat16)
    return high, low


def dot_split(left, right, contract):
    (left_high, left_low), (right_high, right_low) = left, right
    return (
        dot(left_high, right_low, contract)
        + dot(left_low, right_high, contract)
        + dot(left_high, right_high, contract)
    )


def lanes_of(values, index):
    return jnp.take_along_axis(values, index, axis=1)


def merge_columns(tiles):
    lane = lax.broadcasted_iota(jnp.int32, tiles[0].shape, 1)
    out = []
    for t in range(5):
        column = lane + 128 * t
        element = (column * 13108) >> 16
        node = column - 5 * element
        picked = lanes_of(tiles[0], element)
        for i in range(1, 5):
            picked = jnp.where(node == i, lanes_of(tiles[i], element), picked)
        out.append(picked)
    return out


def exchange_chunks(values):
    values = list(values)
    lane = lax.broadcasted_iota(jnp.int32, values[0].shape, 1)
    for bit in (1, 2, 4, 8):
        upper = (lane & (8 * bit)) != 0
        other = lane ^ (8 * bit)
        for a in range(16):
            if a & bit == 0:
                first, second = values[a], values[a | bit]
                moved = jnp.where(upper, first, second)
                if bit == 8:
                    moved = pltpu.roll(moved, 64, 1)
                else:
                    moved = lanes_of(moved, other)
                values[a] = jnp.where(upper, moved, first)
                values[a | bit] = jnp.where(upper, second, moved)
    return values


def column_order():
    column = lax.broadcasted_iota(jnp.int32, (640, 128), 0)
    element = lax.broadcasted_iota(jnp.int32, (640, 128), 1)
    tiles = [jnp.where(column == 5 * element + i, 1.0, 0.0).astype(jnp.bfloat16) for i in range(5)]
    return jnp.concatenate(tiles, axis=1)


def pack_rows(out_ref, d, whole, rest, count):
    out_ref[d, 0:32, :] = whole
    lane = lax.broadcasted_iota(jnp.int32, (8, 128), 1)
    free = 16 - count
    for g in range(3):
        tile = rest[8 * g : 8 * g + 8]
        if g * free < count:
            shift = 8 * (count - g * free)
            tile = jnp.where(lane < 8 * count, tile, pltpu.roll(rest[24:32], shift % 128, 1))
        out_ref[d, 32 + 8 * g : 40 + 8 * g, :] = tile


def unpack_last(tiles, count):
    lane = lax.broadcasted_iota(jnp.int32, (8, 128), 1)
    free = 16 - count
    last = pltpu.roll(tiles[0], 128 - 8 * count, 1)
    for g in range(1, 3):
        if g * free < count:
            shift = 8 * (count - g * free)
            last = jnp.where(lane < 8 * g * free, last, pltpu.roll(tiles[g], (128 - shift) % 128, 1))
    return last


def pack_kernel(state_hbm, out_ref, chunk_ref, state_ref, order_ref, arrived):
    copy = pltpu.make_async_copy(state_hbm, state_ref, arrived)
    copy.start()
    order_ref[...] = column_order()
    copy.wait()
    stacked = jnp.concatenate([state_ref[j] for j in range(5)], axis=0)
    order = order_ref[...]
    contract = ((1,), (0,))
    high, low = halves(stacked)
    nodes = dot(low, order, contract) + dot(high, order, contract)
    for i in range(5):
        chunk_ref[160 * i : 160 * i + 160, :] = nodes[:, 128 * i : 128 * i + 128]
    chunk = [
        jnp.concatenate(
            [chunk_ref[pl.ds(160 * i + 32 * j + t, 8, stride=4), :] for t in range(4)], axis=0
        )
        for j in range(5)
        for i in range(5)
    ]
    lane = lax.broadcasted_iota(jnp.int32, (32, 128), 1) & 7
    sides = [jnp.zeros((32, 128), jnp.float32), jnp.zeros((32, 128), jnp.float32)]
    for j in range(5):
        at = j & 3
        side = jnp.where(lane == at, pltpu.roll(chunk[j * 5 + 4], 1 + at, 1), sides[j // 4])
        sides[j // 4] = jnp.where(lane == 7 - at, pltpu.roll(chunk[j * 5], 127 - at, 1), side)
    chunk = chunk + sides
    whole = exchange_chunks(chunk[:16])
    rest = exchange_chunks(chunk[16:] + [jnp.zeros((32, 128), jnp.float32)] * 5)
    for d in range(GRID):
        pack_rows(out_ref, d, whole[d], rest[d], 11)


def turn(modal_ref, cross_ref, chip_ref):
    last = [
        unpack_last([modal_ref[s, 32 + 8 * g : 40 + 8 * g, :] for g in range(3)], 11)
        for s in range(GRID)
    ]
    nodal = []
    for parity in range(2):
        whole, rest = [], []
        for t in range(2):
            group = 2 * parity + t
            for s in range(GRID):
                whole.append(modal_ref[s, 8 * group : 8 * group + 8, :])
                rest.append(
                    last[s] if group == 3 else modal_ref[s, 32 + 8 * group : 40 + 8 * group, :]
                )
        turned = [jnp.concatenate(part, axis=0).T for part in (whole, rest)]
        nodal.append(jnp.concatenate([turned[0], turned[1][0:88]], axis=0))
        cross_ref[parity], chip_ref[parity] = to_partners(turned[0][0:40], turned[1][32:72])
    return nodal


def synthesize(nodal, table_ref):
    part = [
        dot_split(
            halves(nodal[parity]), (table_ref[0, parity], table_ref[1, parity]), ((1,), (0,))
        )
        for parity in range(2)
    ]
    scale = 1.0 / math.sqrt(KMODES)
    return scale * (part[0] + part[1]), scale * (part[0] - part[1])


def two_point(left, right):
    mean = (left * left + left * right + right * right) * (1.0 / 6.0)
    speed = jnp.maximum(jnp.abs(left), jnp.abs(right))
    return mean - 0.5 * speed * (right - left)


def row_rhs(field_ref, side_ref, lanes, rows):
    row = lax.broadcasted_iota(jnp.int32, (8, 128), 0)
    f = [field_ref[8 * n : 8 * n + 8, lanes] for n in range(25)]
    square = [v * v for v in f]
    out = {}
    for j in rows:
        for i in range(5):
            n = j * 5 + i
            plain = None
            power = None
            for other in range(5):
                terms = [(DIFFER[i][other], j * 5 + other), (DIFFER[j][other], other * 5 + i)]
                for weight, m in terms:
                    if weight == 0.0:
                        continue
                    weight = float(weight) / -3.0
                    plain = weight * f[m] if plain is None else plain + weight * f[m]
                    power = weight * square[m] if power is None else power + weight * square[m]
            total = power + f[n] * plain
            own = (i == 4) + (j == 4) - (i == 0) - (j == 0)
            if own:
                total = total + (5.0 * own) * square[n]
            if i == 0 or i == 4:
                at = j & 3
                side = side_ref[8 * (j // 4) : 8 * (j // 4) + 8, lanes]
                if at:
                    side = pltpu.roll(side, 8 - at if i == 0 else at, 0)
                if i == 0:
                    left = jnp.where(row == 0, side, pltpu.roll(f[j * 5 + 4], 1, 0))
                    total = total + 10.0 * two_point(left, f[n])
                else:
                    right = jnp.where(row == 7, side, pltpu.roll(f[j * 5], 7, 0))
                    total = total - 10.0 * two_point(f[n], right)
            out[n] = total
    return out


def each_lane_block(body):
    def step(block, carry):
        body(pl.ds(pl.multiple_of(block * 128, 128), 128))
        return carry

    lax.fori_loop(0, PLANES // 128, step, 0)


def volume_kernel(
    modal_ref, table_ref, field_ref, side_ref, edge_ref, modal_cross_ref, modal_chip_ref, cross_ref,
    chip_ref,
):
    nodal = turn(modal_ref, modal_cross_ref, modal_chip_ref)
    pair = synthesize(nodal, table_ref)
    for q in range(2):
        field_ref[:, HALF * q : HALF * q + HALF] = pair[q][0:200]
        side_ref[:, HALF * q : HALF * q + HALF] = pair[q][200:216]

    def body(lanes):
        total = row_rhs(field_ref, side_ref, lanes, (0, 4))
        for i in range(5):
            rows = slice(8 * i, 8 * i + 8)
            edge_ref[rows, lanes] = total[i]
            edge_ref[40 + 8 * i : 48 + 8 * i, lanes] = total[20 + i]
            cross_ref[rows, lanes], chip_ref[rows, lanes] = to_partners(total[i], total[20 + i])

    each_lane_block(body)


def project(planar, parity, table_ref):
    folded = planar[:, :HALF] + planar[:, HALF:] if parity == 0 else planar[:, :HALF] - planar[:, HALF:]
    return dot_split((table_ref[0, parity], table_ref[1, parity]), halves(folded), ((1,), (1,)))


def tendency(parity, from_rhs, from_flux):
    k = 2 * lax.broadcasted_iota(jnp.int32, (128, 128), 0) + parity
    scale = jnp.where(k == 0, 1.0, 2.0) * (math.sqrt(KMODES) / PLANES * STEP_SIZE)
    ratio = k.astype(jnp.float32) * (1.0 / KMODES)
    return (
        scale * (from_rhs[0:128] - ratio * from_flux[128:256]),
        scale * (from_rhs[128:256] + ratio * from_flux[0:128]),
    )


def inside_kernel(modal_ref, field_ref, side_ref, edge_ref, table_ref, out_ref, rhs_ref):
    last = [
        unpack_last([modal_ref[s, 32 + 8 * g : 40 + 8 * g, :] for g in range(3)], 11)
        for s in range(GRID)
    ]

    def body(lanes):
        total = row_rhs(field_ref, side_ref, lanes, (1, 2, 3))
        for n in range(5, 20):
            rhs_ref[8 * n - 40 : 8 * n - 32, lanes] = total[n]

    each_lane_block(body)
    field = field_ref[...]
    flux = 0.5 * field * field
    rhs = jnp.concatenate([edge_ref[0:40, :], rhs_ref[...], edge_ref[40:80, :]], axis=0)
    tail = jnp.zeros((56, PLANES), jnp.float32)
    flux = jnp.concatenate([flux, tail], axis=0)
    rhs = jnp.concatenate([rhs, tail], axis=0)
    for parity in range(2):
        from_rhs = project(rhs, parity, table_ref)
        from_flux = project(flux, parity, table_ref)
        for half in range(2):
            lanes = slice(128 * half, 128 * half + 128)
            change = tendency(parity, from_rhs[:, lanes], from_flux[:, lanes])
            for t in range(2):
                first = 16 * parity + 8 * t + 32 * half
                modal = jnp.concatenate(
                    last if first == 56 else [modal_ref[s, first : first + 8, :] for s in range(GRID)],
                    axis=0,
                )
                out_ref[parity, 128 * t : 128 * t + 128, lanes] = modal + change[t]


def project_rows(planar, parity, table_ref):
    folded = planar[:, :HALF] + planar[:, HALF:] if parity == 0 else planar[:, :HALF] - planar[:, HALF:]
    return dot_split(halves(folded), (table_ref[0, parity], table_ref[1, parity]), ((1,), (1,)))


def wave_factors(parity):
    k = 2 * lax.broadcasted_iota(jnp.int32, (80, 128), 1) + parity
    scale = jnp.where(k == 0, 1.0, 2.0) * (math.sqrt(KMODES) / PLANES * STEP_SIZE)
    return scale, scale * (k.astype(jnp.float32) * (1.0 / KMODES))


def lift_kernel(
    tag_ref, field_ref, cross_ref, chip_ref, table_ref, lift_ref, base_ref, outer_ref
):
    bottom, top = at_ends()
    span = lax.axis_index("span")
    row = lax.broadcasted_iota(jnp.int32, (8, 128), 0)
    mirror = jnp.ones((8, 128), jnp.float32)
    for e in range(8):
        mirror = jnp.where((row == e) & (tag_ref[8 * span + e] == 1), -1.0, mirror)
    keep_lower = jnp.where(bottom, 0.0, 1.0)
    keep_upper = jnp.where(top, 0.0, 1.0)
    outer, modal = [], []
    for parity in range(2):
        below, above = from_partners(cross_ref[parity], chip_ref[parity])
        outer.append(jnp.concatenate([below, above], axis=0))
        modal.append(jnp.concatenate([keep_lower * below, keep_upper * above], axis=0))
    pair = synthesize(outer, table_ref)
    for q in range(2):
        outer_ref[:, HALF * q : HALF * q + HALF] = pair[q]
    mirror = jnp.concatenate([mirror] * 6, axis=1)
    mirror = jnp.concatenate([mirror] * 5, axis=0)
    inside = field_ref[0:40, :]
    below = outer_ref[0:40, :]
    lift_ref[0:40, :] = 10.0 * two_point(jnp.where(bottom, mirror * inside, below), inside)
    flux_lower = keep_lower * (0.5 * below * below)
    inside = field_ref[160:200, :]
    above = outer_ref[40:80, :]
    lift_ref[40:80, :] = 10.0 * two_point(inside, jnp.where(top, inside, above))
    flux = jnp.concatenate([flux_lower, keep_upper * (0.5 * above * above)], axis=0)
    for parity in range(2):
        from_flux = project_rows(flux, parity, table_ref)
        _, ratio = wave_factors(parity)
        base_ref[parity, :, 0:128] = modal[parity][:, 0:128] - ratio * from_flux[:, 128:256]
        base_ref[parity, :, 128:256] = modal[parity][:, 128:256] + ratio * from_flux[:, 0:128]


def facing_kernel(inside_ref, lift_ref, base_ref, cross_ref, chip_ref, table_ref, out_ref):
    bottom, top = at_ends()
    below, above = from_partners(cross_ref[...], chip_ref[...])
    lift = lift_ref[0:40, :]
    rhs_lower = lift + jnp.where(bottom, 0.0, below - lift)
    lift = lift_ref[40:80, :]
    rhs_upper = jnp.where(top, 0.0, above + lift) - lift
    rhs = jnp.concatenate([rhs_lower, rhs_upper], axis=0)
    gap = jnp.zeros((48, 128), jnp.float32)
    lane = lax.broadcasted_iota(jnp.int32, (128, 128), 1)
    whole, rest = [], []
    for parity in range(2):
        from_rhs = project_rows(rhs, parity, table_ref)
        scale, _ = wave_factors(parity)
        for t in range(2):
            waves = slice(128 * t, 128 * t + 128)
            nodal = base_ref[parity, :, waves] + scale * from_rhs[:, waves]
            extra = jnp.concatenate([nodal, gap], axis=0).T
            lower = jnp.where(lane < 40, extra, 0.0)
            upper = pltpu.roll(jnp.where(lane < 40, 0.0, extra), 120, 1)
            whole.append(inside_ref[parity, waves, 0:128] + lower)
            rest.append(inside_ref[parity, waves, 128:256] + upper)
    for s in range(GRID):
        part = slice(8 * s, 8 * s + 8)
        pack_rows(
            out_ref,
            s,
            jnp.concatenate([group[part] for group in whole], axis=0),
            jnp.concatenate([group[part] for group in rest], axis=0),
            9,
        )


def energy(values, shift):
    total = None
    for j in range(5):
        for i in range(5):
            n = j * 5 + i
            mass = float(WEIGHTS[j] * WEIGHTS[i])
            diagonal = VISCOUS * float(WEIGHTS[j] * STIFFNESS[i][i] + WEIGHTS[i] * STIFFNESS[j][j])
            value = (shift * mass + diagonal) * values[n]
            for other in range(i + 1, 5):
                weight = 2.0 * VISCOUS * float(WEIGHTS[j] * STIFFNESS[i][other])
                value = value + weight * values[j * 5 + other]
            for other in range(j + 1, 5):
                weight = 2.0 * VISCOUS * float(WEIGHTS[i] * STIFFNESS[j][other])
                value = value + weight * values[other * 5 + i]
            term = value * values[n]
            total = term if total is None else total + term
    return total


def at_ends():
    plane = lax.axis_index("plane")
    return plane == 0, plane == GRID - 1


def to_partners(low, high):
    odd = lax.axis_index("plane") % 2 == 1
    return jnp.where(odd, high, low), jnp.where(odd, low, high)


def from_partners(cross, chip):
    odd = lax.axis_index("plane") % 2 == 1
    return jnp.where(odd, chip, cross), jnp.where(odd, cross, chip)


def local_operator(values, shift, rows):
    out = []
    for j in rows:
        line = []
        for i in range(5):
            n = j * 5 + i
            mass = float(WEIGHTS[j] * WEIGHTS[i])
            diagonal = VISCOUS * float(WEIGHTS[j] * STIFFNESS[i][i] + WEIGHTS[i] * STIFFNESS[j][j])
            value = (shift * mass + diagonal) * values[n]
            for other in range(5):
                if other != i:
                    weight = VISCOUS * float(WEIGHTS[j] * STIFFNESS[i][other])
                    value = value + weight * values[j * 5 + other]
                if other != j:
                    weight = VISCOUS * float(WEIGHTS[i] * STIFFNESS[j][other])
                    value = value + weight * values[other * 5 + i]
            line.append(value)
        out += join_columns(line)
    return out


def join_columns(line):
    joint = line[4] + pltpu.roll(line[0], 127, 1)
    return [pltpu.roll(joint, 1, 1), *line[1:4], joint]


def store_edges(values, shift, edge_ref, cross_ref, chip_ref):
    image = local_operator(values, shift, (0, 4))
    for n in range(10):
        edge_ref[n] = image[n]
    for i in range(4):
        cross_ref[i], chip_ref[i] = to_partners(image[i], image[5 + i])


def fill_kernel(vector_ref, inner_ref):
    shift, _ = mode_terms()
    image = local_operator([vector_ref[n] for n in range(25)], shift, (1, 2, 3))
    for n in range(15):
        inner_ref[n] = image[n]


def unassembled(edge_ref, inner_ref):
    return (
        [edge_ref[n] for n in range(5)]
        + [inner_ref[n] for n in range(15)]
        + [edge_ref[5 + n] for n in range(5)]
    )


def assembled(edge_ref, inner_ref, cross_ref, chip_ref):
    values = unassembled(edge_ref, inner_ref)
    bottom, top = at_ends()
    for i in range(4):
        below, above = from_partners(cross_ref[i], chip_ref[i])
        values[i] = values[i] + jnp.where(bottom, 0.0, below)
        values[20 + i] = values[20 + i] + jnp.where(top, 0.0, above)
    values[4] = pltpu.roll(values[0], 127, 1)
    values[24] = pltpu.roll(values[20], 127, 1)
    return values


def mode_terms():
    row = lax.broadcasted_iota(jnp.int32, (32, 128), 0)
    mode_pair = 16 * lax.axis_index("span") + 2 * (row & 7) + (row >> 4)
    ratio = mode_pair.astype(jnp.float32) * (1.0 / KMODES)
    shift = 1.0 + SPAN_STIFF * ratio * ratio
    return shift, 0.2 * shift + 0.15


def inner(left, right):
    bottom, top = at_ends()
    total = None
    for j in range(5):
        part = None
        for i in range(5):
            term = left[j * 5 + i] * right[j * 5 + i]
            term = term if 0 < i < 4 else 0.5 * term
            part = term if part is None else part + term
        if j == 0:
            part = jnp.where(bottom, 1.0, 0.5) * part
        elif j == 4:
            part = jnp.where(top, 1.0, 0.5) * part
        total = part if total is None else total + part
    return total


def first_kernel(modal_ref, vector_ref, edge_ref, cross_ref, chip_ref):
    shift, _ = mode_terms()
    values = exchange_chunks([modal_ref[s, 0:32, :] for s in range(GRID)])
    rest = []
    for s in range(GRID):
        tiles = [modal_ref[s, 32 + 8 * g : 40 + 8 * g, :] for g in range(3)]
        rest.append(jnp.concatenate(tiles + [unpack_last(tiles, 9)], axis=0))
    values += exchange_chunks(rest)
    values = [float(WEIGHTS[n // 5] * WEIGHTS[n % 5]) * values[n] for n in range(25)]
    vector = []
    for j in range(5):
        vector += join_columns(values[5 * j : 5 * j + 5])
    for n in range(25):
        vector_ref[n] = vector[n]
    store_edges(vector, shift, edge_ref, cross_ref, chip_ref)


def second_kernel(
    edge_in_ref, inner_ref, cross_in_ref, chip_in_ref, before_ref, vector_ref, edge_ref, cross_ref,
    chip_ref,
):
    shift, center = mode_terms()
    applied = assembled(edge_in_ref, inner_ref, cross_in_ref, chip_in_ref)
    vector = [applied[n] - center * before_ref[n] for n in range(25)]
    for n in range(25):
        vector_ref[n] = vector[n]
    store_edges(vector, shift, edge_ref, cross_ref, chip_ref)


def mode_sums(moment, turn_ref):
    for t in range(4):
        turn_ref[pl.ds(t, 8, stride=4), :] = moment[8 * t : 8 * t + 8]
    return jnp.sum(turn_ref[...].T, axis=0, keepdims=True)


def early_kernel(first_ref, second_ref, edge_ref, inner_ref, packed_ref, turn_ref):
    _, center = mode_terms()
    first = [first_ref[n] for n in range(25)]
    second = [second_ref[n] for n in range(25)]
    square = inner(second, second)
    product = None
    image = unassembled(edge_ref, inner_ref)
    for n in range(25):
        term = second[n] * image[n]
        term = term if 0 < n % 5 < 4 else 0.5 * term
        product = term if product is None else product + term
    moments = [inner(first, first), inner(first, second), square, product - center * square]
    packed_ref[...] = jnp.zeros((8, 128), jnp.float32)
    for n, moment in enumerate(moments):
        packed_ref[n : n + 1, 0:32] = mode_sums(moment, turn_ref.at[n])


def store_natural(tiles, out_ref, row, column_ref):
    columns = merge_columns(tiles)
    for i in range(5):
        first = 32 * (5 * row + i)
        for t in range(4):
            column_ref[pl.ds(first + t, 8, stride=4), :] = columns[i][8 * t : 8 * t + 8]
        out_ref[row, :, 128 * i : 128 * i + 128] = column_ref[first : first + 32, :]


def natural_kernel(vector_ref, out_ref, column_ref):
    for j in range(5):
        store_natural([vector_ref[j * 5 + i] for i in range(5)], out_ref, j, column_ref)


def inner_kernel(inner_ref, second_ref, out_ref, column_ref):
    _, center = mode_terms()
    for j in range(1, 4):
        tiles = [
            inner_ref[n - 5] - center * second_ref[n] for n in range(5 * j, 5 * j + 5)
        ]
        store_natural(tiles, out_ref, j - 1, column_ref)


def third_kernel(
    edge_in_ref, inner_ref, cross_in_ref, chip_in_ref, second_ref, packed_ref, edge_ref, sums_ref,
    turn_ref, column_ref,
):
    shift, center = mode_terms()
    applied = assembled(edge_in_ref, inner_ref, cross_in_ref, chip_in_ref)
    second = [second_ref[n] for n in range(25)]
    third = [applied[n] - center * second[n] for n in range(25)]
    for row in range(2):
        store_natural(third[20 * row : 20 * row + 5], edge_ref, row, column_ref)
    fourth = inner(third, third)
    moments = [fourth, energy(third, shift) - center * fourth]
    sums_ref[0] = packed_ref[...]
    for n, moment in enumerate(moments):
        sums_ref[0, 4 + n : 5 + n, 0:32] = mode_sums(moment, turn_ref.at[n])
    sums = sums_ref[0]
    for p in range(1, GRID):
        sums_ref[p] = sums


def tree(terms):
    while len(terms) > 1:
        terms = [sum(terms[n + 1 : n + 2], terms[n]) for n in range(0, len(terms), 2)]
    return terms[0]


def combine_kernel(
    sums_ref, first_ref, second_ref, inner_ref, edge_ref, out_hbm, turn_ref, result_ref, sent
):
    total = tree([sums_ref[p] for p in range(GRID)])
    moment = [total[n : n + 1] for n in range(6)]
    lane = lax.broadcasted_iota(jnp.int32, (1, 128), 1)
    mode_pair = 16 * lax.axis_index("span") + (lane >> 1)
    ratio = mode_pair.astype(jnp.float32) * (1.0 / KMODES)
    center = 0.2 * (1.0 + SPAN_STIFF * ratio * ratio) + 0.15

    def product(left, right):
        return tree(
            [
                tree(
                    [
                        left[a] * right[power - a]
                        for a in range(len(left))
                        if 0 <= power - a < len(right)
                    ]
                )
                * moment[power]
                for power in range(len(left) + len(right) - 1)
            ]
        )

    def operator(c):
        shifted = [center * v for v in c] + [0.0]
        return [shifted[0]] + [shifted[a + 1] + c[a] for a in range(len(c))]

    residual = [jnp.ones((1, 128), jnp.float32)]
    direction = residual
    result = [0.0, 0.0, 0.0]
    norm = moment[0]
    inverse = 1.0 / norm
    for step in range(ITERS):
        applied = operator(direction)
        length = norm / product(direction, applied)
        for a in range(len(direction)):
            result[a] = result[a] + length * direction[a]
        if step < ITERS - 1:
            padded = residual + [0.0]
            residual = [padded[a] - length * applied[a] for a in range(len(applied))]
            fresh = product(residual, residual)
            ratio = fresh * inverse
            norm = fresh
            inverse = 1.0 / norm
            padded = direction + [0.0]
            direction = [residual[a] + ratio * padded[a] for a in range(len(residual))]
    turn_ref[...] = jnp.zeros((8, 128), jnp.float32)
    for a in range(3):
        turn_ref[a : a + 1, :] = result[a]
    turned = turn_ref[...].T[0:32]
    weight = [turned[:, a : a + 1] for a in range(3)]
    copies = []
    for j in range(5):
        third = inner_ref[j - 1] if 0 < j < 4 else edge_ref[j // 4]
        result_ref[j] = weight[0] * first_ref[j] + weight[1] * second_ref[j] + weight[2] * third
        copies.append(pltpu.make_async_copy(result_ref.at[j], out_hbm.at[j], sent.at[j]))
        copies[j].start()
    for copy in copies:
        copy.wait()


def call(kernel, out_shapes, *args, smem=(), anywhere=(), scratch=(), out_space=pltpu.VMEM, covers=True):
    vmem = pl.BlockSpec(memory_space=pltpu.VMEM)
    spaces = {n: pl.BlockSpec(memory_space=pltpu.SMEM) for n in smem}
    spaces |= {n: pl.BlockSpec(memory_space=pltpu.HBM) for n in anywhere}
    return pl.pallas_call(
        kernel,
        out_shape=[jax.ShapeDtypeStruct(s, jnp.float32) for s in out_shapes],
        in_specs=[spaces.get(n, vmem) for n in range(len(args))],
        out_specs=[pl.BlockSpec(memory_space=out_space)] * len(out_shapes),
        scratch_shapes=list(scratch),
        cost_estimate=None if covers else pl.CostEstimate(flops=0, bytes_accessed=0, transcendentals=0),
        compiler_params=pltpu.CompilerParams(vmem_limit_bytes=16 * 1024 * 1024),
    )(*args)


def swap_traces(cross, chip):
    partner = [(p, (p + 1) % GRID if p % 2 else (p - 1) % GRID) for p in range(GRID)]
    chip = lax.ppermute(chip, "plane", [(p, p ^ 1) for p in range(GRID)])
    cross = lax.ppermute(cross, "plane", partner)
    return cross, chip


def on_device(state, wall_tag):
    table = wave_table()
    (packed,) = call(
        pack_kernel, [(16, 56, 128)],
        pltpu.with_memory_space_constraint(jnp.transpose(state, (1, 0, 2)), pltpu.HBM),
        anywhere=(0,),
        scratch=[
            pltpu.VMEM((800, 128), jnp.float32), pltpu.VMEM((5, 32, 640), jnp.float32),
            pltpu.VMEM((640, 640), jnp.bfloat16), pltpu.SemaphoreType.DMA(()),
        ],
    )
    modal = lax.all_to_all(packed, "span", 0, 0, tiled=True)
    trace, rows = (2, 40, 256), (40, PLANES)
    field, side, edge, *modal_traces, cross, chip = call(
        volume_kernel,
        [(200, PLANES), (16, PLANES), (80, PLANES), trace, trace, rows, rows], modal, table,
    )
    modal_traces = swap_traces(*modal_traces)
    rhs_traces = swap_traces(cross, chip)
    (inside,) = call(
        inside_kernel, [(2, 256, 256)], modal, field, side, edge, table, covers=False,
        scratch=[pltpu.VMEM((120, PLANES), jnp.float32)],
    )
    lift, base = call(
        lift_kernel, [(80, PLANES), (2, 80, 256)], wall_tag, field, *modal_traces, table,
        smem=(0,), scratch=[pltpu.VMEM((80, PLANES), jnp.float32)], covers=False,
    )
    (sent,) = call(facing_kernel, [(16, 56, 128)], inside, lift, base, *rhs_traces, table)
    load = lax.all_to_all(sent, "span", 0, 0, tiled=True)
    nodes, trace = (25, 32, 128), (4, 32, 128)
    edges, inner_rows = (10, 32, 128), (15, 32, 128)
    first, edge, cross, chip = call(first_kernel, [nodes, edges, trace, trace], load)
    cross, chip = swap_traces(cross, chip)
    (filled,) = call(fill_kernel, [inner_rows], first)
    second, edge, cross, chip = call(
        second_kernel, [nodes, edges, trace, trace], edge, filled, cross, chip, first
    )
    cross, chip = swap_traces(cross, chip)
    (filled,) = call(fill_kernel, [inner_rows], second)
    (packed,) = call(
        early_kernel, [(8, 128)], first, second, edge, filled,
        scratch=[pltpu.VMEM((4, 32, 128), jnp.float32)],
    )
    natural = [
        call(
            natural_kernel, [(5, 32, 640)], vector,
            scratch=[pltpu.VMEM((800, 128), jnp.float32)],
        )[0]
        for vector in (first, second)
    ]
    (inside,) = call(
        inner_kernel, [(3, 32, 640)], filled, second,
        scratch=[pltpu.VMEM((480, 128), jnp.float32)],
    )
    edges, sums = call(
        third_kernel, [(2, 32, 640), (16, 8, 128)], edge, filled, cross, chip, second,
        packed,
        scratch=[pltpu.VMEM((2, 32, 128), jnp.float32), pltpu.VMEM((320, 128), jnp.float32)],
    )
    sums = lax.all_to_all(sums, "plane", 0, 0, tiled=True)
    (columns,) = call(
        combine_kernel, [(5, 32, 640)], sums, *natural, inside, edges,
        out_space=pltpu.HBM,
        scratch=[
            pltpu.VMEM((8, 128), jnp.float32), pltpu.VMEM((5, 32, 640), jnp.float32),
            pltpu.SemaphoreType.DMA((5,)),
        ],
    )
    return jnp.transpose(columns, (1, 0, 2))


def solution(mesh):
    return jax.shard_map(
        on_device,
        mesh=mesh,
        in_specs=(P("span", "plane", None), P()),
        out_specs=P("span", "plane", None),
        check_vma=False,
    )
```

```python
import math

import jax
import jax.numpy as jnp
import numpy as np
from jax import lax
from jax.experimental import pallas as pl
from jax.experimental.pallas import tpu as pltpu
from jax.sharding import PartitionSpec as P


KMODES = 256
PLANES = 768
HALF = 384
ITERS = 3
GRID = 16
STEP_SIZE = 0.03
VISCOUS = 0.05
SPAN_STIFF = 4.0


def gll_tables():
    abscissae = np.array([-1.0, -math.sqrt(3.0 / 7.0), 0.0, math.sqrt(3.0 / 7.0), 1.0])
    weights = np.array([0.1, 49.0 / 90.0, 32.0 / 45.0, 49.0 / 90.0, 0.1])
    squared = abscissae * abscissae
    legendre = (35.0 * squared * squared - 30.0 * squared + 3.0) / 8.0
    identity = np.eye(5)
    spacing = abscissae[:, None] - abscissae[None, :] + identity
    differ = np.where(identity > 0, 0.0, legendre[:, None] / legendre[None, :] / spacing)
    differ[0, 0] = -5.0
    differ[4, 4] = 5.0
    stiffness = differ.T @ (weights[:, None] * differ)
    return differ, weights, stiffness


DIFFER, WEIGHTS, STIFFNESS = gll_tables()


def split_table(table):
    high = table.astype(np.float32).astype(jnp.bfloat16)
    low = (table - high.astype(np.float64)).astype(np.float32).astype(jnp.bfloat16)
    return jnp.asarray(np.stack([high, low]))


def wave_table():
    plane = np.arange(HALF)
    waves = []
    for parity in range(2):
        k = 2 * np.arange(128) + parity
        angle = (k[:, None] * plane[None, :] % PLANES) * (2.0 * math.pi / PLANES)
        waves.append(np.concatenate([np.cos(angle), np.sin(angle)]))
    return split_table(np.stack(waves))


def dot(left, right, contract):
    return lax.dot_general(
        left, right, (contract, ((), ())), preferred_element_type=jnp.float32
    )


def halves(value):
    high = value.astype(jnp.bfloat16)
    low = (value - high.astype(jnp.float32)).astype(jnp.bfloat16)
    return high, low


def dot_split(left, right, contract):
    (left_high, left_low), (right_high, right_low) = left, right
    return (
        dot(left_high, right_low, contract)
        + dot(left_low, right_high, contract)
        + dot(left_high, right_high, contract)
    )


def lanes_of(values, index):
    return jnp.take_along_axis(values, index, axis=1)


def merge_columns(tiles):
    lane = lax.broadcasted_iota(jnp.int32, tiles[0].shape, 1)
    out = []
    for t in range(5):
        column = lane + 128 * t
        element = (column * 13108) >> 16
        node = column - 5 * element
        picked = lanes_of(tiles[0], element)
        for i in range(1, 5):
            picked = jnp.where(node == i, lanes_of(tiles[i], element), picked)
        out.append(picked)
    return out


def exchange_chunks(values):
    values = list(values)
    lane = lax.broadcasted_iota(jnp.int32, values[0].shape, 1)
    for bit in (1, 2, 4, 8):
        upper = (lane & (8 * bit)) != 0
        other = lane ^ (8 * bit)
        for a in range(16):
            if a & bit == 0:
                first, second = values[a], values[a | bit]
                if first is None:
                    continue
                if second is None:
                    second = jnp.zeros_like(first)
                moved = jnp.where(upper, first, second)
                if bit == 8:
                    moved = pltpu.roll(moved, 64, 1)
                else:
                    moved = lanes_of(moved, other)
                values[a] = jnp.where(upper, moved, first)
                values[a | bit] = jnp.where(upper, second, moved)
    return values


def column_order():
    column = lax.broadcasted_iota(jnp.int32, (640, 128), 0)
    element = lax.broadcasted_iota(jnp.int32, (640, 128), 1)
    tiles = [jnp.where(column == 5 * element + i, 1.0, 0.0).astype(jnp.bfloat16) for i in range(5)]
    return jnp.concatenate(tiles, axis=1)


def pack_rows(out_ref, d, whole, rest, count):
    out_ref[d, 0:32, :] = whole
    lane = lax.broadcasted_iota(jnp.int32, (8, 128), 1)
    free = 16 - count
    for g in range(3):
        tile = rest[8 * g : 8 * g + 8]
        if g * free < count:
            shift = 8 * (count - g * free)
            tile = jnp.where(lane < 8 * count, tile, pltpu.roll(rest[24:32], shift % 128, 1))
        out_ref[d, 32 + 8 * g : 40 + 8 * g, :] = tile


def unpack_last(tiles, count):
    lane = lax.broadcasted_iota(jnp.int32, (8, 128), 1)
    free = 16 - count
    last = pltpu.roll(tiles[0], 128 - 8 * count, 1)
    for g in range(1, 3):
        if g * free < count:
            shift = 8 * (count - g * free)
            last = jnp.where(lane < 8 * g * free, last, pltpu.roll(tiles[g], (128 - shift) % 128, 1))
    return last


def pack_kernel(state_hbm, out_ref, chunk_ref, state_ref, order_ref, arrived):
    copy = pltpu.make_async_copy(state_hbm, state_ref, arrived)
    copy.start()
    order_ref[...] = column_order()
    copy.wait()
    stacked = jnp.concatenate([state_ref[j] for j in range(5)], axis=0)
    order = order_ref[...]
    contract = ((1,), (0,))
    high, low = halves(stacked)
    nodes = dot(low, order, contract) + dot(high, order, contract)
    for i in range(5):
        chunk_ref[160 * i : 160 * i + 160, :] = nodes[:, 128 * i : 128 * i + 128]
    chunk = [
        jnp.concatenate(
            [chunk_ref[pl.ds(160 * i + 32 * j + t, 8, stride=4), :] for t in range(4)], axis=0
        )
        for j in range(5)
        for i in range(5)
    ]
    lane = lax.broadcasted_iota(jnp.int32, (32, 128), 1) & 7
    sides = [jnp.zeros((32, 128), jnp.float32), jnp.zeros((32, 128), jnp.float32)]
    for j in range(5):
        at = j & 3
        side = jnp.where(lane == at, pltpu.roll(chunk[j * 5 + 4], 1 + at, 1), sides[j // 4])
        sides[j // 4] = jnp.where(lane == 7 - at, pltpu.roll(chunk[j * 5], 127 - at, 1), side)
    chunk = chunk + sides
    whole = exchange_chunks(chunk[:16])
    rest = exchange_chunks(chunk[16:] + [None] * 5)
    for d in range(GRID):
        pack_rows(out_ref, d, whole[d], rest[d], 11)


def turn(modal_ref, cross_ref, chip_ref):
    last = [
        unpack_last([modal_ref[s, 32 + 8 * g : 40 + 8 * g, :] for g in range(3)], 11)
        for s in range(GRID)
    ]
    nodal = []
    for parity in range(2):
        whole, rest = [], []
        for t in range(2):
            group = 2 * parity + t
            for s in range(GRID):
                whole.append(modal_ref[s, 8 * group : 8 * group + 8, :])
                rest.append(
                    last[s] if group == 3 else modal_ref[s, 32 + 8 * group : 40 + 8 * group, :]
                )
        turned = [jnp.concatenate(part, axis=0).T for part in (whole, rest)]
        nodal.append(jnp.concatenate([turned[0], turned[1][0:88]], axis=0))
        cross_ref[parity], chip_ref[parity] = to_partners(turned[0][0:40], turned[1][32:72])
    return nodal


def synthesize(nodal, table_ref):
    part = [
        dot_split(
            halves(nodal[parity]), (table_ref[0, parity], table_ref[1, parity]), ((1,), (0,))
        )
        for parity in range(2)
    ]
    scale = 1.0 / math.sqrt(KMODES)
    return scale * (part[0] + part[1]), scale * (part[0] - part[1])


def two_point(left, right):
    mean = (left * left + left * right + right * right) * (1.0 / 6.0)
    speed = jnp.maximum(jnp.abs(left), jnp.abs(right))
    return mean - 0.5 * speed * (right - left)


def row_rhs(field_ref, side_ref, lanes, rows):
    row = lax.broadcasted_iota(jnp.int32, (8, 128), 0)
    f = [field_ref[8 * n : 8 * n + 8, lanes] for n in range(25)]
    square = [v * v for v in f]
    out = {}
    for j in rows:
        for i in range(5):
            n = j * 5 + i
            plain = None
            power = None
            for other in range(5):
                terms = [(DIFFER[i][other], j * 5 + other), (DIFFER[j][other], other * 5 + i)]
                for weight, m in terms:
                    if weight == 0.0:
                        continue
                    weight = float(weight) / -3.0
                    plain = weight * f[m] if plain is None else plain + weight * f[m]
                    power = weight * square[m] if power is None else power + weight * square[m]
            total = power + f[n] * plain
            own = (i == 4) + (j == 4) - (i == 0) - (j == 0)
            if own:
                total = total + (5.0 * own) * square[n]
            if i == 0 or i == 4:
                at = j & 3
                side = side_ref[8 * (j // 4) : 8 * (j // 4) + 8, lanes]
                if at:
                    side = pltpu.roll(side, 8 - at if i == 0 else at, 0)
                if i == 0:
                    left = jnp.where(row == 0, side, pltpu.roll(f[j * 5 + 4], 1, 0))
                    total = total + 10.0 * two_point(left, f[n])
                else:
                    right = jnp.where(row == 7, side, pltpu.roll(f[j * 5], 7, 0))
                    total = total - 10.0 * two_point(f[n], right)
            out[n] = total
    return out


def each_lane_block(body):
    def step(block, carry):
        body(pl.ds(pl.multiple_of(block * 128, 128), 128))
        return carry

    lax.fori_loop(0, PLANES // 128, step, 0)


def volume_kernel(
    modal_ref, table_ref, field_ref, side_ref, edge_ref, modal_cross_ref, modal_chip_ref, cross_ref,
    chip_ref,
):
    nodal = turn(modal_ref, modal_cross_ref, modal_chip_ref)
    pair = synthesize(nodal, table_ref)
    for q in range(2):
        field_ref[:, HALF * q : HALF * q + HALF] = pair[q][0:200]
        side_ref[:, HALF * q : HALF * q + HALF] = pair[q][200:216]

    def body(lanes):
        total = row_rhs(field_ref, side_ref, lanes, (0, 4))
        for i in range(5):
            rows = slice(8 * i, 8 * i + 8)
            edge_ref[rows, lanes] = total[i]
            edge_ref[40 + 8 * i : 48 + 8 * i, lanes] = total[20 + i]
            cross_ref[rows, lanes], chip_ref[rows, lanes] = to_partners(total[i], total[20 + i])

    each_lane_block(body)


def project(planar, parity, table_ref):
    folded = planar[:, :HALF] + planar[:, HALF:] if parity == 0 else planar[:, :HALF] - planar[:, HALF:]
    return dot_split((table_ref[0, parity], table_ref[1, parity]), halves(folded), ((1,), (1,)))


def tendency(parity, from_rhs, from_flux):
    k = 2 * lax.broadcasted_iota(jnp.int32, (128, 128), 0) + parity
    scale = jnp.where(k == 0, 1.0, 2.0) * (math.sqrt(KMODES) / PLANES * STEP_SIZE)
    ratio = k.astype(jnp.float32) * (1.0 / KMODES)
    return (
        scale * (from_rhs[0:128] - ratio * from_flux[128:256]),
        scale * (from_rhs[128:256] + ratio * from_flux[0:128]),
    )


def inside_kernel(modal_ref, field_ref, side_ref, edge_ref, table_ref, out_ref, rhs_ref):
    last = [
        unpack_last([modal_ref[s, 32 + 8 * g : 40 + 8 * g, :] for g in range(3)], 11)
        for s in range(GRID)
    ]

    def body(lanes):
        total = row_rhs(field_ref, side_ref, lanes, (1, 2, 3))
        for n in range(5, 20):
            rhs_ref[8 * n - 40 : 8 * n - 32, lanes] = total[n]

    each_lane_block(body)
    field = field_ref[...]
    flux = 0.5 * field * field
    rhs = jnp.concatenate([edge_ref[0:40, :], rhs_ref[...], edge_ref[40:80, :]], axis=0)
    tail = jnp.zeros((56, PLANES), jnp.float32)
    flux = jnp.concatenate([flux, tail], axis=0)
    rhs = jnp.concatenate([rhs, tail], axis=0)
    for parity in range(2):
        from_rhs = project(rhs, parity, table_ref)
        from_flux = project(flux, parity, table_ref)
        for half in range(2):
            lanes = slice(128 * half, 128 * half + 128)
            change = tendency(parity, from_rhs[:, lanes], from_flux[:, lanes])
            for t in range(2):
                first = 16 * parity + 8 * t + 32 * half
                modal = jnp.concatenate(
                    last if first == 56 else [modal_ref[s, first : first + 8, :] for s in range(GRID)],
                    axis=0,
                )
                out_ref[parity, 128 * t : 128 * t + 128, lanes] = modal + change[t]


def lift_kernel(
    tag_ref, field_ref, cross_ref, chip_ref, table_ref, lift_ref, flux_ref, modal_ref, outer_ref
):
    bottom, top = at_ends()
    span = lax.axis_index("span")
    row = lax.broadcasted_iota(jnp.int32, (8, 128), 0)
    mirror = jnp.ones((8, 128), jnp.float32)
    for e in range(8):
        mirror = jnp.where((row == e) & (tag_ref[8 * span + e] == 1), -1.0, mirror)
    keep_lower = jnp.where(bottom, 0.0, 1.0)
    keep_upper = jnp.where(top, 0.0, 1.0)
    gap = jnp.zeros((48, 256), jnp.float32)
    outer = []
    for parity in range(2):
        below, above = from_partners(cross_ref[parity], chip_ref[parity])
        outer.append(jnp.concatenate([below, above], axis=0))
        modal_ref[parity] = jnp.concatenate(
            [keep_lower * below, keep_upper * above, gap], axis=0
        ).T
    pair = synthesize(outer, table_ref)
    for q in range(2):
        outer_ref[:, HALF * q : HALF * q + HALF] = pair[q]
    mirror = jnp.concatenate([mirror] * 6, axis=1)
    mirror = jnp.concatenate([mirror] * 5, axis=0)
    inside = field_ref[0:40, :]
    below = outer_ref[0:40, :]
    lift_ref[0:40, :] = 10.0 * two_point(jnp.where(bottom, mirror * inside, below), inside)
    flux_ref[0:40, :] = keep_lower * (0.5 * below * below)
    inside = field_ref[160:200, :]
    above = outer_ref[40:80, :]
    lift_ref[40:80, :] = 10.0 * two_point(inside, jnp.where(top, inside, above))
    flux_ref[40:80, :] = keep_upper * (0.5 * above * above)


def facing_kernel(
    inside_ref, lift_ref, flux_ref, facing_ref, cross_ref, chip_ref, table_ref, out_ref
):
    bottom, top = at_ends()
    below, above = from_partners(cross_ref[...], chip_ref[...])
    lift = lift_ref[0:40, :]
    rhs_lower = lift + jnp.where(bottom, 0.0, below - lift)
    lift = lift_ref[40:80, :]
    rhs_upper = jnp.where(top, 0.0, above + lift) - lift
    gap = jnp.zeros((48, PLANES), jnp.float32)
    planar = jnp.concatenate([rhs_lower, rhs_upper, gap, flux_ref[...], gap], axis=0)
    lane = lax.broadcasted_iota(jnp.int32, (128, 128), 1)
    whole, rest = [], []
    for parity in range(2):
        projected = project(planar, parity, table_ref)
        change = tendency(parity, projected[:, 0:128], projected[:, 128:256])
        for t in range(2):
            rows = slice(128 * t, 128 * t + 128)
            extra = change[t] + facing_ref[parity, rows, :]
            lower = jnp.where(lane < 40, extra, 0.0)
            upper = pltpu.roll(jnp.where(lane < 40, 0.0, extra), 120, 1)
            whole.append(inside_ref[parity, rows, 0:128] + lower)
            rest.append(inside_ref[parity, rows, 128:256] + upper)
    for s in range(GRID):
        part = slice(8 * s, 8 * s + 8)
        pack_rows(
            out_ref,
            s,
            jnp.concatenate([group[part] for group in whole], axis=0),
            jnp.concatenate([group[part] for group in rest], axis=0),
            9,
        )


def energy(values, shift):
    total = None
    for j in range(5):
        for i in range(5):
            n = j * 5 + i
            mass = float(WEIGHTS[j] * WEIGHTS[i])
            diagonal = VISCOUS * float(WEIGHTS[j] * STIFFNESS[i][i] + WEIGHTS[i] * STIFFNESS[j][j])
            value = (shift * mass + diagonal) * values[n]
            for other in range(i + 1, 5):
                weight = 2.0 * VISCOUS * float(WEIGHTS[j] * STIFFNESS[i][other])
                value = value + weight * values[j * 5 + other]
            for other in range(j + 1, 5):
                weight = 2.0 * VISCOUS * float(WEIGHTS[i] * STIFFNESS[j][other])
                value = value + weight * values[other * 5 + i]
            term = value * values[n]
            total = term if total is None else total + term
    return total


def at_ends():
    plane = lax.axis_index("plane")
    return plane == 0, plane == GRID - 1


def to_partners(low, high):
    odd = lax.axis_index("plane") % 2 == 1
    return jnp.where(odd, high, low), jnp.where(odd, low, high)


def from_partners(cross, chip):
    odd = lax.axis_index("plane") % 2 == 1
    return jnp.where(odd, chip, cross), jnp.where(odd, cross, chip)


def local_operator(values, shift, rows):
    out = []
    for j in rows:
        line = []
        for i in range(5):
            n = j * 5 + i
            mass = float(WEIGHTS[j] * WEIGHTS[i])
            diagonal = VISCOUS * float(WEIGHTS[j] * STIFFNESS[i][i] + WEIGHTS[i] * STIFFNESS[j][j])
            value = (shift * mass + diagonal) * values[n]
            for other in range(5):
                if other != i:
                    weight = VISCOUS * float(WEIGHTS[j] * STIFFNESS[i][other])
                    value = value + weight * values[j * 5 + other]
                if other != j:
                    weight = VISCOUS * float(WEIGHTS[i] * STIFFNESS[j][other])
                    value = value + weight * values[other * 5 + i]
            line.append(value)
        out += join_columns(line)
    return out


def join_columns(line):
    joint = line[4] + pltpu.roll(line[0], 127, 1)
    return [pltpu.roll(joint, 1, 1), *line[1:4], joint]


def store_edges(values, shift, edge_ref, cross_ref, chip_ref):
    image = local_operator(values, shift, (0, 4))
    for n in range(10):
        edge_ref[n] = image[n]
    for i in range(4):
        cross_ref[i], chip_ref[i] = to_partners(image[i], image[5 + i])


def fill_kernel(vector_ref, inner_ref):
    shift, _ = mode_terms()
    image = local_operator([vector_ref[n] for n in range(25)], shift, (1, 2, 3))
    for n in range(15):
        inner_ref[n] = image[n]


def unassembled(edge_ref, inner_ref):
    return (
        [edge_ref[n] for n in range(5)]
        + [inner_ref[n] for n in range(15)]
        + [edge_ref[5 + n] for n in range(5)]
    )


def assembled(edge_ref, inner_ref, cross_ref, chip_ref):
    values = unassembled(edge_ref, inner_ref)
    bottom, top = at_ends()
    for i in range(4):
        below, above = from_partners(cross_ref[i], chip_ref[i])
        values[i] = values[i] + jnp.where(bottom, 0.0, below)
        values[20 + i] = values[20 + i] + jnp.where(top, 0.0, above)
    values[4] = pltpu.roll(values[0], 127, 1)
    values[24] = pltpu.roll(values[20], 127, 1)
    return values


def mode_terms():
    row = lax.broadcasted_iota(jnp.int32, (32, 128), 0)
    mode_pair = 16 * lax.axis_index("span") + 2 * (row & 7) + (row >> 4)
    ratio = mode_pair.astype(jnp.float32) * (1.0 / KMODES)
    shift = 1.0 + SPAN_STIFF * ratio * ratio
    return shift, 0.2 * shift + 0.15


def inner(left, right):
    bottom, top = at_ends()
    total = None
    for j in range(5):
        part = None
        for i in range(5):
            term = left[j * 5 + i] * right[j * 5 + i]
            term = term if 0 < i < 4 else 0.5 * term
            part = term if part is None else part + term
        if j == 0:
            part = jnp.where(bottom, 1.0, 0.5) * part
        elif j == 4:
            part = jnp.where(top, 1.0, 0.5) * part
        total = part if total is None else total + part
    return total


def first_kernel(modal_ref, vector_ref, edge_ref, cross_ref, chip_ref):
    shift, _ = mode_terms()
    values = exchange_chunks([modal_ref[s, 0:32, :] for s in range(GRID)])
    rest = []
    for s in range(GRID):
        tiles = [modal_ref[s, 32 + 8 * g : 40 + 8 * g, :] for g in range(3)]
        rest.append(jnp.concatenate(tiles + [unpack_last(tiles, 9)], axis=0))
    values += exchange_chunks(rest)
    values = [float(WEIGHTS[n // 5] * WEIGHTS[n % 5]) * values[n] for n in range(25)]
    vector = []
    for j in range(5):
        vector += join_columns(values[5 * j : 5 * j + 5])
    for n in range(25):
        vector_ref[n] = vector[n]
    store_edges(vector, shift, edge_ref, cross_ref, chip_ref)


def second_kernel(
    edge_in_ref, inner_ref, cross_in_ref, chip_in_ref, before_ref, vector_ref, edge_ref, cross_ref,
    chip_ref,
):
    shift, center = mode_terms()
    applied = assembled(edge_in_ref, inner_ref, cross_in_ref, chip_in_ref)
    vector = [applied[n] - center * before_ref[n] for n in range(25)]
    for n in range(25):
        vector_ref[n] = vector[n]
    store_edges(vector, shift, edge_ref, cross_ref, chip_ref)


def mode_sums(moment, turn_ref):
    for t in range(4):
        turn_ref[pl.ds(t, 8, stride=4), :] = moment[8 * t : 8 * t + 8]
    return jnp.sum(turn_ref[...].T, axis=0, keepdims=True)


def early_kernel(first_ref, second_ref, edge_ref, inner_ref, packed_ref, turn_ref):
    _, center = mode_terms()
    first = [first_ref[n] for n in range(25)]
    second = [second_ref[n] for n in range(25)]
    square = inner(second, second)
    product = None
    image = unassembled(edge_ref, inner_ref)
    for n in range(25):
        term = second[n] * image[n]
        term = term if 0 < n % 5 < 4 else 0.5 * term
        product = term if product is None else product + term
    moments = [inner(first, first), inner(first, second), square, product - center * square]
    packed_ref[...] = jnp.zeros((8, 128), jnp.float32)
    for n, moment in enumerate(moments):
        packed_ref[n : n + 1, 0:32] = mode_sums(moment, turn_ref.at[n])


def store_natural(tiles, out_ref, row, column_ref):
    columns = merge_columns(tiles)
    for i in range(5):
        first = 32 * (5 * row + i)
        for t in range(4):
            column_ref[pl.ds(first + t, 8, stride=4), :] = columns[i][8 * t : 8 * t + 8]
        out_ref[row, :, 128 * i : 128 * i + 128] = column_ref[first : first + 32, :]


def natural_kernel(vector_ref, out_ref, column_ref):
    for j in range(5):
        store_natural([vector_ref[j * 5 + i] for i in range(5)], out_ref, j, column_ref)


def inner_kernel(inner_ref, second_ref, out_ref, column_ref):
    _, center = mode_terms()
    for j in range(1, 4):
        tiles = [
            inner_ref[n - 5] - center * second_ref[n] for n in range(5 * j, 5 * j + 5)
        ]
        store_natural(tiles, out_ref, j - 1, column_ref)


def third_kernel(
    edge_in_ref, inner_ref, cross_in_ref, chip_in_ref, second_ref, packed_ref, edge_ref, sums_ref,
    turn_ref, column_ref,
):
    shift, center = mode_terms()
    applied = assembled(edge_in_ref, inner_ref, cross_in_ref, chip_in_ref)
    second = [second_ref[n] for n in range(25)]
    third = [applied[n] - center * second[n] for n in range(25)]
    for row in range(2):
        store_natural(third[20 * row : 20 * row + 5], edge_ref, row, column_ref)
    fourth = inner(third, third)
    moments = [fourth, energy(third, shift) - center * fourth]
    sums_ref[0] = packed_ref[...]
    for n, moment in enumerate(moments):
        sums_ref[0, 4 + n : 5 + n, 0:32] = mode_sums(moment, turn_ref.at[n])
    sums = sums_ref[0]
    for p in range(1, GRID):
        sums_ref[p] = sums


def tree(terms):
    while len(terms) > 1:
        terms = [sum(terms[n + 1 : n + 2], terms[n]) for n in range(0, len(terms), 2)]
    return terms[0]


def combine_kernel(
    sums_ref, first_ref, second_ref, inner_ref, edge_ref, out_hbm, turn_ref, result_ref, sent
):
    total = tree([sums_ref[p] for p in range(GRID)])
    moment = [total[n : n + 1] for n in range(6)]
    lane = lax.broadcasted_iota(jnp.int32, (1, 128), 1)
    mode_pair = 16 * lax.axis_index("span") + (lane >> 1)
    ratio = mode_pair.astype(jnp.float32) * (1.0 / KMODES)
    center = 0.2 * (1.0 + SPAN_STIFF * ratio * ratio) + 0.15

    def product(left, right):
        return tree(
            [
                tree(
                    [
                        left[a] * right[power - a]
                        for a in range(len(left))
                        if 0 <= power - a < len(right)
                    ]
                )
                * moment[power]
                for power in range(len(left) + len(right) - 1)
            ]
        )

    def operator(c):
        shifted = [center * v for v in c] + [0.0]
        return [shifted[0]] + [shifted[a + 1] + c[a] for a in range(len(c))]

    residual = [jnp.ones((1, 128), jnp.float32)]
    direction = residual
    result = [0.0, 0.0, 0.0]
    norm = moment[0]
    inverse = 1.0 / norm
    for step in range(ITERS):
        applied = operator(direction)
        length = norm / product(direction, applied)
        for a in range(len(direction)):
            result[a] = result[a] + length * direction[a]
        if step < ITERS - 1:
            padded = residual + [0.0]
            residual = [padded[a] - length * applied[a] for a in range(len(applied))]
            fresh = product(residual, residual)
            ratio = fresh * inverse
            norm = fresh
            inverse = 1.0 / norm
            padded = direction + [0.0]
            direction = [residual[a] + ratio * padded[a] for a in range(len(residual))]
    turn_ref[...] = jnp.zeros((8, 128), jnp.float32)
    for a in range(3):
        turn_ref[a : a + 1, :] = result[a]
    turned = turn_ref[...].T[0:32]
    weight = [turned[:, a : a + 1] for a in range(3)]
    copies = []
    for j in range(5):
        third = inner_ref[j - 1] if 0 < j < 4 else edge_ref[j // 4]
        result_ref[j] = weight[0] * first_ref[j] + weight[1] * second_ref[j] + weight[2] * third
        copies.append(pltpu.make_async_copy(result_ref.at[j], out_hbm.at[j], sent.at[j]))
        copies[j].start()
    for copy in copies:
        copy.wait()


def call(kernel, out_shapes, *args, smem=(), anywhere=(), scratch=(), out_space=pltpu.VMEM, covers=True):
    vmem = pl.BlockSpec(memory_space=pltpu.VMEM)
    spaces = {n: pl.BlockSpec(memory_space=pltpu.SMEM) for n in smem}
    spaces |= {n: pl.BlockSpec(memory_space=pltpu.HBM) for n in anywhere}
    return pl.pallas_call(
        kernel,
        out_shape=[jax.ShapeDtypeStruct(s, jnp.float32) for s in out_shapes],
        in_specs=[spaces.get(n, vmem) for n in range(len(args))],
        out_specs=[pl.BlockSpec(memory_space=out_space)] * len(out_shapes),
        scratch_shapes=list(scratch),
        cost_estimate=None if covers else pl.CostEstimate(flops=0, bytes_accessed=0, transcendentals=0),
        compiler_params=pltpu.CompilerParams(vmem_limit_bytes=16 * 1024 * 1024),
    )(*args)


def swap_traces(cross, chip):
    partner = [(p, (p + 1) % GRID if p % 2 else (p - 1) % GRID) for p in range(GRID)]
    chip = lax.ppermute(chip, "plane", [(p, p ^ 1) for p in range(GRID)])
    cross = lax.ppermute(cross, "plane", partner)
    return cross, chip


def on_device(state, wall_tag):
    table = wave_table()
    (packed,) = call(
        pack_kernel, [(16, 56, 128)],
        pltpu.with_memory_space_constraint(jnp.transpose(state, (1, 0, 2)), pltpu.HBM),
        anywhere=(0,),
        scratch=[
            pltpu.VMEM((800, 128), jnp.float32), pltpu.VMEM((5, 32, 640), jnp.float32),
            pltpu.VMEM((640, 640), jnp.bfloat16), pltpu.SemaphoreType.DMA(()),
        ],
    )
    modal = lax.all_to_all(packed, "span", 0, 0, tiled=True)
    trace, rows = (2, 40, 256), (40, PLANES)
    field, side, edge, *modal_traces, cross, chip = call(
        volume_kernel,
        [(200, PLANES), (16, PLANES), (80, PLANES), trace, trace, rows, rows], modal, table,
    )
    modal_traces = swap_traces(*modal_traces)
    rhs_traces = swap_traces(cross, chip)
    (inside,) = call(
        inside_kernel, [(2, 256, 256)], modal, field, side, edge, table, covers=False,
        scratch=[pltpu.VMEM((120, PLANES), jnp.float32)],
    )
    lift, flux, facing = call(
        lift_kernel, [(80, PLANES), (80, PLANES), (2, 256, 128)], wall_tag, field,
        *modal_traces, table, smem=(0,), scratch=[pltpu.VMEM((80, PLANES), jnp.float32)],
        covers=False,
    )
    (sent,) = call(facing_kernel, [(16, 56, 128)], inside, lift, flux, facing, *rhs_traces, table)
    load = lax.all_to_all(sent, "span", 0, 0, tiled=True)
    nodes, trace = (25, 32, 128), (4, 32, 128)
    edges, inner_rows = (10, 32, 128), (15, 32, 128)
    first, edge, cross, chip = call(first_kernel, [nodes, edges, trace, trace], load)
    cross, chip = swap_traces(cross, chip)
    (filled,) = call(fill_kernel, [inner_rows], first)
    second, edge, cross, chip = call(
        second_kernel, [nodes, edges, trace, trace], edge, filled, cross, chip, first
    )
    cross, chip = swap_traces(cross, chip)
    (filled,) = call(fill_kernel, [inner_rows], second)
    (packed,) = call(
        early_kernel, [(8, 128)], first, second, edge, filled,
        scratch=[pltpu.VMEM((4, 32, 128), jnp.float32)],
    )
    natural = [
        call(
            natural_kernel, [(5, 32, 640)], vector,
            scratch=[pltpu.VMEM((800, 128), jnp.float32)],
        )[0]
        for vector in (first, second)
    ]
    (inside,) = call(
        inner_kernel, [(3, 32, 640)], filled, second,
        scratch=[pltpu.VMEM((480, 128), jnp.float32)],
    )
    edges, sums = call(
        third_kernel, [(2, 32, 640), (16, 8, 128)], edge, filled, cross, chip, second,
        packed,
        scratch=[pltpu.VMEM((2, 32, 128), jnp.float32), pltpu.VMEM((320, 128), jnp.float32)],
    )
    sums = lax.all_to_all(sums, "plane", 0, 0, tiled=True)
    (columns,) = call(
        combine_kernel, [(5, 32, 640)], sums, *natural, inside, edges,
        out_space=pltpu.HBM,
        scratch=[
            pltpu.VMEM((8, 128), jnp.float32), pltpu.VMEM((5, 32, 640), jnp.float32),
            pltpu.SemaphoreType.DMA((5,)),
        ],
    )
    return jnp.transpose(columns, (1, 0, 2))


def solution(mesh):
    return jax.shard_map(
        on_device,
        mesh=mesh,
        in_specs=(P("span", "plane", None), P()),
        out_specs=P("span", "plane", None),
        check_vma=False,
    )
```

```python
import math

import jax
import jax.numpy as jnp
import numpy as np
from jax import lax
from jax.experimental import pallas as pl
from jax.experimental.pallas import tpu as pltpu
from jax.sharding import PartitionSpec as P


KMODES = 256
PLANES = 768
HALF = 384
ITERS = 3
GRID = 16
STEP_SIZE = 0.03
VISCOUS = 0.05
SPAN_STIFF = 4.0


def gll_tables():
    abscissae = np.array([-1.0, -math.sqrt(3.0 / 7.0), 0.0, math.sqrt(3.0 / 7.0), 1.0])
    weights = np.array([0.1, 49.0 / 90.0, 32.0 / 45.0, 49.0 / 90.0, 0.1])
    squared = abscissae * abscissae
    legendre = (35.0 * squared * squared - 30.0 * squared + 3.0) / 8.0
    identity = np.eye(5)
    spacing = abscissae[:, None] - abscissae[None, :] + identity
    differ = np.where(identity > 0, 0.0, legendre[:, None] / legendre[None, :] / spacing)
    differ[0, 0] = -5.0
    differ[4, 4] = 5.0
    stiffness = differ.T @ (weights[:, None] * differ)
    return differ, weights, stiffness


DIFFER, WEIGHTS, STIFFNESS = gll_tables()


def split_table(table):
    high = table.astype(np.float32).astype(jnp.bfloat16)
    low = (table - high.astype(np.float64)).astype(np.float32).astype(jnp.bfloat16)
    return jnp.asarray(np.stack([high, low]))


def wave_table():
    plane = np.arange(HALF)
    waves = []
    for parity in range(2):
        k = 2 * np.arange(128) + parity
        angle = (k[:, None] * plane[None, :] % PLANES) * (2.0 * math.pi / PLANES)
        waves.append(np.concatenate([np.cos(angle), np.sin(angle)]))
    return split_table(np.stack(waves))


def dot(left, right, contract):
    return lax.dot_general(
        left, right, (contract, ((), ())), preferred_element_type=jnp.float32
    )


def halves(value):
    high = value.astype(jnp.bfloat16)
    low = (value - high.astype(jnp.float32)).astype(jnp.bfloat16)
    return high, low


def dot_split(left, right, contract):
    (left_high, left_low), (right_high, right_low) = left, right
    return (
        dot(left_high, right_low, contract)
        + dot(left_low, right_high, contract)
        + dot(left_high, right_high, contract)
    )


def lanes_of(values, index):
    return jnp.take_along_axis(values, index, axis=1)


def merge_columns(tiles):
    lane = lax.broadcasted_iota(jnp.int32, tiles[0].shape, 1)
    out = []
    for t in range(5):
        column = lane + 128 * t
        element = (column * 13108) >> 16
        node = column - 5 * element
        picked = lanes_of(tiles[0], element)
        for i in range(1, 5):
            picked = jnp.where(node == i, lanes_of(tiles[i], element), picked)
        out.append(picked)
    return out


def exchange_chunks(values):
    values = list(values)
    lane = lax.broadcasted_iota(jnp.int32, values[0].shape, 1)
    for bit in (1, 2, 4, 8):
        upper = (lane & (8 * bit)) != 0
        other = lane ^ (8 * bit)
        for a in range(16):
            if a & bit == 0:
                first, second = values[a], values[a | bit]
                if first is None:
                    continue
                if second is None:
                    second = jnp.zeros_like(first)
                moved = jnp.where(upper, first, second)
                if bit == 8:
                    moved = pltpu.roll(moved, 64, 1)
                else:
                    moved = lanes_of(moved, other)
                values[a] = jnp.where(upper, moved, first)
                values[a | bit] = jnp.where(upper, second, moved)
    return values


def column_order():
    column = lax.broadcasted_iota(jnp.int32, (640, 128), 0)
    element = lax.broadcasted_iota(jnp.int32, (640, 128), 1)
    tiles = [jnp.where(column == 5 * element + i, 1.0, 0.0).astype(jnp.bfloat16) for i in range(5)]
    return jnp.concatenate(tiles, axis=1)


def pack_rows(out_ref, d, whole, rest, count):
    out_ref[d, 0:32, :] = whole
    lane = lax.broadcasted_iota(jnp.int32, (8, 128), 1)
    free = 16 - count
    for g in range(3):
        tile = rest[8 * g : 8 * g + 8]
        if g * free < count:
            shift = 8 * (count - g * free)
            tile = jnp.where(lane < 8 * count, tile, pltpu.roll(rest[24:32], shift % 128, 1))
        out_ref[d, 32 + 8 * g : 40 + 8 * g, :] = tile


def unpack_last(tiles, count):
    lane = lax.broadcasted_iota(jnp.int32, (8, 128), 1)
    free = 16 - count
    last = pltpu.roll(tiles[0], 128 - 8 * count, 1)
    for g in range(1, 3):
        if g * free < count:
            shift = 8 * (count - g * free)
            last = jnp.where(lane < 8 * g * free, last, pltpu.roll(tiles[g], (128 - shift) % 128, 1))
    return last


def pack_kernel(state_hbm, out_ref, chunk_ref, state_ref, order_ref, arrived):
    copies = [
        pltpu.make_async_copy(state_hbm.at[j], state_ref.at[j], arrived.at[j]) for j in range(5)
    ]
    for copy in copies:
        copy.start()
    order_ref[...] = column_order()
    for copy in copies:
        copy.wait()
    stacked = jnp.concatenate([state_ref[j] for j in range(5)], axis=0)
    order = order_ref[...]
    contract = ((1,), (0,))
    both = dot(jnp.concatenate(halves(stacked), axis=0), order, contract)
    nodes = both[160:] + both[:160]
    for i in range(5):
        chunk_ref[160 * i : 160 * i + 160, :] = nodes[:, 128 * i : 128 * i + 128]
    chunk = [
        jnp.concatenate(
            [chunk_ref[pl.ds(160 * i + 32 * j + t, 8, stride=4), :] for t in range(4)], axis=0
        )
        for j in range(5)
        for i in range(5)
    ]
    lane = lax.broadcasted_iota(jnp.int32, (32, 128), 1) & 7
    sides = [jnp.zeros((32, 128), jnp.float32), jnp.zeros((32, 128), jnp.float32)]
    for j in range(5):
        at = j & 3
        side = jnp.where(lane == at, pltpu.roll(chunk[j * 5 + 4], 1 + at, 1), sides[j // 4])
        sides[j // 4] = jnp.where(lane == 7 - at, pltpu.roll(chunk[j * 5], 127 - at, 1), side)
    chunk = chunk + sides
    whole = exchange_chunks(chunk[:16])
    rest = exchange_chunks(chunk[16:] + [None] * 5)
    for d in range(GRID):
        pack_rows(out_ref, d, whole[d], rest[d], 11)


def turn(modal_ref, cross_ref, chip_ref):
    last = [
        unpack_last([modal_ref[s, 32 + 8 * g : 40 + 8 * g, :] for g in range(3)], 11)
        for s in range(GRID)
    ]
    nodal = []
    for parity in range(2):
        whole, rest = [], []
        for t in range(2):
            group = 2 * parity + t
            for s in range(GRID):
                whole.append(modal_ref[s, 8 * group : 8 * group + 8, :])
                rest.append(
                    last[s] if group == 3 else modal_ref[s, 32 + 8 * group : 40 + 8 * group, :]
                )
        turned = [jnp.concatenate(part, axis=0).T for part in (whole, rest)]
        nodal.append(jnp.concatenate([turned[0], turned[1][0:88]], axis=0))
        cross_ref[parity], chip_ref[parity] = to_partners(turned[0][0:40], turned[1][32:72])
    return nodal


def synthesize(nodal, table_ref):
    part = [
        dot_split(
            halves(nodal[parity]), (table_ref[0, parity], table_ref[1, parity]), ((1,), (0,))
        )
        for parity in range(2)
    ]
    scale = 1.0 / math.sqrt(KMODES)
    return scale * (part[0] + part[1]), scale * (part[0] - part[1])


def two_point(left, right):
    mean = (left * left + left * right + right * right) * (1.0 / 6.0)
    speed = jnp.maximum(jnp.abs(left), jnp.abs(right))
    return mean - 0.5 * speed * (right - left)


def row_rhs(field_ref, side_ref, lanes, rows):
    row = lax.broadcasted_iota(jnp.int32, (8, 128), 0)
    f = [field_ref[8 * n : 8 * n + 8, lanes] for n in range(25)]
    square = [v * v for v in f]
    out = {}
    for j in rows:
        for i in range(5):
            n = j * 5 + i
            plain = None
            power = None
            for other in range(5):
                terms = [(DIFFER[i][other], j * 5 + other), (DIFFER[j][other], other * 5 + i)]
                for weight, m in terms:
                    if weight == 0.0:
                        continue
                    weight = float(weight) / -3.0
                    plain = weight * f[m] if plain is None else plain + weight * f[m]
                    power = weight * square[m] if power is None else power + weight * square[m]
            total = power + f[n] * plain
            own = (i == 4) + (j == 4) - (i == 0) - (j == 0)
            if own:
                total = total + (5.0 * own) * square[n]
            if i == 0 or i == 4:
                at = j & 3
                side = side_ref[8 * (j // 4) : 8 * (j // 4) + 8, lanes]
                if at:
                    side = pltpu.roll(side, 8 - at if i == 0 else at, 0)
                if i == 0:
                    left = jnp.where(row == 0, side, pltpu.roll(f[j * 5 + 4], 1, 0))
                    total = total + 10.0 * two_point(left, f[n])
                else:
                    right = jnp.where(row == 7, side, pltpu.roll(f[j * 5], 7, 0))
                    total = total - 10.0 * two_point(f[n], right)
            out[n] = total
    return out


def each_lane_block(body):
    def step(block, carry):
        body(pl.ds(pl.multiple_of(block * 128, 128), 128))
        return carry

    lax.fori_loop(0, PLANES // 128, step, 0)


def volume_kernel(
    modal_ref, table_ref, field_ref, side_ref, edge_ref, modal_cross_ref, modal_chip_ref, cross_ref,
    chip_ref,
):
    nodal = turn(modal_ref, modal_cross_ref, modal_chip_ref)
    pair = synthesize(nodal, table_ref)
    for q in range(2):
        field_ref[:, HALF * q : HALF * q + HALF] = pair[q][0:200]
        side_ref[:, HALF * q : HALF * q + HALF] = pair[q][200:216]

    def body(lanes):
        total = row_rhs(field_ref, side_ref, lanes, (0, 4))
        for i in range(5):
            rows = slice(8 * i, 8 * i + 8)
            edge_ref[rows, lanes] = total[i]
            edge_ref[40 + 8 * i : 48 + 8 * i, lanes] = total[20 + i]
            cross_ref[rows, lanes], chip_ref[rows, lanes] = to_partners(total[i], total[20 + i])

    each_lane_block(body)


def project(planar, parity, table_ref):
    folded = planar[:, :HALF] + planar[:, HALF:] if parity == 0 else planar[:, :HALF] - planar[:, HALF:]
    high, low = halves(folded)
    both = dot(table_ref[:, parity].reshape(512, HALF), high, ((1,), (1,)))
    return dot(table_ref[0, parity], low, ((1,), (1,))) + both[256:] + both[:256]


def tendency(parity, from_rhs, from_flux):
    k = 2 * lax.broadcasted_iota(jnp.int32, (128, 128), 0) + parity
    scale = jnp.where(k == 0, 1.0, 2.0) * (math.sqrt(KMODES) / PLANES * STEP_SIZE)
    ratio = k.astype(jnp.float32) * (1.0 / KMODES)
    return (
        scale * (from_rhs[0:128] - ratio * from_flux[128:256]),
        scale * (from_rhs[128:256] + ratio * from_flux[0:128]),
    )


def inside_kernel(modal_ref, field_ref, side_ref, edge_ref, table_ref, out_ref, rhs_ref):
    last = [
        unpack_last([modal_ref[s, 32 + 8 * g : 40 + 8 * g, :] for g in range(3)], 11)
        for s in range(GRID)
    ]

    def body(lanes):
        total = row_rhs(field_ref, side_ref, lanes, (1, 2, 3))
        for n in range(5, 20):
            rhs_ref[8 * n - 40 : 8 * n - 32, lanes] = total[n]

    each_lane_block(body)
    field = field_ref[...]
    flux = 0.5 * field * field
    rhs = jnp.concatenate([edge_ref[0:40, :], rhs_ref[...], edge_ref[40:80, :]], axis=0)
    tail = jnp.zeros((56, PLANES), jnp.float32)
    flux = jnp.concatenate([flux, tail], axis=0)
    rhs = jnp.concatenate([rhs, tail], axis=0)
    for parity in range(2):
        from_rhs = project(rhs, parity, table_ref)
        from_flux = project(flux, parity, table_ref)
        for half in range(2):
            lanes = slice(128 * half, 128 * half + 128)
            change = tendency(parity, from_rhs[:, lanes], from_flux[:, lanes])
            for t in range(2):
                first = 16 * parity + 8 * t + 32 * half
                modal = jnp.concatenate(
                    last if first == 56 else [modal_ref[s, first : first + 8, :] for s in range(GRID)],
                    axis=0,
                )
                out_ref[parity, 128 * t : 128 * t + 128, lanes] = modal + change[t]


def lift_kernel(
    tag_ref, field_ref, cross_ref, chip_ref, table_ref, lift_ref, flux_ref, modal_ref, outer_ref
):
    bottom, top = at_ends()
    span = lax.axis_index("span")
    row = lax.broadcasted_iota(jnp.int32, (8, 128), 0)
    mirror = jnp.ones((8, 128), jnp.float32)
    for e in range(8):
        mirror = jnp.where((row == e) & (tag_ref[8 * span + e] == 1), -1.0, mirror)
    keep_lower = jnp.where(bottom, 0.0, 1.0)
    keep_upper = jnp.where(top, 0.0, 1.0)
    gap = jnp.zeros((48, 256), jnp.float32)
    outer = []
    for parity in range(2):
        below, above = from_partners(cross_ref[parity], chip_ref[parity])
        outer.append(jnp.concatenate([below, above], axis=0))
        modal_ref[parity] = jnp.concatenate(
            [keep_lower * below, keep_upper * above, gap], axis=0
        ).T
    pair = synthesize(outer, table_ref)
    for q in range(2):
        outer_ref[:, HALF * q : HALF * q + HALF] = pair[q]
    mirror = jnp.concatenate([mirror] * 6, axis=1)
    mirror = jnp.concatenate([mirror] * 5, axis=0)
    inside = field_ref[0:40, :]
    below = outer_ref[0:40, :]
    lift_ref[0:40, :] = 10.0 * two_point(jnp.where(bottom, mirror * inside, below), inside)
    flux_ref[0:40, :] = keep_lower * (0.5 * below * below)
    inside = field_ref[160:200, :]
    above = outer_ref[40:80, :]
    lift_ref[40:80, :] = 10.0 * two_point(inside, jnp.where(top, inside, above))
    flux_ref[40:80, :] = keep_upper * (0.5 * above * above)


def facing_kernel(
    inside_ref, lift_ref, flux_ref, facing_ref, cross_ref, chip_ref, table_ref, out_ref
):
    bottom, top = at_ends()
    below, above = from_partners(cross_ref[...], chip_ref[...])
    lift = lift_ref[0:40, :]
    rhs_lower = lift + jnp.where(bottom, 0.0, below - lift)
    lift = lift_ref[40:80, :]
    rhs_upper = jnp.where(top, 0.0, above + lift) - lift
    gap = jnp.zeros((48, PLANES), jnp.float32)
    planar = jnp.concatenate([rhs_lower, rhs_upper, gap, flux_ref[...], gap], axis=0)
    lane = lax.broadcasted_iota(jnp.int32, (128, 128), 1)
    whole, rest = [], []
    for parity in range(2):
        projected = project(planar, parity, table_ref)
        change = tendency(parity, projected[:, 0:128], projected[:, 128:256])
        for t in range(2):
            rows = slice(128 * t, 128 * t + 128)
            extra = change[t] + facing_ref[parity, rows, :]
            lower = jnp.where(lane < 40, extra, 0.0)
            upper = pltpu.roll(jnp.where(lane < 40, 0.0, extra), 120, 1)
            whole.append(inside_ref[parity, rows, 0:128] + lower)
            rest.append(inside_ref[parity, rows, 128:256] + upper)
    for s in range(GRID):
        part = slice(8 * s, 8 * s + 8)
        pack_rows(
            out_ref,
            s,
            jnp.concatenate([group[part] for group in whole], axis=0),
            jnp.concatenate([group[part] for group in rest], axis=0),
            9,
        )


def energy(values, shift):
    total = None
    for j in range(5):
        for i in range(5):
            n = j * 5 + i
            mass = float(WEIGHTS[j] * WEIGHTS[i])
            diagonal = VISCOUS * float(WEIGHTS[j] * STIFFNESS[i][i] + WEIGHTS[i] * STIFFNESS[j][j])
            value = (shift * mass + diagonal) * values[n]
            for other in range(i + 1, 5):
                weight = 2.0 * VISCOUS * float(WEIGHTS[j] * STIFFNESS[i][other])
                value = value + weight * values[j * 5 + other]
            for other in range(j + 1, 5):
                weight = 2.0 * VISCOUS * float(WEIGHTS[i] * STIFFNESS[j][other])
                value = value + weight * values[other * 5 + i]
            term = value * values[n]
            total = term if total is None else total + term
    return total


def at_ends():
    plane = lax.axis_index("plane")
    return plane == 0, plane == GRID - 1


def to_partners(low, high):
    odd = lax.axis_index("plane") % 2 == 1
    return jnp.where(odd, high, low), jnp.where(odd, low, high)


def from_partners(cross, chip):
    odd = lax.axis_index("plane") % 2 == 1
    return jnp.where(odd, chip, cross), jnp.where(odd, cross, chip)


def local_operator(values, shift, rows):
    out = []
    for j in rows:
        line = []
        for i in range(5):
            n = j * 5 + i
            mass = float(WEIGHTS[j] * WEIGHTS[i])
            diagonal = VISCOUS * float(WEIGHTS[j] * STIFFNESS[i][i] + WEIGHTS[i] * STIFFNESS[j][j])
            value = (shift * mass + diagonal) * values[n]
            for other in range(5):
                if other != i:
                    weight = VISCOUS * float(WEIGHTS[j] * STIFFNESS[i][other])
                    value = value + weight * values[j * 5 + other]
                if other != j:
                    weight = VISCOUS * float(WEIGHTS[i] * STIFFNESS[j][other])
                    value = value + weight * values[other * 5 + i]
            line.append(value)
        out += join_columns(line)
    return out


def join_columns(line):
    joint = line[4] + pltpu.roll(line[0], 127, 1)
    return [pltpu.roll(joint, 1, 1), *line[1:4], joint]


def store_edges(values, shift, edge_ref, cross_ref, chip_ref):
    image = local_operator(values, shift, (0, 4))
    for n in range(10):
        edge_ref[n] = image[n]
    for i in range(4):
        cross_ref[i], chip_ref[i] = to_partners(image[i], image[5 + i])


def fill_kernel(vector_ref, inner_ref):
    shift, _ = mode_terms()
    image = local_operator([vector_ref[n] for n in range(25)], shift, (1, 2, 3))
    for n in range(15):
        inner_ref[n] = image[n]


def unassembled(edge_ref, inner_ref):
    return (
        [edge_ref[n] for n in range(5)]
        + [inner_ref[n] for n in range(15)]
        + [edge_ref[5 + n] for n in range(5)]
    )


def assembled(edge_ref, inner_ref, cross_ref, chip_ref):
    values = unassembled(edge_ref, inner_ref)
    bottom, top = at_ends()
    for i in range(4):
        below, above = from_partners(cross_ref[i], chip_ref[i])
        values[i] = values[i] + jnp.where(bottom, 0.0, below)
        values[20 + i] = values[20 + i] + jnp.where(top, 0.0, above)
    values[4] = pltpu.roll(values[0], 127, 1)
    values[24] = pltpu.roll(values[20], 127, 1)
    return values


def mode_terms():
    row = lax.broadcasted_iota(jnp.int32, (32, 128), 0)
    mode_pair = 16 * lax.axis_index("span") + 2 * (row & 7) + (row >> 4)
    ratio = mode_pair.astype(jnp.float32) * (1.0 / KMODES)
    shift = 1.0 + SPAN_STIFF * ratio * ratio
    return shift, 0.2 * shift + 0.15


def inner(left, right):
    bottom, top = at_ends()
    total = None
    for j in range(5):
        part = None
        for i in range(5):
            term = left[j * 5 + i] * right[j * 5 + i]
            term = term if 0 < i < 4 else 0.5 * term
            part = term if part is None else part + term
        if j == 0:
            part = jnp.where(bottom, 1.0, 0.5) * part
        elif j == 4:
            part = jnp.where(top, 1.0, 0.5) * part
        total = part if total is None else total + part
    return total


def first_kernel(modal_ref, vector_ref, edge_ref, cross_ref, chip_ref):
    shift, _ = mode_terms()
    values = exchange_chunks([modal_ref[s, 0:32, :] for s in range(GRID)])
    rest = []
    for s in range(GRID):
        tiles = [modal_ref[s, 32 + 8 * g : 40 + 8 * g, :] for g in range(3)]
        rest.append(jnp.concatenate(tiles + [unpack_last(tiles, 9)], axis=0))
    values += exchange_chunks(rest)
    values = [float(WEIGHTS[n // 5] * WEIGHTS[n % 5]) * values[n] for n in range(25)]
    vector = []
    for j in range(5):
        vector += join_columns(values[5 * j : 5 * j + 5])
    for n in range(25):
        vector_ref[n] = vector[n]
    store_edges(vector, shift, edge_ref, cross_ref, chip_ref)


def second_kernel(
    edge_in_ref, inner_ref, cross_in_ref, chip_in_ref, before_ref, vector_ref, edge_ref, cross_ref,
    chip_ref,
):
    shift, center = mode_terms()
    applied = assembled(edge_in_ref, inner_ref, cross_in_ref, chip_in_ref)
    vector = [applied[n] - center * before_ref[n] for n in range(25)]
    for n in range(25):
        vector_ref[n] = vector[n]
    store_edges(vector, shift, edge_ref, cross_ref, chip_ref)


def mode_sums(moment, turn_ref):
    for t in range(4):
        turn_ref[pl.ds(t, 8, stride=4), :] = moment[8 * t : 8 * t + 8]
    return jnp.sum(turn_ref[...].T, axis=0, keepdims=True)


def early_kernel(first_ref, second_ref, edge_ref, inner_ref, packed_ref, turn_ref):
    _, center = mode_terms()
    first = [first_ref[n] for n in range(25)]
    second = [second_ref[n] for n in range(25)]
    square = inner(second, second)
    product = None
    image = unassembled(edge_ref, inner_ref)
    for n in range(25):
        term = second[n] * image[n]
        term = term if 0 < n % 5 < 4 else 0.5 * term
        product = term if product is None else product + term
    moments = [inner(first, first), inner(first, second), square, product - center * square]
    packed_ref[...] = jnp.zeros((8, 128), jnp.float32)
    for n, moment in enumerate(moments):
        packed_ref[n : n + 1, 0:32] = mode_sums(moment, turn_ref.at[n])


def store_natural(tiles, out_ref, row, column_ref):
    columns = merge_columns(tiles)
    for i in range(5):
        first = 32 * (5 * row + i)
        for t in range(4):
            column_ref[pl.ds(first + t, 8, stride=4), :] = columns[i][8 * t : 8 * t + 8]
        out_ref[row, :, 128 * i : 128 * i + 128] = column_ref[first : first + 32, :]


def natural_kernel(vector_ref, out_ref, column_ref):
    for j in range(5):
        store_natural([vector_ref[j * 5 + i] for i in range(5)], out_ref, j, column_ref)


def inner_kernel(inner_ref, second_ref, out_ref, column_ref):
    _, center = mode_terms()
    for j in range(1, 4):
        tiles = [
            inner_ref[n - 5] - center * second_ref[n] for n in range(5 * j, 5 * j + 5)
        ]
        store_natural(tiles, out_ref, j - 1, column_ref)


def third_kernel(
    edge_in_ref, inner_ref, cross_in_ref, chip_in_ref, second_ref, packed_ref, edge_ref, sums_ref,
    turn_ref, column_ref,
):
    shift, center = mode_terms()
    applied = assembled(edge_in_ref, inner_ref, cross_in_ref, chip_in_ref)
    second = [second_ref[n] for n in range(25)]
    third = [applied[n] - center * second[n] for n in range(25)]
    for row in range(2):
        store_natural(third[20 * row : 20 * row + 5], edge_ref, row, column_ref)
    fourth = inner(third, third)
    moments = [fourth, energy(third, shift) - center * fourth]
    sums_ref[0] = packed_ref[...]
    for n, moment in enumerate(moments):
        sums_ref[0, 4 + n : 5 + n, 0:32] = mode_sums(moment, turn_ref.at[n])
    sums = sums_ref[0]
    for p in range(1, GRID):
        sums_ref[p] = sums


def tree(terms):
    while len(terms) > 1:
        terms = [sum(terms[n + 1 : n + 2], terms[n]) for n in range(0, len(terms), 2)]
    return terms[0]


def combine_kernel(
    sums_ref, first_ref, second_ref, inner_ref, edge_ref, out_hbm, turn_ref, result_ref, sent
):
    total = tree([sums_ref[p] for p in range(GRID)])
    moment = [total[n : n + 1] for n in range(6)]
    lane = lax.broadcasted_iota(jnp.int32, (1, 128), 1)
    mode_pair = 16 * lax.axis_index("span") + (lane >> 1)
    ratio = mode_pair.astype(jnp.float32) * (1.0 / KMODES)
    center = 0.2 * (1.0 + SPAN_STIFF * ratio * ratio) + 0.15

    def product(left, right):
        return tree(
            [
                tree(
                    [
                        left[a] * right[power - a]
                        for a in range(len(left))
                        if 0 <= power - a < len(right)
                    ]
                )
                * moment[power]
                for power in range(len(left) + len(right) - 1)
            ]
        )

    def operator(c):
        shifted = [center * v for v in c] + [0.0]
        return [shifted[0]] + [shifted[a + 1] + c[a] for a in range(len(c))]

    residual = [jnp.ones((1, 128), jnp.float32)]
    direction = residual
    result = [0.0, 0.0, 0.0]
    norm = moment[0]
    inverse = 1.0 / norm
    for step in range(ITERS):
        applied = operator(direction)
        length = norm / product(direction, applied)
        for a in range(len(direction)):
            result[a] = result[a] + length * direction[a]
        if step < ITERS - 1:
            padded = residual + [0.0]
            residual = [padded[a] - length * applied[a] for a in range(len(applied))]
            fresh = product(residual, residual)
            ratio = fresh * inverse
            norm = fresh
            inverse = 1.0 / norm
            padded = direction + [0.0]
            direction = [residual[a] + ratio * padded[a] for a in range(len(residual))]
    turn_ref[...] = jnp.zeros((8, 128), jnp.float32)
    for a in range(3):
        turn_ref[a : a + 1, :] = result[a]
    turned = turn_ref[...].T[0:32]
    weight = [turned[:, a : a + 1] for a in range(3)]
    copies = []
    for j in range(5):
        third = inner_ref[j - 1] if 0 < j < 4 else edge_ref[j // 4]
        result_ref[j] = weight[0] * first_ref[j] + weight[1] * second_ref[j] + weight[2] * third
        copies.append(pltpu.make_async_copy(result_ref.at[j], out_hbm.at[j], sent.at[j]))
        copies[j].start()
    for copy in copies:
        copy.wait()


def call(kernel, out_shapes, *args, smem=(), anywhere=(), scratch=(), out_space=pltpu.VMEM, covers=True):
    vmem = pl.BlockSpec(memory_space=pltpu.VMEM)
    spaces = {n: pl.BlockSpec(memory_space=pltpu.SMEM) for n in smem}
    spaces |= {n: pl.BlockSpec(memory_space=pltpu.HBM) for n in anywhere}
    return pl.pallas_call(
        kernel,
        out_shape=[jax.ShapeDtypeStruct(s, jnp.float32) for s in out_shapes],
        in_specs=[spaces.get(n, vmem) for n in range(len(args))],
        out_specs=[pl.BlockSpec(memory_space=out_space)] * len(out_shapes),
        scratch_shapes=list(scratch),
        cost_estimate=None if covers else pl.CostEstimate(flops=0, bytes_accessed=0, transcendentals=0),
        compiler_params=pltpu.CompilerParams(vmem_limit_bytes=16 * 1024 * 1024),
    )(*args)


def swap_traces(cross, chip):
    partner = [(p, (p + 1) % GRID if p % 2 else (p - 1) % GRID) for p in range(GRID)]
    chip = lax.ppermute(chip, "plane", [(p, p ^ 1) for p in range(GRID)])
    cross = lax.ppermute(cross, "plane", partner)
    return cross, chip


def on_device(state, wall_tag):
    table = wave_table()
    (packed,) = call(
        pack_kernel, [(16, 56, 128)],
        pltpu.with_memory_space_constraint(jnp.transpose(state, (1, 0, 2)), pltpu.HBM),
        anywhere=(0,),
        scratch=[
            pltpu.VMEM((800, 128), jnp.float32), pltpu.VMEM((5, 32, 640), jnp.float32),
            pltpu.VMEM((640, 640), jnp.bfloat16), pltpu.SemaphoreType.DMA((5,)),
        ],
    )
    modal = lax.all_to_all(packed, "span", 0, 0, tiled=True)
    trace, rows = (2, 40, 256), (40, PLANES)
    field, side, edge, *modal_traces, cross, chip = call(
        volume_kernel,
        [(200, PLANES), (16, PLANES), (80, PLANES), trace, trace, rows, rows], modal, table,
    )
    modal_traces = swap_traces(*modal_traces)
    rhs_traces = swap_traces(cross, chip)
    (inside,) = call(
        inside_kernel, [(2, 256, 256)], modal, field, side, edge, table, covers=False,
        scratch=[pltpu.VMEM((120, PLANES), jnp.float32)],
    )
    lift, flux, facing = call(
        lift_kernel, [(80, PLANES), (80, PLANES), (2, 256, 128)], wall_tag, field,
        *modal_traces, table, smem=(0,), scratch=[pltpu.VMEM((80, PLANES), jnp.float32)],
        covers=False,
    )
    (sent,) = call(facing_kernel, [(16, 56, 128)], inside, lift, flux, facing, *rhs_traces, table)
    load = lax.all_to_all(sent, "span", 0, 0, tiled=True)
    nodes, trace = (25, 32, 128), (4, 32, 128)
    edges, inner_rows = (10, 32, 128), (15, 32, 128)
    first, edge, cross, chip = call(first_kernel, [nodes, edges, trace, trace], load)
    cross, chip = swap_traces(cross, chip)
    (filled,) = call(fill_kernel, [inner_rows], first)
    second, edge, cross, chip = call(
        second_kernel, [nodes, edges, trace, trace], edge, filled, cross, chip, first
    )
    cross, chip = swap_traces(cross, chip)
    (filled,) = call(fill_kernel, [inner_rows], second)
    (packed,) = call(
        early_kernel, [(8, 128)], first, second, edge, filled,
        scratch=[pltpu.VMEM((4, 32, 128), jnp.float32)],
    )
    natural = [
        call(
            natural_kernel, [(5, 32, 640)], vector,
            scratch=[pltpu.VMEM((800, 128), jnp.float32)],
        )[0]
        for vector in (first, second)
    ]
    (inside,) = call(
        inner_kernel, [(3, 32, 640)], filled, second,
        scratch=[pltpu.VMEM((480, 128), jnp.float32)],
    )
    edges, sums = call(
        third_kernel, [(2, 32, 640), (16, 8, 128)], edge, filled, cross, chip, second,
        packed,
        scratch=[pltpu.VMEM((2, 32, 128), jnp.float32), pltpu.VMEM((320, 128), jnp.float32)],
    )
    sums = lax.all_to_all(sums, "plane", 0, 0, tiled=True)
    (columns,) = call(
        combine_kernel, [(5, 32, 640)], sums, *natural, inside, edges,
        out_space=pltpu.HBM,
        scratch=[
            pltpu.VMEM((8, 128), jnp.float32), pltpu.VMEM((5, 32, 640), jnp.float32),
            pltpu.SemaphoreType.DMA((5,)),
        ],
    )
    return jnp.transpose(columns, (1, 0, 2))


def solution(mesh):
    return jax.shard_map(
        on_device,
        mesh=mesh,
        in_specs=(P("span", "plane", None), P()),
        out_specs=P("span", "plane", None),
        check_vma=False,
    )
```

```python
import math

import jax
import jax.numpy as jnp
import numpy as np
from jax import lax
from jax.experimental import pallas as pl
from jax.experimental.pallas import tpu as pltpu
from jax.sharding import PartitionSpec as P


KMODES = 256
PLANES = 768
HALF = 384
ITERS = 3
GRID = 16
STEP_SIZE = 0.03
VISCOUS = 0.05
SPAN_STIFF = 4.0


def gll_tables():
    abscissae = np.array([-1.0, -math.sqrt(3.0 / 7.0), 0.0, math.sqrt(3.0 / 7.0), 1.0])
    weights = np.array([0.1, 49.0 / 90.0, 32.0 / 45.0, 49.0 / 90.0, 0.1])
    squared = abscissae * abscissae
    legendre = (35.0 * squared * squared - 30.0 * squared + 3.0) / 8.0
    identity = np.eye(5)
    spacing = abscissae[:, None] - abscissae[None, :] + identity
    differ = np.where(identity > 0, 0.0, legendre[:, None] / legendre[None, :] / spacing)
    differ[0, 0] = -5.0
    differ[4, 4] = 5.0
    stiffness = differ.T @ (weights[:, None] * differ)
    return differ, weights, stiffness


DIFFER, WEIGHTS, STIFFNESS = gll_tables()


def split_table(table):
    high = table.astype(np.float32).astype(jnp.bfloat16)
    low = (table - high.astype(np.float64)).astype(np.float32).astype(jnp.bfloat16)
    return jnp.asarray(np.stack([high, low]))


def wave_table():
    plane = np.arange(HALF)
    waves = []
    for parity in range(2):
        k = 2 * np.arange(128) + parity
        angle = (k[:, None] * plane[None, :] % PLANES) * (2.0 * math.pi / PLANES)
        waves.append(np.concatenate([np.cos(angle), np.sin(angle)]))
    return split_table(np.stack(waves))


def dot(left, right, contract):
    return lax.dot_general(
        left, right, (contract, ((), ())), preferred_element_type=jnp.float32
    )


def halves(value):
    high = value.astype(jnp.bfloat16)
    low = (value - high.astype(jnp.float32)).astype(jnp.bfloat16)
    return high, low


def dot_split(left, right, contract):
    (left_high, left_low), (right_high, right_low) = left, right
    return (
        dot(left_high, right_low, contract)
        + dot(left_low, right_high, contract)
        + dot(left_high, right_high, contract)
    )


def lanes_of(values, index):
    return jnp.take_along_axis(values, index, axis=1)


def merge_columns(tiles):
    lane = lax.broadcasted_iota(jnp.int32, tiles[0].shape, 1)
    out = []
    for t in range(5):
        column = lane + 128 * t
        element = (column * 13108) >> 16
        node = column - 5 * element
        picked = lanes_of(tiles[0], element)
        for i in range(1, 5):
            picked = jnp.where(node == i, lanes_of(tiles[i], element), picked)
        out.append(picked)
    return out


def exchange_chunks(values):
    values = list(values)
    lane = lax.broadcasted_iota(jnp.int32, values[0].shape, 1)
    for bit in (1, 2, 4, 8):
        upper = (lane & (8 * bit)) != 0
        other = lane ^ (8 * bit)
        for a in range(16):
            if a & bit == 0:
                first, second = values[a], values[a | bit]
                if first is None:
                    continue
                if second is None:
                    second = jnp.zeros_like(first)
                moved = jnp.where(upper, first, second)
                if bit == 8:
                    moved = pltpu.roll(moved, 64, 1)
                else:
                    moved = lanes_of(moved, other)
                values[a] = jnp.where(upper, moved, first)
                values[a | bit] = jnp.where(upper, second, moved)
    return values


def column_order():
    column = lax.broadcasted_iota(jnp.int32, (640, 128), 0)
    element = lax.broadcasted_iota(jnp.int32, (640, 128), 1)
    tiles = [jnp.where(column == 5 * element + i, 1.0, 0.0).astype(jnp.bfloat16) for i in range(5)]
    return jnp.concatenate(tiles, axis=1)


def pack_rows(out_ref, d, whole, rest, count):
    out_ref[d, 0:32, :] = whole
    lane = lax.broadcasted_iota(jnp.int32, (8, 128), 1)
    free = 16 - count
    for g in range(3):
        tile = rest[8 * g : 8 * g + 8]
        if g * free < count:
            shift = 8 * (count - g * free)
            tile = jnp.where(lane < 8 * count, tile, pltpu.roll(rest[24:32], shift % 128, 1))
        out_ref[d, 32 + 8 * g : 40 + 8 * g, :] = tile


def unpack_last(tiles, count):
    lane = lax.broadcasted_iota(jnp.int32, (8, 128), 1)
    free = 16 - count
    last = pltpu.roll(tiles[0], 128 - 8 * count, 1)
    for g in range(1, 3):
        if g * free < count:
            shift = 8 * (count - g * free)
            last = jnp.where(lane < 8 * g * free, last, pltpu.roll(tiles[g], (128 - shift) % 128, 1))
    return last


def pack_kernel(state_hbm, out_ref, chunk_ref, state_ref, order_ref, arrived):
    copy = pltpu.make_async_copy(state_hbm, state_ref, arrived)
    copy.start()
    order_ref[...] = column_order()
    copy.wait()
    stacked = jnp.concatenate([state_ref[j] for j in range(5)], axis=0)
    order = order_ref[...]
    contract = ((1,), (0,))
    both = dot(jnp.concatenate(halves(stacked), axis=0), order, contract)
    nodes = both[160:] + both[:160]
    for i in range(5):
        chunk_ref[160 * i : 160 * i + 160, :] = nodes[:, 128 * i : 128 * i + 128]
    chunk = [
        jnp.concatenate(
            [chunk_ref[pl.ds(160 * i + 32 * j + t, 8, stride=4), :] for t in range(4)], axis=0
        )
        for j in range(5)
        for i in range(5)
    ]
    lane = lax.broadcasted_iota(jnp.int32, (32, 128), 1) & 7
    sides = [jnp.zeros((32, 128), jnp.float32), jnp.zeros((32, 128), jnp.float32)]
    for j in range(5):
        at = j & 3
        side = jnp.where(lane == at, pltpu.roll(chunk[j * 5 + 4], 1 + at, 1), sides[j // 4])
        sides[j // 4] = jnp.where(lane == 7 - at, pltpu.roll(chunk[j * 5], 127 - at, 1), side)
    chunk = chunk + sides
    whole = exchange_chunks(chunk[:16])
    rest = exchange_chunks(chunk[16:] + [None] * 5)
    for d in range(GRID):
        pack_rows(out_ref, d, whole[d], rest[d], 11)


def turn(modal_ref, cross_ref, chip_ref):
    last = [
        unpack_last([modal_ref[s, 32 + 8 * g : 40 + 8 * g, :] for g in range(3)], 11)
        for s in range(GRID)
    ]
    nodal = []
    for parity in range(2):
        whole, rest = [], []
        for t in range(2):
            group = 2 * parity + t
            for s in range(GRID):
                whole.append(modal_ref[s, 8 * group : 8 * group + 8, :])
                rest.append(
                    last[s] if group == 3 else modal_ref[s, 32 + 8 * group : 40 + 8 * group, :]
                )
        turned = [jnp.concatenate(part, axis=0).T for part in (whole, rest)]
        nodal.append(jnp.concatenate([turned[0], turned[1][0:88]], axis=0))
        cross_ref[parity], chip_ref[parity] = to_partners(turned[0][0:40], turned[1][32:72])
    return nodal


def synthesize(nodal, table_ref):
    part = [
        dot_split(
            halves(nodal[parity]), (table_ref[0, parity], table_ref[1, parity]), ((1,), (0,))
        )
        for parity in range(2)
    ]
    scale = 1.0 / math.sqrt(KMODES)
    return scale * (part[0] + part[1]), scale * (part[0] - part[1])


def two_point(left, right):
    mean = (left * left + left * right + right * right) * (1.0 / 6.0)
    speed = jnp.maximum(jnp.abs(left), jnp.abs(right))
    return mean - 0.5 * speed * (right - left)


def row_rhs(field_ref, side_ref, lanes, rows):
    row = lax.broadcasted_iota(jnp.int32, (8, 128), 0)
    f = [field_ref[8 * n : 8 * n + 8, lanes] for n in range(25)]
    square = [v * v for v in f]
    out = {}
    for j in rows:
        for i in range(5):
            n = j * 5 + i
            plain = None
            power = None
            for other in range(5):
                terms = [(DIFFER[i][other], j * 5 + other), (DIFFER[j][other], other * 5 + i)]
                for weight, m in terms:
                    if weight == 0.0:
                        continue
                    weight = float(weight) / -3.0
                    plain = weight * f[m] if plain is None else plain + weight * f[m]
                    power = weight * square[m] if power is None else power + weight * square[m]
            total = power + f[n] * plain
            own = (i == 4) + (j == 4) - (i == 0) - (j == 0)
            if own:
                total = total + (5.0 * own) * square[n]
            if i == 0 or i == 4:
                at = j & 3
                side = side_ref[8 * (j // 4) : 8 * (j // 4) + 8, lanes]
                if at:
                    side = pltpu.roll(side, 8 - at if i == 0 else at, 0)
                if i == 0:
                    left = jnp.where(row == 0, side, pltpu.roll(f[j * 5 + 4], 1, 0))
                    total = total + 10.0 * two_point(left, f[n])
                else:
                    right = jnp.where(row == 7, side, pltpu.roll(f[j * 5], 7, 0))
                    total = total - 10.0 * two_point(f[n], right)
            out[n] = total
    return out


def each_lane_block(body):
    def step(block, carry):
        body(pl.ds(pl.multiple_of(block * 128, 128), 128))
        return carry

    lax.fori_loop(0, PLANES // 128, step, 0)


def volume_kernel(
    modal_ref, table_ref, field_ref, side_ref, edge_ref, modal_cross_ref, modal_chip_ref, cross_ref,
    chip_ref,
):
    nodal = turn(modal_ref, modal_cross_ref, modal_chip_ref)
    pair = synthesize(nodal, table_ref)
    for q in range(2):
        field_ref[:, HALF * q : HALF * q + HALF] = pair[q][0:200]
        side_ref[:, HALF * q : HALF * q + HALF] = pair[q][200:216]

    def body(lanes):
        total = row_rhs(field_ref, side_ref, lanes, (0, 4))
        for i in range(5):
            rows = slice(8 * i, 8 * i + 8)
            edge_ref[rows, lanes] = total[i]
            edge_ref[40 + 8 * i : 48 + 8 * i, lanes] = total[20 + i]
            cross_ref[rows, lanes], chip_ref[rows, lanes] = to_partners(total[i], total[20 + i])

    each_lane_block(body)


def project(planar, parity, table_ref):
    folded = planar[:, :HALF] + planar[:, HALF:] if parity == 0 else planar[:, :HALF] - planar[:, HALF:]
    high, low = halves(folded)
    both = dot(table_ref[:, parity].reshape(512, HALF), high, ((1,), (1,)))
    return dot(table_ref[0, parity], low, ((1,), (1,))) + both[256:] + both[:256]


def tendency(parity, from_rhs, from_flux):
    k = 2 * lax.broadcasted_iota(jnp.int32, (128, 128), 0) + parity
    scale = jnp.where(k == 0, 1.0, 2.0) * (math.sqrt(KMODES) / PLANES * STEP_SIZE)
    ratio = k.astype(jnp.float32) * (1.0 / KMODES)
    return (
        scale * (from_rhs[0:128] - ratio * from_flux[128:256]),
        scale * (from_rhs[128:256] + ratio * from_flux[0:128]),
    )


def inside_kernel(modal_ref, field_ref, side_ref, edge_ref, table_ref, out_ref, rhs_ref):
    last = [
        unpack_last([modal_ref[s, 32 + 8 * g : 40 + 8 * g, :] for g in range(3)], 11)
        for s in range(GRID)
    ]

    def body(lanes):
        total = row_rhs(field_ref, side_ref, lanes, (1, 2, 3))
        for n in range(5, 20):
            rhs_ref[8 * n - 40 : 8 * n - 32, lanes] = total[n]

    each_lane_block(body)
    field = field_ref[...]
    flux = 0.5 * field * field
    rhs = jnp.concatenate([edge_ref[0:40, :], rhs_ref[...], edge_ref[40:80, :]], axis=0)
    tail = jnp.zeros((56, PLANES), jnp.float32)
    flux = jnp.concatenate([flux, tail], axis=0)
    rhs = jnp.concatenate([rhs, tail], axis=0)
    for parity in range(2):
        from_rhs = project(rhs, parity, table_ref)
        from_flux = project(flux, parity, table_ref)
        for half in range(2):
            lanes = slice(128 * half, 128 * half + 128)
            change = tendency(parity, from_rhs[:, lanes], from_flux[:, lanes])
            for t in range(2):
                first = 16 * parity + 8 * t + 32 * half
                modal = jnp.concatenate(
                    last if first == 56 else [modal_ref[s, first : first + 8, :] for s in range(GRID)],
                    axis=0,
                )
                out_ref[parity, 128 * t : 128 * t + 128, lanes] = modal + change[t]


def lift_kernel(
    tag_ref, field_ref, cross_ref, chip_ref, table_ref, lift_ref, flux_ref, modal_ref, outer_ref
):
    bottom, top = at_ends()
    span = lax.axis_index("span")
    row = lax.broadcasted_iota(jnp.int32, (8, 128), 0)
    mirror = jnp.ones((8, 128), jnp.float32)
    for e in range(8):
        mirror = jnp.where((row == e) & (tag_ref[8 * span + e] == 1), -1.0, mirror)
    keep_lower = jnp.where(bottom, 0.0, 1.0)
    keep_upper = jnp.where(top, 0.0, 1.0)
    gap = jnp.zeros((48, 256), jnp.float32)
    outer = []
    for parity in range(2):
        below, above = from_partners(cross_ref[parity], chip_ref[parity])
        outer.append(jnp.concatenate([below, above], axis=0))
        modal_ref[parity] = jnp.concatenate(
            [keep_lower * below, keep_upper * above, gap], axis=0
        ).T
    pair = synthesize(outer, table_ref)
    for q in range(2):
        outer_ref[:, HALF * q : HALF * q + HALF] = pair[q]
    mirror = jnp.concatenate([mirror] * 6, axis=1)
    mirror = jnp.concatenate([mirror] * 5, axis=0)
    inside = field_ref[0:40, :]
    below = outer_ref[0:40, :]
    lift_ref[0:40, :] = 10.0 * two_point(jnp.where(bottom, mirror * inside, below), inside)
    flux_ref[0:40, :] = keep_lower * (0.5 * below * below)
    inside = field_ref[160:200, :]
    above = outer_ref[40:80, :]
    lift_ref[40:80, :] = 10.0 * two_point(inside, jnp.where(top, inside, above))
    flux_ref[40:80, :] = keep_upper * (0.5 * above * above)


def facing_kernel(
    inside_ref, lift_ref, flux_ref, facing_ref, cross_ref, chip_ref, table_ref, out_ref
):
    bottom, top = at_ends()
    below, above = from_partners(cross_ref[...], chip_ref[...])
    lift = lift_ref[0:40, :]
    rhs_lower = lift + jnp.where(bottom, 0.0, below - lift)
    lift = lift_ref[40:80, :]
    rhs_upper = jnp.where(top, 0.0, above + lift) - lift
    gap = jnp.zeros((48, PLANES), jnp.float32)
    planar = jnp.concatenate([rhs_lower, rhs_upper, gap, flux_ref[...], gap], axis=0)
    lane = lax.broadcasted_iota(jnp.int32, (128, 128), 1)
    whole, rest = [], []
    for parity in range(2):
        projected = project(planar, parity, table_ref)
        change = tendency(parity, projected[:, 0:128], projected[:, 128:256])
        for t in range(2):
            rows = slice(128 * t, 128 * t + 128)
            extra = change[t] + facing_ref[parity, rows, :]
            lower = jnp.where(lane < 40, extra, 0.0)
            upper = pltpu.roll(jnp.where(lane < 40, 0.0, extra), 120, 1)
            whole.append(inside_ref[parity, rows, 0:128] + lower)
            rest.append(inside_ref[parity, rows, 128:256] + upper)
    for s in range(GRID):
        part = slice(8 * s, 8 * s + 8)
        pack_rows(
            out_ref,
            s,
            jnp.concatenate([group[part] for group in whole], axis=0),
            jnp.concatenate([group[part] for group in rest], axis=0),
            9,
        )


def energy(values, shift):
    total = None
    for j in range(5):
        for i in range(5):
            n = j * 5 + i
            mass = float(WEIGHTS[j] * WEIGHTS[i])
            diagonal = VISCOUS * float(WEIGHTS[j] * STIFFNESS[i][i] + WEIGHTS[i] * STIFFNESS[j][j])
            value = (shift * mass + diagonal) * values[n]
            for other in range(i + 1, 5):
                weight = 2.0 * VISCOUS * float(WEIGHTS[j] * STIFFNESS[i][other])
                value = value + weight * values[j * 5 + other]
            for other in range(j + 1, 5):
                weight = 2.0 * VISCOUS * float(WEIGHTS[i] * STIFFNESS[j][other])
                value = value + weight * values[other * 5 + i]
            term = value * values[n]
            total = term if total is None else total + term
    return total


def at_ends():
    plane = lax.axis_index("plane")
    return plane == 0, plane == GRID - 1


def to_partners(low, high):
    odd = lax.axis_index("plane") % 2 == 1
    return jnp.where(odd, high, low), jnp.where(odd, low, high)


def from_partners(cross, chip):
    odd = lax.axis_index("plane") % 2 == 1
    return jnp.where(odd, chip, cross), jnp.where(odd, cross, chip)


def local_operator(values, shift, rows):
    out = []
    for j in rows:
        line = []
        for i in range(5):
            n = j * 5 + i
            mass = float(WEIGHTS[j] * WEIGHTS[i])
            diagonal = VISCOUS * float(WEIGHTS[j] * STIFFNESS[i][i] + WEIGHTS[i] * STIFFNESS[j][j])
            value = (shift * mass + diagonal) * values[n]
            for other in range(5):
                if other != i:
                    weight = VISCOUS * float(WEIGHTS[j] * STIFFNESS[i][other])
                    value = value + weight * values[j * 5 + other]
                if other != j:
                    weight = VISCOUS * float(WEIGHTS[i] * STIFFNESS[j][other])
                    value = value + weight * values[other * 5 + i]
            line.append(value)
        out += join_columns(line)
    return out


def join_columns(line):
    joint = line[4] + pltpu.roll(line[0], 127, 1)
    return [pltpu.roll(joint, 1, 1), *line[1:4], joint]


def store_edges(values, shift, edge_ref, cross_ref, chip_ref):
    image = local_operator(values, shift, (0, 4))
    for n in range(10):
        edge_ref[n] = image[n]
    for i in range(4):
        cross_ref[i], chip_ref[i] = to_partners(image[i], image[5 + i])


def fill_kernel(vector_ref, inner_ref):
    shift, _ = mode_terms()
    image = local_operator([vector_ref[n] for n in range(25)], shift, (1, 2, 3))
    for n in range(15):
        inner_ref[n] = image[n]


def unassembled(edge_ref, inner_ref):
    return (
        [edge_ref[n] for n in range(5)]
        + [inner_ref[n] for n in range(15)]
        + [edge_ref[5 + n] for n in range(5)]
    )


def assembled(edge_ref, inner_ref, cross_ref, chip_ref):
    values = unassembled(edge_ref, inner_ref)
    bottom, top = at_ends()
    for i in range(4):
        below, above = from_partners(cross_ref[i], chip_ref[i])
        values[i] = values[i] + jnp.where(bottom, 0.0, below)
        values[20 + i] = values[20 + i] + jnp.where(top, 0.0, above)
    values[4] = pltpu.roll(values[0], 127, 1)
    values[24] = pltpu.roll(values[20], 127, 1)
    return values


def mode_terms():
    row = lax.broadcasted_iota(jnp.int32, (32, 128), 0)
    mode_pair = 16 * lax.axis_index("span") + 2 * (row & 7) + (row >> 4)
    ratio = mode_pair.astype(jnp.float32) * (1.0 / KMODES)
    shift = 1.0 + SPAN_STIFF * ratio * ratio
    return shift, 0.2 * shift + 0.15


def inner(left, right):
    bottom, top = at_ends()
    total = None
    for j in range(5):
        part = None
        for i in range(5):
            term = left[j * 5 + i] * right[j * 5 + i]
            term = term if 0 < i < 4 else 0.5 * term
            part = term if part is None else part + term
        if j == 0:
            part = jnp.where(bottom, 1.0, 0.5) * part
        elif j == 4:
            part = jnp.where(top, 1.0, 0.5) * part
        total = part if total is None else total + part
    return total


def first_kernel(modal_ref, vector_ref, edge_ref, cross_ref, chip_ref):
    shift, _ = mode_terms()
    values = exchange_chunks([modal_ref[s, 0:32, :] for s in range(GRID)])
    rest = []
    for s in range(GRID):
        tiles = [modal_ref[s, 32 + 8 * g : 40 + 8 * g, :] for g in range(3)]
        rest.append(jnp.concatenate(tiles + [unpack_last(tiles, 9)], axis=0))
    values += exchange_chunks(rest)
    values = [float(WEIGHTS[n // 5] * WEIGHTS[n % 5]) * values[n] for n in range(25)]
    vector = []
    for j in range(5):
        vector += join_columns(values[5 * j : 5 * j + 5])
    for n in range(25):
        vector_ref[n] = vector[n]
    store_edges(vector, shift, edge_ref, cross_ref, chip_ref)


def second_kernel(
    edge_in_ref, inner_ref, cross_in_ref, chip_in_ref, before_ref, vector_ref, edge_ref, cross_ref,
    chip_ref,
):
    shift, center = mode_terms()
    applied = assembled(edge_in_ref, inner_ref, cross_in_ref, chip_in_ref)
    vector = [applied[n] - center * before_ref[n] for n in range(25)]
    for n in range(25):
        vector_ref[n] = vector[n]
    store_edges(vector, shift, edge_ref, cross_ref, chip_ref)


def mode_sums(moment, turn_ref):
    for t in range(4):
        turn_ref[pl.ds(t, 8, stride=4), :] = moment[8 * t : 8 * t + 8]
    return jnp.sum(turn_ref[...].T, axis=0, keepdims=True)


def early_kernel(first_ref, second_ref, edge_ref, inner_ref, packed_ref, turn_ref):
    _, center = mode_terms()
    first = [first_ref[n] for n in range(25)]
    second = [second_ref[n] for n in range(25)]
    square = inner(second, second)
    product = None
    image = unassembled(edge_ref, inner_ref)
    for n in range(25):
        term = second[n] * image[n]
        term = term if 0 < n % 5 < 4 else 0.5 * term
        product = term if product is None else product + term
    moments = [inner(first, first), inner(first, second), square, product - center * square]
    packed_ref[...] = jnp.zeros((8, 128), jnp.float32)
    for n, moment in enumerate(moments):
        packed_ref[n : n + 1, 0:32] = mode_sums(moment, turn_ref.at[n])


def store_natural(tiles, out_ref, row, column_ref):
    columns = merge_columns(tiles)
    for i in range(5):
        first = 32 * (5 * row + i)
        for t in range(4):
            column_ref[pl.ds(first + t, 8, stride=4), :] = columns[i][8 * t : 8 * t + 8]
        out_ref[row, :, 128 * i : 128 * i + 128] = column_ref[first : first + 32, :]


def natural_kernel(vector_ref, out_ref, column_ref):
    for j in range(5):
        store_natural([vector_ref[j * 5 + i] for i in range(5)], out_ref, j, column_ref)


def inner_kernel(inner_ref, second_ref, out_ref, column_ref):
    _, center = mode_terms()
    for j in range(1, 4):
        tiles = [
            inner_ref[n - 5] - center * second_ref[n] for n in range(5 * j, 5 * j + 5)
        ]
        store_natural(tiles, out_ref, j - 1, column_ref)


def third_kernel(
    edge_in_ref, inner_ref, cross_in_ref, chip_in_ref, second_ref, packed_ref, edge_ref, sums_ref,
    turn_ref, column_ref,
):
    shift, center = mode_terms()
    applied = assembled(edge_in_ref, inner_ref, cross_in_ref, chip_in_ref)
    second = [second_ref[n] for n in range(25)]
    third = [applied[n] - center * second[n] for n in range(25)]
    for row in range(2):
        store_natural(third[20 * row : 20 * row + 5], edge_ref, row, column_ref)
    fourth = inner(third, third)
    moments = [fourth, energy(third, shift) - center * fourth]
    sums_ref[0] = packed_ref[...]
    for n, moment in enumerate(moments):
        sums_ref[0, 4 + n : 5 + n, 0:32] = mode_sums(moment, turn_ref.at[n])
    sums = sums_ref[0]
    for p in range(1, GRID):
        sums_ref[p] = sums


def tree(terms):
    while len(terms) > 1:
        terms = [sum(terms[n + 1 : n + 2], terms[n]) for n in range(0, len(terms), 2)]
    return terms[0]


def combine_kernel(
    sums_ref, first_ref, second_ref, inner_ref, edge_ref, out_hbm, turn_ref, result_ref, sent
):
    total = tree([sums_ref[p] for p in range(GRID)])
    moment = [total[n : n + 1] for n in range(6)]
    lane = lax.broadcasted_iota(jnp.int32, (1, 128), 1)
    mode_pair = 16 * lax.axis_index("span") + (lane >> 1)
    ratio = mode_pair.astype(jnp.float32) * (1.0 / KMODES)
    center = 0.2 * (1.0 + SPAN_STIFF * ratio * ratio) + 0.15

    def product(left, right):
        return tree(
            [
                tree(
                    [
                        left[a] * right[power - a]
                        for a in range(len(left))
                        if 0 <= power - a < len(right)
                    ]
                )
                * moment[power]
                for power in range(len(left) + len(right) - 1)
            ]
        )

    def operator(c):
        shifted = [center * v for v in c] + [0.0]
        return [shifted[0]] + [shifted[a + 1] + c[a] for a in range(len(c))]

    residual = [jnp.ones((1, 128), jnp.float32)]
    direction = residual
    result = [0.0, 0.0, 0.0]
    norm = moment[0]
    inverse = 1.0 / norm
    for step in range(ITERS):
        applied = operator(direction)
        length = norm / product(direction, applied)
        for a in range(len(direction)):
            result[a] = result[a] + length * direction[a]
        if step < ITERS - 1:
            padded = residual + [0.0]
            residual = [padded[a] - length * applied[a] for a in range(len(applied))]
            fresh = product(residual, residual)
            ratio = fresh * inverse
            norm = fresh
            inverse = 1.0 / norm
            padded = direction + [0.0]
            direction = [residual[a] + ratio * padded[a] for a in range(len(residual))]
    turn_ref[...] = jnp.zeros((8, 128), jnp.float32)
    for a in range(3):
        turn_ref[a : a + 1, :] = result[a]
    turned = turn_ref[...].T[0:32]
    weight = [turned[:, a : a + 1] for a in range(3)]
    copies = []
    for j in range(5):
        third = inner_ref[j - 1] if 0 < j < 4 else edge_ref[j // 4]
        result_ref[j] = weight[0] * first_ref[j] + weight[1] * second_ref[j] + weight[2] * third
        copies.append(pltpu.make_async_copy(result_ref.at[j], out_hbm.at[j], sent.at[j]))
        copies[j].start()
    for copy in copies:
        copy.wait()


def call(kernel, out_shapes, *args, smem=(), anywhere=(), scratch=(), out_space=pltpu.VMEM, covers=True):
    vmem = pl.BlockSpec(memory_space=pltpu.VMEM)
    spaces = {n: pl.BlockSpec(memory_space=pltpu.SMEM) for n in smem}
    spaces |= {n: pl.BlockSpec(memory_space=pltpu.HBM) for n in anywhere}
    return pl.pallas_call(
        kernel,
        out_shape=[jax.ShapeDtypeStruct(s, jnp.float32) for s in out_shapes],
        in_specs=[spaces.get(n, vmem) for n in range(len(args))],
        out_specs=[pl.BlockSpec(memory_space=out_space)] * len(out_shapes),
        scratch_shapes=list(scratch),
        cost_estimate=None if covers else pl.CostEstimate(flops=0, bytes_accessed=0, transcendentals=0),
        compiler_params=pltpu.CompilerParams(vmem_limit_bytes=16 * 1024 * 1024),
    )(*args)


def swap_traces(cross, chip):
    partner = [(p, min(p + 1, GRID - 1) if p % 2 else max(p - 1, 0)) for p in range(GRID)]
    chip = lax.ppermute(chip, "plane", [(p, p ^ 1) for p in range(GRID)])
    cross = lax.ppermute(cross, "plane", partner)
    return cross, chip


def on_device(state, wall_tag):
    table = wave_table()
    (packed,) = call(
        pack_kernel, [(16, 56, 128)],
        pltpu.with_memory_space_constraint(jnp.transpose(state, (1, 0, 2)), pltpu.HBM),
        anywhere=(0,),
        scratch=[
            pltpu.VMEM((800, 128), jnp.float32), pltpu.VMEM((5, 32, 640), jnp.float32),
            pltpu.VMEM((640, 640), jnp.bfloat16), pltpu.SemaphoreType.DMA(()),
        ],
    )
    modal = lax.all_to_all(packed, "span", 0, 0, tiled=True)
    trace, rows = (2, 40, 256), (40, PLANES)
    field, side, edge, *modal_traces, cross, chip = call(
        volume_kernel,
        [(200, PLANES), (16, PLANES), (80, PLANES), trace, trace, rows, rows], modal, table,
    )
    modal_traces = swap_traces(*modal_traces)
    rhs_traces = swap_traces(cross, chip)
    (inside,) = call(
        inside_kernel, [(2, 256, 256)], modal, field, side, edge, table, covers=False,
        scratch=[pltpu.VMEM((120, PLANES), jnp.float32)],
    )
    lift, flux, facing = call(
        lift_kernel, [(80, PLANES), (80, PLANES), (2, 256, 128)], wall_tag, field,
        *modal_traces, table, smem=(0,), scratch=[pltpu.VMEM((80, PLANES), jnp.float32)],
        covers=False,
    )
    (sent,) = call(facing_kernel, [(16, 56, 128)], inside, lift, flux, facing, *rhs_traces, table)
    load = lax.all_to_all(sent, "span", 0, 0, tiled=True)
    nodes, trace = (25, 32, 128), (4, 32, 128)
    edges, inner_rows = (10, 32, 128), (15, 32, 128)
    first, edge, cross, chip = call(first_kernel, [nodes, edges, trace, trace], load)
    cross, chip = swap_traces(cross, chip)
    (filled,) = call(fill_kernel, [inner_rows], first)
    second, edge, cross, chip = call(
        second_kernel, [nodes, edges, trace, trace], edge, filled, cross, chip, first
    )
    cross, chip = swap_traces(cross, chip)
    (filled,) = call(fill_kernel, [inner_rows], second)
    (packed,) = call(
        early_kernel, [(8, 128)], first, second, edge, filled,
        scratch=[pltpu.VMEM((4, 32, 128), jnp.float32)],
    )
    natural = [
        call(
            natural_kernel, [(5, 32, 640)], vector,
            scratch=[pltpu.VMEM((800, 128), jnp.float32)],
        )[0]
        for vector in (first, second)
    ]
    (inside,) = call(
        inner_kernel, [(3, 32, 640)], filled, second,
        scratch=[pltpu.VMEM((480, 128), jnp.float32)],
    )
    edges, sums = call(
        third_kernel, [(2, 32, 640), (16, 8, 128)], edge, filled, cross, chip, second,
        packed,
        scratch=[pltpu.VMEM((2, 32, 128), jnp.float32), pltpu.VMEM((320, 128), jnp.float32)],
    )
    sums = lax.all_to_all(sums, "plane", 0, 0, tiled=True)
    (columns,) = call(
        combine_kernel, [(5, 32, 640)], sums, *natural, inside, edges,
        out_space=pltpu.HBM,
        scratch=[
            pltpu.VMEM((8, 128), jnp.float32), pltpu.VMEM((5, 32, 640), jnp.float32),
            pltpu.SemaphoreType.DMA((5,)),
        ],
    )
    return jnp.transpose(columns, (1, 0, 2))


def solution(mesh):
    return jax.shard_map(
        on_device,
        mesh=mesh,
        in_specs=(P("span", "plane", None), P()),
        out_specs=P("span", "plane", None),
        check_vma=False,
    )
```
